32 devices in a mesh: ctx: 8 (over z, y), fsdp: 4 (over x, core).
Axes of the slice: x: 2, y: 2, z: 4, core: 2. Of those that a mesh axis runs over, the one named last changes fastest.
Arguments:
- tokens: bfloat16 [4, 8, 2, 128, 1024], P('fsdp', 'ctx'), may hold values from -6 to 6
- doc_starts: int32 [4, 8, 2, 128], P('fsdp', 'ctx'), may hold values from 0 to 2047, as said below
- expert_ids: int32 [4, 8, 2, 128, 1], P('fsdp', 'ctx'), may hold values from 0 to 63; in each aligned block of 256 rows (0 to 255, 256 to 511, ..., all dimensions but the last counted through in order) at most 8 rows name the same one
- query_key_value_weight: float32 [1024, 3072], P('fsdp'), may hold values from -0.1875 to 0.1875
- output_weight_matrix: float32 [1024, 1024], P('fsdp'), may hold values from -1.5 to 1.5
- expert_in: float32 [64, 1024, 4096], P('ctx', None, 'fsdp'), may hold values from -0.1875 to 0.1875
- expert_out: float32 [64, 4096, 1024], P('ctx', 'fsdp'), may hold values from -0.09375 to 0.09375
- gain_one: float32 [1024], replicated, may hold values from 0.5 to 1.5
- gain_two: float32 [1024], replicated, may hold values from 0.5 to 1.5
- grad_output: bfloat16 [4, 8, 2, 128, 1024], P('fsdp', 'ctx'), may hold values from -6 to 6
Outputs:
- block_out: bfloat16 [4, 8, 2, 128, 1024], P('fsdp', 'ctx')
- grad_tokens: float32 [4, 8, 2, 128, 1024], P('fsdp', 'ctx')
- grad_qkv_weight: float32 [1024, 3072], P('fsdp')
- grad_out_weight: float32 [1024, 1024], P('fsdp')
- grad_expert_in: float32 [64, 1024, 4096], P('ctx', None, 'fsdp')
- grad_expert_out: float32 [64, 4096, 1024], P('ctx', 'fsdp')
- grad_gain_one: float32 [1024], P('fsdp')
- grad_gain_two: float32 [1024], P('fsdp')
The draws below stay inside these ranges and needn't reach their ends.
Inputs may be any that keep to these rules, and one draw needn't show every extreme that they name: `doc_starts`: each entry is the stream position at which the token's document begins, never after the token's own position; documents are contiguous runs of at most 1024 tokens, every stream holds one document of exactly 1024 tokens, and the last token of every stream begins a document of its own. `expert_ids`: among the 256 rows of one stream on one device, no expert is named more than 8 times, and in some of these blocks one expert is named exactly 8 times.
All inputs are finite; a program needn't handle non-finite values.
Results may differ from the reference program's by a relative error of at most 0.018.
Values may be sent and summed in bfloat16 or wider, within the bound.
A program may use at most 320 MiB of HBM per device.

```python
import math
import jax
import jax.numpy as jnp
import numpy as np
from jax import lax

D = 1024
HEADS = 16
HEAD_DIM = 64
FF = 4096
EXPERTS = 64
HALF = 128
CAP = 8
SEQS = 4
N_CTX = 8


def draw_doc_starts(key, part):
    half_len = HALF * N_CTX

    def one_stream(stream_key):
        side = jax.random.randint(jax.random.fold_in(stream_key, 1), (), 0, 2)
        marks = jax.random.randint(jax.random.fold_in(stream_key, 2), (half_len,), 0, half_len) < 8
        local_pos = jnp.arange(half_len, dtype=jnp.int32)
        marks = marks.at[0].set(True)
        marks = marks.at[half_len - 1].set(True)
        begun = lax.cummax(jnp.where(marks, local_pos, 0), axis=0)
        long_first = jnp.zeros((half_len,), jnp.int32)
        long_second = jnp.where(local_pos == half_len - 1, 2 * half_len - 1, half_len - 1)
        first_half = jnp.where(side == 0, long_first, begun)
        second_half = jnp.where(side == 0, begun + half_len, long_second)
        return jnp.concatenate([first_half, second_half])
    stream_keys = jax.random.split(key, SEQS)
    whole = jax.vmap(one_stream)(stream_keys)
    lead = whole[:, :half_len].reshape(SEQS, N_CTX, HALF)
    tail = whole[:, half_len:].reshape(SEQS, N_CTX, HALF)[:, ::-1]
    return jnp.stack([lead, tail], axis=2).astype(jnp.int32)


def levels(own_key, dims, shards, smallest, top_value):
    factor_of = 1.0
    for dim, blocks in shards:
        draws = jax.random.uniform(jax.random.fold_in(jax.random.fold_in(own_key, 6), dim), (blocks,), jnp.float32, smallest / len(shards), top_value / len(shards))
        factor_of = factor_of * jnp.repeat(jnp.exp(draws), dims[dim] // blocks).reshape((-1,) + (1,) * (len(dims) - 1 - dim))
    return factor_of


def shared_out(key, own, number, rows, amount, top, reach, slope):
    sequence = jax.random.permutation(key, amount)
    crowded, common = load_shares(amount, rows * top, reach, slope, True), load_shares(amount, rows * top, reach, slope, False)
    places = jnp.arange(amount)

    def named(lengths, offset_by):
        used = int((lengths > 0).sum())
        fixed = max(1, used // 4)
        shifted = fixed + (places - fixed + offset_by * (used - fixed)) % max(1, amount - fixed)
        return jnp.zeros((amount,), jnp.int32).at[sequence[jnp.where(places < fixed, places, shifted)]].set(jnp.asarray(lengths, jnp.int32))

    lengths = jnp.where(number % 4 == 0, named(crowded, number // 4), named(common, number - number // 4 - 1))
    mixed = jax.random.permutation(jax.random.fold_in(own, 3), amount)
    source_of, taker = mixed[0:amount // 2 * 2:2], mixed[1:amount // 2 * 2:2]
    slack = jnp.minimum(lengths[source_of] - 1, reach - lengths[taker]) // 2
    slack = jnp.where((source_of == sequence[0]) | (taker == sequence[0]) | (lengths[taker] == 0), 0, jnp.maximum(slack, 0))
    shifted = jax.random.randint(jax.random.fold_in(own, 4), (amount // 2,), 0, 1 << 20) % (slack + 1)
    lengths = lengths.at[source_of].add(-shifted).at[taker].add(shifted)
    labels = jnp.searchsorted(jnp.cumsum(lengths), jnp.arange(rows * top), side="right").astype(jnp.int32)
    listing = labels.reshape(top, rows).T
    listing = listing[jax.random.permutation(jax.random.fold_in(own, 1), rows)]
    offset_by = jax.random.randint(jax.random.fold_in(own, 2), (rows, 1), 0, top)
    return jnp.take_along_axis(listing, (jnp.arange(top)[None, :] + offset_by) % top, axis=1)


def load_shares(number_of, total, bound, lean, full):
    portions = [(1 << 20) // math.isqrt(standing ** lean) + 1 for standing in range(1, number_of + 1)]
    largest = bound if full else min(bound, max(-(-total // number_of), total * portions[0] // sum(portions)))
    least = 1 if total - largest >= number_of - 1 else 0
    counts, surplus = [largest] + [least] * (number_of - 1), total - largest - least * (number_of - 1)
    while surplus > 0:
        free = [i for i in range(1, number_of) if counts[i] < largest] or [i for i in range(1, number_of) if counts[i] < bound]
        whole, remaining = sum([portions[i] for i in free]), surplus
        for i in free:
            extra = min(bound - counts[i], max(1, remaining * portions[i] // whole), surplus)
            counts[i] = counts[i] + extra
            surplus = surplus - extra
    return np.array(counts)


def gaussian(rng, shape, spread, reach, pieces=(), kind=jnp.bfloat16):
    loudness = levels(rng, shape, pieces, -0.22, 0.18) if pieces else 1.0
    values = jax.random.normal(rng, shape, jnp.float32) * spread * loudness
    return jnp.minimum(jnp.maximum(values, -reach), reach).astype(kind)


def setup_inputs(seed: int = 0) -> dict:
    key_list = jax.random.split(jax.random.key(seed), 11)
    tokens = gaussian(key_list[0], (SEQS, N_CTX, 2, HALF, D), 1.0, 6.0, ((0, 4), (1, 8)))
    doc_starts = draw_doc_starts(jax.random.fold_in(key_list[10], 71), 0)
    expert_ids_keys = jax.random.split(jax.random.fold_in(key_list[2], 1), SEQS * N_CTX * 2 * HALF // (2 * HALF))
    expert_ids_turns = jax.random.permutation(jax.random.fold_in(key_list[2], 3), SEQS * N_CTX * 2 * HALF // (2 * HALF))
    expert_ids = jax.vmap(lambda own, number: shared_out(jax.random.fold_in(key_list[2], 2), own, number, 2 * HALF, EXPERTS, 1, CAP, 2))(expert_ids_keys, expert_ids_turns).reshape((SEQS, N_CTX, 2, HALF, 1))
    query_key_value_weight = gaussian(key_list[3], (D, 3 * D), D ** -0.5, 0.1875, ((0, 4),), jnp.float32)
    output_weight_matrix = gaussian(key_list[4], (D, D), (max(D // 64, 1)) ** -0.5, 1.5, ((0, 4),), jnp.float32)
    expert_in = gaussian(key_list[5], (EXPERTS, D, FF), D ** -0.5, 0.1875, ((0, 8), (2, 4)), jnp.float32)
    expert_out = gaussian(key_list[6], (EXPERTS, FF, D), FF ** -0.5, 0.09375, ((0, 8), (1, 4)), jnp.float32)
    gain_one = jnp.clip(1.0 + 0.1 * jax.random.normal(key_list[7], (D,), jnp.float32), 0.5, 1.5)
    gain_two = jnp.clip(1.0 + 0.1 * jax.random.normal(key_list[8], (D,), jnp.float32), 0.5, 1.5)
    grad_output = gaussian(key_list[9], (SEQS, N_CTX, 2, HALF, D), 1.0, 6.0, ((0, 4), (1, 8)))
    return {"tokens": tokens, "doc_starts": doc_starts, "expert_ids": expert_ids, "query_key_value_weight": query_key_value_weight, "output_weight_matrix": output_weight_matrix, "expert_in": expert_in, "expert_out": expert_out, "gain_one": gain_one, "gain_two": gain_two, "grad_output": grad_output}


@jax.custom_vjp
def reduced_precision(v):
    return lax.optimization_barrier(v.astype(jnp.bfloat16)).astype(jnp.float32)

@jax.custom_vjp
def reduced_backward(v):
    return v

def low_keep(v):
    return (reduced_precision(v), None)

def low_pass(kept, grad):
    return (grad,)

def back_keep(v):
    return (v, None)

def back_low(kept, grad):
    return (reduced_precision(grad),)
reduced_precision.defvjp(low_keep, low_pass)
reduced_backward.defvjp(back_keep, back_low)
EPS = 1e-05
NEGATIVE = -1e+30
EXACT_PRECISION = lax.Precision.HIGHEST

def natural(array):
    lead = array[:, :, 0]
    tail = array[:, ::-1, 1]
    new_shape = (array.shape[0], array.shape[1] * array.shape[3]) + array.shape[4:]
    return jnp.concatenate([lead.reshape(new_shape), tail.reshape(new_shape)], axis=1)

def layout(array):
    streams = array.shape[0]
    half_len = array.shape[1] // 2
    rest = array.shape[2:]
    lead = array[:, :half_len].reshape((streams, N_CTX, HALF) + rest)
    tail = array[:, half_len:].reshape((streams, N_CTX, HALF) + rest)[:, ::-1]
    return jnp.stack([lead, tail], axis=2)

def layer_norm(value, gain):
    row_mean = lax.optimization_barrier(jnp.mean(value, axis=-1, keepdims=True))
    centred = value - row_mean
    variance = lax.optimization_barrier(jnp.mean(centred * centred, axis=-1, keepdims=True))
    return centred * lax.rsqrt(variance + EPS) * gain

def attend_stream(inputs):
    query, keys, values, starts = inputs
    length = query.shape[0]
    query_block = min(512, length)
    positions = jnp.arange(length, dtype=jnp.int32)
    score_scale = HEAD_DIM ** (-0.5)

    def one_block(part):
        query_rows, query_pos, query_start = part
        raw_scores = reduced_backward(jnp.einsum('qhe,khe->hqk', query_rows, keys, precision=EXACT_PRECISION) * score_scale)
        visible = (positions[None, None, :] <= query_pos[None, :, None]) & (positions[None, None, :] >= query_start[None, :, None])
        masked = jnp.where(visible, raw_scores, NEGATIVE)
        running_max = lax.optimization_barrier(jnp.max(masked, axis=-1, keepdims=True))
        log_total = running_max + jnp.log(lax.optimization_barrier(jnp.sum(jnp.exp(masked - running_max), axis=-1, keepdims=True)))
        weights = reduced_precision(jnp.exp(masked - log_total))
        return jnp.einsum('hqk,khe->qhe', weights, values, precision=EXACT_PRECISION)
    block_count = length // query_block
    mixed_heads_out = lax.map(jax.checkpoint(one_block), (query.reshape(block_count, query_block, HEADS, HEAD_DIM), positions.reshape(block_count, query_block), starts.reshape(block_count, query_block)))
    return mixed_heads_out.reshape(length, HEADS * HEAD_DIM)

def reference(tokens, doc_starts, expert_ids, query_key_value_weight, output_weight_matrix, expert_in, expert_out, gain_one, gain_two, grad_output):
    streams = tokens.shape[0]
    length = 2 * HALF * N_CTX
    start_x = natural(tokens.astype(jnp.float32))
    starts = natural(doc_starts)
    cotangent = natural(grad_output.astype(jnp.float32))
    block_ids = expert_ids.reshape(streams * N_CTX, 2 * HALF)
    chosen = (block_ids[..., None] == jnp.arange(EXPERTS, dtype=jnp.int32)).astype(jnp.int32)
    rank_within = lax.optimization_barrier(jnp.sum(chosen * jnp.cumsum(chosen, axis=1), axis=-1)) - 1
    per_expert = streams * N_CTX * CAP
    flat_slot = block_ids * per_expert + jnp.arange(streams * N_CTX, dtype=jnp.int32)[:, None] * CAP + rank_within
    token_slot = natural(flat_slot.reshape(streams, N_CTX, 2, HALF)).reshape(-1).astype(jnp.int32)
    token_count = streams * length
    slot_rows = jnp.full((EXPERTS * per_expert,), token_count, jnp.int32).at[token_slot].set(jnp.arange(token_count, dtype=jnp.int32))

    def forward(start_x, query_key_value_weight, output_weight_matrix, expert_in, expert_out, gain_one, gain_two):
        model_width = start_x.shape[-1]
        first_normed_rows = reduced_precision(layer_norm(start_x, gain_one))
        projected_rows = reduced_precision(reduced_backward(jnp.einsum('fbg,gw->fbw', first_normed_rows, reduced_precision(query_key_value_weight), precision=EXACT_PRECISION)))
        head_shape = (streams, length, HEADS, HEAD_DIM)
        query = projected_rows[..., :model_width].reshape(head_shape)
        keys = projected_rows[..., model_width:2 * model_width].reshape(head_shape)
        values = projected_rows[..., 2 * model_width:].reshape(head_shape)
        mixed_heads_out = lax.map(attend_stream, (query, keys, values, starts))
        mixed_heads_out = reduced_precision(reduced_backward(mixed_heads_out))
        attention_rows_out = reduced_backward(jnp.einsum('fbg,gw->fbw', mixed_heads_out, reduced_precision(output_weight_matrix), precision=EXACT_PRECISION))
        middle = start_x + attention_rows_out
        routed = reduced_precision(reduced_backward(layer_norm(middle, gain_two)))
        padded = jnp.concatenate([routed.reshape(token_count, model_width), jnp.zeros((1, model_width), jnp.float32)], axis=0)
        gathered = padded[slot_rows].reshape(EXPERTS, per_expert, model_width)

        def expert_apply(part):
            row_block, first_proj, second_proj = part
            hidden = reduced_backward(jnp.einsum('rd,df->rf', row_block, first_proj, precision=EXACT_PRECISION))
            active = reduced_precision(jax.nn.gelu(hidden))
            return jnp.einsum('rf,fd->rd', active, second_proj, precision=EXACT_PRECISION)
        result = reduced_precision(lax.map(jax.checkpoint(expert_apply), (gathered, reduced_precision(expert_in), reduced_precision(expert_out))))
        expert_sum = result.reshape(EXPERTS * per_expert, model_width)[token_slot].reshape(streams, length, model_width)
        return middle + expert_sum
    output_rows, backward = jax.vjp(forward, start_x, query_key_value_weight, output_weight_matrix, expert_in, expert_out, gain_one, gain_two)
    grads = backward(cotangent)
    return (layout(output_rows).astype(jnp.bfloat16), layout(grads[0]), grads[1], grads[2], grads[3], grads[4], grads[5], grads[6])
```

```python
import math

import jax
import jax.numpy as jnp
from jax import lax
from jax.experimental import pallas as pl
from jax.experimental.pallas import tpu as pltpu
from jax.sharding import PartitionSpec as P

HEADS = 16
EXPERTS = 64
CAP = 8


EPS = 1e-05
NEGATIVE = -1e30


def position_of(row_ids, ctx_count, half_rows):
    device = row_ids // (2 * half_rows)
    upper_half = row_ids // half_rows % 2
    offset = row_ids % half_rows
    return jnp.where(
        upper_half == 0,
        device * half_rows + offset,
        (2 * ctx_count - 1 - device) * half_rows + offset,
    )


def norm_forward(value, gain):
    row_mean = jnp.mean(value, axis=-1, keepdims=True)
    centred = value - row_mean
    inverse = lax.rsqrt(jnp.mean(centred * centred, axis=-1, keepdims=True) + EPS)
    normed = centred * inverse
    return (normed * gain, normed, inverse)


def norm_backward(gradient, normed, inverse, gain):
    scaled = gradient * gain
    mean_grad = jnp.mean(scaled, axis=-1, keepdims=True)
    mean_proj = jnp.mean(scaled * normed, axis=-1, keepdims=True)
    return (
        inverse * (scaled - mean_grad - normed * mean_proj),
        jnp.sum(gradient * normed, axis=(0, 1)),
    )


def scores(query, keys, query_pos, key_pos, query_start, score_scale):
    raw_scores = (
        jnp.einsum("qshe,kshe->shqk", query, keys, preferred_element_type=jnp.float32) * score_scale
    )
    visible = (key_pos[None, None, None, :] <= query_pos[None, None, :, None]) & (
        key_pos[None, None, None, :] >= query_start.T[:, None, :, None]
    )
    return jnp.where(visible, raw_scores, NEGATIVE)


def log_totals(query, keys, query_pos, query_start, score_scale, ctx_count, half_rows, key_block):
    block_count = keys.shape[0] // key_block
    carry_shape = (query.shape[1], query.shape[2], query.shape[0])

    def log_one_block(block_index, carried):
        running_max, running = carried
        first_row = block_index * key_block
        key_piece = lax.dynamic_slice_in_dim(keys, first_row, key_block, 0)
        key_pos = position_of(
            first_row + jnp.arange(key_block, dtype=jnp.int32), ctx_count, half_rows
        )
        score_rows = scores(query, key_piece, query_pos, key_pos, query_start, score_scale)
        new_max = jnp.maximum(running_max, jnp.max(score_rows, axis=-1))
        running = running * jnp.exp(running_max - new_max) + jnp.sum(
            jnp.exp(score_rows - new_max[..., None]), axis=-1
        )
        return (new_max, running)

    running_max, running = lax.fori_loop(
        0,
        block_count,
        log_one_block,
        (jnp.full(carry_shape, NEGATIVE, jnp.float32), jnp.zeros(carry_shape, jnp.float32)),
    )
    return running_max + jnp.log(running)


def attend(
    query,
    keys,
    values,
    query_pos,
    query_start,
    log_total,
    score_scale,
    ctx_count,
    half_rows,
    key_block,
):
    block_count = keys.shape[0] // key_block
    zeros_init = jnp.zeros(query.shape, jnp.float32)

    def attend_one_block(block_index, carried):
        output, remainder = carried
        first_row = block_index * key_block
        key_piece = lax.dynamic_slice_in_dim(keys, first_row, key_block, 0)
        value_piece = lax.dynamic_slice_in_dim(values, first_row, key_block, 0)
        key_pos = position_of(
            first_row + jnp.arange(key_block, dtype=jnp.int32), ctx_count, half_rows
        )
        weights = jnp.exp(
            scores(query, key_piece, query_pos, key_pos, query_start, score_scale)
            - log_total[..., None]
        )
        rounded = weights.astype(jnp.bfloat16)
        leftover = (weights - rounded.astype(jnp.float32)).astype(jnp.bfloat16)
        output = output + jnp.einsum(
            "shqk,kshe->qshe", rounded, value_piece, preferred_element_type=jnp.float32
        )
        remainder = remainder + jnp.einsum(
            "shqk,kshe->qshe", leftover, value_piece, preferred_element_type=jnp.float32
        )
        return (output, remainder)

    return lax.fori_loop(0, block_count, attend_one_block, (zeros_init, zeros_init))


def query_grads(
    query,
    keys,
    values,
    grad_heads,
    query_pos,
    query_start,
    log_total,
    row_delta,
    score_scale,
    ctx_count,
    half_rows,
    key_block,
):
    block_count = keys.shape[0] // key_block

    def query_one_block(block_index, running):
        first_row = block_index * key_block
        key_piece = lax.dynamic_slice_in_dim(keys, first_row, key_block, 0)
        value_piece = lax.dynamic_slice_in_dim(values, first_row, key_block, 0)
        key_pos = position_of(
            first_row + jnp.arange(key_block, dtype=jnp.int32), ctx_count, half_rows
        )
        weights = jnp.exp(
            scores(query, key_piece, query_pos, key_pos, query_start, score_scale)
            - log_total[..., None]
        )
        grad_weight = jnp.einsum(
            "qshe,kshe->shqk", grad_heads, value_piece, preferred_element_type=jnp.float32
        )
        grad_score = (weights * (grad_weight - row_delta[..., None])).astype(jnp.bfloat16)
        return running + jnp.einsum(
            "shqk,kshe->qshe", grad_score, key_piece, preferred_element_type=jnp.float32
        )

    return (
        lax.fori_loop(0, block_count, query_one_block, jnp.zeros(query.shape, jnp.float32))
        * score_scale
    )


def key_grads(
    query,
    grad_heads,
    query_pos,
    query_start,
    log_total,
    row_delta,
    key_piece,
    value_piece,
    key_pos,
    score_scale,
):
    weights = jnp.exp(
        scores(query, key_piece, query_pos, key_pos, query_start, score_scale)
        - log_total[..., None]
    )
    grad_weight = jnp.einsum(
        "qshe,kshe->shqk", grad_heads, value_piece, preferred_element_type=jnp.float32
    )
    grad_score = (weights * (grad_weight - row_delta[..., None])).astype(jnp.bfloat16)
    key_part = (
        jnp.einsum("shqk,qshe->kshe", grad_score, query, preferred_element_type=jnp.float32)
        * score_scale
    )
    value_part = jnp.einsum(
        "shqk,qshe->kshe",
        weights.astype(jnp.bfloat16),
        grad_heads,
        preferred_element_type=jnp.float32,
    )
    return (key_part, value_part)


def shards(
    tokens,
    doc_starts,
    expert_ids,
    query_key_value_weight,
    output_weight_matrix,
    expert_in,
    expert_out,
    gain_one,
    gain_two,
    grad_output,
):
    seq_dev = tokens.shape[0]
    half_rows = tokens.shape[3]
    model_width = tokens.shape[4]
    local_rows = 2 * half_rows
    ctx_count = lax.axis_size("ctx")
    head_count = HEADS
    head_size = model_width // head_count
    score_scale = head_size ** (-0.5)
    keys_total = ctx_count * local_rows
    key_block = min(512, keys_total)
    own_rows = lax.axis_index("ctx") * local_rows + jnp.arange(local_rows, dtype=jnp.int32)
    query_pos = position_of(own_rows, ctx_count, half_rows)
    query_start = doc_starts.reshape(seq_dev, local_rows).T
    routes_local = expert_ids.reshape(seq_dev, local_rows).T
    start_x = (
        tokens.reshape(seq_dev, local_rows, model_width).transpose(1, 0, 2).astype(jnp.float32)
    )
    cotangent = grad_output.reshape(seq_dev, local_rows, model_width).transpose(1, 0, 2)
    projection, out_proj = (
        lax.all_gather(query_key_value_weight.astype(jnp.bfloat16), "fsdp", axis=0, tiled=True),
        lax.all_gather(output_weight_matrix.astype(jnp.bfloat16), "fsdp", axis=0, tiled=True),
    )
    first_normed_rows, hat_one, inverse_one = norm_forward(start_x, gain_one)
    normed_low = first_normed_rows.astype(jnp.bfloat16)
    projected_rows = jnp.einsum(
        "tsd,de->tse", normed_low, projection, preferred_element_type=jnp.float32
    ).astype(jnp.bfloat16)
    query = projected_rows[..., :model_width]
    keys = projected_rows[..., model_width : 2 * model_width]
    values = projected_rows[..., 2 * model_width :]
    key_all, value_all = (
        lax.all_gather(keys, "ctx", axis=0, tiled=True),
        lax.all_gather(values, "ctx", axis=0, tiled=True),
    )
    query_heads = query.reshape(local_rows, seq_dev, head_count, head_size)
    key_heads = key_all.reshape(keys_total, seq_dev, head_count, head_size)
    value_heads = value_all.reshape(keys_total, seq_dev, head_count, head_size)
    log_total = log_totals(
        query_heads, key_heads, query_pos, query_start, score_scale, ctx_count, half_rows, key_block
    )
    mixed_heads_out, remainder = attend(
        query_heads,
        key_heads,
        value_heads,
        query_pos,
        query_start,
        log_total,
        score_scale,
        ctx_count,
        half_rows,
        key_block,
    )
    mixed_low = mixed_heads_out.astype(jnp.bfloat16).reshape(local_rows, seq_dev, model_width)
    attention_rows_out = jnp.einsum(
        "tsd,de->tse", mixed_low, out_proj, preferred_element_type=jnp.float32
    )
    middle = start_x + attention_rows_out
    normed_two, hat_two, inverse_two = norm_forward(middle, gain_two)
    routed = normed_two.astype(jnp.bfloat16)
    slot_count = EXPERTS * CAP
    per_owner = EXPERTS // ctx_count
    chosen = (routes_local[..., None] == jnp.arange(EXPERTS, dtype=jnp.int32)).astype(jnp.int32)
    earlier = (
        jnp.arange(local_rows)[:, None] >= jnp.arange(local_rows)[None, :]
    ).astype(jnp.bfloat16)
    running = jnp.einsum(
        "tu,use->tse", earlier, chosen.astype(jnp.bfloat16), preferred_element_type=jnp.float32
    )
    rank_within = jnp.sum(chosen * running.astype(jnp.int32), axis=-1) - 1
    slot_index = routes_local * CAP + rank_within
    dispatch = (
        slot_index.T[:, None, :] == jnp.arange(slot_count, dtype=jnp.int32)[None, :, None]
    ).astype(jnp.bfloat16)
    dispatch = dispatch.reshape(seq_dev, ctx_count, per_owner, CAP, local_rows)
    send_rows = jnp.einsum(
        "snect,tsd->nescd", dispatch, routed, preferred_element_type=jnp.float32
    ).astype(jnp.bfloat16)
    send_grads = jnp.einsum(
        "snect,tsd->nescd", dispatch, cotangent, preferred_element_type=jnp.float32
    ).astype(jnp.bfloat16)
    got_rows, got_grads = (
        lax.all_to_all(send_rows, "ctx", split_axis=0, concat_axis=0, tiled=True),
        lax.all_to_all(send_grads, "ctx", split_axis=0, concat_axis=0, tiled=True),
    )
    in_low = expert_in.astype(jnp.bfloat16)
    out_low = expert_out.astype(jnp.bfloat16)
    all_rows, all_grads = (
        lax.all_gather(got_rows, "fsdp", axis=2, tiled=True),
        lax.all_gather(got_grads, "fsdp", axis=2, tiled=True),
    )
    hidden = jnp.einsum("nercd,edf->nercf", all_rows, in_low, preferred_element_type=jnp.float32)
    active = jax.nn.gelu(hidden).astype(jnp.bfloat16)
    partial_rows = jnp.einsum(
        "nercf,efd->nercd", active, out_low, preferred_element_type=jnp.float32
    )
    result = lax.psum_scatter(
        partial_rows.astype(jnp.bfloat16), "fsdp", scatter_dimension=2, tiled=True
    )
    upstream = jnp.einsum(
        "nercd,efd->nercf", all_grads, out_low, preferred_element_type=jnp.float32
    )
    unused, gelu_back = jax.vjp(jax.nn.gelu, hidden)
    grad_hidden = gelu_back(upstream)[0].astype(jnp.bfloat16)
    grad_in = jnp.einsum(
        "nercd,nercf->edf", all_rows, grad_hidden, preferred_element_type=jnp.float32
    )
    grad_outw = jnp.einsum(
        "nercf,nercd->efd", active, all_grads, preferred_element_type=jnp.float32
    )
    row_part = jnp.einsum(
        "nercf,edf->nercd", grad_hidden, in_low, preferred_element_type=jnp.float32
    )
    row_grad = lax.psum_scatter(row_part, "fsdp", scatter_dimension=2, tiled=True).astype(
        jnp.bfloat16
    )
    back_rows = lax.all_to_all(result, "ctx", split_axis=0, concat_axis=0, tiled=True)
    expert_sum = jnp.einsum(
        "snect,nescd->tsd", dispatch, back_rows, preferred_element_type=jnp.float32
    )
    output_rows = middle + expert_sum
    returned = lax.all_to_all(row_grad, "ctx", split_axis=0, concat_axis=0, tiled=True)
    grad_routed = jnp.einsum(
        "snect,nescd->tsd", dispatch, returned, preferred_element_type=jnp.float32
    )
    grad_mid_norm, grad_gain_two = norm_backward(grad_routed, hat_two, inverse_two, gain_two)
    grad_middle = cotangent.astype(jnp.float32) + grad_mid_norm
    grad_attn = grad_middle.astype(jnp.bfloat16)
    grad_outproj = jnp.einsum(
        "tsd,tse->de", mixed_low, grad_attn, preferred_element_type=jnp.float32
    )
    grad_mixed = jnp.einsum(
        "tse,de->tsd", grad_attn, out_proj, preferred_element_type=jnp.float32
    ).astype(jnp.bfloat16)
    grad_heads = grad_mixed.reshape(local_rows, seq_dev, head_count, head_size)
    full_mixed = mixed_heads_out + remainder
    row_delta = jnp.sum(grad_heads.astype(jnp.float32) * full_mixed, axis=-1).transpose(1, 2, 0)
    grad_query = query_grads(
        query_heads,
        key_heads,
        value_heads,
        grad_heads,
        query_pos,
        query_start,
        log_total,
        row_delta,
        score_scale,
        ctx_count,
        half_rows,
        key_block,
    ).astype(jnp.bfloat16)
    sub_rows = math.gcd(local_rows * lax.axis_size("ctx"), key_block)

    def one_piece(piece_index):
        piece_start = piece_index * sub_rows
        key_piece = lax.dynamic_slice_in_dim(key_heads, piece_start, sub_rows, 0)
        value_piece = lax.dynamic_slice_in_dim(value_heads, piece_start, sub_rows, 0)
        key_pos = position_of(
            piece_start + jnp.arange(sub_rows, dtype=jnp.int32), ctx_count, half_rows
        )
        key_part, value_part = key_grads(
            query_heads,
            grad_heads,
            query_pos,
            query_start,
            log_total,
            row_delta,
            key_piece,
            value_piece,
            key_pos,
            score_scale,
        )
        return jnp.concatenate(
            [
                key_part.reshape(sub_rows, seq_dev, model_width),
                value_part.reshape(sub_rows, seq_dev, model_width),
            ],
            axis=-1,
        )

    summed = lax.psum_scatter(
        lax.map(
            one_piece, jnp.arange(local_rows * lax.axis_size("ctx") // sub_rows, dtype=jnp.int32)
        ).reshape(local_rows * lax.axis_size("ctx"), seq_dev, 2 * model_width),
        "ctx",
        scatter_dimension=0,
        tiled=True,
    )
    grad_key = summed[..., :model_width].astype(jnp.bfloat16)
    grad_value = summed[..., model_width:].astype(jnp.bfloat16)
    grad_projected = jnp.concatenate(
        [grad_query.reshape(local_rows, seq_dev, model_width), grad_key, grad_value], axis=-1
    )
    grad_projection = jnp.einsum(
        "tsd,tse->de", normed_low, grad_projected, preferred_element_type=jnp.float32
    )
    grad_normed = jnp.einsum(
        "tse,de->tsd", grad_projected, projection, preferred_element_type=jnp.float32
    )
    grad_in_norm, grad_gain_one = norm_backward(grad_normed, hat_one, inverse_one, gain_one)
    grad_start = grad_middle + grad_in_norm
    shard_proj, shard_outproj, shard_gain_one, shard_gain_two = (
        lax.psum_scatter(
            grad_projection.astype(jnp.bfloat16), "fsdp", scatter_dimension=0, tiled=True
        ).astype(jnp.float32),
        lax.psum_scatter(
            grad_outproj.astype(jnp.bfloat16), "fsdp", scatter_dimension=0, tiled=True
        ).astype(jnp.float32),
        lax.psum_scatter(
            grad_gain_one.astype(jnp.bfloat16), "fsdp", scatter_dimension=0, tiled=True
        ).astype(jnp.float32),
        lax.psum_scatter(
            grad_gain_two.astype(jnp.bfloat16), "fsdp", scatter_dimension=0, tiled=True
        ).astype(jnp.float32),
    )
    shard_proj, shard_outproj, shard_gain_one, shard_gain_two = (
        lax.psum(shard_proj.astype(jnp.bfloat16), "ctx").astype(jnp.float32),
        lax.psum(shard_outproj.astype(jnp.bfloat16), "ctx").astype(jnp.float32),
        lax.psum(shard_gain_one.astype(jnp.bfloat16), "ctx").astype(jnp.float32),
        lax.psum(shard_gain_two.astype(jnp.bfloat16), "ctx").astype(jnp.float32),
    )
    block_out = output_rows.transpose(1, 0, 2).reshape(tokens.shape).astype(jnp.bfloat16)
    grad_tokens = grad_start.transpose(1, 0, 2).reshape(tokens.shape)
    return (
        block_out,
        grad_tokens,
        shard_proj,
        shard_outproj,
        grad_in,
        grad_outw,
        shard_gain_one,
        shard_gain_two,
    )


BF = jnp.bfloat16
F32 = jnp.float32
MESH_ID = pl.DeviceIdType.MESH
ANY = pl.BlockSpec(memory_space=pl.ANY)
DMA = pltpu.SemaphoreType.DMA
VMEM_CAP = 56 << 20


def place():
    c = lax.axis_index("ctx")
    f = lax.axis_index("fsdp")
    return c, f, c // 2, c % 2, f // 2, f % 2


def remote(src, dst, send, recv, device):
    return pltpu.make_async_remote_copy(
        src_ref=src, dst_ref=dst, send_sem=send, recv_sem=recv, device_id=device, device_id_type=MESH_ID
    )


def block_at(c, half, count):
    return c if half == 0 else 2 * count - 1 - c


def params(side=True):
    return pltpu.CompilerParams(has_side_effects=side, vmem_limit_bytes=VMEM_CAP)


def gather_stream(normed, starts, weight):
    count = lax.axis_size("ctx")
    depth = count // 2
    rows, width = weight.shape
    pieces = 4
    piece = rows // pieces

    def kernel(n_ref, s_ref, w_ref, tok, st, wall, rs_t, ss_p, ss_up, ss_dn, ss_sib, rs_s, ss_s, rs_wx, ss_wx, rs_ws, ss_ws, rs_wf, ss_wf, loc):
        c, f, z, y, x, k = place()
        sib = (c, f + 1 - 2 * k)
        xn = (c, (f + 2) % 4)
        partner = (c + 1 - 2 * y, f + 1 - 2 * k)
        up = (c + 2, f)
        down = (c - 2, f)
        holder = k == y

        def wpart(ref, shard, i):
            return ref.at[shard, pl.ds(i * piece, piece)]

        for i in range(pieces):
            remote(w_ref.at[pl.ds(i * piece, piece)], wpart(wall, f, i), ss_wx.at[i], rs_wx.at[i], xn).start()

        def send_in(h):
            return remote(
                n_ref.at[h], tok.at[block_at(c, h, count)], ss_p.at[h], rs_t.at[block_at(c, h, count)], partner
            )

        def local_in(h):
            return pltpu.make_async_copy(
                n_ref.at[h], tok.at[block_at(c, h, count)], rs_t.at[block_at(c, h, count)]
            )

        @pl.when(holder)
        def _():
            for h in range(2):
                local_in(h).start()

        @pl.when(jnp.logical_not(holder))
        def _():
            for h in range(2):
                send_in(h).start()

        for zt in range(depth):
            for kt in range(2):
                dev = (2 * zt + k, 2 * x + kt)
                slot = 2 * zt + kt
                mine = holder & (z == zt) & (k == kt)

                @pl.when(mine)
                def _(dev=dev, slot=slot):
                    pltpu.make_async_copy(s_ref, st.at[c], rs_s.at[c]).start()

                @pl.when(jnp.logical_not(mine))
                def _(dev=dev, slot=slot):
                    remote(s_ref, st.at[c], ss_s.at[slot], rs_s.at[c], dev).start()

        remote(w_ref, wall.at[f], ss_ws, rs_ws, sib).start()
        pltpu.make_async_copy(w_ref, wall.at[f], loc).start()

        def copy_block(zb, h, ss, dev):
            b = block_at(2 * zb + k, h, count)
            return remote(tok.at[b], tok.at[b], ss, rs_t.at[b], dev)

        def wait_block(zb):
            for h in range(2):
                b = block_at(2 * zb + k, h, count)
                remote(tok.at[b], tok.at[b], ss_p.at[h], rs_t.at[b], sib).wait_recv()

        def send_up(j):
            for h in range(2):
                copy_block(z - j, h, ss_up.at[j, h], up).start()

        def send_down(j):
            for h in range(2):
                copy_block(z + j, h, ss_dn.at[j, h], down).start()

        def send_sib(zb):
            for h in range(2):
                copy_block(zb, h, ss_sib.at[zb, h], sib).start()

        def w_forward(i):
            shard = (f + 2) % 4
            remote(wpart(wall, shard, i), wpart(wall, shard, i), ss_wx.at[i], rs_wx.at[i], xn).wait_recv()
            remote(wpart(wall, shard, i), wpart(wall, shard, i), ss_wf.at[i], rs_wf.at[i], sib).start()

        wait_block(z)

        @pl.when(z < depth - 1)
        def _():
            send_up(0)

        @pl.when(z > 0)
        def _():
            send_down(0)

        send_sib(z)
        for j in range(1, depth):
            if j < pieces:
                w_forward(j - 1)

            @pl.when(z - j >= 0)
            def _(j=j):
                wait_block(z - j)

                @pl.when(z < depth - 1)
                def _():
                    send_up(j)

                send_sib(z - j)

            @pl.when(z + j <= depth - 1)
            def _(j=j):
                wait_block(z + j)

                @pl.when(z > 0)
                def _():
                    send_down(j)

                send_sib(z + j)

        for i in range(min(depth, pieces) - 1, pieces):
            w_forward(i)

        for zt in range(depth):
            for h in range(2):
                b = block_at(2 * zt + 1 - k, h, count)
                remote(tok.at[b], tok.at[b], ss_p.at[h], rs_t.at[b], sib).wait_recv()
                copy_block(zt, h, ss_sib.at[zt, h], sib).wait_send()
        for ct in range(count):
            remote(s_ref, st.at[ct], ss_s.at[0], rs_s.at[ct], sib).wait_recv()
        for i in range(pieces):
            shard = sib[1] + 2 - 4 * (sib[1] // 2)
            remote(wpart(wall, shard, i), wpart(wall, shard, i), ss_wf.at[i], rs_wf.at[i], sib).wait_recv()
            remote(wpart(wall, shard, i), wpart(wall, shard, i), ss_wf.at[i], rs_wf.at[i], sib).wait_send()
            remote(w_ref.at[pl.ds(i * piece, piece)], wpart(wall, f, i), ss_wx.at[i], rs_wx.at[i], xn).wait_send()
        remote(w_ref, wall.at[sib[1]], ss_ws, rs_ws, sib).wait()
        pltpu.make_async_copy(w_ref, wall.at[f], loc).wait()

        @pl.when(jnp.logical_not(holder))
        def _():
            for h in range(2):
                send_in(h).wait_send()

        for j in range(depth):

            @pl.when((z < depth - 1) & (z - j >= 0))
            def _(j=j):
                for h in range(2):
                    copy_block(z - j, h, ss_up.at[j, h], up).wait_send()

            @pl.when((z > 0) & (z + j <= depth - 1))
            def _(j=j):
                for h in range(2):
                    copy_block(z + j, h, ss_dn.at[j, h], down).wait_send()

        for zt in range(depth):
            for kt in range(2):
                mine = holder & (z == zt) & (k == kt)

                @pl.when(jnp.logical_not(mine))
                def _(zt=zt, kt=kt):
                    remote(s_ref, st.at[c], ss_s.at[2 * zt + kt], rs_s.at[c], sib).wait_send()

    return pl.pallas_call(
        kernel,
        name="gather_stream",
        out_shape=(
            jax.ShapeDtypeStruct((2 * count,) + normed.shape[1:], normed.dtype),
            jax.ShapeDtypeStruct((count,) + starts.shape, starts.dtype),
            jax.ShapeDtypeStruct((4, rows, width), weight.dtype),
        ),
        in_specs=[ANY] * 3,
        out_specs=(ANY,) * 3,
        scratch_shapes=[
            DMA((2 * count,)), DMA((2,)), DMA((depth, 2)), DMA((depth, 2)), DMA((depth, 2)),
            DMA((count,)), DMA((count,)), DMA((pieces,)), DMA((pieces,)), DMA, DMA,
            DMA((pieces,)), DMA((pieces,)), DMA,
        ],
        compiler_params=params(),
    )(normed, starts, weight)


def heads_to_tokens(arrays, name):
    count = lax.axis_size("ctx")
    number = len(arrays)
    lanes = arrays[0].shape[2]
    width = count * lanes

    def kernel(*refs):
        ins, (out, ss, rs) = refs[:number], refs[number:]
        c, f, z, y, x, k = place()
        pair = 2 * z + k
        target = 2 * x + y

        def there(half, a):
            return out.at[half, :, pl.ds(pl.multiple_of(a * width + pair * lanes, lanes), lanes)]

        def send(i, half, a):
            ct = (c + i) % count
            return remote(
                ins[a].at[block_at(ct, half, count)], there(half, a), ss.at[i, half, a], rs.at[pair, half, a], (ct, target)
            )

        def own(half, a):
            return pltpu.make_async_copy(ins[a].at[block_at(c, half, count)], there(half, a), rs.at[pair, half, a])

        pieces = [(half, a) for a in range(number) for half in range(2)]
        for i in [*range(1, count), 0]:
            if i:
                for half, a in pieces:
                    send(i, half, a).start()
            else:

                @pl.when(k == y)
                def _():
                    for half, a in pieces:
                        own(half, a).start()

                @pl.when(k != y)
                def _():
                    for half, a in pieces:
                        send(0, half, a).start()

        for half, a in pieces:
            for other in range(count):
                cols = pl.ds(a * width + other * lanes, lanes)
                remote(ins[a].at[0], out.at[half, :, cols], ss.at[0, half, a], rs.at[other, half, a], (c, f + 1 - 2 * k)).wait_recv()
        for i in range(1, count):
            for half, a in pieces:
                send(i, half, a).wait_send()

        @pl.when(k != y)
        def _():
            for half, a in pieces:
                send(0, half, a).wait_send()

    return pl.pallas_call(
        kernel,
        name=name,
        out_shape=jax.ShapeDtypeStruct((2, arrays[0].shape[1], number * width), arrays[0].dtype),
        in_specs=[ANY] * number,
        out_specs=ANY,
        scratch_shapes=[DMA((count, 2, number)), DMA((count, 2, number))],
        compiler_params=params(),
    )(*arrays)


def tokens_to_heads(array, name):
    count = lax.axis_size("ctx")
    lanes = array.shape[2] // count

    def kernel(a_ref, out, ss, rs):
        c, f, z, y, x, k = place()

        def part(half, pair):
            return a_ref.at[half, :, pl.ds(pl.multiple_of(pair * lanes, lanes), lanes)]

        def peer(i):
            pair = (2 * z + k + i) % count
            return pair, (2 * (pair // 2) + k, 2 * x + pair % 2)

        def send(i, half):
            pair, dev = peer(i)
            b = block_at(c, half, count)
            return remote(part(half, pair), out.at[b], ss.at[i, half], rs.at[b], dev)

        for i in range(1, count):
            for half in range(2):
                send(i, half).start()

        @pl.when(k == y)
        def _():
            for half in range(2):
                b = block_at(c, half, count)
                pltpu.make_async_copy(part(half, 2 * z + k), out.at[b], rs.at[b]).start()

        @pl.when(k != y)
        def _():
            for half in range(2):
                send(0, half).start()

        for b in range(2 * count):
            remote(part(0, 0), out.at[b], ss.at[0, 0], rs.at[b], (c, f + 1 - 2 * k)).wait_recv()
        for i in range(1, count):
            for half in range(2):
                send(i, half).wait_send()

        @pl.when(k != y)
        def _():
            for half in range(2):
                send(0, half).wait_send()

    return pl.pallas_call(
        kernel,
        name=name,
        out_shape=jax.ShapeDtypeStruct((2 * count, array.shape[1], lanes), array.dtype),
        in_specs=[ANY],
        out_specs=ANY,
        scratch_shapes=[DMA((count, 2)), DMA((2 * count,))],
        compiler_params=params(),
    )(array)


TILE = 256


def attend_forward(qkv, start_column, first_tile, scale):
    length = qkv.shape[0]
    tiles = length // TILE
    lanes = 128
    size = lanes // 2

    def kernel(first, q_ref, k_ref, v_ref, s_ref, o32, o16, lse):
        i = pl.program_id(0)
        lane = lax.broadcasted_iota(jnp.int32, (TILE, lanes), 1)
        query = q_ref[...]
        zero = jnp.zeros_like(query)
        heads = [jnp.where(lane < size, query, zero), jnp.where(lane >= size, query, zero)]
        start = s_ref[...]
        row = i * TILE + lax.broadcasted_iota(jnp.int32, (TILE, TILE), 0)
        column = lax.broadcasted_iota(jnp.int32, (TILE, TILE), 1)

        def step(j, carried):
            at = pl.multiple_of(j * TILE, TILE)
            keys = k_ref[pl.ds(at, TILE), :]
            values = v_ref[pl.ds(at, TILE), :]
            seen = (column + at <= row) & (column + at >= start)
            out = []
            for h in range(2):
                top, total, mixed = carried[h]
                score = lax.dot_general(heads[h], keys, (((1,), (1,)), ((), ())), preferred_element_type=F32) * scale
                score = jnp.where(seen, score, NEGATIVE)
                new_top = jnp.maximum(top, jnp.max(score, axis=1, keepdims=True))
                weight = jnp.where(seen, jnp.exp(score - new_top), 0.0)
                shrink = jnp.exp(top - new_top)
                total = total * shrink + jnp.sum(weight, axis=1, keepdims=True)
                mixed = mixed * shrink + jnp.dot(weight.astype(BF), values, preferred_element_type=F32)
                out.append((new_top, total, mixed))
            return tuple(out)

        begin = (
            jnp.full((TILE, 1), NEGATIVE, F32),
            jnp.zeros((TILE, 1), F32),
            jnp.zeros((TILE, lanes), F32),
        )
        done = lax.fori_loop(first[i], i + 1, step, (begin, begin))
        ready = [mixed / total for _, total, mixed in done]
        logs = [top + jnp.log(total) for top, total, _ in done]
        mixed = jnp.where(lane < size, ready[0], ready[1])
        o32[...] = mixed
        o16[...] = mixed.astype(BF)
        lse[...] = jnp.where(lane < size, logs[0], logs[1])

    return pl.pallas_call(
        kernel,
        name="attend_forward",
        grid_spec=pltpu.PrefetchScalarGridSpec(
            num_scalar_prefetch=1,
            grid=(tiles,),
            in_specs=[
                pl.BlockSpec((TILE, lanes), lambda i, first: (i, 0)),
                pl.BlockSpec((length, lanes), lambda i, first: (0, 1)),
                pl.BlockSpec((length, lanes), lambda i, first: (0, 2)),
                pl.BlockSpec((TILE, 1), lambda i, first: (i, 0)),
            ],
            out_specs=[pl.BlockSpec((TILE, lanes), lambda i, first: (i, 0))] * 3,
        ),
        out_shape=(
            jax.ShapeDtypeStruct((length, lanes), F32),
            jax.ShapeDtypeStruct((length, lanes), BF),
            jax.ShapeDtypeStruct((length, lanes), F32),
        ),
        compiler_params=params(False),
    )(first_tile, qkv, qkv, qkv, start_column)


def attend_backward(qkv, grad, start_row, log_rows, delta_rows, first_tile, scale):
    length = qkv.shape[0]
    tiles = length // TILE
    lanes = 128
    size = lanes // 2

    def kernel(first, q_ref, k_ref, v_ref, g_ref, s_ref, l_ref, d_ref, dq, dk, dv, acc_k, acc_v):
        i = pl.program_id(0)

        @pl.when(i == 0)
        def _():
            acc_k[...] = jnp.zeros_like(acc_k)
            acc_v[...] = jnp.zeros_like(acc_v)

        lane = lax.broadcasted_iota(jnp.int32, (TILE, lanes), 1)

        def split(value):
            zero = jnp.zeros_like(value)
            return [jnp.where(lane < size, value, zero), jnp.where(lane >= size, value, zero)]

        queries, grads = split(q_ref[...]), split(g_ref[...])
        start = s_ref[...]
        key_row = lax.broadcasted_iota(jnp.int32, (TILE, TILE), 0)
        query_column = i * TILE + lax.broadcasted_iota(jnp.int32, (TILE, TILE), 1)

        def step(j, running):
            at = pl.multiple_of(j * TILE, TILE)
            keys = k_ref[pl.ds(at, TILE), :]
            values = v_ref[pl.ds(at, TILE), :]
            key_parts = split(keys)
            seen = (key_row + at <= query_column) & (key_row + at >= start)
            key_sum = jnp.zeros((TILE, lanes), F32)
            value_sum = jnp.zeros((TILE, lanes), F32)
            for h in range(2):
                score = lax.dot_general(keys, queries[h], (((1,), (1,)), ((), ())), preferred_element_type=F32) * scale
                weight = jnp.where(seen, jnp.exp(score - l_ref[h : h + 1, :]), 0.0)
                grad_weight = lax.dot_general(
                    values, grads[h], (((1,), (1,)), ((), ())), preferred_element_type=F32
                )
                grad_score = (weight * (grad_weight - d_ref[h : h + 1, :])).astype(BF)
                value_sum += jnp.dot(weight.astype(BF), grads[h], preferred_element_type=F32)
                key_sum += jnp.dot(grad_score, queries[h], preferred_element_type=F32)
                running += lax.dot_general(
                    grad_score, key_parts[h], (((0,), (0,)), ((), ())), preferred_element_type=F32
                )
            acc_k[pl.ds(at, TILE), :] += key_sum
            acc_v[pl.ds(at, TILE), :] += value_sum
            return running

        total = lax.fori_loop(first[i], i + 1, step, jnp.zeros((TILE, lanes), F32))
        dq[...] = (total * scale).astype(BF)

        @pl.when(i == tiles - 1)
        def _():
            dk[...] = (acc_k[...] * scale).astype(BF)
            dv[...] = acc_v[...].astype(BF)

    return pl.pallas_call(
        kernel,
        name="attend_backward",
        grid_spec=pltpu.PrefetchScalarGridSpec(
            num_scalar_prefetch=1,
            grid=(tiles,),
            in_specs=[
                pl.BlockSpec((TILE, lanes), lambda i, first: (i, 0)),
                pl.BlockSpec((length, lanes), lambda i, first: (0, 1)),
                pl.BlockSpec((length, lanes), lambda i, first: (0, 2)),
                pl.BlockSpec((TILE, lanes), lambda i, first: (i, 0)),
                pl.BlockSpec((1, TILE), lambda i, first: (0, i)),
                pl.BlockSpec((2, TILE), lambda i, first: (0, i)),
                pl.BlockSpec((2, TILE), lambda i, first: (0, i)),
            ],
            out_specs=[
                pl.BlockSpec((TILE, lanes), lambda i, first: (i, 0)),
                pl.BlockSpec((length, lanes), lambda i, first: (0, 0)),
                pl.BlockSpec((length, lanes), lambda i, first: (0, 0)),
            ],
            scratch_shapes=[pltpu.VMEM((length, lanes), F32), pltpu.VMEM((length, lanes), F32)],
        ),
        out_shape=(jax.ShapeDtypeStruct((length, lanes), BF),) * 3,
        compiler_params=params(False),
    )(first_tile, qkv, qkv, qkv, grad, start_row, log_rows, delta_rows)


def dispatch_rows(arrays):
    count = lax.axis_size("ctx")
    number = len(arrays)
    _, own_experts, cap, width = arrays[0].shape

    def kernel(*refs):
        ins, outs = refs[:number], refs[number : 2 * number]
        ss1, rs1, ssx, rsx, sss, rss, ssf, rsf = refs[2 * number :]
        c, f, z, y, x, k = place()
        sib = (c, f + 1 - 2 * k)
        xn = (c, (f + 2) % 4)

        def here(a, stream, source):
            return outs[a].at[:, stream, source]

        def first(a, i):
            ct = (c + i) % count
            return remote(ins[a].at[ct], here(a, f, c), ss1.at[a, i], rs1.at[a, c], (ct, f))

        for a in range(number):
            pltpu.make_async_copy(ins[a].at[c], here(a, f, c), rs1.at[a, c]).start()
            for i in range(1, count):
                first(a, i).start()

        def hop(a, stream, source, ss, rs, dev):
            return remote(here(a, stream, source), here(a, stream, source), ss.at[a, source], rs.at[a, source], dev)

        other = (f + 2) % 4
        for a in range(number):
            for i in range(count):
                cs = (c + i) % count
                remote(here(a, f, cs), here(a, f, cs), ss1.at[a, 0], rs1.at[a, cs], sib).wait_recv()
                hop(a, f, cs, ssx, rsx, xn).start()
                hop(a, f, cs, sss, rss, sib).start()
        for a in range(number):
            for i in range(count):
                cs = (c + i) % count
                hop(a, other, cs, ssx, rsx, xn).wait_recv()
                hop(a, other, cs, ssf, rsf, sib).start()
        for a in range(number):
            for i in range(count):
                if i:
                    first(a, i).wait_send()
                cs = (c + i) % count
                hop(a, f, cs, ssx, rsx, xn).wait_send()
                hop(a, sib[1], cs, sss, rss, sib).wait()
                hop(a, (sib[1] + 2) % 4, cs, ssf, rsf, sib).wait()

    return pl.pallas_call(
        kernel,
        name="dispatch_rows",
        out_shape=(jax.ShapeDtypeStruct((own_experts, 4, count, cap, width), arrays[0].dtype),) * number,
        in_specs=[ANY] * number,
        out_specs=(ANY,) * number,
        scratch_shapes=[DMA((number, count))] * 8,
        compiler_params=params(),
    )(*arrays)


def return_rows(arrays):
    count = lax.axis_size("ctx")
    number = len(arrays)
    _, experts, _, cap, width = arrays[0].shape
    groups = 2
    chunk = experts // groups

    def kernel(*refs):
        ins, outs = refs[:number], refs[number : 2 * number]
        near, far, got_near, got_far, got_x = refs[2 * number : 2 * number + 5]
        ssn, rsn, ssf, rsf, ssx, rsx, sso, rso, loc = refs[2 * number + 5 :]
        c, f, z, y, x, k = place()
        sib = (c, f + 1 - 2 * k)
        other = (f + 2) % 4
        xn = (c, other)
        sib_other = (sib[1] + 2) % 4

        def to_near(a):
            return remote(ins[a].at[sib[1]], got_near.at[a], ssn.at[a], rsn.at[a], sib)

        def to_far(a):
            return remote(ins[a].at[sib_other], got_far.at[a], ssf.at[a], rsf.at[a], sib)

        def load(a, stream, buf, i):
            return pltpu.make_async_copy(ins[a].at[stream], buf.at[a], loc.at[a, i])

        for a in range(number):
            to_far(a).start()
            load(a, other, far, 0).start()
        for a in range(number):
            to_near(a).start()
            load(a, f, near, 1).start()

        def across(a, e):
            return remote(far.at[a, e], got_x.at[a, e], ssx.at[a, e], rsx.at[a, e], xn)

        for a in range(number):
            load(a, other, far, 0).wait()
            to_far(a).wait_recv()
            for e in range(experts):
                far[a, e] = (far[a, e].astype(F32) + got_far[a, e].astype(F32)).astype(BF)
                across(a, e).start()

        def home(a, g, i):
            ct = (c + i) % count
            return remote(
                near.at[a, pl.ds(g * chunk, chunk), ct],
                outs[a].at[c, pl.ds(g * chunk, chunk)],
                sso.at[a, g, i],
                rso.at[a, g, c],
                (ct, f),
            )

        def stay(a, g):
            return pltpu.make_async_copy(
                near.at[a, pl.ds(g * chunk, chunk), c], outs[a].at[c, pl.ds(g * chunk, chunk)], rso.at[a, g, c]
            )

        for a in range(number):
            load(a, f, near, 1).wait()
            to_near(a).wait_recv()
            for g in range(groups):
                for e in range(g * chunk, (g + 1) * chunk):
                    across(a, e).wait_recv()
                    near[a, e] = (
                        near[a, e].astype(F32) + got_near[a, e].astype(F32) + got_x[a, e].astype(F32)
                    ).astype(BF)
                for i in range(1, count):
                    home(a, g, i).start()
                stay(a, g).start()
        for a in range(number):
            to_far(a).wait_send()
            to_near(a).wait_send()
            for e in range(experts):
                across(a, e).wait_send()
            for g in range(groups):
                for i in range(count):
                    cs = (c + i) % count
                    remote(
                        near.at[a, pl.ds(g * chunk, chunk), cs],
                        outs[a].at[cs, pl.ds(g * chunk, chunk)],
                        sso.at[a, g, i],
                        rso.at[a, g, cs],
                        sib,
                    ).wait_recv()
                    if i:
                        home(a, g, i).wait_send()

    buffer = pltpu.VMEM((number, experts, count, cap, width), BF)
    return pl.pallas_call(
        kernel,
        name="return_rows",
        out_shape=(jax.ShapeDtypeStruct((count, experts, cap, width), BF),) * number,
        in_specs=[ANY] * number,
        out_specs=(ANY,) * number,
        scratch_shapes=[buffer] * 5
        + [DMA((number,))] * 4
        + [DMA((number, experts))] * 2
        + [DMA((number, groups, count))] * 2
        + [DMA((number, 2))],
        compiler_params=params(),
    )(*arrays)


ROOT = math.sqrt(2.0 / math.pi)
CUBIC = 0.044715


def experts_step(rows, grads, first_proj, second_proj):
    number, count, width = rows.shape
    units = first_proj.shape[2]
    quarter = count // 4

    def kernel(r_ref, g_ref, a_ref, b_ref, out, back, da, db):
        row, grad = r_ref[0], g_ref[0]
        first = a_ref[0].astype(BF)
        second = b_ref[0].astype(BF)
        hidden = jnp.dot(row, first, preferred_element_type=F32)
        upstream = lax.dot_general(grad, second, (((1,), (1,)), ((), ())), preferred_element_type=F32)
        bent = jnp.tanh(ROOT * (hidden + CUBIC * hidden * hidden * hidden))
        active = (0.5 * hidden * (1.0 + bent)).astype(BF)
        slope = 0.5 * (1.0 + bent) + 0.5 * hidden * (1.0 - bent * bent) * (ROOT * (1.0 + 3.0 * CUBIC * hidden * hidden))
        grad_hidden = (upstream * slope).astype(BF)
        term = lax.dot_general(grad_hidden, first, (((1,), (1,)), ((), ())), preferred_element_type=F32).astype(BF)
        mixed = jnp.dot(active, second, preferred_element_type=F32).astype(BF)
        for s in range(4):
            back[s, 0] = term[s * quarter : (s + 1) * quarter]
            out[s, 0] = mixed[s * quarter : (s + 1) * quarter]
        da[0] = lax.dot_general(row, grad_hidden, (((0,), (0,)), ((), ())), preferred_element_type=F32)
        db[0] = lax.dot_general(active, grad, (((0,), (0,)), ((), ())), preferred_element_type=F32)

    whole = pl.BlockSpec((1, count, width), lambda e: (e, 0, 0))
    left = pl.BlockSpec((1, width, units), lambda e: (e, 0, 0))
    right = pl.BlockSpec((1, units, width), lambda e: (e, 0, 0))
    parts = pl.BlockSpec((4, 1, quarter, width), lambda e: (0, e, 0, 0))
    return pl.pallas_call(
        kernel,
        name="experts_step",
        grid=(number,),
        in_specs=[whole, whole, left, right],
        out_specs=[parts, parts, left, right],
        out_shape=(
            jax.ShapeDtypeStruct((4, number, quarter, width), BF),
            jax.ShapeDtypeStruct((4, number, quarter, width), BF),
            jax.ShapeDtypeStruct(first_proj.shape, F32),
            jax.ShapeDtypeStruct(second_proj.shape, F32),
        ),
        compiler_params=params(False),
    )(rows, grads, first_proj, second_proj)


def sum_weight_grads(parts):
    count = lax.axis_size("ctx")
    depth = count // 2
    _, rows, wide = parts.shape
    lanes = wide // 3
    width = count * lanes

    def kernel(p_ref, out, got, held, ss_r, rs_r, ss_up, ss_dn, rs_z, ss_a, ss_b, rs_o):
        c, f, z, y, x, k = place()
        peers = [
            (2 * z + 1 - y, f, 2 * x + 1 - y),
            (c, (f + 2) % 4, 2 * (1 - x) + y),
            (2 * z + 1 - y, (f + 2) % 4, 2 * (1 - x) + 1 - y),
        ]
        sib = (c, f + 1 - 2 * k)
        up = (c + 2, f)
        down = (c - 2, f)

        def scatter(d):
            cp, fp, shard = peers[d]
            return remote(p_ref.at[shard], got.at[d], ss_r.at[d], rs_r.at[d], (cp, fp))

        for d in (2, 1, 0):
            scatter(d).start()
        total = p_ref[2 * x + y].astype(F32)
        for d in range(3):
            scatter(d).wait_recv()
            total += got[d].astype(F32)
        held[z] = total.astype(BF)

        def chain(zb, ss, dev):
            return remote(held.at[zb], held.at[zb], ss, rs_z.at[zb], dev)

        def piece(zb, j):
            return held.at[zb, :, pl.ds(j * lanes, lanes)]

        def there(zb, j):
            return out.at[:, pl.ds(pl.multiple_of(j * width + (2 * zb + k) * lanes, lanes), lanes)]

        def own_column(zb, j):
            return remote(piece(zb, j), there(zb, j), ss_a.at[zb, j], rs_o.at[2 * zb + k, j], (c, 2 * x + y))

        def own_local(zb, j):
            return pltpu.make_async_copy(piece(zb, j), there(zb, j), rs_o.at[2 * zb + k, j])

        def next_column(zb, j):
            return remote(
                piece(zb, j), there(zb, j), ss_b.at[zb, j], rs_o.at[2 * zb + k, j], (2 * z + 1 - y, 2 * x + y)
            )

        def spread(zb):
            for j in range(3):
                next_column(zb, j).start()

            @pl.when(k == y)
            def _():
                for j in range(3):
                    own_local(zb, j).start()

            @pl.when(k != y)
            def _():
                for j in range(3):
                    own_column(zb, j).start()

        @pl.when(z < depth - 1)
        def _():
            chain(z, ss_up.at[0], up).start()

        @pl.when(z > 0)
        def _():
            chain(z, ss_dn.at[0], down).start()

        spread(z)
        for j in range(1, depth):

            @pl.when(z - j >= 0)
            def _(j=j):
                chain(z - j, ss_up.at[j], sib).wait_recv()

                @pl.when(z < depth - 1)
                def _():
                    chain(z - j, ss_up.at[j], up).start()

                spread(z - j)

            @pl.when(z + j <= depth - 1)
            def _(j=j):
                chain(z + j, ss_dn.at[j], sib).wait_recv()

                @pl.when(z > 0)
                def _():
                    chain(z + j, ss_dn.at[j], down).start()

                spread(z + j)

        for d in range(3):
            scatter(d).wait_send()
        for pair in range(count):
            for j in range(3):
                remote(
                    piece(0, j), out.at[:, pl.ds(j * width + pair * lanes, lanes)], ss_a.at[0, j], rs_o.at[pair, j], sib
                ).wait_recv()
        for j in range(depth):

            @pl.when((z < depth - 1) & (z - j >= 0))
            def _(j=j):
                chain(z - j, ss_up.at[j], up).wait_send()

            @pl.when((z > 0) & (z + j <= depth - 1))
            def _(j=j):
                chain(z + j, ss_dn.at[j], down).wait_send()

        for zb in range(depth):
            for j in range(3):
                next_column(zb, j).wait_send()

        @pl.when(k != y)
        def _():
            for zb in range(depth):
                for j in range(3):
                    own_column(zb, j).wait_send()

    return pl.pallas_call(
        kernel,
        name="sum_weight_grads",
        out_shape=jax.ShapeDtypeStruct((rows, 3 * width), BF),
        in_specs=[pl.BlockSpec(memory_space=pltpu.VMEM)],
        out_specs=ANY,
        scratch_shapes=[
            pltpu.VMEM((3, rows, wide), BF),
            pltpu.VMEM((depth, rows, wide), BF),
            DMA((3,)), DMA((3,)), DMA((depth,)), DMA((depth,)), DMA((depth,)),
            DMA((depth, 3)), DMA((depth, 3)), DMA((count, 3)),
        ],
        compiler_params=params(),
    )(parts)


def slots_of(routes):
    tokens = routes.shape[0]
    chosen = routes[:, None] == jnp.arange(EXPERTS, dtype=jnp.int32)[None, :]
    earlier = (jnp.arange(tokens)[:, None] >= jnp.arange(tokens)[None, :]).astype(BF)
    running = jnp.dot(earlier, chosen.astype(BF), preferred_element_type=F32)
    rank = jnp.sum(jnp.where(chosen, running, 0.0), axis=1).astype(jnp.int32) - 1
    slot = routes * CAP + rank
    return (jnp.arange(EXPERTS * CAP, dtype=jnp.int32)[:, None] == slot[None, :]).astype(BF)


def by_head_pairs(
    tokens, doc_starts, expert_ids, query_key_value_weight, output_weight_matrix, expert_in, expert_out, gain_one, gain_two, grad_output
):
    half_rows = tokens.shape[3]
    width = tokens.shape[4]
    count = lax.axis_size("ctx")
    rows = 2 * half_rows
    length = count * rows
    scale = (width // HEADS) ** (-0.5)
    c, f, z, y, x, k = place()
    pair = 2 * z + k
    lanes = 2 * (width // HEADS)
    start_x = tokens.reshape(rows, width).astype(F32)
    cotangent = grad_output.reshape(rows, width)
    qkv_low = query_key_value_weight.astype(BF)
    out_proj = lax.all_gather(output_weight_matrix.astype(BF), "fsdp", axis=0, tiled=True)
    first_normed, hat_one, inverse_one = norm_forward(start_x, gain_one)
    normed = first_normed.astype(BF)
    stream, starts, projection = gather_stream(
        normed.reshape(2, half_rows, width), doc_starts.reshape(2, half_rows), qkv_low
    )
    stream = stream.reshape(length, width)
    projection = projection.reshape(width, 3 * width)
    own_columns = jnp.concatenate(
        [lax.dynamic_slice(projection, (0, j * width + pair * lanes), (width, lanes)) for j in range(3)], axis=1
    )
    qkv = jnp.dot(stream, own_columns, preferred_element_type=F32).astype(BF)
    start_line = jnp.concatenate([starts[:, 0].reshape(-1), starts[::-1, 1].reshape(-1)])
    first_tile = jnp.min(start_line.reshape(-1, TILE), axis=1) // TILE
    mixed32, mixed16, logs = attend_forward(qkv, start_line[:, None], first_tile, scale)
    mixed = heads_to_tokens([mixed16.reshape(2 * count, half_rows, lanes)], "mixed_to_tokens").reshape(rows, width)
    middle = start_x + jnp.dot(mixed, out_proj, preferred_element_type=F32)
    normed_two, hat_two, inverse_two = norm_forward(middle, gain_two)
    routed = normed_two.astype(BF)
    dispatch = slots_of(expert_ids.reshape(rows))
    own_experts = EXPERTS // count
    shape = (count, own_experts, CAP, width)
    send_rows = jnp.dot(dispatch, routed, preferred_element_type=F32).astype(BF).reshape(shape)
    send_grads = jnp.dot(dispatch, cotangent, preferred_element_type=F32).astype(BF).reshape(shape)
    all_rows, all_grads = dispatch_rows([send_rows, send_grads])
    flat = (own_experts, 4 * count * CAP, width)
    out_terms, back_terms, grad_in, grad_outw = experts_step(
        all_rows.reshape(flat), all_grads.reshape(flat), expert_in, expert_out
    )
    folded = (4, own_experts, count, CAP, width)
    returned, back_rows = return_rows([back_terms.reshape(folded), out_terms.reshape(folded)])
    slots = (EXPERTS * CAP, width)
    pick = (((0,), (0,)), ((), ()))
    grad_routed = lax.dot_general(dispatch, returned.reshape(slots), pick, preferred_element_type=F32)
    expert_sum = lax.dot_general(dispatch, back_rows.reshape(slots), pick, preferred_element_type=F32)
    block_out = (middle + expert_sum).astype(BF)
    grad_mid_norm, grad_gain_two = norm_backward(grad_routed[None], hat_two[None], inverse_two[None], gain_two)
    grad_middle = cotangent.astype(F32) + grad_mid_norm[0]
    grad_attn = grad_middle.astype(BF)
    grad_outproj = lax.dot_general(mixed, grad_attn, pick, preferred_element_type=F32)
    grad_mixed = lax.dot_general(grad_attn, out_proj, (((1,), (1,)), ((), ())), preferred_element_type=F32).astype(BF)
    grad_heads = tokens_to_heads(grad_mixed.reshape(2, half_rows, width), "grad_to_heads").reshape(length, lanes)
    delta = jnp.sum((grad_heads.astype(F32) * mixed32).reshape(length, 2, lanes // 2), axis=2).T
    log_rows = logs[:, :: lanes // 2].T
    grad_q, grad_k, grad_v = attend_backward(qkv, grad_heads, start_line[None], log_rows, delta, first_tile, scale)
    blocks = (2 * count, half_rows, lanes)
    grad_projected = heads_to_tokens(
        [grad_q.reshape(blocks), grad_k.reshape(blocks), grad_v.reshape(blocks)], "grad_to_tokens"
    ).reshape(rows, 3 * width)
    own_grads = jnp.concatenate([grad_q, grad_k, grad_v], axis=1)
    parts = lax.dot_general(stream, own_grads, pick, preferred_element_type=F32).astype(BF)
    shard_rows = width // 4
    weight_grad = sum_weight_grads(parts.reshape(4, shard_rows, 3 * lanes)).astype(F32)
    grad_normed = lax.dot_general(grad_projected, projection, (((1,), (1,)), ((), ())), preferred_element_type=F32)
    grad_in_norm, _ = norm_backward(grad_normed[None], hat_one[None], inverse_one[None], gain_one)
    grad_start = grad_middle + grad_in_norm[0]
    own_gain = lax.dynamic_slice(gain_one, (f * shard_rows,), (shard_rows,))
    shard_gain_one = jnp.sum(weight_grad * qkv_low.astype(F32), axis=1) / own_gain
    summed_gain = lax.psum(grad_gain_two, ("ctx", "fsdp"))
    shard_gain_two = lax.dynamic_slice(summed_gain, (f * shard_rows,), (shard_rows,))
    shard_out = lax.psum_scatter(grad_outproj.astype(BF), "fsdp", scatter_dimension=0, tiled=True)
    shard_out = lax.psum(shard_out, "ctx").astype(F32)
    return (
        block_out.reshape(tokens.shape),
        grad_start.reshape(tokens.shape),
        weight_grad,
        shard_out,
        grad_in,
        grad_outw,
        shard_gain_one,
        shard_gain_two,
    )


def solution(mesh):
    pairs = mesh.shape["ctx"] * 2 == HEADS and mesh.shape["fsdp"] == 4
    return jax.shard_map(
        by_head_pairs if pairs else shards,
        mesh=mesh,
        in_specs=(
            P("fsdp", "ctx", None, None, None),
            P("fsdp", "ctx", None, None),
            P("fsdp", "ctx", None, None, None),
            P("fsdp", None),
            P("fsdp", None),
            P("ctx", None, "fsdp"),
            P("ctx", "fsdp", None),
            P(),
            P(),
            P("fsdp", "ctx", None, None, None),
        ),
        out_specs=(
            P("fsdp", "ctx", None, None, None),
            P("fsdp", "ctx", None, None, None),
            P("fsdp", None),
            P("fsdp", None),
            P("ctx", None, "fsdp"),
            P("ctx", "fsdp", None),
            P("fsdp"),
            P("fsdp"),
        ),
        check_vma=False,
    )
```

```python
import math

import jax
import jax.numpy as jnp
from jax import lax
from jax.experimental import pallas as pl
from jax.experimental.pallas import tpu as pltpu
from jax.sharding import PartitionSpec as P

HEADS = 16
EXPERTS = 64
CAP = 8


EPS = 1e-05
NEGATIVE = -1e30


def position_of(row_ids, ctx_count, half_rows):
    device = row_ids // (2 * half_rows)
    upper_half = row_ids // half_rows % 2
    offset = row_ids % half_rows
    return jnp.where(
        upper_half == 0,
        device * half_rows + offset,
        (2 * ctx_count - 1 - device) * half_rows + offset,
    )


def norm_forward(value, gain):
    row_mean = jnp.mean(value, axis=-1, keepdims=True)
    centred = value - row_mean
    inverse = lax.rsqrt(jnp.mean(centred * centred, axis=-1, keepdims=True) + EPS)
    normed = centred * inverse
    return (normed * gain, normed, inverse)


def norm_backward(gradient, normed, inverse, gain):
    scaled = gradient * gain
    mean_grad = jnp.mean(scaled, axis=-1, keepdims=True)
    mean_proj = jnp.mean(scaled * normed, axis=-1, keepdims=True)
    return (
        inverse * (scaled - mean_grad - normed * mean_proj),
        jnp.sum(gradient * normed, axis=(0, 1)),
    )


def scores(query, keys, query_pos, key_pos, query_start, score_scale):
    raw_scores = (
        jnp.einsum("qshe,kshe->shqk", query, keys, preferred_element_type=jnp.float32) * score_scale
    )
    visible = (key_pos[None, None, None, :] <= query_pos[None, None, :, None]) & (
        key_pos[None, None, None, :] >= query_start.T[:, None, :, None]
    )
    return jnp.where(visible, raw_scores, NEGATIVE)


def log_totals(query, keys, query_pos, query_start, score_scale, ctx_count, half_rows, key_block):
    block_count = keys.shape[0] // key_block
    carry_shape = (query.shape[1], query.shape[2], query.shape[0])

    def log_one_block(block_index, carried):
        running_max, running = carried
        first_row = block_index * key_block
        key_piece = lax.dynamic_slice_in_dim(keys, first_row, key_block, 0)
        key_pos = position_of(
            first_row + jnp.arange(key_block, dtype=jnp.int32), ctx_count, half_rows
        )
        score_rows = scores(query, key_piece, query_pos, key_pos, query_start, score_scale)
        new_max = jnp.maximum(running_max, jnp.max(score_rows, axis=-1))
        running = running * jnp.exp(running_max - new_max) + jnp.sum(
            jnp.exp(score_rows - new_max[..., None]), axis=-1
        )
        return (new_max, running)

    running_max, running = lax.fori_loop(
        0,
        block_count,
        log_one_block,
        (jnp.full(carry_shape, NEGATIVE, jnp.float32), jnp.zeros(carry_shape, jnp.float32)),
    )
    return running_max + jnp.log(running)


def attend(
    query,
    keys,
    values,
    query_pos,
    query_start,
    log_total,
    score_scale,
    ctx_count,
    half_rows,
    key_block,
):
    block_count = keys.shape[0] // key_block
    zeros_init = jnp.zeros(query.shape, jnp.float32)

    def attend_one_block(block_index, carried):
        output, remainder = carried
        first_row = block_index * key_block
        key_piece = lax.dynamic_slice_in_dim(keys, first_row, key_block, 0)
        value_piece = lax.dynamic_slice_in_dim(values, first_row, key_block, 0)
        key_pos = position_of(
            first_row + jnp.arange(key_block, dtype=jnp.int32), ctx_count, half_rows
        )
        weights = jnp.exp(
            scores(query, key_piece, query_pos, key_pos, query_start, score_scale)
            - log_total[..., None]
        )
        rounded = weights.astype(jnp.bfloat16)
        leftover = (weights - rounded.astype(jnp.float32)).astype(jnp.bfloat16)
        output = output + jnp.einsum(
            "shqk,kshe->qshe", rounded, value_piece, preferred_element_type=jnp.float32
        )
        remainder = remainder + jnp.einsum(
            "shqk,kshe->qshe", leftover, value_piece, preferred_element_type=jnp.float32
        )
        return (output, remainder)

    return lax.fori_loop(0, block_count, attend_one_block, (zeros_init, zeros_init))


def query_grads(
    query,
    keys,
    values,
    grad_heads,
    query_pos,
    query_start,
    log_total,
    row_delta,
    score_scale,
    ctx_count,
    half_rows,
    key_block,
):
    block_count = keys.shape[0] // key_block

    def query_one_block(block_index, running):
        first_row = block_index * key_block
        key_piece = lax.dynamic_slice_in_dim(keys, first_row, key_block, 0)
        value_piece = lax.dynamic_slice_in_dim(values, first_row, key_block, 0)
        key_pos = position_of(
            first_row + jnp.arange(key_block, dtype=jnp.int32), ctx_count, half_rows
        )
        weights = jnp.exp(
            scores(query, key_piece, query_pos, key_pos, query_start, score_scale)
            - log_total[..., None]
        )
        grad_weight = jnp.einsum(
            "qshe,kshe->shqk", grad_heads, value_piece, preferred_element_type=jnp.float32
        )
        grad_score = (weights * (grad_weight - row_delta[..., None])).astype(jnp.bfloat16)
        return running + jnp.einsum(
            "shqk,kshe->qshe", grad_score, key_piece, preferred_element_type=jnp.float32
        )

    return (
        lax.fori_loop(0, block_count, query_one_block, jnp.zeros(query.shape, jnp.float32))
        * score_scale
    )


def key_grads(
    query,
    grad_heads,
    query_pos,
    query_start,
    log_total,
    row_delta,
    key_piece,
    value_piece,
    key_pos,
    score_scale,
):
    weights = jnp.exp(
        scores(query, key_piece, query_pos, key_pos, query_start, score_scale)
        - log_total[..., None]
    )
    grad_weight = jnp.einsum(
        "qshe,kshe->shqk", grad_heads, value_piece, preferred_element_type=jnp.float32
    )
    grad_score = (weights * (grad_weight - row_delta[..., None])).astype(jnp.bfloat16)
    key_part = (
        jnp.einsum("shqk,qshe->kshe", grad_score, query, preferred_element_type=jnp.float32)
        * score_scale
    )
    value_part = jnp.einsum(
        "shqk,qshe->kshe",
        weights.astype(jnp.bfloat16),
        grad_heads,
        preferred_element_type=jnp.float32,
    )
    return (key_part, value_part)


def shards(
    tokens,
    doc_starts,
    expert_ids,
    query_key_value_weight,
    output_weight_matrix,
    expert_in,
    expert_out,
    gain_one,
    gain_two,
    grad_output,
):
    seq_dev = tokens.shape[0]
    half_rows = tokens.shape[3]
    model_width = tokens.shape[4]
    local_rows = 2 * half_rows
    ctx_count = lax.axis_size("ctx")
    head_count = HEADS
    head_size = model_width // head_count
    score_scale = head_size ** (-0.5)
    keys_total = ctx_count * local_rows
    key_block = min(512, keys_total)
    own_rows = lax.axis_index("ctx") * local_rows + jnp.arange(local_rows, dtype=jnp.int32)
    query_pos = position_of(own_rows, ctx_count, half_rows)
    query_start = doc_starts.reshape(seq_dev, local_rows).T
    routes_local = expert_ids.reshape(seq_dev, local_rows).T
    start_x = (
        tokens.reshape(seq_dev, local_rows, model_width).transpose(1, 0, 2).astype(jnp.float32)
    )
    cotangent = grad_output.reshape(seq_dev, local_rows, model_width).transpose(1, 0, 2)
    projection, out_proj = (
        lax.all_gather(query_key_value_weight.astype(jnp.bfloat16), "fsdp", axis=0, tiled=True),
        lax.all_gather(output_weight_matrix.astype(jnp.bfloat16), "fsdp", axis=0, tiled=True),
    )
    first_normed_rows, hat_one, inverse_one = norm_forward(start_x, gain_one)
    normed_low = first_normed_rows.astype(jnp.bfloat16)
    projected_rows = jnp.einsum(
        "tsd,de->tse", normed_low, projection, preferred_element_type=jnp.float32
    ).astype(jnp.bfloat16)
    query = projected_rows[..., :model_width]
    keys = projected_rows[..., model_width : 2 * model_width]
    values = projected_rows[..., 2 * model_width :]
    key_all, value_all = (
        lax.all_gather(keys, "ctx", axis=0, tiled=True),
        lax.all_gather(values, "ctx", axis=0, tiled=True),
    )
    query_heads = query.reshape(local_rows, seq_dev, head_count, head_size)
    key_heads = key_all.reshape(keys_total, seq_dev, head_count, head_size)
    value_heads = value_all.reshape(keys_total, seq_dev, head_count, head_size)
    log_total = log_totals(
        query_heads, key_heads, query_pos, query_start, score_scale, ctx_count, half_rows, key_block
    )
    mixed_heads_out, remainder = attend(
        query_heads,
        key_heads,
        value_heads,
        query_pos,
        query_start,
        log_total,
        score_scale,
        ctx_count,
        half_rows,
        key_block,
    )
    mixed_low = mixed_heads_out.astype(jnp.bfloat16).reshape(local_rows, seq_dev, model_width)
    attention_rows_out = jnp.einsum(
        "tsd,de->tse", mixed_low, out_proj, preferred_element_type=jnp.float32
    )
    middle = start_x + attention_rows_out
    normed_two, hat_two, inverse_two = norm_forward(middle, gain_two)
    routed = normed_two.astype(jnp.bfloat16)
    slot_count = EXPERTS * CAP
    per_owner = EXPERTS // ctx_count
    chosen = (routes_local[..., None] == jnp.arange(EXPERTS, dtype=jnp.int32)).astype(jnp.int32)
    earlier = (
        jnp.arange(local_rows)[:, None] >= jnp.arange(local_rows)[None, :]
    ).astype(jnp.bfloat16)
    running = jnp.einsum(
        "tu,use->tse", earlier, chosen.astype(jnp.bfloat16), preferred_element_type=jnp.float32
    )
    rank_within = jnp.sum(chosen * running.astype(jnp.int32), axis=-1) - 1
    slot_index = routes_local * CAP + rank_within
    dispatch = (
        slot_index.T[:, None, :] == jnp.arange(slot_count, dtype=jnp.int32)[None, :, None]
    ).astype(jnp.bfloat16)
    dispatch = dispatch.reshape(seq_dev, ctx_count, per_owner, CAP, local_rows)
    send_rows = jnp.einsum(
        "snect,tsd->nescd", dispatch, routed, preferred_element_type=jnp.float32
    ).astype(jnp.bfloat16)
    send_grads = jnp.einsum(
        "snect,tsd->nescd", dispatch, cotangent, preferred_element_type=jnp.float32
    ).astype(jnp.bfloat16)
    got_rows, got_grads = (
        lax.all_to_all(send_rows, "ctx", split_axis=0, concat_axis=0, tiled=True),
        lax.all_to_all(send_grads, "ctx", split_axis=0, concat_axis=0, tiled=True),
    )
    in_low = expert_in.astype(jnp.bfloat16)
    out_low = expert_out.astype(jnp.bfloat16)
    all_rows, all_grads = (
        lax.all_gather(got_rows, "fsdp", axis=2, tiled=True),
        lax.all_gather(got_grads, "fsdp", axis=2, tiled=True),
    )
    hidden = jnp.einsum("nercd,edf->nercf", all_rows, in_low, preferred_element_type=jnp.float32)
    active = jax.nn.gelu(hidden).astype(jnp.bfloat16)
    partial_rows = jnp.einsum(
        "nercf,efd->nercd", active, out_low, preferred_element_type=jnp.float32
    )
    result = lax.psum_scatter(
        partial_rows.astype(jnp.bfloat16), "fsdp", scatter_dimension=2, tiled=True
    )
    upstream = jnp.einsum(
        "nercd,efd->nercf", all_grads, out_low, preferred_element_type=jnp.float32
    )
    unused, gelu_back = jax.vjp(jax.nn.gelu, hidden)
    grad_hidden = gelu_back(upstream)[0].astype(jnp.bfloat16)
    grad_in = jnp.einsum(
        "nercd,nercf->edf", all_rows, grad_hidden, preferred_element_type=jnp.float32
    )
    grad_outw = jnp.einsum(
        "nercf,nercd->efd", active, all_grads, preferred_element_type=jnp.float32
    )
    row_part = jnp.einsum(
        "nercf,edf->nercd", grad_hidden, in_low, preferred_element_type=jnp.float32
    )
    row_grad = lax.psum_scatter(row_part, "fsdp", scatter_dimension=2, tiled=True).astype(
        jnp.bfloat16
    )
    back_rows = lax.all_to_all(result, "ctx", split_axis=0, concat_axis=0, tiled=True)
    expert_sum = jnp.einsum(
        "snect,nescd->tsd", dispatch, back_rows, preferred_element_type=jnp.float32
    )
    output_rows = middle + expert_sum
    returned = lax.all_to_all(row_grad, "ctx", split_axis=0, concat_axis=0, tiled=True)
    grad_routed = jnp.einsum(
        "snect,nescd->tsd", dispatch, returned, preferred_element_type=jnp.float32
    )
    grad_mid_norm, grad_gain_two = norm_backward(grad_routed, hat_two, inverse_two, gain_two)
    grad_middle = cotangent.astype(jnp.float32) + grad_mid_norm
    grad_attn = grad_middle.astype(jnp.bfloat16)
    grad_outproj = jnp.einsum(
        "tsd,tse->de", mixed_low, grad_attn, preferred_element_type=jnp.float32
    )
    grad_mixed = jnp.einsum(
        "tse,de->tsd", grad_attn, out_proj, preferred_element_type=jnp.float32
    ).astype(jnp.bfloat16)
    grad_heads = grad_mixed.reshape(local_rows, seq_dev, head_count, head_size)
    full_mixed = mixed_heads_out + remainder
    row_delta = jnp.sum(grad_heads.astype(jnp.float32) * full_mixed, axis=-1).transpose(1, 2, 0)
    grad_query = query_grads(
        query_heads,
        key_heads,
        value_heads,
        grad_heads,
        query_pos,
        query_start,
        log_total,
        row_delta,
        score_scale,
        ctx_count,
        half_rows,
        key_block,
    ).astype(jnp.bfloat16)
    sub_rows = math.gcd(local_rows * lax.axis_size("ctx"), key_block)

    def one_piece(piece_index):
        piece_start = piece_index * sub_rows
        key_piece = lax.dynamic_slice_in_dim(key_heads, piece_start, sub_rows, 0)
        value_piece = lax.dynamic_slice_in_dim(value_heads, piece_start, sub_rows, 0)
        key_pos = position_of(
            piece_start + jnp.arange(sub_rows, dtype=jnp.int32), ctx_count, half_rows
        )
        key_part, value_part = key_grads(
            query_heads,
            grad_heads,
            query_pos,
            query_start,
            log_total,
            row_delta,
            key_piece,
            value_piece,
            key_pos,
            score_scale,
        )
        return jnp.concatenate(
            [
                key_part.reshape(sub_rows, seq_dev, model_width),
                value_part.reshape(sub_rows, seq_dev, model_width),
            ],
            axis=-1,
        )

    summed = lax.psum_scatter(
        lax.map(
            one_piece, jnp.arange(local_rows * lax.axis_size("ctx") // sub_rows, dtype=jnp.int32)
        ).reshape(local_rows * lax.axis_size("ctx"), seq_dev, 2 * model_width),
        "ctx",
        scatter_dimension=0,
        tiled=True,
    )
    grad_key = summed[..., :model_width].astype(jnp.bfloat16)
    grad_value = summed[..., model_width:].astype(jnp.bfloat16)
    grad_projected = jnp.concatenate(
        [grad_query.reshape(local_rows, seq_dev, model_width), grad_key, grad_value], axis=-1
    )
    grad_projection = jnp.einsum(
        "tsd,tse->de", normed_low, grad_projected, preferred_element_type=jnp.float32
    )
    grad_normed = jnp.einsum(
        "tse,de->tsd", grad_projected, projection, preferred_element_type=jnp.float32
    )
    grad_in_norm, grad_gain_one = norm_backward(grad_normed, hat_one, inverse_one, gain_one)
    grad_start = grad_middle + grad_in_norm
    shard_proj, shard_outproj, shard_gain_one, shard_gain_two = (
        lax.psum_scatter(
            grad_projection.astype(jnp.bfloat16), "fsdp", scatter_dimension=0, tiled=True
        ).astype(jnp.float32),
        lax.psum_scatter(
            grad_outproj.astype(jnp.bfloat16), "fsdp", scatter_dimension=0, tiled=True
        ).astype(jnp.float32),
        lax.psum_scatter(
            grad_gain_one.astype(jnp.bfloat16), "fsdp", scatter_dimension=0, tiled=True
        ).astype(jnp.float32),
        lax.psum_scatter(
            grad_gain_two.astype(jnp.bfloat16), "fsdp", scatter_dimension=0, tiled=True
        ).astype(jnp.float32),
    )
    shard_proj, shard_outproj, shard_gain_one, shard_gain_two = (
        lax.psum(shard_proj.astype(jnp.bfloat16), "ctx").astype(jnp.float32),
        lax.psum(shard_outproj.astype(jnp.bfloat16), "ctx").astype(jnp.float32),
        lax.psum(shard_gain_one.astype(jnp.bfloat16), "ctx").astype(jnp.float32),
        lax.psum(shard_gain_two.astype(jnp.bfloat16), "ctx").astype(jnp.float32),
    )
    block_out = output_rows.transpose(1, 0, 2).reshape(tokens.shape).astype(jnp.bfloat16)
    grad_tokens = grad_start.transpose(1, 0, 2).reshape(tokens.shape)
    return (
        block_out,
        grad_tokens,
        shard_proj,
        shard_outproj,
        grad_in,
        grad_outw,
        shard_gain_one,
        shard_gain_two,
    )


BF = jnp.bfloat16
F32 = jnp.float32
MESH_ID = pl.DeviceIdType.MESH
ANY = pl.BlockSpec(memory_space=pl.ANY)
DMA = pltpu.SemaphoreType.DMA
VMEM_CAP = 56 << 20


def place():
    c = lax.axis_index("ctx")
    f = lax.axis_index("fsdp")
    return c, f, c // 2, c % 2, f // 2, f % 2


def remote(src, dst, send, recv, device):
    return pltpu.make_async_remote_copy(
        src_ref=src, dst_ref=dst, send_sem=send, recv_sem=recv, device_id=device, device_id_type=MESH_ID
    )


def block_at(c, half, count):
    return c if half == 0 else 2 * count - 1 - c


def params(side=True):
    return pltpu.CompilerParams(has_side_effects=side, vmem_limit_bytes=VMEM_CAP)


def gather_stream(normed, starts, weight):
    count = lax.axis_size("ctx")
    depth = count // 2
    rows, width = weight.shape
    pieces = 4
    piece = rows // pieces

    def kernel(n_ref, s_ref, w_ref, tok, st, wall, rs_t, ss_p, ss_up, ss_dn, ss_sib, rs_s, ss_s, rs_wx, ss_wx, rs_ws, ss_ws, rs_wf, ss_wf, loc):
        c, f, z, y, x, k = place()
        sib = (c, f + 1 - 2 * k)
        xn = (c, (f + 2) % 4)
        partner = (c + 1 - 2 * y, f + 1 - 2 * k)
        up = (c + 2, f)
        down = (c - 2, f)
        holder = k == y

        def wpart(ref, shard, i):
            return ref.at[shard, pl.ds(i * piece, piece)]

        for i in range(pieces):
            remote(w_ref.at[pl.ds(i * piece, piece)], wpart(wall, f, i), ss_wx.at[i], rs_wx.at[i], xn).start()

        def send_in(h):
            return remote(
                n_ref.at[h], tok.at[block_at(c, h, count)], ss_p.at[h], rs_t.at[block_at(c, h, count)], partner
            )

        def local_in(h):
            return pltpu.make_async_copy(
                n_ref.at[h], tok.at[block_at(c, h, count)], rs_t.at[block_at(c, h, count)]
            )

        @pl.when(holder)
        def _():
            for h in range(2):
                local_in(h).start()

        @pl.when(jnp.logical_not(holder))
        def _():
            for h in range(2):
                send_in(h).start()

        for zt in range(depth):
            for kt in range(2):
                dev = (2 * zt + k, 2 * x + kt)
                slot = 2 * zt + kt
                mine = holder & (z == zt) & (k == kt)

                @pl.when(mine)
                def _(dev=dev, slot=slot):
                    pltpu.make_async_copy(s_ref, st.at[c], rs_s.at[c]).start()

                @pl.when(jnp.logical_not(mine))
                def _(dev=dev, slot=slot):
                    remote(s_ref, st.at[c], ss_s.at[slot], rs_s.at[c], dev).start()

        remote(w_ref, wall.at[f], ss_ws, rs_ws, sib).start()
        pltpu.make_async_copy(w_ref, wall.at[f], loc).start()

        def copy_block(zb, h, ss, dev):
            b = block_at(2 * zb + k, h, count)
            return remote(tok.at[b], tok.at[b], ss, rs_t.at[b], dev)

        def wait_block(zb):
            for h in range(2):
                b = block_at(2 * zb + k, h, count)
                remote(tok.at[b], tok.at[b], ss_p.at[h], rs_t.at[b], sib).wait_recv()

        def send_up(j):
            for h in range(2):
                copy_block(z - j, h, ss_up.at[j, h], up).start()

        def send_down(j):
            for h in range(2):
                copy_block(z + j, h, ss_dn.at[j, h], down).start()

        def send_sib(zb):
            for h in range(2):
                copy_block(zb, h, ss_sib.at[zb, h], sib).start()

        def w_forward(i):
            shard = (f + 2) % 4
            remote(wpart(wall, shard, i), wpart(wall, shard, i), ss_wx.at[i], rs_wx.at[i], xn).wait_recv()
            remote(wpart(wall, shard, i), wpart(wall, shard, i), ss_wf.at[i], rs_wf.at[i], sib).start()

        wait_block(z)

        @pl.when(z < depth - 1)
        def _():
            send_up(0)

        @pl.when(z > 0)
        def _():
            send_down(0)

        send_sib(z)
        for j in range(1, depth):
            if j < pieces:
                w_forward(j - 1)

            @pl.when(z - j >= 0)
            def _(j=j):
                wait_block(z - j)

                @pl.when(z < depth - 1)
                def _():
                    send_up(j)

                send_sib(z - j)

            @pl.when(z + j <= depth - 1)
            def _(j=j):
                wait_block(z + j)

                @pl.when(z > 0)
                def _():
                    send_down(j)

                send_sib(z + j)

        for i in range(min(depth, pieces) - 1, pieces):
            w_forward(i)

        for zt in range(depth):
            for h in range(2):
                b = block_at(2 * zt + 1 - k, h, count)
                remote(tok.at[b], tok.at[b], ss_p.at[h], rs_t.at[b], sib).wait_recv()
                copy_block(zt, h, ss_sib.at[zt, h], sib).wait_send()
        for ct in range(count):
            remote(s_ref, st.at[ct], ss_s.at[0], rs_s.at[ct], sib).wait_recv()
        for i in range(pieces):
            shard = sib[1] + 2 - 4 * (sib[1] // 2)
            remote(wpart(wall, shard, i), wpart(wall, shard, i), ss_wf.at[i], rs_wf.at[i], sib).wait_recv()
            remote(wpart(wall, shard, i), wpart(wall, shard, i), ss_wf.at[i], rs_wf.at[i], sib).wait_send()
            remote(w_ref.at[pl.ds(i * piece, piece)], wpart(wall, f, i), ss_wx.at[i], rs_wx.at[i], xn).wait_send()
        remote(w_ref, wall.at[sib[1]], ss_ws, rs_ws, sib).wait()
        pltpu.make_async_copy(w_ref, wall.at[f], loc).wait()

        @pl.when(jnp.logical_not(holder))
        def _():
            for h in range(2):
                send_in(h).wait_send()

        for j in range(depth):

            @pl.when((z < depth - 1) & (z - j >= 0))
            def _(j=j):
                for h in range(2):
                    copy_block(z - j, h, ss_up.at[j, h], up).wait_send()

            @pl.when((z > 0) & (z + j <= depth - 1))
            def _(j=j):
                for h in range(2):
                    copy_block(z + j, h, ss_dn.at[j, h], down).wait_send()

        for zt in range(depth):
            for kt in range(2):
                mine = holder & (z == zt) & (k == kt)

                @pl.when(jnp.logical_not(mine))
                def _(zt=zt, kt=kt):
                    remote(s_ref, st.at[c], ss_s.at[2 * zt + kt], rs_s.at[c], sib).wait_send()

    return pl.pallas_call(
        kernel,
        name="gather_stream",
        out_shape=(
            jax.ShapeDtypeStruct((2 * count,) + normed.shape[1:], normed.dtype),
            jax.ShapeDtypeStruct((count,) + starts.shape, starts.dtype),
            jax.ShapeDtypeStruct((4, rows, width), weight.dtype),
        ),
        in_specs=[ANY] * 3,
        out_specs=(ANY,) * 3,
        scratch_shapes=[
            DMA((2 * count,)), DMA((2,)), DMA((depth, 2)), DMA((depth, 2)), DMA((depth, 2)),
            DMA((count,)), DMA((count,)), DMA((pieces,)), DMA((pieces,)), DMA, DMA,
            DMA((pieces,)), DMA((pieces,)), DMA,
        ],
        compiler_params=params(),
    )(normed, starts, weight)


def heads_to_tokens(arrays, name):
    count = lax.axis_size("ctx")
    number = len(arrays)
    lanes = arrays[0].shape[2]
    width = count * lanes

    def kernel(*refs):
        ins, (out, ss, rs) = refs[:number], refs[number:]
        c, f, z, y, x, k = place()
        pair = 2 * z + k
        target = 2 * x + y

        def there(half, a):
            return out.at[half, :, pl.ds(pl.multiple_of(a * width + pair * lanes, lanes), lanes)]

        def send(i, half, a):
            ct = (c + i) % count
            return remote(
                ins[a].at[block_at(ct, half, count)], there(half, a), ss.at[i, half, a], rs.at[pair, half, a], (ct, target)
            )

        def own(half, a):
            return pltpu.make_async_copy(ins[a].at[block_at(c, half, count)], there(half, a), rs.at[pair, half, a])

        pieces = [(half, a) for a in range(number) for half in range(2)]
        for i in [*range(1, count), 0]:
            if i:
                for half, a in pieces:
                    send(i, half, a).start()
            else:

                @pl.when(k == y)
                def _():
                    for half, a in pieces:
                        own(half, a).start()

                @pl.when(k != y)
                def _():
                    for half, a in pieces:
                        send(0, half, a).start()

        for half, a in pieces:
            for other in range(count):
                cols = pl.ds(a * width + other * lanes, lanes)
                remote(ins[a].at[0], out.at[half, :, cols], ss.at[0, half, a], rs.at[other, half, a], (c, f + 1 - 2 * k)).wait_recv()
        for i in range(1, count):
            for half, a in pieces:
                send(i, half, a).wait_send()

        @pl.when(k != y)
        def _():
            for half, a in pieces:
                send(0, half, a).wait_send()

    return pl.pallas_call(
        kernel,
        name=name,
        out_shape=jax.ShapeDtypeStruct((2, arrays[0].shape[1], number * width), arrays[0].dtype),
        in_specs=[ANY] * number,
        out_specs=ANY,
        scratch_shapes=[DMA((count, 2, number)), DMA((count, 2, number))],
        compiler_params=params(),
    )(*arrays)


def tokens_to_heads(array, name):
    count = lax.axis_size("ctx")
    lanes = array.shape[2] // count

    def kernel(a_ref, out, ss, rs):
        c, f, z, y, x, k = place()

        def part(half, pair):
            return a_ref.at[half, :, pl.ds(pl.multiple_of(pair * lanes, lanes), lanes)]

        def peer(i):
            pair = (2 * z + k + i) % count
            return pair, (2 * (pair // 2) + k, 2 * x + pair % 2)

        def send(i, half):
            pair, dev = peer(i)
            b = block_at(c, half, count)
            return remote(part(half, pair), out.at[b], ss.at[i, half], rs.at[b], dev)

        for i in range(1, count):
            for half in range(2):
                send(i, half).start()

        @pl.when(k == y)
        def _():
            for half in range(2):
                b = block_at(c, half, count)
                pltpu.make_async_copy(part(half, 2 * z + k), out.at[b], rs.at[b]).start()

        @pl.when(k != y)
        def _():
            for half in range(2):
                send(0, half).start()

        for b in range(2 * count):
            remote(part(0, 0), out.at[b], ss.at[0, 0], rs.at[b], (c, f + 1 - 2 * k)).wait_recv()
        for i in range(1, count):
            for half in range(2):
                send(i, half).wait_send()

        @pl.when(k != y)
        def _():
            for half in range(2):
                send(0, half).wait_send()

    return pl.pallas_call(
        kernel,
        name=name,
        out_shape=jax.ShapeDtypeStruct((2 * count, array.shape[1], lanes), array.dtype),
        in_specs=[ANY],
        out_specs=ANY,
        scratch_shapes=[DMA((count, 2)), DMA((2 * count,))],
        compiler_params=params(),
    )(array)


TILE = 256


def halves(value, axis):
    size = value.shape[axis] // 2
    at = lax.broadcasted_iota(jnp.int32, value.shape, axis)
    zero = jnp.zeros_like(value)
    return [jnp.where(at < size, value, zero), jnp.where(at >= size, value, zero)]


def attend_forward(stream, projection, start_row, numbers, scale):
    length, width = stream.shape
    tiles = length // TILE
    lanes = 128
    size = lanes // 2

    def kernel(first, x_ref, wq_ref, wk_ref, wv_ref, s_ref, q_out, k_out, v_out, m16, m32, lse, v_turned):
        i = pl.program_id(0)
        own = pl.ds(pl.multiple_of(i * TILE, TILE), TILE)
        rows = x_ref[...]
        query = jnp.dot(rows, wq_ref[...], preferred_element_type=F32).astype(BF)
        key = jnp.dot(rows, wk_ref[...], preferred_element_type=F32).astype(BF)
        value = jnp.dot(rows, wv_ref[...], preferred_element_type=F32).astype(BF)
        q_out[...] = query
        k_out[own, :] = key
        v_out[...] = value
        v_turned[:, own] = value.T
        queries = halves((query * scale).T, 0)
        start = s_ref[...]
        key_row = lax.broadcasted_iota(jnp.int32, (TILE, TILE), 0)
        query_column = i * TILE + lax.broadcasted_iota(jnp.int32, (TILE, TILE), 1)

        def step(j, carried):
            at = pl.multiple_of(j * TILE, TILE)
            keys = k_out[pl.ds(at, TILE), :]
            seen = (key_row + at <= query_column) & (key_row + at >= start)
            out = []
            for h in range(2):
                top, total, mixed = carried[h]
                score = jnp.where(seen, jnp.dot(keys, queries[h], preferred_element_type=F32), NEGATIVE)
                new_top = jnp.maximum(top, jnp.max(score, axis=0, keepdims=True))
                weight = jnp.exp(score - new_top)
                shrink = jnp.exp(top - new_top)
                total = total * shrink + jnp.sum(weight, axis=0, keepdims=True)
                values = v_turned[h * size : (h + 1) * size, pl.ds(at, TILE)]
                mixed = mixed * shrink + jnp.dot(values, weight.astype(BF), preferred_element_type=F32)
                out.append((new_top, total, mixed))
            return tuple(out)

        begin = (
            jnp.full((1, TILE), NEGATIVE, F32),
            jnp.zeros((1, TILE), F32),
            jnp.zeros((size, TILE), F32),
        )
        done = lax.fori_loop(first[i], i + 1, step, (begin, begin))
        mixed = jnp.concatenate([part / total for _, total, part in done], axis=0)
        m32[...] = mixed
        m16[...] = mixed.T.astype(BF)
        lse[...] = jnp.concatenate([top + jnp.log(total) for top, total, _ in done], axis=0)

    groups = width // lanes
    tile = pl.BlockSpec((TILE, lanes), lambda i, n: (i, 0))
    turned = pl.BlockSpec((lanes, TILE), lambda i, n: (0, i))
    return pl.pallas_call(
        kernel,
        name="attend_forward",
        grid_spec=pltpu.PrefetchScalarGridSpec(
            num_scalar_prefetch=1,
            grid=(tiles,),
            in_specs=[
                pl.BlockSpec((TILE, width), lambda i, n: (i, 0)),
                pl.BlockSpec((width, lanes), lambda i, n: (0, n[tiles])),
                pl.BlockSpec((width, lanes), lambda i, n: (0, groups + n[tiles])),
                pl.BlockSpec((width, lanes), lambda i, n: (0, 2 * groups + n[tiles])),
                pl.BlockSpec((1, TILE), lambda i, n: (0, i)),
            ],
            out_specs=[
                tile,
                pl.BlockSpec((length, lanes), lambda i, n: (0, 0)),
                tile,
                tile,
                turned,
                pl.BlockSpec((2, TILE), lambda i, n: (0, i)),
            ],
            scratch_shapes=[pltpu.VMEM((lanes, length), BF)],
        ),
        out_shape=(
            jax.ShapeDtypeStruct((length, lanes), BF),
            jax.ShapeDtypeStruct((length, lanes), BF),
            jax.ShapeDtypeStruct((length, lanes), BF),
            jax.ShapeDtypeStruct((length, lanes), BF),
            jax.ShapeDtypeStruct((lanes, length), F32),
            jax.ShapeDtypeStruct((2, length), F32),
        ),
        compiler_params=params(False),
    )(numbers, stream, projection, projection, projection, start_row)


def attend_backward(query, key, value, grad, mixed, logs, start_row, numbers, scale):
    length, lanes = query.shape
    tiles = length // TILE
    size = lanes // 2

    def kernel(first, q_ref, k_ref, v_ref, g_ref, m_ref, l_ref, s_ref, dq, dk, dv, acc_k, acc_v, k_turned):
        i = pl.program_id(0)

        @pl.when(i == 0)
        def _():
            acc_k[...] = jnp.zeros_like(acc_k)
            acc_v[...] = jnp.zeros_like(acc_v)
            for t in range(tiles):
                k_turned[:, t * TILE : (t + 1) * TILE] = k_ref[t * TILE : (t + 1) * TILE, :].T

        scaled = q_ref[...] * scale
        grads = g_ref[...]
        turned = grads.T
        queries, queries_turned = halves(scaled, 1), halves(scaled.T, 0)
        grad_rows, grads_turned = halves(grads, 1), halves(turned, 0)
        product = turned.astype(F32) * m_ref[...]
        deltas = [jnp.sum(product[h * size : (h + 1) * size], axis=0, keepdims=True) for h in range(2)]
        logs_row = [l_ref[h : h + 1, :] for h in range(2)]
        start = s_ref[...]
        key_row = lax.broadcasted_iota(jnp.int32, (TILE, TILE), 0)
        query_column = i * TILE + lax.broadcasted_iota(jnp.int32, (TILE, TILE), 1)

        def step(j, running):
            at = pl.multiple_of(j * TILE, TILE)
            keys = k_ref[pl.ds(at, TILE), :]
            values = v_ref[pl.ds(at, TILE), :]
            seen = (key_row + at <= query_column) & (key_row + at >= start)
            key_sum = jnp.zeros((TILE, lanes), F32)
            value_sum = jnp.zeros((TILE, lanes), F32)
            out = []
            for h in range(2):
                score = jnp.dot(keys, queries_turned[h], preferred_element_type=F32)
                weight = jnp.exp(jnp.where(seen, score - logs_row[h], NEGATIVE))
                grad_weight = jnp.dot(values, grads_turned[h], preferred_element_type=F32)
                grad_score = (weight * (grad_weight - deltas[h])).astype(BF)
                value_sum += jnp.dot(weight.astype(BF), grad_rows[h], preferred_element_type=F32)
                key_sum += jnp.dot(grad_score, queries[h], preferred_element_type=F32)
                part = k_turned[h * size : (h + 1) * size, pl.ds(at, TILE)]
                out.append(running[h] + jnp.dot(part, grad_score, preferred_element_type=F32))
            acc_k[pl.ds(at, TILE), :] += key_sum
            acc_v[pl.ds(at, TILE), :] += value_sum
            return tuple(out)

        zero = jnp.zeros((size, TILE), F32)
        total = lax.fori_loop(first[i], i + 1, step, (zero, zero))
        dq[...] = (jnp.concatenate(total, axis=0) * scale).T.astype(BF)

        @pl.when(i == tiles - 1)
        def _():
            dk[...] = acc_k[...].astype(BF)
            dv[...] = acc_v[...].astype(BF)

    tile = pl.BlockSpec((TILE, lanes), lambda i, n: (i, 0))
    full = pl.BlockSpec((length, lanes), lambda i, n: (0, 0))
    return pl.pallas_call(
        kernel,
        name="attend_backward",
        grid_spec=pltpu.PrefetchScalarGridSpec(
            num_scalar_prefetch=1,
            grid=(tiles,),
            in_specs=[
                tile,
                full,
                full,
                tile,
                pl.BlockSpec((lanes, TILE), lambda i, n: (0, i)),
                pl.BlockSpec((2, TILE), lambda i, n: (0, i)),
                pl.BlockSpec((1, TILE), lambda i, n: (0, i)),
            ],
            out_specs=[tile, full, full],
            scratch_shapes=[
                pltpu.VMEM((length, lanes), F32),
                pltpu.VMEM((length, lanes), F32),
                pltpu.VMEM((lanes, length), BF),
            ],
        ),
        out_shape=(jax.ShapeDtypeStruct((length, lanes), BF),) * 3,
        compiler_params=params(False),
    )(numbers, query, key, value, grad, mixed, logs, start_row)


def dispatch_rows(arrays):
    count = lax.axis_size("ctx")
    number = len(arrays)
    _, own_experts, cap, width = arrays[0].shape

    def kernel(*refs):
        ins, outs = refs[:number], refs[number : 2 * number]
        ss1, rs1, ssx, rsx, sss, rss, ssf, rsf = refs[2 * number :]
        c, f, z, y, x, k = place()
        sib = (c, f + 1 - 2 * k)
        xn = (c, (f + 2) % 4)

        def here(a, stream, source):
            return outs[a].at[:, stream, source]

        def first(a, i):
            ct = (c + i) % count
            return remote(ins[a].at[ct], here(a, f, c), ss1.at[a, i], rs1.at[a, c], (ct, f))

        for a in range(number):
            pltpu.make_async_copy(ins[a].at[c], here(a, f, c), rs1.at[a, c]).start()
            for i in range(1, count):
                first(a, i).start()

        def hop(a, stream, source, ss, rs, dev):
            return remote(here(a, stream, source), here(a, stream, source), ss.at[a, source], rs.at[a, source], dev)

        other = (f + 2) % 4
        for a in range(number):
            for i in range(count):
                cs = (c + i) % count
                remote(here(a, f, cs), here(a, f, cs), ss1.at[a, 0], rs1.at[a, cs], sib).wait_recv()
                hop(a, f, cs, ssx, rsx, xn).start()
                hop(a, f, cs, sss, rss, sib).start()
        for a in range(number):
            for i in range(count):
                cs = (c + i) % count
                hop(a, other, cs, ssx, rsx, xn).wait_recv()
                hop(a, other, cs, ssf, rsf, sib).start()
        for a in range(number):
            for i in range(count):
                if i:
                    first(a, i).wait_send()
                cs = (c + i) % count
                hop(a, f, cs, ssx, rsx, xn).wait_send()
                hop(a, sib[1], cs, sss, rss, sib).wait()
                hop(a, (sib[1] + 2) % 4, cs, ssf, rsf, sib).wait()

    return pl.pallas_call(
        kernel,
        name="dispatch_rows",
        out_shape=(jax.ShapeDtypeStruct((own_experts, 4, count, cap, width), arrays[0].dtype),) * number,
        in_specs=[ANY] * number,
        out_specs=(ANY,) * number,
        scratch_shapes=[DMA((number, count))] * 8,
        compiler_params=params(),
    )(*arrays)


def return_rows(arrays):
    count = lax.axis_size("ctx")
    number = len(arrays)
    _, experts, _, cap, width = arrays[0].shape
    groups = 2
    chunk = experts // groups

    def kernel(*refs):
        ins, outs = refs[:number], refs[number : 2 * number]
        near, far, got_near, got_far, got_x = refs[2 * number : 2 * number + 5]
        ssn, rsn, ssf, rsf, ssx, rsx, sso, rso, loc = refs[2 * number + 5 :]
        c, f, z, y, x, k = place()
        sib = (c, f + 1 - 2 * k)
        other = (f + 2) % 4
        xn = (c, other)
        sib_other = (sib[1] + 2) % 4

        def to_near(a):
            return remote(ins[a].at[sib[1]], got_near.at[a], ssn.at[a], rsn.at[a], sib)

        def to_far(a):
            return remote(ins[a].at[sib_other], got_far.at[a], ssf.at[a], rsf.at[a], sib)

        def load(a, stream, buf, i):
            return pltpu.make_async_copy(ins[a].at[stream], buf.at[a], loc.at[a, i])

        for a in range(number):
            to_far(a).start()
            load(a, other, far, 0).start()
        for a in range(number):
            to_near(a).start()
            load(a, f, near, 1).start()

        def across(a, e):
            return remote(far.at[a, e], got_x.at[a, e], ssx.at[a, e], rsx.at[a, e], xn)

        for a in range(number):
            load(a, other, far, 0).wait()
            to_far(a).wait_recv()
            for e in range(experts):
                far[a, e] = (far[a, e].astype(F32) + got_far[a, e].astype(F32)).astype(BF)
                across(a, e).start()

        def home(a, g, i):
            ct = (c + i) % count
            return remote(
                near.at[a, pl.ds(g * chunk, chunk), ct],
                outs[a].at[c, pl.ds(g * chunk, chunk)],
                sso.at[a, g, i],
                rso.at[a, g, c],
                (ct, f),
            )

        def stay(a, g):
            return pltpu.make_async_copy(
                near.at[a, pl.ds(g * chunk, chunk), c], outs[a].at[c, pl.ds(g * chunk, chunk)], rso.at[a, g, c]
            )

        for a in range(number):
            load(a, f, near, 1).wait()
            to_near(a).wait_recv()
            for g in range(groups):
                for e in range(g * chunk, (g + 1) * chunk):
                    across(a, e).wait_recv()
                    near[a, e] = (
                        near[a, e].astype(F32) + got_near[a, e].astype(F32) + got_x[a, e].astype(F32)
                    ).astype(BF)
                for i in range(1, count):
                    home(a, g, i).start()
                stay(a, g).start()
        for a in range(number):
            to_far(a).wait_send()
            to_near(a).wait_send()
            for e in range(experts):
                across(a, e).wait_send()
            for g in range(groups):
                for i in range(count):
                    cs = (c + i) % count
                    remote(
                        near.at[a, pl.ds(g * chunk, chunk), cs],
                        outs[a].at[cs, pl.ds(g * chunk, chunk)],
                        sso.at[a, g, i],
                        rso.at[a, g, cs],
                        sib,
                    ).wait_recv()
                    if i:
                        home(a, g, i).wait_send()

    buffer = pltpu.VMEM((number, experts, count, cap, width), BF)
    return pl.pallas_call(
        kernel,
        name="return_rows",
        out_shape=(jax.ShapeDtypeStruct((count, experts, cap, width), BF),) * number,
        in_specs=[ANY] * number,
        out_specs=(ANY,) * number,
        scratch_shapes=[buffer] * 5
        + [DMA((number,))] * 4
        + [DMA((number, experts))] * 2
        + [DMA((number, groups, count))] * 2
        + [DMA((number, 2))],
        compiler_params=params(),
    )(*arrays)


ROOT = math.sqrt(2.0 / math.pi)
CUBIC = 0.044715


def experts_step(rows, grads, first_proj, second_proj):
    number, count, width = rows.shape
    units = first_proj.shape[2]
    quarter = count // 4

    def kernel(r_ref, g_ref, a_ref, b_ref, out, back, da, db):
        row, grad = r_ref[0], g_ref[0]
        first = a_ref[0].astype(BF)
        second = b_ref[0].astype(BF)
        hidden = jnp.dot(row, first, preferred_element_type=F32)
        upstream = lax.dot_general(grad, second, (((1,), (1,)), ((), ())), preferred_element_type=F32)
        bent = jnp.tanh(ROOT * (hidden + CUBIC * hidden * hidden * hidden))
        active = (0.5 * hidden * (1.0 + bent)).astype(BF)
        slope = 0.5 * (1.0 + bent) + 0.5 * hidden * (1.0 - bent * bent) * (ROOT * (1.0 + 3.0 * CUBIC * hidden * hidden))
        grad_hidden = (upstream * slope).astype(BF)
        term = lax.dot_general(grad_hidden, first, (((1,), (1,)), ((), ())), preferred_element_type=F32).astype(BF)
        mixed = jnp.dot(active, second, preferred_element_type=F32).astype(BF)
        for s in range(4):
            back[s, 0] = term[s * quarter : (s + 1) * quarter]
            out[s, 0] = mixed[s * quarter : (s + 1) * quarter]
        da[0] = lax.dot_general(row, grad_hidden, (((0,), (0,)), ((), ())), preferred_element_type=F32)
        db[0] = lax.dot_general(active, grad, (((0,), (0,)), ((), ())), preferred_element_type=F32)

    whole = pl.BlockSpec((1, count, width), lambda e: (e, 0, 0))
    left = pl.BlockSpec((1, width, units), lambda e: (e, 0, 0))
    right = pl.BlockSpec((1, units, width), lambda e: (e, 0, 0))
    parts = pl.BlockSpec((4, 1, quarter, width), lambda e: (0, e, 0, 0))
    return pl.pallas_call(
        kernel,
        name="experts_step",
        grid=(number,),
        in_specs=[whole, whole, left, right],
        out_specs=[parts, parts, left, right],
        out_shape=(
            jax.ShapeDtypeStruct((4, number, quarter, width), BF),
            jax.ShapeDtypeStruct((4, number, quarter, width), BF),
            jax.ShapeDtypeStruct(first_proj.shape, F32),
            jax.ShapeDtypeStruct(second_proj.shape, F32),
        ),
        compiler_params=params(False),
    )(rows, grads, first_proj, second_proj)


def finish_exchange(arrays, parts, out_parts, gain_part):
    count = lax.axis_size("ctx")
    depth = count // 2
    number = len(arrays)
    lanes = arrays[0].shape[2]
    width = count * lanes
    _, rows, wide = parts.shape
    slab = rows // count

    def kernel(*refs):
        ins, (p_ref, o_ref, g_ref), (tok_out, w_out, o_out, g_out) = (
            refs[:number],
            refs[number : number + 3],
            refs[number + 3 : number + 7],
        )
        (
            got, held, got_a, far, got_x, mine, got_c, slab_out, got_g, sum_g, got_gc,
            ss, rs, ss_r, rs_r, ss_up, ss_dn, rs_z, ss_a, ss_b, rs_o,
            ss_oa, rs_oa, ss_ox, rs_ox, ss_oc, rs_oc, ss_of, rs_of, ss_g, rs_g, ss_gc, rs_gc,
        ) = refs[number + 7 :]
        c, f, z, y, x, k = place()
        pair = 2 * z + k
        target = 2 * x + y
        sib = (c, f + 1 - 2 * k)
        xn = (c, (f + 2) % 4)
        up = (c + 2, f)
        down = (c - 2, f)

        def core_send(j):
            shard = 2 * (1 - x) + 1 - k if j == 0 else 2 * x + 1 - k
            return remote(o_ref.at[shard], got_a.at[j], ss_oa.at[j], rs_oa.at[j], sib)

        def gain_send(j):
            return remote(sum_g.at[j], got_g.at[j], ss_g.at[j], rs_g.at[j], sib if j == 0 else xn)

        core_send(0).start()
        core_send(1).start()
        sum_g[0] = g_ref[...]
        gain_send(0).start()

        peers = [
            (2 * z + 1 - y, f, 2 * x + 1 - y),
            (c, (f + 2) % 4, 2 * (1 - x) + y),
            (2 * z + 1 - y, (f + 2) % 4, 2 * (1 - x) + 1 - y),
        ]

        def scatter(d):
            cp, fp, shard = peers[d]
            return remote(p_ref.at[shard], got.at[d], ss_r.at[d], rs_r.at[d], (cp, fp))

        for d in (2, 1, 0):
            scatter(d).start()

        def there(half, a):
            return tok_out.at[half, :, pl.ds(pl.multiple_of(a * width + pair * lanes, lanes), lanes)]

        def send(i, half, a):
            ct = (c + i) % count
            return remote(
                ins[a].at[block_at(ct, half, count)], there(half, a), ss.at[i, half, a], rs.at[pair, half, a], (ct, target)
            )

        def own(half, a):
            return pltpu.make_async_copy(ins[a].at[block_at(c, half, count)], there(half, a), rs.at[pair, half, a])

        pieces = [(half, a) for a in range(number) for half in range(2)]
        for i in range(1, count):
            for half, a in pieces:
                send(i, half, a).start()

        @pl.when(k == y)
        def _():
            for half, a in pieces:
                own(half, a).start()

        @pl.when(k != y)
        def _():
            for half, a in pieces:
                send(0, half, a).start()

        across = remote(far, got_x, ss_ox, rs_ox, xn)
        core_send(0).wait_recv()
        far[...] = (o_ref[2 * (1 - x) + k].astype(F32) + got_a[0].astype(F32)).astype(BF)
        across.start()
        gain_send(0).wait_recv()
        sum_g[1] = sum_g[0] + got_g[0]
        gain_send(1).start()

        total = p_ref[2 * x + y].astype(F32)
        for d in range(3):
            scatter(d).wait_recv()
            total += got[d].astype(F32)
        held[z] = total.astype(BF)

        def chain(zb, sem, dev):
            return remote(held.at[zb], held.at[zb], sem, rs_z.at[zb], dev)

        def piece(zb, j):
            return held.at[zb, :, pl.ds(j * lanes, lanes)]

        def goal(zb, j):
            return w_out.at[:, pl.ds(pl.multiple_of(j * width + (2 * zb + k) * lanes, lanes), lanes)]

        def own_column(zb, j):
            return remote(piece(zb, j), goal(zb, j), ss_a.at[zb, j], rs_o.at[2 * zb + k, j], (c, target))

        def own_local(zb, j):
            return pltpu.make_async_copy(piece(zb, j), goal(zb, j), rs_o.at[2 * zb + k, j])

        def next_column(zb, j):
            return remote(piece(zb, j), goal(zb, j), ss_b.at[zb, j], rs_o.at[2 * zb + k, j], (2 * z + 1 - y, target))

        def spread(zb):
            for j in range(3):
                next_column(zb, j).start()

            @pl.when(k == y)
            def _():
                for j in range(3):
                    own_local(zb, j).start()

            @pl.when(k != y)
            def _():
                for j in range(3):
                    own_column(zb, j).start()

        @pl.when(z < depth - 1)
        def _():
            chain(z, ss_up.at[0], up).start()

        @pl.when(z > 0)
        def _():
            chain(z, ss_dn.at[0], down).start()

        spread(z)

        core_send(1).wait_recv()
        across.wait_recv()
        for b in range(count):
            at = pl.ds(b * slab, slab)
            mine[b] = (
                o_ref[2 * x + k, at, :].astype(F32) + got_a[1, at, :].astype(F32) + got_x[at, :].astype(F32)
            ).astype(BF)
        gain_send(1).wait_recv()
        sum_g[2] = sum_g[1] + got_g[1]

        def slab_send(i):
            ct = (c + i) % count
            return remote(mine.at[ct], got_c.at[c], ss_oc.at[i], rs_oc.at[c], (ct, f))

        def gain_spread(i):
            return remote(sum_g.at[2], got_gc.at[c], ss_gc.at[i], rs_gc.at[c], ((c + i) % count, f))

        for i in range(1, count):
            slab_send(i).start()
            gain_spread(i).start()

        for j in range(1, depth):

            @pl.when(z - j >= 0)
            def _(j=j):
                chain(z - j, ss_up.at[j], sib).wait_recv()

                @pl.when(z < depth - 1)
                def _():
                    chain(z - j, ss_up.at[j], up).start()

                spread(z - j)

            @pl.when(z + j <= depth - 1)
            def _(j=j):
                chain(z + j, ss_dn.at[j], sib).wait_recv()

                @pl.when(z > 0)
                def _():
                    chain(z + j, ss_dn.at[j], down).start()

                spread(z + j)

        sum_o = mine[c].astype(F32)
        total_g = sum_g[2]
        for i in range(1, count):
            cs = (c + i) % count
            remote(mine.at[cs], got_c.at[cs], ss_oc.at[i], rs_oc.at[cs], sib).wait_recv()
            remote(sum_g.at[2], got_gc.at[cs], ss_gc.at[i], rs_gc.at[cs], sib).wait_recv()
            sum_o += got_c[cs].astype(F32)
            total_g += got_gc[cs]
        g_out[...] = total_g
        slab_out[...] = sum_o.astype(BF)

        def slab_spread(i):
            return remote(slab_out, o_out.at[c], ss_of.at[i], rs_of.at[c], ((c + i) % count, f))

        slab_own = pltpu.make_async_copy(slab_out, o_out.at[c], rs_of.at[c])
        for i in range(1, count):
            slab_spread(i).start()
        slab_own.start()

        core_send(0).wait_send()
        core_send(1).wait_send()
        gain_send(0).wait_send()
        gain_send(1).wait_send()
        across.wait_send()
        for d in range(3):
            scatter(d).wait_send()
        for half, a in pieces:
            for other in range(count):
                cols = pl.ds(a * width + other * lanes, lanes)
                remote(ins[a].at[0], tok_out.at[half, :, cols], ss.at[0, half, a], rs.at[other, half, a], sib).wait_recv()
        for i in range(1, count):
            for half, a in pieces:
                send(i, half, a).wait_send()
            slab_send(i).wait_send()
            gain_spread(i).wait_send()
            slab_spread(i).wait_send()
            cs = (c + i) % count
            remote(slab_out, o_out.at[cs], ss_of.at[i], rs_of.at[cs], sib).wait_recv()
        slab_own.wait()

        @pl.when(k != y)
        def _():
            for half, a in pieces:
                send(0, half, a).wait_send()
            for zb in range(depth):
                for j in range(3):
                    own_column(zb, j).wait_send()

        for other in range(count):
            for j in range(3):
                remote(
                    piece(0, j), w_out.at[:, pl.ds(j * width + other * lanes, lanes)], ss_a.at[0, j], rs_o.at[other, j], sib
                ).wait_recv()
        for j in range(depth):

            @pl.when((z < depth - 1) & (z - j >= 0))
            def _(j=j):
                chain(z - j, ss_up.at[j], up).wait_send()

            @pl.when((z > 0) & (z + j <= depth - 1))
            def _(j=j):
                chain(z + j, ss_dn.at[j], down).wait_send()

        for zb in range(depth):
            for j in range(3):
                next_column(zb, j).wait_send()

    vmem = pl.BlockSpec(memory_space=pltpu.VMEM)
    eighth = gain_part.shape
    return pl.pallas_call(
        kernel,
        name="finish_exchange",
        out_shape=(
            jax.ShapeDtypeStruct((2, arrays[0].shape[1], number * width), BF),
            jax.ShapeDtypeStruct((rows, 3 * width), BF),
            jax.ShapeDtypeStruct((count, slab, width), BF),
            jax.ShapeDtypeStruct(eighth, F32),
        ),
        in_specs=[ANY] * number + [vmem] * 3,
        out_specs=(ANY, ANY, ANY, vmem),
        scratch_shapes=[
            pltpu.VMEM((3, rows, wide), BF),
            pltpu.VMEM((depth, rows, wide), BF),
            pltpu.VMEM((2, rows, width), BF),
            pltpu.VMEM((rows, width), BF),
            pltpu.VMEM((rows, width), BF),
            pltpu.VMEM((count, slab, width), BF),
            pltpu.VMEM((count, slab, width), BF),
            pltpu.VMEM((slab, width), BF),
            pltpu.VMEM((2,) + eighth, F32),
            pltpu.VMEM((3,) + eighth, F32),
            pltpu.VMEM((count,) + eighth, F32),
            DMA((count, 2, number)), DMA((count, 2, number)),
            DMA((3,)), DMA((3,)), DMA((depth,)), DMA((depth,)), DMA((depth,)),
            DMA((depth, 3)), DMA((depth, 3)), DMA((count, 3)),
            DMA((2,)), DMA((2,)), DMA, DMA, DMA((count,)), DMA((count,)), DMA((count,)), DMA((count,)),
            DMA((2,)), DMA((2,)), DMA((count,)), DMA((count,)),
        ],
        compiler_params=params(),
    )(*arrays, parts, out_parts, gain_part)


def slots_of(routes):
    tokens = routes.shape[0]
    chosen = routes[:, None] == jnp.arange(EXPERTS, dtype=jnp.int32)[None, :]
    earlier = (jnp.arange(tokens)[:, None] >= jnp.arange(tokens)[None, :]).astype(BF)
    running = jnp.dot(earlier, chosen.astype(BF), preferred_element_type=F32)
    rank = jnp.sum(jnp.where(chosen, running, 0.0), axis=1).astype(jnp.int32) - 1
    slot = routes * CAP + rank
    return (jnp.arange(EXPERTS * CAP, dtype=jnp.int32)[:, None] == slot[None, :]).astype(BF)


def by_head_pairs(
    tokens, doc_starts, expert_ids, query_key_value_weight, output_weight_matrix, expert_in, expert_out, gain_one, gain_two, grad_output
):
    half_rows = tokens.shape[3]
    width = tokens.shape[4]
    count = lax.axis_size("ctx")
    rows = 2 * half_rows
    length = count * rows
    scale = (width // HEADS) ** (-0.5)
    c, f, z, y, x, k = place()
    pair = 2 * z + k
    lanes = 2 * (width // HEADS)
    start_x = tokens.reshape(rows, width).astype(F32)
    cotangent = grad_output.reshape(rows, width)
    qkv_low = query_key_value_weight.astype(BF)
    out_proj = lax.all_gather(output_weight_matrix.astype(BF), "fsdp", axis=0, tiled=True)
    first_normed, hat_one, inverse_one = norm_forward(start_x, gain_one)
    normed = first_normed.astype(BF)
    stream, starts, projection = gather_stream(
        normed.reshape(2, half_rows, width), doc_starts.reshape(2, half_rows), qkv_low
    )
    stream = stream.reshape(length, width)
    projection = projection.reshape(width, 3 * width)
    start_row = jnp.concatenate([starts[:, 0].reshape(-1), starts[::-1, 1].reshape(-1)])[None]
    numbers = jnp.concatenate([jnp.min(start_row.reshape(-1, TILE), axis=1) // TILE, pair[None]])
    query, key, value, mixed16, mixed32, logs = attend_forward(stream, projection, start_row, numbers, scale)
    mixed = heads_to_tokens([mixed16.reshape(2 * count, half_rows, lanes)], "mixed_to_tokens").reshape(rows, width)
    middle = start_x + jnp.dot(mixed, out_proj, preferred_element_type=F32)
    normed_two, hat_two, inverse_two = norm_forward(middle, gain_two)
    routed = normed_two.astype(BF)
    dispatch = slots_of(expert_ids.reshape(rows))
    own_experts = EXPERTS // count
    shape = (count, own_experts, CAP, width)
    send_rows = jnp.dot(dispatch, routed, preferred_element_type=F32).astype(BF).reshape(shape)
    send_grads = jnp.dot(dispatch, cotangent, preferred_element_type=F32).astype(BF).reshape(shape)
    all_rows, all_grads = dispatch_rows([send_rows, send_grads])
    flat = (own_experts, 4 * count * CAP, width)
    out_terms, back_terms, grad_in, grad_outw = experts_step(
        all_rows.reshape(flat), all_grads.reshape(flat), expert_in, expert_out
    )
    folded = (4, own_experts, count, CAP, width)
    returned, back_rows = return_rows([back_terms.reshape(folded), out_terms.reshape(folded)])
    slots = (EXPERTS * CAP, width)
    pick = (((0,), (0,)), ((), ()))
    grad_routed = lax.dot_general(dispatch, returned.reshape(slots), pick, preferred_element_type=F32)
    expert_sum = lax.dot_general(dispatch, back_rows.reshape(slots), pick, preferred_element_type=F32)
    block_out = (middle + expert_sum).astype(BF)
    grad_mid_norm, grad_gain_two = norm_backward(grad_routed[None], hat_two[None], inverse_two[None], gain_two)
    grad_middle = cotangent.astype(F32) + grad_mid_norm[0]
    grad_attn = grad_middle.astype(BF)
    grad_outproj = lax.dot_general(mixed, grad_attn, pick, preferred_element_type=F32).astype(BF)
    grad_mixed = lax.dot_general(grad_attn, out_proj, (((1,), (1,)), ((), ())), preferred_element_type=F32).astype(BF)
    grad_heads = tokens_to_heads(grad_mixed.reshape(2, half_rows, width), "grad_to_heads").reshape(length, lanes)
    grad_q, grad_k, grad_v = attend_backward(
        query, key, value, grad_heads, mixed32, logs, start_row, numbers, scale
    )
    blocks = (2 * count, half_rows, lanes)
    own_grads = jnp.concatenate([grad_q, grad_k, grad_v], axis=1)
    parts = lax.dot_general(stream, own_grads, pick, preferred_element_type=F32).astype(BF)
    shard_rows = width // 4
    grad_projected, weight_grad, shard_out, gain_sum = finish_exchange(
        [grad_q.reshape(blocks), grad_k.reshape(blocks), grad_v.reshape(blocks)],
        parts.reshape(4, shard_rows, 3 * lanes),
        grad_outproj.reshape(4, shard_rows, width),
        grad_gain_two.reshape(8, width // 8),
    )
    grad_projected = grad_projected.reshape(rows, 3 * width)
    weight_grad = weight_grad.astype(F32)
    shard_out = shard_out.reshape(shard_rows, width).astype(F32)
    grad_normed = lax.dot_general(grad_projected, projection, (((1,), (1,)), ((), ())), preferred_element_type=F32)
    grad_in_norm, _ = norm_backward(grad_normed[None], hat_one[None], inverse_one[None], gain_one)
    grad_start = grad_middle + grad_in_norm[0]
    own_gain = lax.dynamic_slice(gain_one, (f * shard_rows,), (shard_rows,))
    shard_gain_one = jnp.sum(weight_grad * qkv_low.astype(F32), axis=1) / own_gain
    shard_gain_two = lax.dynamic_slice(gain_sum.reshape(width), (f * shard_rows,), (shard_rows,))
    return (
        block_out.reshape(tokens.shape),
        grad_start.reshape(tokens.shape),
        weight_grad,
        shard_out,
        grad_in,
        grad_outw,
        shard_gain_one,
        shard_gain_two,
    )


def solution(mesh):
    pairs = mesh.shape["ctx"] * 2 == HEADS and mesh.shape["fsdp"] == 4
    return jax.shard_map(
        by_head_pairs if pairs else shards,
        mesh=mesh,
        in_specs=(
            P("fsdp", "ctx", None, None, None),
            P("fsdp", "ctx", None, None),
            P("fsdp", "ctx", None, None, None),
            P("fsdp", None),
            P("fsdp", None),
            P("ctx", None, "fsdp"),
            P("ctx", "fsdp", None),
            P(),
            P(),
            P("fsdp", "ctx", None, None, None),
        ),
        out_specs=(
            P("fsdp", "ctx", None, None, None),
            P("fsdp", "ctx", None, None, None),
            P("fsdp", None),
            P("fsdp", None),
            P("ctx", None, "fsdp"),
            P("ctx", "fsdp", None),
            P("fsdp"),
            P("fsdp"),
        ),
        check_vma=False,
    )
```

```python
import math

import jax
import jax.numpy as jnp
from jax import lax
from jax.experimental import pallas as pl
from jax.experimental.pallas import tpu as pltpu
from jax.sharding import PartitionSpec as P

HEADS = 16
EXPERTS = 64
CAP = 8


EPS = 1e-05
NEGATIVE = -1e30


def position_of(row_ids, ctx_count, half_rows):
    device = row_ids // (2 * half_rows)
    upper_half = row_ids // half_rows % 2
    offset = row_ids % half_rows
    return jnp.where(
        upper_half == 0,
        device * half_rows + offset,
        (2 * ctx_count - 1 - device) * half_rows + offset,
    )


def norm_forward(value, gain):
    row_mean = jnp.mean(value, axis=-1, keepdims=True)
    centred = value - row_mean
    inverse = lax.rsqrt(jnp.mean(centred * centred, axis=-1, keepdims=True) + EPS)
    normed = centred * inverse
    return (normed * gain, normed, inverse)


def norm_backward(gradient, normed, inverse, gain):
    scaled = gradient * gain
    mean_grad = jnp.mean(scaled, axis=-1, keepdims=True)
    mean_proj = jnp.mean(scaled * normed, axis=-1, keepdims=True)
    return (
        inverse * (scaled - mean_grad - normed * mean_proj),
        jnp.sum(gradient * normed, axis=(0, 1)),
    )


def scores(query, keys, query_pos, key_pos, query_start, score_scale):
    raw_scores = (
        jnp.einsum("qshe,kshe->shqk", query, keys, preferred_element_type=jnp.float32) * score_scale
    )
    visible = (key_pos[None, None, None, :] <= query_pos[None, None, :, None]) & (
        key_pos[None, None, None, :] >= query_start.T[:, None, :, None]
    )
    return jnp.where(visible, raw_scores, NEGATIVE)


def log_totals(query, keys, query_pos, query_start, score_scale, ctx_count, half_rows, key_block):
    block_count = keys.shape[0] // key_block
    carry_shape = (query.shape[1], query.shape[2], query.shape[0])

    def log_one_block(block_index, carried):
        running_max, running = carried
        first_row = block_index * key_block
        key_piece = lax.dynamic_slice_in_dim(keys, first_row, key_block, 0)
        key_pos = position_of(
            first_row + jnp.arange(key_block, dtype=jnp.int32), ctx_count, half_rows
        )
        score_rows = scores(query, key_piece, query_pos, key_pos, query_start, score_scale)
        new_max = jnp.maximum(running_max, jnp.max(score_rows, axis=-1))
        running = running * jnp.exp(running_max - new_max) + jnp.sum(
            jnp.exp(score_rows - new_max[..., None]), axis=-1
        )
        return (new_max, running)

    running_max, running = lax.fori_loop(
        0,
        block_count,
        log_one_block,
        (jnp.full(carry_shape, NEGATIVE, jnp.float32), jnp.zeros(carry_shape, jnp.float32)),
    )
    return running_max + jnp.log(running)


def attend(
    query,
    keys,
    values,
    query_pos,
    query_start,
    log_total,
    score_scale,
    ctx_count,
    half_rows,
    key_block,
):
    block_count = keys.shape[0] // key_block
    zeros_init = jnp.zeros(query.shape, jnp.float32)

    def attend_one_block(block_index, carried):
        output, remainder = carried
        first_row = block_index * key_block
        key_piece = lax.dynamic_slice_in_dim(keys, first_row, key_block, 0)
        value_piece = lax.dynamic_slice_in_dim(values, first_row, key_block, 0)
        key_pos = position_of(
            first_row + jnp.arange(key_block, dtype=jnp.int32), ctx_count, half_rows
        )
        weights = jnp.exp(
            scores(query, key_piece, query_pos, key_pos, query_start, score_scale)
            - log_total[..., None]
        )
        rounded = weights.astype(jnp.bfloat16)
        leftover = (weights - rounded.astype(jnp.float32)).astype(jnp.bfloat16)
        output = output + jnp.einsum(
            "shqk,kshe->qshe", rounded, value_piece, preferred_element_type=jnp.float32
        )
        remainder = remainder + jnp.einsum(
            "shqk,kshe->qshe", leftover, value_piece, preferred_element_type=jnp.float32
        )
        return (output, remainder)

    return lax.fori_loop(0, block_count, attend_one_block, (zeros_init, zeros_init))


def query_grads(
    query,
    keys,
    values,
    grad_heads,
    query_pos,
    query_start,
    log_total,
    row_delta,
    score_scale,
    ctx_count,
    half_rows,
    key_block,
):
    block_count = keys.shape[0] // key_block

    def query_one_block(block_index, running):
        first_row = block_index * key_block
        key_piece = lax.dynamic_slice_in_dim(keys, first_row, key_block, 0)
        value_piece = lax.dynamic_slice_in_dim(values, first_row, key_block, 0)
        key_pos = position_of(
            first_row + jnp.arange(key_block, dtype=jnp.int32), ctx_count, half_rows
        )
        weights = jnp.exp(
            scores(query, key_piece, query_pos, key_pos, query_start, score_scale)
            - log_total[..., None]
        )
        grad_weight = jnp.einsum(
            "qshe,kshe->shqk", grad_heads, value_piece, preferred_element_type=jnp.float32
        )
        grad_score = (weights * (grad_weight - row_delta[..., None])).astype(jnp.bfloat16)
        return running + jnp.einsum(
            "shqk,kshe->qshe", grad_score, key_piece, preferred_element_type=jnp.float32
        )

    return (
        lax.fori_loop(0, block_count, query_one_block, jnp.zeros(query.shape, jnp.float32))
        * score_scale
    )


def key_grads(
    query,
    grad_heads,
    query_pos,
    query_start,
    log_total,
    row_delta,
    key_piece,
    value_piece,
    key_pos,
    score_scale,
):
    weights = jnp.exp(
        scores(query, key_piece, query_pos, key_pos, query_start, score_scale)
        - log_total[..., None]
    )
    grad_weight = jnp.einsum(
        "qshe,kshe->shqk", grad_heads, value_piece, preferred_element_type=jnp.float32
    )
    grad_score = (weights * (grad_weight - row_delta[..., None])).astype(jnp.bfloat16)
    key_part = (
        jnp.einsum("shqk,qshe->kshe", grad_score, query, preferred_element_type=jnp.float32)
        * score_scale
    )
    value_part = jnp.einsum(
        "shqk,qshe->kshe",
        weights.astype(jnp.bfloat16),
        grad_heads,
        preferred_element_type=jnp.float32,
    )
    return (key_part, value_part)


def shards(
    tokens,
    doc_starts,
    expert_ids,
    query_key_value_weight,
    output_weight_matrix,
    expert_in,
    expert_out,
    gain_one,
    gain_two,
    grad_output,
):
    seq_dev = tokens.shape[0]
    half_rows = tokens.shape[3]
    model_width = tokens.shape[4]
    local_rows = 2 * half_rows
    ctx_count = lax.axis_size("ctx")
    head_count = HEADS
    head_size = model_width // head_count
    score_scale = head_size ** (-0.5)
    keys_total = ctx_count * local_rows
    key_block = min(512, keys_total)
    own_rows = lax.axis_index("ctx") * local_rows + jnp.arange(local_rows, dtype=jnp.int32)
    query_pos = position_of(own_rows, ctx_count, half_rows)
    query_start = doc_starts.reshape(seq_dev, local_rows).T
    routes_local = expert_ids.reshape(seq_dev, local_rows).T
    start_x = (
        tokens.reshape(seq_dev, local_rows, model_width).transpose(1, 0, 2).astype(jnp.float32)
    )
    cotangent = grad_output.reshape(seq_dev, local_rows, model_width).transpose(1, 0, 2)
    projection, out_proj = (
        lax.all_gather(query_key_value_weight.astype(jnp.bfloat16), "fsdp", axis=0, tiled=True),
        lax.all_gather(output_weight_matrix.astype(jnp.bfloat16), "fsdp", axis=0, tiled=True),
    )
    first_normed_rows, hat_one, inverse_one = norm_forward(start_x, gain_one)
    normed_low = first_normed_rows.astype(jnp.bfloat16)
    projected_rows = jnp.einsum(
        "tsd,de->tse", normed_low, projection, preferred_element_type=jnp.float32
    ).astype(jnp.bfloat16)
    query = projected_rows[..., :model_width]
    keys = projected_rows[..., model_width : 2 * model_width]
    values = projected_rows[..., 2 * model_width :]
    key_all, value_all = (
        lax.all_gather(keys, "ctx", axis=0, tiled=True),
        lax.all_gather(values, "ctx", axis=0, tiled=True),
    )
    query_heads = query.reshape(local_rows, seq_dev, head_count, head_size)
    key_heads = key_all.reshape(keys_total, seq_dev, head_count, head_size)
    value_heads = value_all.reshape(keys_total, seq_dev, head_count, head_size)
    log_total = log_totals(
        query_heads, key_heads, query_pos, query_start, score_scale, ctx_count, half_rows, key_block
    )
    mixed_heads_out, remainder = attend(
        query_heads,
        key_heads,
        value_heads,
        query_pos,
        query_start,
        log_total,
        score_scale,
        ctx_count,
        half_rows,
        key_block,
    )
    mixed_low = mixed_heads_out.astype(jnp.bfloat16).reshape(local_rows, seq_dev, model_width)
    attention_rows_out = jnp.einsum(
        "tsd,de->tse", mixed_low, out_proj, preferred_element_type=jnp.float32
    )
    middle = start_x + attention_rows_out
    normed_two, hat_two, inverse_two = norm_forward(middle, gain_two)
    routed = normed_two.astype(jnp.bfloat16)
    slot_count = EXPERTS * CAP
    per_owner = EXPERTS // ctx_count
    chosen = (routes_local[..., None] == jnp.arange(EXPERTS, dtype=jnp.int32)).astype(jnp.int32)
    earlier = (
        jnp.arange(local_rows)[:, None] >= jnp.arange(local_rows)[None, :]
    ).astype(jnp.bfloat16)
    running = jnp.einsum(
        "tu,use->tse", earlier, chosen.astype(jnp.bfloat16), preferred_element_type=jnp.float32
    )
    rank_within = jnp.sum(chosen * running.astype(jnp.int32), axis=-1) - 1
    slot_index = routes_local * CAP + rank_within
    dispatch = (
        slot_index.T[:, None, :] == jnp.arange(slot_count, dtype=jnp.int32)[None, :, None]
    ).astype(jnp.bfloat16)
    dispatch = dispatch.reshape(seq_dev, ctx_count, per_owner, CAP, local_rows)
    send_rows = jnp.einsum(
        "snect,tsd->nescd", dispatch, routed, preferred_element_type=jnp.float32
    ).astype(jnp.bfloat16)
    send_grads = jnp.einsum(
        "snect,tsd->nescd", dispatch, cotangent, preferred_element_type=jnp.float32
    ).astype(jnp.bfloat16)
    got_rows, got_grads = (
        lax.all_to_all(send_rows, "ctx", split_axis=0, concat_axis=0, tiled=True),
        lax.all_to_all(send_grads, "ctx", split_axis=0, concat_axis=0, tiled=True),
    )
    in_low = expert_in.astype(jnp.bfloat16)
    out_low = expert_out.astype(jnp.bfloat16)
    all_rows, all_grads = (
        lax.all_gather(got_rows, "fsdp", axis=2, tiled=True),
        lax.all_gather(got_grads, "fsdp", axis=2, tiled=True),
    )
    hidden = jnp.einsum("nercd,edf->nercf", all_rows, in_low, preferred_element_type=jnp.float32)
    active = jax.nn.gelu(hidden).astype(jnp.bfloat16)
    partial_rows = jnp.einsum(
        "nercf,efd->nercd", active, out_low, preferred_element_type=jnp.float32
    )
    result = lax.psum_scatter(
        partial_rows.astype(jnp.bfloat16), "fsdp", scatter_dimension=2, tiled=True
    )
    upstream = jnp.einsum(
        "nercd,efd->nercf", all_grads, out_low, preferred_element_type=jnp.float32
    )
    unused, gelu_back = jax.vjp(jax.nn.gelu, hidden)
    grad_hidden = gelu_back(upstream)[0].astype(jnp.bfloat16)
    grad_in = jnp.einsum(
        "nercd,nercf->edf", all_rows, grad_hidden, preferred_element_type=jnp.float32
    )
    grad_outw = jnp.einsum(
        "nercf,nercd->efd", active, all_grads, preferred_element_type=jnp.float32
    )
    row_part = jnp.einsum(
        "nercf,edf->nercd", grad_hidden, in_low, preferred_element_type=jnp.float32
    )
    row_grad = lax.psum_scatter(row_part, "fsdp", scatter_dimension=2, tiled=True).astype(
        jnp.bfloat16
    )
    back_rows = lax.all_to_all(result, "ctx", split_axis=0, concat_axis=0, tiled=True)
    expert_sum = jnp.einsum(
        "snect,nescd->tsd", dispatch, back_rows, preferred_element_type=jnp.float32
    )
    output_rows = middle + expert_sum
    returned = lax.all_to_all(row_grad, "ctx", split_axis=0, concat_axis=0, tiled=True)
    grad_routed = jnp.einsum(
        "snect,nescd->tsd", dispatch, returned, preferred_element_type=jnp.float32
    )
    grad_mid_norm, grad_gain_two = norm_backward(grad_routed, hat_two, inverse_two, gain_two)
    grad_middle = cotangent.astype(jnp.float32) + grad_mid_norm
    grad_attn = grad_middle.astype(jnp.bfloat16)
    grad_outproj = jnp.einsum(
        "tsd,tse->de", mixed_low, grad_attn, preferred_element_type=jnp.float32
    )
    grad_mixed = jnp.einsum(
        "tse,de->tsd", grad_attn, out_proj, preferred_element_type=jnp.float32
    ).astype(jnp.bfloat16)
    grad_heads = grad_mixed.reshape(local_rows, seq_dev, head_count, head_size)
    full_mixed = mixed_heads_out + remainder
    row_delta = jnp.sum(grad_heads.astype(jnp.float32) * full_mixed, axis=-1).transpose(1, 2, 0)
    grad_query = query_grads(
        query_heads,
        key_heads,
        value_heads,
        grad_heads,
        query_pos,
        query_start,
        log_total,
        row_delta,
        score_scale,
        ctx_count,
        half_rows,
        key_block,
    ).astype(jnp.bfloat16)
    sub_rows = math.gcd(local_rows * lax.axis_size("ctx"), key_block)

    def one_piece(piece_index):
        piece_start = piece_index * sub_rows
        key_piece = lax.dynamic_slice_in_dim(key_heads, piece_start, sub_rows, 0)
        value_piece = lax.dynamic_slice_in_dim(value_heads, piece_start, sub_rows, 0)
        key_pos = position_of(
            piece_start + jnp.arange(sub_rows, dtype=jnp.int32), ctx_count, half_rows
        )
        key_part, value_part = key_grads(
            query_heads,
            grad_heads,
            query_pos,
            query_start,
            log_total,
            row_delta,
            key_piece,
            value_piece,
            key_pos,
            score_scale,
        )
        return jnp.concatenate(
            [
                key_part.reshape(sub_rows, seq_dev, model_width),
                value_part.reshape(sub_rows, seq_dev, model_width),
            ],
            axis=-1,
        )

    summed = lax.psum_scatter(
        lax.map(
            one_piece, jnp.arange(local_rows * lax.axis_size("ctx") // sub_rows, dtype=jnp.int32)
        ).reshape(local_rows * lax.axis_size("ctx"), seq_dev, 2 * model_width),
        "ctx",
        scatter_dimension=0,
        tiled=True,
    )
    grad_key = summed[..., :model_width].astype(jnp.bfloat16)
    grad_value = summed[..., model_width:].astype(jnp.bfloat16)
    grad_projected = jnp.concatenate(
        [grad_query.reshape(local_rows, seq_dev, model_width), grad_key, grad_value], axis=-1
    )
    grad_projection = jnp.einsum(
        "tsd,tse->de", normed_low, grad_projected, preferred_element_type=jnp.float32
    )
    grad_normed = jnp.einsum(
        "tse,de->tsd", grad_projected, projection, preferred_element_type=jnp.float32
    )
    grad_in_norm, grad_gain_one = norm_backward(grad_normed, hat_one, inverse_one, gain_one)
    grad_start = grad_middle + grad_in_norm
    shard_proj, shard_outproj, shard_gain_one, shard_gain_two = (
        lax.psum_scatter(
            grad_projection.astype(jnp.bfloat16), "fsdp", scatter_dimension=0, tiled=True
        ).astype(jnp.float32),
        lax.psum_scatter(
            grad_outproj.astype(jnp.bfloat16), "fsdp", scatter_dimension=0, tiled=True
        ).astype(jnp.float32),
        lax.psum_scatter(
            grad_gain_one.astype(jnp.bfloat16), "fsdp", scatter_dimension=0, tiled=True
        ).astype(jnp.float32),
        lax.psum_scatter(
            grad_gain_two.astype(jnp.bfloat16), "fsdp", scatter_dimension=0, tiled=True
        ).astype(jnp.float32),
    )
    shard_proj, shard_outproj, shard_gain_one, shard_gain_two = (
        lax.psum(shard_proj.astype(jnp.bfloat16), "ctx").astype(jnp.float32),
        lax.psum(shard_outproj.astype(jnp.bfloat16), "ctx").astype(jnp.float32),
        lax.psum(shard_gain_one.astype(jnp.bfloat16), "ctx").astype(jnp.float32),
        lax.psum(shard_gain_two.astype(jnp.bfloat16), "ctx").astype(jnp.float32),
    )
    block_out = output_rows.transpose(1, 0, 2).reshape(tokens.shape).astype(jnp.bfloat16)
    grad_tokens = grad_start.transpose(1, 0, 2).reshape(tokens.shape)
    return (
        block_out,
        grad_tokens,
        shard_proj,
        shard_outproj,
        grad_in,
        grad_outw,
        shard_gain_one,
        shard_gain_two,
    )


BF = jnp.bfloat16
F32 = jnp.float32
MESH_ID = pl.DeviceIdType.MESH
ANY = pl.BlockSpec(memory_space=pl.ANY)
DMA = pltpu.SemaphoreType.DMA
VMEM_CAP = 56 << 20


def place():
    c = lax.axis_index("ctx")
    f = lax.axis_index("fsdp")
    return c, f, c // 2, c % 2, f // 2, f % 2


def remote(src, dst, send, recv, device):
    return pltpu.make_async_remote_copy(
        src_ref=src, dst_ref=dst, send_sem=send, recv_sem=recv, device_id=device, device_id_type=MESH_ID
    )


def block_at(c, half, count):
    return c if half == 0 else 2 * count - 1 - c


def relative(a, b):
    return (a // 2 + b // 2) % 2 * 2 + (a + b) % 2


def swap(value, axis, bit):
    size = lax.axis_size(axis)
    return lax.ppermute(value, axis, [(i, i ^ bit) for i in range(size)])


def lasting(microseconds):
    return pl.CostEstimate(flops=0, bytes_accessed=int(microseconds * 3.3e6), transcendentals=0)


def params(side=True):
    return pltpu.CompilerParams(has_side_effects=side, vmem_limit_bytes=VMEM_CAP)


def gather_stream(normed, starts, weight):
    count = lax.axis_size("ctx")
    depth = count // 2
    rows, wide = weight.shape
    lanes = wide // 3 // count

    def kernel(n_ref, s_ref, w_ref, tok, st, cols, rs_t, ss_p, ss_up, ss_dn, ss_sib, rs_s, ss_s, rs_w, ss_w):
        c, f, z, y, x, k = place()
        sib = (c, f + 1 - 2 * k)
        partner = (c + 1 - 2 * y, f + 1 - 2 * k)
        up = (c + 2, f)
        down = (c - 2, f)
        holder = k == y

        def send_in(h):
            b = block_at(c, h, count)
            return remote(n_ref.at[h], tok.at[b], ss_p.at[h], rs_t.at[b], partner)

        def local_in(h):
            b = block_at(c, h, count)
            return pltpu.make_async_copy(n_ref.at[h], tok.at[b], rs_t.at[b])

        @pl.when(holder)
        def _():
            for h in range(2):
                local_in(h).start()

        @pl.when(jnp.logical_not(holder))
        def _():
            for h in range(2):
                send_in(h).start()

        for zt in range(depth):
            for kt in range(2):
                mine = holder & (z == zt) & (k == kt)

                @pl.when(mine)
                def _():
                    pltpu.make_async_copy(s_ref, st.at[c], rs_s.at[c]).start()

                @pl.when(jnp.logical_not(mine))
                def _(zt=zt, kt=kt):
                    remote(s_ref, st.at[c], ss_s.at[2 * zt + kt], rs_s.at[c], (2 * zt + k, 2 * x + kt)).start()

        goals = [(2 * z + k, (c, (f + 2) % 4)), (2 * z + 1 - k, (c, (sib[1] + 2) % 4)), (2 * z + 1 - k, sib)]

        def columns(pair, j):
            return w_ref.at[:, pl.ds(pl.multiple_of(j * count * lanes + pair * lanes, lanes), lanes)]

        def weight_place(shard, j):
            return cols.at[j, pl.ds(pl.multiple_of(shard * rows, rows), rows)]

        def weight_send(t, j):
            pair, dev = goals[t]
            return remote(columns(pair, j), weight_place(f, j), ss_w.at[t, j], rs_w.at[f, j], dev)

        for j in range(3):
            for t in range(3):
                weight_send(t, j).start()
            pltpu.make_async_copy(columns(2 * z + k, j), weight_place(f, j), rs_w.at[f, j]).start()

        def copy_block(zb, h, ss, dev):
            b = block_at(2 * zb + k, h, count)
            return remote(tok.at[b], tok.at[b], ss, rs_t.at[b], dev)

        for j in range(depth):
            for h in range(2):
                if j == 0:
                    copy_block(z, h, ss_p.at[h], sib).wait_recv()

                    @pl.when(z < depth - 1)
                    def _(h=h):
                        copy_block(z, h, ss_up.at[0, h], up).start()

                    @pl.when(z > 0)
                    def _(h=h):
                        copy_block(z, h, ss_dn.at[0, h], down).start()

                    copy_block(z, h, ss_sib.at[z, h], sib).start()
                    continue

                @pl.when(z - j >= 0)
                def _(j=j, h=h):
                    copy_block(z - j, h, ss_p.at[h], sib).wait_recv()

                    @pl.when(z < depth - 1)
                    def _():
                        copy_block(z - j, h, ss_up.at[j, h], up).start()

                    copy_block(z - j, h, ss_sib.at[z - j, h], sib).start()

                @pl.when(z + j <= depth - 1)
                def _(j=j, h=h):
                    copy_block(z + j, h, ss_p.at[h], sib).wait_recv()

                    @pl.when(z > 0)
                    def _():
                        copy_block(z + j, h, ss_dn.at[j, h], down).start()

                    copy_block(z + j, h, ss_sib.at[z + j, h], sib).start()

        for zt in range(depth):
            for h in range(2):
                b = block_at(2 * zt + 1 - k, h, count)
                remote(tok.at[b], tok.at[b], ss_p.at[h], rs_t.at[b], sib).wait_recv()
                copy_block(zt, h, ss_sib.at[zt, h], sib).wait_send()
        for ct in range(count):
            remote(s_ref, st.at[ct], ss_s.at[0], rs_s.at[ct], sib).wait_recv()
        for j in range(3):
            for shard in range(4):
                remote(columns(0, j), weight_place(shard, j), ss_w.at[0, j], rs_w.at[shard, j], sib).wait_recv()
            for t in range(3):
                weight_send(t, j).wait_send()

        @pl.when(jnp.logical_not(holder))
        def _():
            for h in range(2):
                send_in(h).wait_send()

        for j in range(depth):

            @pl.when((z < depth - 1) & (z - j >= 0))
            def _(j=j):
                for h in range(2):
                    copy_block(z - j, h, ss_up.at[j, h], up).wait_send()

            @pl.when((z > 0) & (z + j <= depth - 1))
            def _(j=j):
                for h in range(2):
                    copy_block(z + j, h, ss_dn.at[j, h], down).wait_send()

        for zt in range(depth):
            for kt in range(2):
                mine = holder & (z == zt) & (k == kt)

                @pl.when(jnp.logical_not(mine))
                def _(zt=zt, kt=kt):
                    remote(s_ref, st.at[c], ss_s.at[2 * zt + kt], rs_s.at[c], sib).wait_send()

    return pl.pallas_call(
        kernel,
        name="gather_stream",
        cost_estimate=lasting(50),
        out_shape=(
            jax.ShapeDtypeStruct((2 * count,) + normed.shape[1:], normed.dtype),
            jax.ShapeDtypeStruct((count,) + starts.shape, starts.dtype),
            jax.ShapeDtypeStruct((3, 4 * rows, lanes), weight.dtype),
        ),
        in_specs=[ANY] * 3,
        out_specs=(ANY,) * 3,
        scratch_shapes=[
            DMA((2 * count,)), DMA((2,)), DMA((depth, 2)), DMA((depth, 2)), DMA((depth, 2)),
            DMA((count,)), DMA((count,)), DMA((4, 3)), DMA((3, 3)),
        ],
        compiler_params=params(),
    )(normed, starts, weight)


TILE = 256


def halves(value, axis):
    size = value.shape[axis] // 2
    at = lax.broadcasted_iota(jnp.int32, value.shape, axis)
    zero = jnp.zeros_like(value)
    return [jnp.where(at < size, value, zero), jnp.where(at >= size, value, zero)]


def attend_forward(stream, columns, start_row, numbers, scale):
    length, width = stream.shape
    tiles = length // TILE
    lanes = 128
    size = lanes // 2

    def kernel(first, x_ref, w_ref, s_ref, q_out, k_out, v_out, m16, m32, lse, v_turned):
        i = pl.program_id(0)
        own = pl.ds(pl.multiple_of(i * TILE, TILE), TILE)
        rows = x_ref[...]
        query, key, value = [jnp.dot(rows, w_ref[j], preferred_element_type=F32).astype(BF) for j in range(3)]
        q_out[...] = query
        k_out[own, :] = key
        v_out[...] = value
        v_turned[:, own] = value.T
        queries = halves((query * scale).T, 0)
        start = s_ref[...]
        key_row = lax.broadcasted_iota(jnp.int32, (TILE, TILE), 0)
        query_column = i * TILE + lax.broadcasted_iota(jnp.int32, (TILE, TILE), 1)

        def step(j, carried):
            at = pl.multiple_of(j * TILE, TILE)
            keys = k_out[pl.ds(at, TILE), :]
            seen = (key_row + at <= query_column) & (key_row + at >= start)
            out = []
            for h in range(2):
                top, total, mixed = carried[h]
                score = jnp.where(seen, jnp.dot(keys, queries[h], preferred_element_type=F32), NEGATIVE)
                new_top = jnp.maximum(top, jnp.max(score, axis=0, keepdims=True))
                weight = jnp.exp(score - new_top)
                shrink = jnp.exp(top - new_top)
                total = total * shrink + jnp.sum(weight, axis=0, keepdims=True)
                values = v_turned[h * size : (h + 1) * size, pl.ds(at, TILE)]
                mixed = mixed * shrink + jnp.dot(values, weight.astype(BF), preferred_element_type=F32)
                out.append((new_top, total, mixed))
            return tuple(out)

        begin = (
            jnp.full((1, TILE), NEGATIVE, F32),
            jnp.zeros((1, TILE), F32),
            jnp.zeros((size, TILE), F32),
        )
        done = lax.fori_loop(first[i], i + 1, step, (begin, begin))
        mixed = jnp.concatenate([part / total for _, total, part in done], axis=0)
        m32[...] = mixed
        m16[...] = mixed.T.astype(BF)
        lse[...] = jnp.concatenate([top + jnp.log(total) for top, total, _ in done], axis=0)

    tile = pl.BlockSpec((TILE, lanes), lambda i, n: (i, 0))
    turned = pl.BlockSpec((lanes, TILE), lambda i, n: (0, i))
    return pl.pallas_call(
        kernel,
        name="attend_forward",
        cost_estimate=lasting(22),
        grid_spec=pltpu.PrefetchScalarGridSpec(
            num_scalar_prefetch=1,
            grid=(tiles,),
            in_specs=[
                pl.BlockSpec((TILE, width), lambda i, n: (i, 0)),
                pl.BlockSpec((3, width, lanes), lambda i, n: (0, 0, 0)),
                pl.BlockSpec((1, TILE), lambda i, n: (0, i)),
            ],
            out_specs=[
                tile,
                pl.BlockSpec((length, lanes), lambda i, n: (0, 0)),
                tile,
                tile,
                turned,
                pl.BlockSpec((2, TILE), lambda i, n: (0, i)),
            ],
            scratch_shapes=[pltpu.VMEM((lanes, length), BF)],
        ),
        out_shape=(
            jax.ShapeDtypeStruct((length, lanes), BF),
            jax.ShapeDtypeStruct((length, lanes), BF),
            jax.ShapeDtypeStruct((length, lanes), BF),
            jax.ShapeDtypeStruct((length, lanes), BF),
            jax.ShapeDtypeStruct((lanes, length), F32),
            jax.ShapeDtypeStruct((2, length), F32),
        ),
        compiler_params=params(False),
    )(numbers, stream, columns, start_row)


def attend_backward(query, key, value, grad, mixed, logs, start_row, numbers, scale):
    length, lanes = query.shape
    tiles = length // TILE
    size = lanes // 2

    def kernel(first, q_ref, k_ref, v_ref, g_ref, m_ref, l_ref, s_ref, dq, dk, dv, acc_k, acc_v, k_turned):
        i = pl.program_id(0)

        @pl.when(i == 0)
        def _():
            acc_k[...] = jnp.zeros_like(acc_k)
            acc_v[...] = jnp.zeros_like(acc_v)
            for t in range(tiles):
                k_turned[:, t * TILE : (t + 1) * TILE] = k_ref[t * TILE : (t + 1) * TILE, :].T

        scaled = q_ref[...] * scale
        grads = g_ref[...]
        turned = grads.T
        queries, queries_turned = halves(scaled, 1), halves(scaled.T, 0)
        grad_rows, grads_turned = halves(grads, 1), halves(turned, 0)
        product = turned.astype(F32) * m_ref[...]
        deltas = [jnp.sum(product[h * size : (h + 1) * size], axis=0, keepdims=True) for h in range(2)]
        logs_row = [l_ref[h : h + 1, :] for h in range(2)]
        start = s_ref[...]
        key_row = lax.broadcasted_iota(jnp.int32, (TILE, TILE), 0)
        query_column = i * TILE + lax.broadcasted_iota(jnp.int32, (TILE, TILE), 1)

        def step(j, running):
            at = pl.multiple_of(j * TILE, TILE)
            keys = k_ref[pl.ds(at, TILE), :]
            values = v_ref[pl.ds(at, TILE), :]
            seen = (key_row + at <= query_column) & (key_row + at >= start)
            key_sum = jnp.zeros((TILE, lanes), F32)
            value_sum = jnp.zeros((TILE, lanes), F32)
            out = []
            for h in range(2):
                score = jnp.dot(keys, queries_turned[h], preferred_element_type=F32)
                weight = jnp.exp(jnp.where(seen, score - logs_row[h], NEGATIVE))
                grad_weight = jnp.dot(values, grads_turned[h], preferred_element_type=F32)
                grad_score = (weight * (grad_weight - deltas[h])).astype(BF)
                value_sum += jnp.dot(weight.astype(BF), grad_rows[h], preferred_element_type=F32)
                key_sum += jnp.dot(grad_score, queries[h], preferred_element_type=F32)
                part = k_turned[h * size : (h + 1) * size, pl.ds(at, TILE)]
                out.append(running[h] + jnp.dot(part, grad_score, preferred_element_type=F32))
            acc_k[pl.ds(at, TILE), :] += key_sum
            acc_v[pl.ds(at, TILE), :] += value_sum
            return tuple(out)

        zero = jnp.zeros((size, TILE), F32)
        total = lax.fori_loop(first[i], i + 1, step, (zero, zero))
        dq[...] = (jnp.concatenate(total, axis=0) * scale).T.astype(BF)

        @pl.when(i == tiles - 1)
        def _():
            dk[...] = acc_k[...].astype(BF)
            dv[...] = acc_v[...].astype(BF)

    tile = pl.BlockSpec((TILE, lanes), lambda i, n: (i, 0))
    full = pl.BlockSpec((length, lanes), lambda i, n: (0, 0))
    return pl.pallas_call(
        kernel,
        name="attend_backward",
        cost_estimate=lasting(19),
        grid_spec=pltpu.PrefetchScalarGridSpec(
            num_scalar_prefetch=1,
            grid=(tiles,),
            in_specs=[
                tile,
                full,
                full,
                tile,
                pl.BlockSpec((lanes, TILE), lambda i, n: (0, i)),
                pl.BlockSpec((2, TILE), lambda i, n: (0, i)),
                pl.BlockSpec((1, TILE), lambda i, n: (0, i)),
            ],
            out_specs=[tile, full, full],
            scratch_shapes=[
                pltpu.VMEM((length, lanes), F32),
                pltpu.VMEM((length, lanes), F32),
                pltpu.VMEM((lanes, length), BF),
            ],
        ),
        out_shape=(jax.ShapeDtypeStruct((length, lanes), BF),) * 3,
        compiler_params=params(False),
    )(numbers, query, key, value, grad, mixed, logs, start_row)


def statistics(value):
    row_mean = jnp.mean(value, axis=1, keepdims=True)
    centred = value - row_mean
    inverse = lax.rsqrt(jnp.mean(centred * centred, axis=1, keepdims=True) + EPS)
    return centred * inverse, inverse


def route_rows(by_head, out_proj, tokens, dispatch, gain):
    count = lax.axis_size("ctx")
    early = count // 2
    lanes = by_head.shape[2]
    half_rows = by_head.shape[1]
    rows, width = tokens.shape
    experts = EXPERTS // count

    def kernel(
        a_ref, w_ref, x_ref, d_ref, g_ref, mixed, middle, out, routed, slots, mirror,
        ss, rs, ss1, rs1, ssm, rsm, ss2, rs2, sse, ssx, sss, rss, ssf, rsf,
    ):
        c, f, z, y, x, k = place()
        sib = (c, f + 1 - 2 * k)
        xn = (c, (f + 2) % 4)
        pair = 2 * z + k
        target = 2 * x + y

        def there(half):
            column = (2 * relative(z, target) + k) * lanes
            return mixed.at[half, :, pl.ds(pl.multiple_of(column, lanes), lanes)]

        def send(i, half):
            ct = (c + i) % count
            return remote(a_ref.at[block_at(ct, half, count)], there(half), ss.at[i, half], rs.at[pair, half], (ct, target))

        def keep(half):
            return pltpu.make_async_copy(a_ref.at[block_at(c, half, count)], there(half), rs.at[pair, half])

        for half in range(2):
            for i in range(1, count):
                send(i, half).start()

            @pl.when(k == y)
            def _(half=half):
                keep(half).start()

            @pl.when(k != y)
            def _(half=half):
                send(0, half).start()

        for half in range(2):
            for other in range(count):
                column = (2 * relative(other // 2, f) + other % 2) * lanes
                cols = pl.ds(pl.multiple_of(column, lanes), lanes)
                remote(a_ref.at[0], mixed.at[half, :, cols], ss.at[0, half], rs.at[other, half], sib).wait_recv()
            here = pl.ds(half * half_rows, half_rows)
            value = x_ref[here, :].astype(F32) + jnp.dot(mixed[half], w_ref[...], preferred_element_type=F32)
            middle[here, :] = value
            hat, _ = statistics(value)
            routed[here, :] = (hat * g_ref[...]).astype(BF)
        slots[...] = jnp.dot(d_ref[...], routed[...], preferred_element_type=F32).astype(BF).reshape(slots.shape)

        def owner(i):
            return (c + i) % count

        def straight(i):
            return remote(slots.at[owner(i)], out.at[0, c], ss1.at[i], rs1.at[c], (owner(i), f))

        def over(i):
            return remote(slots.at[owner(i)], mirror.at[i], ssm.at[i], rsm.at[i], xn)

        def onward(i):
            return remote(mirror.at[i], out.at[2, c], sse.at[i], rs2.at[c], (owner(i), f))

        own = pltpu.make_async_copy(slots.at[c], out.at[0, c], rs1.at[c])
        beside = remote(slots.at[c], out.at[2, c], ss2, rs2.at[c], xn)
        beside.start()
        for i in range(1, early):
            over(i).start()
        own.start()
        for i in [*range(early, count), *range(1, early)]:
            straight(i).start()

        def hop(source, send_sem, recv_sem, first, dst, dev):
            return remote(out.at[first, source], out.at[dst, source], send_sem.at[source], recv_sem.at[source], dev)

        def across(source):
            return hop(source, ssx, rs2, 0, 2, xn)

        def share(source):
            return hop(source, sss, rss, 0, 1, sib)

        def share_other(source):
            return hop(source, ssf, rsf, 2, 3, sib)

        def arrived(rel, source, recv_sem):
            remote(out.at[rel, source], out.at[rel, source], ss2, recv_sem.at[source], sib).wait_recv()

        def source_of(i):
            return (c + count - i) % count

        arrived(0, c, rs1)
        share(c).start()
        for i in range(early, count):
            arrived(0, source_of(i), rs1)
            across(source_of(i)).start()
            share(source_of(i)).start()
            j = i - early + 1
            if j < early:
                over(j).wait_recv()
                onward(j).start()
        for i in range(1, early):
            arrived(0, source_of(i), rs1)
            share(source_of(i)).start()
        for i in range(count):
            arrived(2, source_of(i), rs2)
            share_other(source_of(i)).start()
        for i in range(count):
            cs = source_of(i)
            share(cs).wait_send()
            share_other(cs).wait_send()
            arrived(1, cs, rss)
            arrived(3, cs, rsf)
            if i:
                straight(i).wait_send()
            if 1 <= i < early:
                over(i).wait_send()
                onward(i).wait_send()
            if i >= early:
                across(cs).wait_send()
        beside.wait_send()
        for i in range(1, count):
            for half in range(2):
                send(i, half).wait_send()

        @pl.when(k != y)
        def _():
            for half in range(2):
                send(0, half).wait_send()

    vmem = pl.BlockSpec(memory_space=pltpu.VMEM)
    block = (experts, CAP, width)
    return pl.pallas_call(
        kernel,
        name="route_rows",
        cost_estimate=lasting(50),
        out_shape=(
            jax.ShapeDtypeStruct((2, half_rows, width), BF),
            jax.ShapeDtypeStruct((rows, width), F32),
            jax.ShapeDtypeStruct((4, count) + block, BF),
        ),
        in_specs=[ANY] + [vmem] * 4,
        out_specs=(vmem, vmem, ANY),
        scratch_shapes=[
            pltpu.VMEM((rows, width), BF),
            pltpu.VMEM((count,) + block, BF),
            pltpu.VMEM((early,) + block, BF),
            DMA((count, 2)), DMA((count, 2)),
            DMA((count,)), DMA((count,)), DMA((early,)), DMA((early,)), DMA, DMA((count,)), DMA((early,)),
            DMA((count,)), DMA((count,)), DMA((count,)), DMA((count,)), DMA((count,)),
        ],
        compiler_params=params(),
    )(by_head, out_proj, tokens, dispatch, gain)


def return_grads(own, near, far, ready, dispatch, cotangent, middle, mixed, out_proj, gain):
    count = lax.axis_size("ctx")
    lanes = width_of_pair = out_proj.shape[1] // count
    rows, width = middle.shape
    half_rows = rows // 2
    quarter = width // 4

    def kernel(
        o_ref, n_ref, f_ref, z_ref, d_ref, c_ref, m_ref, a_ref, w_ref, g_ref, heads, grad_middle, gain_out, shard,
        own_v, near_v, total, got, back, parts, got_near, far_v, got_far,
        loc, ss, rs, ss_h, rs_h, ss_n, rs_n, ss_f, rs_f,
    ):
        c, f, z, y, x, k = place()
        sib = (c, f + 1 - 2 * k)
        xn = (c, (f + 2) % 4)
        loads = [
            pltpu.make_async_copy(o_ref.at[0], own_v, loc.at[0]),
            pltpu.make_async_copy(n_ref.at[0], near_v, loc.at[1]),
        ]
        for load in loads:
            load.start()
        for load in loads:
            load.wait()

        def home(i):
            ct = (c + i) % count
            return remote(total.at[ct], got.at[c], ss.at[i], rs.at[c], (ct, f))

        zero = z_ref[0:1, 0:1]
        for i in [*range(1, count), 0]:
            ct = (c + i) % count
            value = own_v[ct].astype(F32) + near_v[ct].astype(F32) + f_ref[ct].astype(F32) + zero
            if i:
                total[ct] = value.astype(BF)
                home(i).start()
            else:
                got[c] = value.astype(BF)
        hat, inverse = statistics(m_ref[...])
        for i in range(1, count):
            cs = (c + i) % count
            remote(total.at[cs], got.at[cs], ss.at[i], rs.at[cs], sib).wait_recv()
        routed = lax.dot_general(
            d_ref[...], got[...].reshape(-1, width), (((0,), (0,)), ((), ())), preferred_element_type=F32
        )
        scaled = routed * g_ref[...]
        mean_grad = jnp.mean(scaled, axis=1, keepdims=True)
        mean_proj = jnp.mean(scaled * hat, axis=1, keepdims=True)
        gain_out[...] = jnp.sum(routed * hat, axis=0, keepdims=True)
        grad = c_ref[...].astype(F32) + inverse * (scaled - mean_grad - hat * mean_proj)
        grad_middle[...] = grad
        low = grad.astype(BF)
        back[...] = (
            lax.dot_general(low, w_ref[...], (((1,), (1,)), ((), ())), preferred_element_type=F32)
            .astype(BF)
            .reshape(back.shape)
        )

        def part(half, pair):
            column = (2 * relative(pair // 2, f) + pair % 2) * lanes
            return back.at[half, :, pl.ds(pl.multiple_of(column, lanes), lanes)]

        def send(i, half):
            pair = (2 * z + k + i) % count
            b = block_at(c, half, count)
            dev = (2 * (pair // 2) + k, 2 * x + pair % 2)
            return remote(part(half, pair), heads.at[b], ss_h.at[i, half], rs_h.at[b], dev)

        for i in range(1, count):
            for half in range(2):
                send(i, half).start()

        @pl.when(k == y)
        def _():
            for half in range(2):
                b = block_at(c, half, count)
                pltpu.make_async_copy(part(half, 2 * z + k), heads.at[b], rs_h.at[b]).start()

        @pl.when(k != y)
        def _():
            for half in range(2):
                send(0, half).start()

        def term(j):
            return lax.dot_general(
                a_ref[:, j * quarter : (j + 1) * quarter], low, (((0,), (0,)), ((), ())), preferred_element_type=F32
            ).astype(BF)

        def core_send(j):
            return remote(parts.at[2 * j + 1], got_near.at[j], ss_n.at[j], rs_n.at[j], sib)

        across = remote(far_v, got_far, ss_f, rs_f, xn)
        for j in (1, 0):
            parts[2 * j + 1] = term(2 * j + 1)
            core_send(j).start()
        parts[2] = term(2)
        core_send(1).wait_recv()
        far_v[...] = (parts[2].astype(F32) + got_near[1].astype(F32)).astype(BF)
        across.start()
        parts[0] = term(0)
        core_send(0).wait_recv()
        across.wait_recv()
        shard[...] = (parts[0].astype(F32) + got_near[0].astype(F32) + got_far[...].astype(F32)).astype(BF)

        for b in range(2 * count):
            remote(part(0, 0), heads.at[b], ss_h.at[0, 0], rs_h.at[b], sib).wait_recv()
        for i in range(1, count):
            home(i).wait_send()
            for half in range(2):
                send(i, half).wait_send()

        @pl.when(k != y)
        def _():
            for half in range(2):
                send(0, half).wait_send()

        core_send(0).wait_send()
        core_send(1).wait_send()
        across.wait_send()

    vmem = pl.BlockSpec(memory_space=pltpu.VMEM)
    slots = pltpu.VMEM(far.shape, BF)
    shard_shape = pltpu.VMEM((quarter, width), BF)
    return pl.pallas_call(
        kernel,
        name="return_grads",
        cost_estimate=lasting(35),
        out_shape=(
            jax.ShapeDtypeStruct((2 * count, half_rows, width_of_pair), BF),
            jax.ShapeDtypeStruct((rows, width), F32),
            jax.ShapeDtypeStruct((1, width), F32),
            jax.ShapeDtypeStruct((quarter, width), BF),
        ),
        in_specs=[ANY, ANY] + [vmem] * 8,
        out_specs=(ANY, vmem, vmem, vmem),
        scratch_shapes=[
            slots, slots, slots, slots,
            pltpu.VMEM((2, half_rows, width), BF),
            pltpu.VMEM((4, quarter, width), BF),
            pltpu.VMEM((2, quarter, width), BF),
            shard_shape, shard_shape,
            DMA((2,)), DMA((count,)), DMA((count,)), DMA((count, 2)), DMA((2 * count,)), DMA((2,)), DMA((2,)), DMA, DMA,
        ],
        compiler_params=params(),
    )(own, near, far, ready, dispatch, cotangent, middle, mixed, out_proj, gain)


ROOT = math.sqrt(2.0 / math.pi)
CUBIC = 0.044715


def stacked(ref):
    return ref[...].reshape(-1, ref.shape[-1])


def experts_rows(rows, near, far, beside, first_proj, second_proj):
    _, count, number, cap, width = rows.shape
    units = first_proj.shape[2]
    total = 4 * count * cap

    def kernel(r_ref, n_ref, f_ref, b_ref, w1, w2, back, back_odd, out, out_odd, active_out, hidden_out, grad_out):
        row = stacked(r_ref)
        grad = jnp.concatenate(
            [stacked(n_ref), b_ref[0].reshape(-1, width), stacked(f_ref), b_ref[1].reshape(-1, width)], axis=0
        )
        grad_out[0] = grad
        first = w1[0].astype(BF)
        second = w2[0].astype(BF)
        hidden = jnp.dot(row, first, preferred_element_type=F32)
        upstream = lax.dot_general(grad, second, (((1,), (1,)), ((), ())), preferred_element_type=F32)
        bent = jnp.tanh(ROOT * (hidden + CUBIC * hidden * hidden * hidden))
        active = (0.5 * hidden * (1.0 + bent)).astype(BF)
        slope = 0.5 * (1.0 + bent) + 0.5 * hidden * (1.0 - bent * bent) * (ROOT * (1.0 + 3.0 * CUBIC * hidden * hidden))
        grad_hidden = (upstream * slope).astype(BF)
        active_out[0] = active
        hidden_out[0] = grad_hidden
        term = lax.dot_general(grad_hidden, first, (((1,), (1,)), ((), ())), preferred_element_type=F32)
        result = jnp.dot(active, second, preferred_element_type=F32)
        for j in range(4):
            here = slice(j * total // 4, (j + 1) * total // 4)
            (back_odd if j % 2 else back)[j // 2] = term[here].astype(BF).reshape(back.shape[1:])
            (out_odd if j % 2 else out)[j // 2] = result[here].astype(BF).reshape(out.shape[1:])

    parts = pl.BlockSpec((4, count, 1, cap, width), lambda e: (0, 0, e, 0, 0))
    quarter = pl.BlockSpec((count, 1, cap, width), lambda e: (0, e, 0, 0))
    pair = pl.BlockSpec((2, count, 1, cap, width), lambda e: (0, 0, e, 0, 0))
    left = pl.BlockSpec((1, width, units), lambda e: (e, 0, 0))
    right = pl.BlockSpec((1, units, width), lambda e: (e, 0, 0))
    wide = pl.BlockSpec((1, total, units), lambda e: (e, 0, 0))
    flat = pl.BlockSpec((1, total, width), lambda e: (e, 0, 0))
    return pl.pallas_call(
        kernel,
        name="experts_rows",
        grid=(number,),
        in_specs=[parts, quarter, quarter, pair, left, right],
        out_specs=[pair] * 4 + [wide, wide, flat],
        out_shape=(
            *[jax.ShapeDtypeStruct((2,) + rows.shape[1:], BF)] * 4,
            jax.ShapeDtypeStruct((number, total, units), BF),
            jax.ShapeDtypeStruct((number, total, units), BF),
            jax.ShapeDtypeStruct((number, total, width), BF),
        ),
        cost_estimate=pl.CostEstimate(
            flops=8 * number * total * units * width, bytes_accessed=8 * number * units * width, transcendentals=0
        ),
        compiler_params=params(False),
    )(rows, near, far, beside, first_proj, second_proj)


def experts_weights(rows, grads, active, grad_hidden):
    _, count, number, cap, width = rows.shape
    total, units = active.shape[1:]

    def kernel(r_ref, g_ref, a_ref, h_ref, da, db, done):
        done[...] = jnp.zeros_like(done)
        turn = (((0,), (0,)), ((), ()))
        da[0] = lax.dot_general(stacked(r_ref), h_ref[0], turn, preferred_element_type=F32)
        db[0] = lax.dot_general(a_ref[0], g_ref[0], turn, preferred_element_type=F32)

    parts = pl.BlockSpec((4, count, 1, cap, width), lambda e: (0, 0, e, 0, 0))
    wide = pl.BlockSpec((1, total, units), lambda e: (e, 0, 0))
    flat = pl.BlockSpec((1, total, width), lambda e: (e, 0, 0))
    return pl.pallas_call(
        kernel,
        name="experts_weights",
        grid=(number,),
        in_specs=[parts, flat, wide, wide],
        out_specs=[
            pl.BlockSpec((1, width, units), lambda e: (e, 0, 0)),
            pl.BlockSpec((1, units, width), lambda e: (e, 0, 0)),
            pl.BlockSpec((8, 128), lambda e: (0, 0)),
        ],
        out_shape=(
            jax.ShapeDtypeStruct((number, width, units), F32),
            jax.ShapeDtypeStruct((number, units, width), F32),
            jax.ShapeDtypeStruct((8, 128), F32),
        ),
        cost_estimate=pl.CostEstimate(
            flops=4 * number * total * units * width, bytes_accessed=12 * number * units * width, transcendentals=0
        ),
        compiler_params=params(False),
    )(rows, grads, active, grad_hidden)


def after(value, *others):
    return lax.optimization_barrier((value,) + others)[0]


def finish_exchange(arrays, parts, out_slab, gain_part, weight):
    count = lax.axis_size("ctx")
    depth = count // 2
    number = len(arrays)
    lanes = arrays[0].shape[2]
    width = count * lanes
    _, rows, wide = parts.shape
    slab = rows // count
    pieces_w = 4
    piece_w = rows // pieces_w

    def kernel(*refs):
        ins, (p_ref, o_ref, g_ref, w_ref), (tok_out, w_out, o_out, g_out, w_all) = (
            refs[:number],
            refs[number : number + 4],
            refs[number + 4 : number + 9],
        )
        (
            got, held, got_g, sum_g, got_gc,
            ss, rs, ss_r, rs_r, ss_up, ss_dn, rs_z, ss_a, ss_b, rs_o,
            ss_of, rs_of, ss_g, rs_g, ss_gc, rs_gc, ss_wx, rs_wx, ss_ws, rs_ws, ss_wf, rs_wf, loc,
        ) = refs[number + 9 :]
        c, f, z, y, x, k = place()
        pair = 2 * z + k
        target = 2 * x + y
        sib = (c, f + 1 - 2 * k)
        xn = (c, (f + 2) % 4)
        up = (c + 2, f)
        down = (c - 2, f)

        def gain_send(j):
            return remote(sum_g.at[j], got_g.at[j], ss_g.at[j], rs_g.at[j], sib if j == 0 else xn)

        sum_g[0] = g_ref[...]
        gain_send(0).start()

        def slab_spread(i):
            return remote(o_ref, o_out.at[c], ss_of.at[i], rs_of.at[c], ((c + i) % count, f))

        slab_own = pltpu.make_async_copy(o_ref, o_out.at[c], rs_of.at[c])

        def weight_part(shard, i):
            return w_all.at[shard, pl.ds(i * piece_w, piece_w)]

        def weight_across(i):
            return remote(w_ref.at[pl.ds(i * piece_w, piece_w)], weight_part(f, i), ss_wx.at[i], rs_wx.at[i], xn)

        def weight_on(i, shard):
            return remote(weight_part(shard, i), weight_part(shard, i), ss_wf.at[i], rs_wf.at[i], sib)

        weight_share = remote(w_ref, w_all.at[f], ss_ws, rs_ws, sib)
        weight_own = pltpu.make_async_copy(w_ref, w_all.at[f], loc)

        peers = [
            (2 * z + 1 - y, f, 2 * x + 1 - y),
            (c, (f + 2) % 4, 2 * (1 - x) + y),
            (2 * z + 1 - y, (f + 2) % 4, 2 * (1 - x) + 1 - y),
        ]

        def scatter(d):
            cp, fp, shard = peers[d]
            return remote(p_ref.at[shard], got.at[d], ss_r.at[d], rs_r.at[d], (cp, fp))

        for d in (2, 1, 0):
            scatter(d).start()

        def there(half, a):
            return tok_out.at[half, :, pl.ds(pl.multiple_of(a * width + pair * lanes, lanes), lanes)]

        def send(i, half, a):
            ct = (c + i) % count
            return remote(
                ins[a].at[block_at(ct, half, count)], there(half, a), ss.at[i, half, a], rs.at[pair, half, a], (ct, target)
            )

        def own(half, a):
            return pltpu.make_async_copy(ins[a].at[block_at(c, half, count)], there(half, a), rs.at[pair, half, a])

        pieces = [(half, a) for a in range(number) for half in range(2)]
        for i in range(1, count):
            for half, a in pieces:
                send(i, half, a).start()

        @pl.when(k == y)
        def _():
            for half, a in pieces:
                own(half, a).start()

        @pl.when(k != y)
        def _():
            for half, a in pieces:
                send(0, half, a).start()

        for i in range(pieces_w):
            weight_across(i).start()
        weight_share.start()
        weight_own.start()
        slab_own.start()
        gain_send(0).wait_recv()
        sum_g[1] = sum_g[0] + got_g[0]
        gain_send(1).start()

        total = p_ref[2 * x + y].astype(F32)
        for d in range(3):
            scatter(d).wait_recv()
            total += got[d].astype(F32)
        held[z] = total.astype(BF)

        def chain(zb, sem, dev):
            return remote(held.at[zb], held.at[zb], sem, rs_z.at[zb], dev)

        def piece(zb, j):
            return held.at[zb, :, pl.ds(j * lanes, lanes)]

        def goal(zb, j):
            return w_out.at[:, pl.ds(pl.multiple_of(j * width + (2 * zb + k) * lanes, lanes), lanes)]

        def own_column(zb, j):
            return remote(piece(zb, j), goal(zb, j), ss_a.at[zb, j], rs_o.at[2 * zb + k, j], (c, target))

        def own_local(zb, j):
            return pltpu.make_async_copy(piece(zb, j), goal(zb, j), rs_o.at[2 * zb + k, j])

        def next_column(zb, j):
            return remote(piece(zb, j), goal(zb, j), ss_b.at[zb, j], rs_o.at[2 * zb + k, j], (2 * z + 1 - y, target))

        def spread(zb):
            for j in range(3):
                next_column(zb, j).start()

            @pl.when(k == y)
            def _():
                for j in range(3):
                    own_local(zb, j).start()

            @pl.when(k != y)
            def _():
                for j in range(3):
                    own_column(zb, j).start()

        @pl.when(z < depth - 1)
        def _():
            chain(z, ss_up.at[0], up).start()

        @pl.when(z > 0)
        def _():
            chain(z, ss_dn.at[0], down).start()

        spread(z)

        gain_send(1).wait_recv()
        sum_g[2] = sum_g[1] + got_g[1]

        def gain_spread(i):
            return remote(sum_g.at[2], got_gc.at[c], ss_gc.at[i], rs_gc.at[c], ((c + i) % count, f))

        for i in range(1, count):
            gain_spread(i).start()
            slab_spread(i).start()

        def weight_pass(i):
            shard = (f + 2) % 4
            remote(weight_part(shard, i), weight_part(shard, i), ss_wf.at[i], rs_wx.at[i], sib).wait_recv()
            weight_on(i, shard).start()

        for j in range(1, depth):

            @pl.when(z - j >= 0)
            def _(j=j):
                chain(z - j, ss_up.at[j], sib).wait_recv()

                @pl.when(z < depth - 1)
                def _():
                    chain(z - j, ss_up.at[j], up).start()

                spread(z - j)

            @pl.when(z + j <= depth - 1)
            def _(j=j):
                chain(z + j, ss_dn.at[j], sib).wait_recv()

                @pl.when(z > 0)
                def _():
                    chain(z + j, ss_dn.at[j], down).start()

                spread(z + j)

            weight_pass(j - 1)
        for i in range(depth - 1, pieces_w):
            weight_pass(i)

        total_g = sum_g[2]
        for i in range(1, count):
            cs = (c + i) % count
            remote(sum_g.at[2], got_gc.at[cs], ss_gc.at[i], rs_gc.at[cs], sib).wait_recv()
            total_g += got_gc[cs]
        g_out[...] = total_g

        gain_send(0).wait_send()
        gain_send(1).wait_send()
        for i in range(pieces_w):
            weight_across(i).wait_send()
            weight_on(i, (f + 2) % 4).wait_send()
            remote(weight_part(0, i), weight_part(0, i), ss_wf.at[i], rs_wf.at[i], sib).wait_recv()
        weight_share.wait()
        weight_own.wait()
        for d in range(3):
            scatter(d).wait_send()
        for half, a in pieces:
            for other in range(count):
                cols = pl.ds(a * width + other * lanes, lanes)
                remote(ins[a].at[0], tok_out.at[half, :, cols], ss.at[0, half, a], rs.at[other, half, a], sib).wait_recv()
        for i in range(1, count):
            for half, a in pieces:
                send(i, half, a).wait_send()
            gain_spread(i).wait_send()
            slab_spread(i).wait_send()
            cs = (c + i) % count
            remote(o_ref, o_out.at[cs], ss_of.at[i], rs_of.at[cs], sib).wait_recv()
        slab_own.wait()

        @pl.when(k != y)
        def _():
            for half, a in pieces:
                send(0, half, a).wait_send()
            for zb in range(depth):
                for j in range(3):
                    own_column(zb, j).wait_send()

        for other in range(count):
            for j in range(3):
                remote(
                    piece(0, j), w_out.at[:, pl.ds(j * width + other * lanes, lanes)], ss_a.at[0, j], rs_o.at[other, j], sib
                ).wait_recv()
        for j in range(depth):

            @pl.when((z < depth - 1) & (z - j >= 0))
            def _(j=j):
                chain(z - j, ss_up.at[j], up).wait_send()

            @pl.when((z > 0) & (z + j <= depth - 1))
            def _(j=j):
                chain(z + j, ss_dn.at[j], down).wait_send()

        for zb in range(depth):
            for j in range(3):
                next_column(zb, j).wait_send()

    vmem = pl.BlockSpec(memory_space=pltpu.VMEM)
    eighth = gain_part.shape
    return pl.pallas_call(
        kernel,
        name="finish_exchange",
        cost_estimate=lasting(70),
        out_shape=(
            jax.ShapeDtypeStruct((2, arrays[0].shape[1], number * width), BF),
            jax.ShapeDtypeStruct((rows, 3 * width), BF),
            jax.ShapeDtypeStruct((count, slab, width), BF),
            jax.ShapeDtypeStruct(eighth, F32),
            jax.ShapeDtypeStruct((4,) + weight.shape, BF),
        ),
        in_specs=[ANY] * number + [vmem, ANY, vmem, ANY],
        out_specs=(ANY, ANY, ANY, vmem, ANY),
        scratch_shapes=[
            pltpu.VMEM((3, rows, wide), BF),
            pltpu.VMEM((depth, rows, wide), BF),
            pltpu.VMEM((2,) + eighth, F32),
            pltpu.VMEM((3,) + eighth, F32),
            pltpu.VMEM((count,) + eighth, F32),
            DMA((count, 2, number)), DMA((count, 2, number)),
            DMA((3,)), DMA((3,)), DMA((depth,)), DMA((depth,)), DMA((depth,)),
            DMA((depth, 3)), DMA((depth, 3)), DMA((count, 3)),
            DMA((count,)), DMA((count,)), DMA((2,)), DMA((2,)), DMA((count,)), DMA((count,)),
            DMA((pieces_w,)), DMA((pieces_w,)), DMA, DMA, DMA((pieces_w,)), DMA((pieces_w,)), DMA,
        ],
        compiler_params=params(),
    )(*arrays, parts, out_slab, gain_part, weight)


def slots_of(routes):
    tokens = routes.shape[0]
    chosen = routes[:, None] == jnp.arange(EXPERTS, dtype=jnp.int32)[None, :]
    earlier = (jnp.arange(tokens)[:, None] >= jnp.arange(tokens)[None, :]).astype(BF)
    running = jnp.dot(earlier, chosen.astype(BF), preferred_element_type=F32)
    rank = jnp.sum(jnp.where(chosen, running, 0.0), axis=1).astype(jnp.int32) - 1
    slot = routes * CAP + rank
    return (jnp.arange(EXPERTS * CAP, dtype=jnp.int32)[:, None] == slot[None, :]).astype(BF)


def by_head_pairs(
    tokens, doc_starts, expert_ids, query_key_value_weight, output_weight_matrix, expert_in, expert_out, gain_one, gain_two, grad_output
):
    half_rows = tokens.shape[3]
    width = tokens.shape[4]
    count = lax.axis_size("ctx")
    rows = 2 * half_rows
    length = count * rows
    scale = (width // HEADS) ** (-0.5)
    f = lax.axis_index("fsdp")
    lanes = 2 * (width // HEADS)
    shard_rows = width // 4
    pick = (((0,), (0,)), ((), ()))
    turn = (((1,), (1,)), ((), ()))
    start_x = tokens.reshape(rows, width).astype(F32)
    cotangent = grad_output.reshape(rows, width)
    qkv_low = query_key_value_weight.astype(BF)
    first_normed, hat_one, inverse_one = norm_forward(start_x, gain_one)
    normed = first_normed.astype(BF)
    stream, starts, columns = gather_stream(
        normed.reshape(2, half_rows, width), doc_starts.reshape(2, half_rows), qkv_low
    )
    dispatch = slots_of(expert_ids.reshape(rows))
    own_experts = EXPERTS // count
    shape = (count, own_experts, CAP, width)
    send_grads = jnp.dot(dispatch, cotangent, preferred_element_type=F32).astype(BF).reshape(shape)
    grads_near = lax.all_to_all(send_grads, "ctx", split_axis=0, concat_axis=0, tiled=True)
    grads_near = after(grads_near, stream)
    out_own = output_weight_matrix.astype(BF)
    grads_far = swap(grads_near, "fsdp", 2)
    out_far = swap(after(out_own, stream), "fsdp", 2)
    stream = stream.reshape(length, width)
    start_row = jnp.concatenate([starts[:, 0].reshape(-1), starts[::-1, 1].reshape(-1)])[None]
    numbers = jnp.min(start_row.reshape(-1, TILE), axis=1) // TILE
    query, key, value, mixed16, mixed32, logs = attend_forward(stream, columns, start_row, numbers, scale)
    grads_far, out_far = after(grads_far, mixed16), after(out_far, mixed16)
    grads_beside = swap(jnp.stack([grads_near, grads_far]), "fsdp", 1)
    out_beside = swap(jnp.stack([out_own, out_far]), "fsdp", 1)
    out_proj = jnp.concatenate([out_own, out_beside[0], out_far, out_beside[1]], axis=0)
    gain_row = gain_two.reshape(1, width)
    mixed, middle, all_rows = route_rows(
        mixed16.reshape(2 * count, half_rows, lanes), out_proj, tokens.reshape(rows, width), dispatch, gain_row
    )
    mixed = mixed.reshape(rows, width)
    back_terms, back_odd, out_terms, out_odd, active, grad_hidden, all_grads = experts_rows(
        all_rows, grads_near, grads_far, after(grads_beside, all_rows), expert_in, expert_out
    )
    slots = (EXPERTS * CAP, width)
    back_near = swap(back_odd, "fsdp", 1)
    back_send = (back_terms[1].astype(F32) + back_near[1].astype(F32)).astype(BF)
    back_far = swap(back_send, "fsdp", 2)
    grad_in, grad_outw, done = experts_weights(after(all_rows, back_send), all_grads, active, grad_hidden)
    out_near = swap(after(out_odd, back_send), "fsdp", 1)
    out_send = (out_terms[1].astype(F32) + out_near[1].astype(F32) + done[0, 0]).astype(BF)
    out_far_rows = swap(out_send, "fsdp", 2)
    grad_heads, grad_middle, grad_gain_two, out_shard = return_grads(
        back_terms, back_near, back_far, after(done, out_send), dispatch, cotangent, middle, mixed, out_proj, gain_row
    )
    out_far_rows = after(out_far_rows, grad_heads)
    out_sum = (out_terms[0].astype(F32) + out_near[0].astype(F32) + out_far_rows.astype(F32)).astype(BF)
    out_slabs = lax.all_to_all(
        out_shard.reshape(count, shard_rows // count, width), "ctx", split_axis=0, concat_axis=0, tiled=True
    )
    back_rows = lax.all_to_all(out_sum, "ctx", split_axis=0, concat_axis=0, tiled=True)
    grad_q, grad_k, grad_v = attend_backward(
        query, key, value, after(grad_heads, out_sum).reshape(length, lanes), mixed32, logs, start_row, numbers, scale
    )
    out_slabs, back_rows = after(out_slabs, grad_q), after(back_rows, grad_q)
    out_slab = jnp.sum(out_slabs.astype(F32), axis=0).astype(BF)
    blocks = (2 * count, half_rows, lanes)
    own_grads = jnp.concatenate([grad_q, grad_k, grad_v], axis=1)
    parts = lax.dot_general(stream, own_grads, pick, preferred_element_type=F32).astype(BF)
    grad_projected, weight_grad, shard_out, gain_sum, projection = finish_exchange(
        [grad_q.reshape(blocks), grad_k.reshape(blocks), grad_v.reshape(blocks)],
        parts.reshape(4, shard_rows, 3 * lanes),
        out_slab,
        grad_gain_two,
        qkv_low,
    )
    grad_projected = grad_projected.reshape(rows, 3 * width)
    projection = projection.reshape(width, 3 * width)
    back_rows = after(back_rows, weight_grad)
    expert_sum = lax.dot_general(dispatch, back_rows.reshape(slots), pick, preferred_element_type=F32)
    block_out = (middle + expert_sum).astype(BF)
    weight_grad = weight_grad.astype(F32)
    shard_out = shard_out.reshape(shard_rows, width).astype(F32)
    grad_normed = lax.dot_general(grad_projected, projection, turn, preferred_element_type=F32)
    grad_in_norm, _ = norm_backward(grad_normed[None], hat_one[None], inverse_one[None], gain_one)
    grad_start = grad_middle + grad_in_norm[0]
    own_gain = lax.dynamic_slice(gain_one, (f * shard_rows,), (shard_rows,))
    shard_gain_one = jnp.sum(weight_grad * qkv_low.astype(F32), axis=1) / own_gain
    shard_gain_two = lax.dynamic_slice(gain_sum.reshape(width), (f * shard_rows,), (shard_rows,))
    return (
        block_out.reshape(tokens.shape),
        grad_start.reshape(tokens.shape),
        weight_grad,
        shard_out,
        grad_in,
        grad_outw,
        shard_gain_one,
        shard_gain_two,
    )


def solution(mesh):
    pairs = mesh.shape["ctx"] * 2 == HEADS and mesh.shape["fsdp"] == 4
    return jax.shard_map(
        by_head_pairs if pairs else shards,
        mesh=mesh,
        in_specs=(
            P("fsdp", "ctx", None, None, None),
            P("fsdp", "ctx", None, None),
            P("fsdp", "ctx", None, None, None),
            P("fsdp", None),
            P("fsdp", None),
            P("ctx", None, "fsdp"),
            P("ctx", "fsdp", None),
            P(),
            P(),
            P("fsdp", "ctx", None, None, None),
        ),
        out_specs=(
            P("fsdp", "ctx", None, None, None),
            P("fsdp", "ctx", None, None, None),
            P("fsdp", None),
            P("fsdp", None),
            P("ctx", None, "fsdp"),
            P("ctx", "fsdp", None),
            P("fsdp"),
            P("fsdp"),
        ),
        check_vma=False,
    )
```

```python
import math

import jax
import jax.numpy as jnp
from jax import lax
from jax.experimental import pallas as pl
from jax.experimental.pallas import tpu as pltpu
from jax.sharding import PartitionSpec as P

HEADS = 16
EXPERTS = 64
CAP = 8


EPS = 1e-05
NEGATIVE = -1e30


def position_of(row_ids, ctx_count, half_rows):
    device = row_ids // (2 * half_rows)
    upper_half = row_ids // half_rows % 2
    offset = row_ids % half_rows
    return jnp.where(
        upper_half == 0,
        device * half_rows + offset,
        (2 * ctx_count - 1 - device) * half_rows + offset,
    )


def norm_forward(value, gain):
    row_mean = jnp.mean(value, axis=-1, keepdims=True)
    centred = value - row_mean
    inverse = lax.rsqrt(jnp.mean(centred * centred, axis=-1, keepdims=True) + EPS)
    normed = centred * inverse
    return (normed * gain, normed, inverse)


def norm_backward(gradient, normed, inverse, gain):
    scaled = gradient * gain
    mean_grad = jnp.mean(scaled, axis=-1, keepdims=True)
    mean_proj = jnp.mean(scaled * normed, axis=-1, keepdims=True)
    return (
        inverse * (scaled - mean_grad - normed * mean_proj),
        jnp.sum(gradient * normed, axis=(0, 1)),
    )


def scores(query, keys, query_pos, key_pos, query_start, score_scale):
    raw_scores = (
        jnp.einsum("qshe,kshe->shqk", query, keys, preferred_element_type=jnp.float32) * score_scale
    )
    visible = (key_pos[None, None, None, :] <= query_pos[None, None, :, None]) & (
        key_pos[None, None, None, :] >= query_start.T[:, None, :, None]
    )
    return jnp.where(visible, raw_scores, NEGATIVE)


def log_totals(query, keys, query_pos, query_start, score_scale, ctx_count, half_rows, key_block):
    block_count = keys.shape[0] // key_block
    carry_shape = (query.shape[1], query.shape[2], query.shape[0])

    def log_one_block(block_index, carried):
        running_max, running = carried
        first_row = block_index * key_block
        key_piece = lax.dynamic_slice_in_dim(keys, first_row, key_block, 0)
        key_pos = position_of(
            first_row + jnp.arange(key_block, dtype=jnp.int32), ctx_count, half_rows
        )
        score_rows = scores(query, key_piece, query_pos, key_pos, query_start, score_scale)
        new_max = jnp.maximum(running_max, jnp.max(score_rows, axis=-1))
        running = running * jnp.exp(running_max - new_max) + jnp.sum(
            jnp.exp(score_rows - new_max[..., None]), axis=-1
        )
        return (new_max, running)

    running_max, running = lax.fori_loop(
        0,
        block_count,
        log_one_block,
        (jnp.full(carry_shape, NEGATIVE, jnp.float32), jnp.zeros(carry_shape, jnp.float32)),
    )
    return running_max + jnp.log(running)


def attend(
    query,
    keys,
    values,
    query_pos,
    query_start,
    log_total,
    score_scale,
    ctx_count,
    half_rows,
    key_block,
):
    block_count = keys.shape[0] // key_block
    zeros_init = jnp.zeros(query.shape, jnp.float32)

    def attend_one_block(block_index, carried):
        output, remainder = carried
        first_row = block_index * key_block
        key_piece = lax.dynamic_slice_in_dim(keys, first_row, key_block, 0)
        value_piece = lax.dynamic_slice_in_dim(values, first_row, key_block, 0)
        key_pos = position_of(
            first_row + jnp.arange(key_block, dtype=jnp.int32), ctx_count, half_rows
        )
        weights = jnp.exp(
            scores(query, key_piece, query_pos, key_pos, query_start, score_scale)
            - log_total[..., None]
        )
        rounded = weights.astype(jnp.bfloat16)
        leftover = (weights - rounded.astype(jnp.float32)).astype(jnp.bfloat16)
        output = output + jnp.einsum(
            "shqk,kshe->qshe", rounded, value_piece, preferred_element_type=jnp.float32
        )
        remainder = remainder + jnp.einsum(
            "shqk,kshe->qshe", leftover, value_piece, preferred_element_type=jnp.float32
        )
        return (output, remainder)

    return lax.fori_loop(0, block_count, attend_one_block, (zeros_init, zeros_init))


def query_grads(
    query,
    keys,
    values,
    grad_heads,
    query_pos,
    query_start,
    log_total,
    row_delta,
    score_scale,
    ctx_count,
    half_rows,
    key_block,
):
    block_count = keys.shape[0] // key_block

    def query_one_block(block_index, running):
        first_row = block_index * key_block
        key_piece = lax.dynamic_slice_in_dim(keys, first_row, key_block, 0)
        value_piece = lax.dynamic_slice_in_dim(values, first_row, key_block, 0)
        key_pos = position_of(
            first_row + jnp.arange(key_block, dtype=jnp.int32), ctx_count, half_rows
        )
        weights = jnp.exp(
            scores(query, key_piece, query_pos, key_pos, query_start, score_scale)
            - log_total[..., None]
        )
        grad_weight = jnp.einsum(
            "qshe,kshe->shqk", grad_heads, value_piece, preferred_element_type=jnp.float32
        )
        grad_score = (weights * (grad_weight - row_delta[..., None])).astype(jnp.bfloat16)
        return running + jnp.einsum(
            "shqk,kshe->qshe", grad_score, key_piece, preferred_element_type=jnp.float32
        )

    return (
        lax.fori_loop(0, block_count, query_one_block, jnp.zeros(query.shape, jnp.float32))
        * score_scale
    )


def key_grads(
    query,
    grad_heads,
    query_pos,
    query_start,
    log_total,
    row_delta,
    key_piece,
    value_piece,
    key_pos,
    score_scale,
):
    weights = jnp.exp(
        scores(query, key_piece, query_pos, key_pos, query_start, score_scale)
        - log_total[..., None]
    )
    grad_weight = jnp.einsum(
        "qshe,kshe->shqk", grad_heads, value_piece, preferred_element_type=jnp.float32
    )
    grad_score = (weights * (grad_weight - row_delta[..., None])).astype(jnp.bfloat16)
    key_part = (
        jnp.einsum("shqk,qshe->kshe", grad_score, query, preferred_element_type=jnp.float32)
        * score_scale
    )
    value_part = jnp.einsum(
        "shqk,qshe->kshe",
        weights.astype(jnp.bfloat16),
        grad_heads,
        preferred_element_type=jnp.float32,
    )
    return (key_part, value_part)


def shards(
    tokens,
    doc_starts,
    expert_ids,
    query_key_value_weight,
    output_weight_matrix,
    expert_in,
    expert_out,
    gain_one,
    gain_two,
    grad_output,
):
    seq_dev = tokens.shape[0]
    half_rows = tokens.shape[3]
    model_width = tokens.shape[4]
    local_rows = 2 * half_rows
    ctx_count = lax.axis_size("ctx")
    head_count = HEADS
    head_size = model_width // head_count
    score_scale = head_size ** (-0.5)
    keys_total = ctx_count * local_rows
    key_block = min(512, keys_total)
    own_rows = lax.axis_index("ctx") * local_rows + jnp.arange(local_rows, dtype=jnp.int32)
    query_pos = position_of(own_rows, ctx_count, half_rows)
    query_start = doc_starts.reshape(seq_dev, local_rows).T
    routes_local = expert_ids.reshape(seq_dev, local_rows).T
    start_x = (
        tokens.reshape(seq_dev, local_rows, model_width).transpose(1, 0, 2).astype(jnp.float32)
    )
    cotangent = grad_output.reshape(seq_dev, local_rows, model_width).transpose(1, 0, 2)
    projection, out_proj = (
        lax.all_gather(query_key_value_weight.astype(jnp.bfloat16), "fsdp", axis=0, tiled=True),
        lax.all_gather(output_weight_matrix.astype(jnp.bfloat16), "fsdp", axis=0, tiled=True),
    )
    first_normed_rows, hat_one, inverse_one = norm_forward(start_x, gain_one)
    normed_low = first_normed_rows.astype(jnp.bfloat16)
    projected_rows = jnp.einsum(
        "tsd,de->tse", normed_low, projection, preferred_element_type=jnp.float32
    ).astype(jnp.bfloat16)
    query = projected_rows[..., :model_width]
    keys = projected_rows[..., model_width : 2 * model_width]
    values = projected_rows[..., 2 * model_width :]
    key_all, value_all = (
        lax.all_gather(keys, "ctx", axis=0, tiled=True),
        lax.all_gather(values, "ctx", axis=0, tiled=True),
    )
    query_heads = query.reshape(local_rows, seq_dev, head_count, head_size)
    key_heads = key_all.reshape(keys_total, seq_dev, head_count, head_size)
    value_heads = value_all.reshape(keys_total, seq_dev, head_count, head_size)
    log_total = log_totals(
        query_heads, key_heads, query_pos, query_start, score_scale, ctx_count, half_rows, key_block
    )
    mixed_heads_out, remainder = attend(
        query_heads,
        key_heads,
        value_heads,
        query_pos,
        query_start,
        log_total,
        score_scale,
        ctx_count,
        half_rows,
        key_block,
    )
    mixed_low = mixed_heads_out.astype(jnp.bfloat16).reshape(local_rows, seq_dev, model_width)
    attention_rows_out = jnp.einsum(
        "tsd,de->tse", mixed_low, out_proj, preferred_element_type=jnp.float32
    )
    middle = start_x + attention_rows_out
    normed_two, hat_two, inverse_two = norm_forward(middle, gain_two)
    routed = normed_two.astype(jnp.bfloat16)
    slot_count = EXPERTS * CAP
    per_owner = EXPERTS // ctx_count
    chosen = (routes_local[..., None] == jnp.arange(EXPERTS, dtype=jnp.int32)).astype(jnp.int32)
    earlier = (
        jnp.arange(local_rows)[:, None] >= jnp.arange(local_rows)[None, :]
    ).astype(jnp.bfloat16)
    running = jnp.einsum(
        "tu,use->tse", earlier, chosen.astype(jnp.bfloat16), preferred_element_type=jnp.float32
    )
    rank_within = jnp.sum(chosen * running.astype(jnp.int32), axis=-1) - 1
    slot_index = routes_local * CAP + rank_within
    dispatch = (
        slot_index.T[:, None, :] == jnp.arange(slot_count, dtype=jnp.int32)[None, :, None]
    ).astype(jnp.bfloat16)
    dispatch = dispatch.reshape(seq_dev, ctx_count, per_owner, CAP, local_rows)
    send_rows = jnp.einsum(
        "snect,tsd->nescd", dispatch, routed, preferred_element_type=jnp.float32
    ).astype(jnp.bfloat16)
    send_grads = jnp.einsum(
        "snect,tsd->nescd", dispatch, cotangent, preferred_element_type=jnp.float32
    ).astype(jnp.bfloat16)
    got_rows, got_grads = (
        lax.all_to_all(send_rows, "ctx", split_axis=0, concat_axis=0, tiled=True),
        lax.all_to_all(send_grads, "ctx", split_axis=0, concat_axis=0, tiled=True),
    )
    in_low = expert_in.astype(jnp.bfloat16)
    out_low = expert_out.astype(jnp.bfloat16)
    all_rows, all_grads = (
        lax.all_gather(got_rows, "fsdp", axis=2, tiled=True),
        lax.all_gather(got_grads, "fsdp", axis=2, tiled=True),
    )
    hidden = jnp.einsum("nercd,edf->nercf", all_rows, in_low, preferred_element_type=jnp.float32)
    active = jax.nn.gelu(hidden).astype(jnp.bfloat16)
    partial_rows = jnp.einsum(
        "nercf,efd->nercd", active, out_low, preferred_element_type=jnp.float32
    )
    result = lax.psum_scatter(
        partial_rows.astype(jnp.bfloat16), "fsdp", scatter_dimension=2, tiled=True
    )
    upstream = jnp.einsum(
        "nercd,efd->nercf", all_grads, out_low, preferred_element_type=jnp.float32
    )
    unused, gelu_back = jax.vjp(jax.nn.gelu, hidden)
    grad_hidden = gelu_back(upstream)[0].astype(jnp.bfloat16)
    grad_in = jnp.einsum(
        "nercd,nercf->edf", all_rows, grad_hidden, preferred_element_type=jnp.float32
    )
    grad_outw = jnp.einsum(
        "nercf,nercd->efd", active, all_grads, preferred_element_type=jnp.float32
    )
    row_part = jnp.einsum(
        "nercf,edf->nercd", grad_hidden, in_low, preferred_element_type=jnp.float32
    )
    row_grad = lax.psum_scatter(row_part, "fsdp", scatter_dimension=2, tiled=True).astype(
        jnp.bfloat16
    )
    back_rows = lax.all_to_all(result, "ctx", split_axis=0, concat_axis=0, tiled=True)
    expert_sum = jnp.einsum(
        "snect,nescd->tsd", dispatch, back_rows, preferred_element_type=jnp.float32
    )
    output_rows = middle + expert_sum
    returned = lax.all_to_all(row_grad, "ctx", split_axis=0, concat_axis=0, tiled=True)
    grad_routed = jnp.einsum(
        "snect,nescd->tsd", dispatch, returned, preferred_element_type=jnp.float32
    )
    grad_mid_norm, grad_gain_two = norm_backward(grad_routed, hat_two, inverse_two, gain_two)
    grad_middle = cotangent.astype(jnp.float32) + grad_mid_norm
    grad_attn = grad_middle.astype(jnp.bfloat16)
    grad_outproj = jnp.einsum(
        "tsd,tse->de", mixed_low, grad_attn, preferred_element_type=jnp.float32
    )
    grad_mixed = jnp.einsum(
        "tse,de->tsd", grad_attn, out_proj, preferred_element_type=jnp.float32
    ).astype(jnp.bfloat16)
    grad_heads = grad_mixed.reshape(local_rows, seq_dev, head_count, head_size)
    full_mixed = mixed_heads_out + remainder
    row_delta = jnp.sum(grad_heads.astype(jnp.float32) * full_mixed, axis=-1).transpose(1, 2, 0)
    grad_query = query_grads(
        query_heads,
        key_heads,
        value_heads,
        grad_heads,
        query_pos,
        query_start,
        log_total,
        row_delta,
        score_scale,
        ctx_count,
        half_rows,
        key_block,
    ).astype(jnp.bfloat16)
    sub_rows = math.gcd(local_rows * lax.axis_size("ctx"), key_block)

    def one_piece(piece_index):
        piece_start = piece_index * sub_rows
        key_piece = lax.dynamic_slice_in_dim(key_heads, piece_start, sub_rows, 0)
        value_piece = lax.dynamic_slice_in_dim(value_heads, piece_start, sub_rows, 0)
        key_pos = position_of(
            piece_start + jnp.arange(sub_rows, dtype=jnp.int32), ctx_count, half_rows
        )
        key_part, value_part = key_grads(
            query_heads,
            grad_heads,
            query_pos,
            query_start,
            log_total,
            row_delta,
            key_piece,
            value_piece,
            key_pos,
            score_scale,
        )
        return jnp.concatenate(
            [
                key_part.reshape(sub_rows, seq_dev, model_width),
                value_part.reshape(sub_rows, seq_dev, model_width),
            ],
            axis=-1,
        )

    summed = lax.psum_scatter(
        lax.map(
            one_piece, jnp.arange(local_rows * lax.axis_size("ctx") // sub_rows, dtype=jnp.int32)
        ).reshape(local_rows * lax.axis_size("ctx"), seq_dev, 2 * model_width),
        "ctx",
        scatter_dimension=0,
        tiled=True,
    )
    grad_key = summed[..., :model_width].astype(jnp.bfloat16)
    grad_value = summed[..., model_width:].astype(jnp.bfloat16)
    grad_projected = jnp.concatenate(
        [grad_query.reshape(local_rows, seq_dev, model_width), grad_key, grad_value], axis=-1
    )
    grad_projection = jnp.einsum(
        "tsd,tse->de", normed_low, grad_projected, preferred_element_type=jnp.float32
    )
    grad_normed = jnp.einsum(
        "tse,de->tsd", grad_projected, projection, preferred_element_type=jnp.float32
    )
    grad_in_norm, grad_gain_one = norm_backward(grad_normed, hat_one, inverse_one, gain_one)
    grad_start = grad_middle + grad_in_norm
    shard_proj, shard_outproj, shard_gain_one, shard_gain_two = (
        lax.psum_scatter(
            grad_projection.astype(jnp.bfloat16), "fsdp", scatter_dimension=0, tiled=True
        ).astype(jnp.float32),
        lax.psum_scatter(
            grad_outproj.astype(jnp.bfloat16), "fsdp", scatter_dimension=0, tiled=True
        ).astype(jnp.float32),
        lax.psum_scatter(
            grad_gain_one.astype(jnp.bfloat16), "fsdp", scatter_dimension=0, tiled=True
        ).astype(jnp.float32),
        lax.psum_scatter(
            grad_gain_two.astype(jnp.bfloat16), "fsdp", scatter_dimension=0, tiled=True
        ).astype(jnp.float32),
    )
    shard_proj, shard_outproj, shard_gain_one, shard_gain_two = (
        lax.psum(shard_proj.astype(jnp.bfloat16), "ctx").astype(jnp.float32),
        lax.psum(shard_outproj.astype(jnp.bfloat16), "ctx").astype(jnp.float32),
        lax.psum(shard_gain_one.astype(jnp.bfloat16), "ctx").astype(jnp.float32),
        lax.psum(shard_gain_two.astype(jnp.bfloat16), "ctx").astype(jnp.float32),
    )
    block_out = output_rows.transpose(1, 0, 2).reshape(tokens.shape).astype(jnp.bfloat16)
    grad_tokens = grad_start.transpose(1, 0, 2).reshape(tokens.shape)
    return (
        block_out,
        grad_tokens,
        shard_proj,
        shard_outproj,
        grad_in,
        grad_outw,
        shard_gain_one,
        shard_gain_two,
    )


BF = jnp.bfloat16
F32 = jnp.float32
MESH_ID = pl.DeviceIdType.MESH
ANY = pl.BlockSpec(memory_space=pl.ANY)
DMA = pltpu.SemaphoreType.DMA
VMEM_CAP = 56 << 20


def place():
    c = lax.axis_index("ctx")
    f = lax.axis_index("fsdp")
    return c, f, c // 2, c % 2, f // 2, f % 2


def remote(src, dst, send, recv, device):
    return pltpu.make_async_remote_copy(
        src_ref=src, dst_ref=dst, send_sem=send, recv_sem=recv, device_id=device, device_id_type=MESH_ID
    )


def block_at(c, half, count):
    return c if half == 0 else 2 * count - 1 - c


def relative(a, b):
    return (a // 2 + b // 2) % 2 * 2 + (a + b) % 2


def swap(value, axis, bit):
    size = lax.axis_size(axis)
    return lax.ppermute(value, axis, [(i, i ^ bit) for i in range(size)])


def lasting(microseconds):
    return pl.CostEstimate(flops=0, bytes_accessed=int(microseconds * 3.3e6), transcendentals=0)


def params(side=True):
    return pltpu.CompilerParams(has_side_effects=side, vmem_limit_bytes=VMEM_CAP)


def gather_stream(normed, starts, weight):
    count = lax.axis_size("ctx")
    depth = count // 2
    rows, wide = weight.shape
    lanes = wide // 3 // count

    def kernel(n_ref, s_ref, w_ref, tok, st, cols, rs_t, ss_p, ss_up, ss_dn, ss_sib, rs_s, ss_s, rs_w, ss_w):
        c, f, z, y, x, k = place()
        sib = (c, f + 1 - 2 * k)
        partner = (c + 1 - 2 * y, f + 1 - 2 * k)
        up = (c + 2, f)
        down = (c - 2, f)
        holder = k == y

        def send_in(h):
            b = block_at(c, h, count)
            return remote(n_ref.at[h], tok.at[b], ss_p.at[h], rs_t.at[b], partner)

        def local_in(h):
            b = block_at(c, h, count)
            return pltpu.make_async_copy(n_ref.at[h], tok.at[b], rs_t.at[b])

        @pl.when(holder)
        def _():
            for h in range(2):
                local_in(h).start()

        @pl.when(jnp.logical_not(holder))
        def _():
            for h in range(2):
                send_in(h).start()

        for zt in range(depth):
            for kt in range(2):
                mine = holder & (z == zt) & (k == kt)

                @pl.when(mine)
                def _():
                    pltpu.make_async_copy(s_ref, st.at[c], rs_s.at[c]).start()

                @pl.when(jnp.logical_not(mine))
                def _(zt=zt, kt=kt):
                    remote(s_ref, st.at[c], ss_s.at[2 * zt + kt], rs_s.at[c], (2 * zt + k, 2 * x + kt)).start()

        goals = [(2 * z + k, (c, (f + 2) % 4)), (2 * z + 1 - k, (c, (sib[1] + 2) % 4)), (2 * z + 1 - k, sib)]

        def columns(pair, j):
            return w_ref.at[:, pl.ds(pl.multiple_of(j * count * lanes + pair * lanes, lanes), lanes)]

        def weight_place(shard, j):
            return cols.at[j, pl.ds(pl.multiple_of(shard * rows, rows), rows)]

        def weight_send(t, j):
            pair, dev = goals[t]
            return remote(columns(pair, j), weight_place(f, j), ss_w.at[t, j], rs_w.at[f, j], dev)

        for j in range(3):
            for t in range(3):
                weight_send(t, j).start()
            pltpu.make_async_copy(columns(2 * z + k, j), weight_place(f, j), rs_w.at[f, j]).start()

        def copy_block(zb, h, ss, dev):
            b = block_at(2 * zb + k, h, count)
            return remote(tok.at[b], tok.at[b], ss, rs_t.at[b], dev)

        for j in range(depth):
            for h in range(2):
                if j == 0:
                    copy_block(z, h, ss_p.at[h], sib).wait_recv()

                    @pl.when(z < depth - 1)
                    def _(h=h):
                        copy_block(z, h, ss_up.at[0, h], up).start()

                    @pl.when(z > 0)
                    def _(h=h):
                        copy_block(z, h, ss_dn.at[0, h], down).start()

                    copy_block(z, h, ss_sib.at[z, h], sib).start()
                    continue

                @pl.when(z - j >= 0)
                def _(j=j, h=h):
                    copy_block(z - j, h, ss_p.at[h], sib).wait_recv()

                    @pl.when(z < depth - 1)
                    def _():
                        copy_block(z - j, h, ss_up.at[j, h], up).start()

                    copy_block(z - j, h, ss_sib.at[z - j, h], sib).start()

                @pl.when(z + j <= depth - 1)
                def _(j=j, h=h):
                    copy_block(z + j, h, ss_p.at[h], sib).wait_recv()

                    @pl.when(z > 0)
                    def _():
                        copy_block(z + j, h, ss_dn.at[j, h], down).start()

                    copy_block(z + j, h, ss_sib.at[z + j, h], sib).start()

        for zt in range(depth):
            for h in range(2):
                b = block_at(2 * zt + 1 - k, h, count)
                remote(tok.at[b], tok.at[b], ss_p.at[h], rs_t.at[b], sib).wait_recv()
                copy_block(zt, h, ss_sib.at[zt, h], sib).wait_send()
        for ct in range(count):
            remote(s_ref, st.at[ct], ss_s.at[0], rs_s.at[ct], sib).wait_recv()
        for j in range(3):
            for shard in range(4):
                remote(columns(0, j), weight_place(shard, j), ss_w.at[0, j], rs_w.at[shard, j], sib).wait_recv()
            for t in range(3):
                weight_send(t, j).wait_send()

        @pl.when(jnp.logical_not(holder))
        def _():
            for h in range(2):
                send_in(h).wait_send()

        for j in range(depth):

            @pl.when((z < depth - 1) & (z - j >= 0))
            def _(j=j):
                for h in range(2):
                    copy_block(z - j, h, ss_up.at[j, h], up).wait_send()

            @pl.when((z > 0) & (z + j <= depth - 1))
            def _(j=j):
                for h in range(2):
                    copy_block(z + j, h, ss_dn.at[j, h], down).wait_send()

        for zt in range(depth):
            for kt in range(2):
                mine = holder & (z == zt) & (k == kt)

                @pl.when(jnp.logical_not(mine))
                def _(zt=zt, kt=kt):
                    remote(s_ref, st.at[c], ss_s.at[2 * zt + kt], rs_s.at[c], sib).wait_send()

    return pl.pallas_call(
        kernel,
        name="gather_stream",
        cost_estimate=lasting(50),
        out_shape=(
            jax.ShapeDtypeStruct((2 * count,) + normed.shape[1:], normed.dtype),
            jax.ShapeDtypeStruct((count,) + starts.shape, starts.dtype),
            jax.ShapeDtypeStruct((3, 4 * rows, lanes), weight.dtype),
        ),
        in_specs=[ANY] * 3,
        out_specs=(ANY,) * 3,
        scratch_shapes=[
            DMA((2 * count,)), DMA((2,)), DMA((depth, 2)), DMA((depth, 2)), DMA((depth, 2)),
            DMA((count,)), DMA((count,)), DMA((4, 3)), DMA((3, 3)),
        ],
        compiler_params=params(),
    )(normed, starts, weight)


TILE = 256


def halves(value, axis):
    size = value.shape[axis] // 2
    at = lax.broadcasted_iota(jnp.int32, value.shape, axis)
    zero = jnp.zeros_like(value)
    return [jnp.where(at < size, value, zero), jnp.where(at >= size, value, zero)]


def attend_forward(stream, columns, start_row, numbers, scale):
    length, width = stream.shape
    tiles = length // TILE
    lanes = 128
    size = lanes // 2

    def kernel(first, x_ref, w_ref, s_ref, q_out, k_out, v_out, m16, m32, lse, v_turned):
        i = pl.program_id(0)
        own = pl.ds(pl.multiple_of(i * TILE, TILE), TILE)
        rows = x_ref[...]
        query, key, value = [jnp.dot(rows, w_ref[j], preferred_element_type=F32).astype(BF) for j in range(3)]
        q_out[...] = query
        k_out[own, :] = key
        v_out[...] = value
        v_turned[:, own] = value.T
        queries = halves((query * scale).T, 0)
        start = s_ref[...]
        key_row = lax.broadcasted_iota(jnp.int32, (TILE, TILE), 0)
        query_column = i * TILE + lax.broadcasted_iota(jnp.int32, (TILE, TILE), 1)

        def step(j, carried):
            at = pl.multiple_of(j * TILE, TILE)
            keys = k_out[pl.ds(at, TILE), :]
            seen = (key_row + at <= query_column) & (key_row + at >= start)
            out = []
            for h in range(2):
                top, total, mixed = carried[h]
                score = jnp.where(seen, jnp.dot(keys, queries[h], preferred_element_type=F32), NEGATIVE)
                new_top = jnp.maximum(top, jnp.max(score, axis=0, keepdims=True))
                weight = jnp.exp(score - new_top)
                shrink = jnp.exp(top - new_top)
                total = total * shrink + jnp.sum(weight, axis=0, keepdims=True)
                values = v_turned[h * size : (h + 1) * size, pl.ds(at, TILE)]
                mixed = mixed * shrink + jnp.dot(values, weight.astype(BF), preferred_element_type=F32)
                out.append((new_top, total, mixed))
            return tuple(out)

        begin = (
            jnp.full((1, TILE), NEGATIVE, F32),
            jnp.zeros((1, TILE), F32),
            jnp.zeros((size, TILE), F32),
        )
        done = lax.fori_loop(first[i], i + 1, step, (begin, begin))
        mixed = jnp.concatenate([part / total for _, total, part in done], axis=0)
        m32[...] = mixed
        m16[...] = mixed.T.astype(BF)
        lse[...] = jnp.concatenate([top + jnp.log(total) for top, total, _ in done], axis=0)

    tile = pl.BlockSpec((TILE, lanes), lambda i, n: (i, 0))
    turned = pl.BlockSpec((lanes, TILE), lambda i, n: (0, i))
    return pl.pallas_call(
        kernel,
        name="attend_forward",
        cost_estimate=lasting(22),
        grid_spec=pltpu.PrefetchScalarGridSpec(
            num_scalar_prefetch=1,
            grid=(tiles,),
            in_specs=[
                pl.BlockSpec((TILE, width), lambda i, n: (i, 0)),
                pl.BlockSpec((3, width, lanes), lambda i, n: (0, 0, 0)),
                pl.BlockSpec((1, TILE), lambda i, n: (0, i)),
            ],
            out_specs=[
                tile,
                pl.BlockSpec((length, lanes), lambda i, n: (0, 0)),
                tile,
                tile,
                turned,
                pl.BlockSpec((2, TILE), lambda i, n: (0, i)),
            ],
            scratch_shapes=[pltpu.VMEM((lanes, length), BF)],
        ),
        out_shape=(
            jax.ShapeDtypeStruct((length, lanes), BF),
            jax.ShapeDtypeStruct((length, lanes), BF),
            jax.ShapeDtypeStruct((length, lanes), BF),
            jax.ShapeDtypeStruct((length, lanes), BF),
            jax.ShapeDtypeStruct((lanes, length), F32),
            jax.ShapeDtypeStruct((2, length), F32),
        ),
        compiler_params=params(False),
    )(numbers, stream, columns, start_row)


def attend_backward(query, key, value, grad, mixed, logs, start_row, numbers, scale):
    length, lanes = query.shape
    tiles = length // TILE
    size = lanes // 2

    def kernel(first, q_ref, k_ref, v_ref, g_ref, m_ref, l_ref, s_ref, dq, dk, dv, acc_k, acc_v, k_turned):
        i = pl.program_id(0)

        @pl.when(i == 0)
        def _():
            acc_k[...] = jnp.zeros_like(acc_k)
            acc_v[...] = jnp.zeros_like(acc_v)
            for t in range(tiles):
                k_turned[:, t * TILE : (t + 1) * TILE] = k_ref[t * TILE : (t + 1) * TILE, :].T

        scaled = q_ref[...] * scale
        grads = g_ref[...]
        turned = grads.T
        queries, queries_turned = halves(scaled, 1), halves(scaled.T, 0)
        grad_rows, grads_turned = halves(grads, 1), halves(turned, 0)
        product = turned.astype(F32) * m_ref[...]
        deltas = [jnp.sum(product[h * size : (h + 1) * size], axis=0, keepdims=True) for h in range(2)]
        logs_row = [l_ref[h : h + 1, :] for h in range(2)]
        start = s_ref[...]
        key_row = lax.broadcasted_iota(jnp.int32, (TILE, TILE), 0)
        query_column = i * TILE + lax.broadcasted_iota(jnp.int32, (TILE, TILE), 1)

        def step(j, running):
            at = pl.multiple_of(j * TILE, TILE)
            keys = k_ref[pl.ds(at, TILE), :]
            values = v_ref[pl.ds(at, TILE), :]
            seen = (key_row + at <= query_column) & (key_row + at >= start)
            key_sum = jnp.zeros((TILE, lanes), F32)
            value_sum = jnp.zeros((TILE, lanes), F32)
            out = []
            for h in range(2):
                score = jnp.dot(keys, queries_turned[h], preferred_element_type=F32)
                weight = jnp.exp(jnp.where(seen, score - logs_row[h], NEGATIVE))
                grad_weight = jnp.dot(values, grads_turned[h], preferred_element_type=F32)
                grad_score = (weight * (grad_weight - deltas[h])).astype(BF)
                value_sum += jnp.dot(weight.astype(BF), grad_rows[h], preferred_element_type=F32)
                key_sum += jnp.dot(grad_score, queries[h], preferred_element_type=F32)
                part = k_turned[h * size : (h + 1) * size, pl.ds(at, TILE)]
                out.append(running[h] + jnp.dot(part, grad_score, preferred_element_type=F32))
            acc_k[pl.ds(at, TILE), :] += key_sum
            acc_v[pl.ds(at, TILE), :] += value_sum
            return tuple(out)

        zero = jnp.zeros((size, TILE), F32)
        total = lax.fori_loop(first[i], i + 1, step, (zero, zero))
        dq[...] = (jnp.concatenate(total, axis=0) * scale).T.astype(BF)

        @pl.when(i == tiles - 1)
        def _():
            dk[...] = acc_k[...].astype(BF)
            dv[...] = acc_v[...].astype(BF)

    tile = pl.BlockSpec((TILE, lanes), lambda i, n: (i, 0))
    full = pl.BlockSpec((length, lanes), lambda i, n: (0, 0))
    return pl.pallas_call(
        kernel,
        name="attend_backward",
        cost_estimate=lasting(19),
        grid_spec=pltpu.PrefetchScalarGridSpec(
            num_scalar_prefetch=1,
            grid=(tiles,),
            in_specs=[
                tile,
                full,
                full,
                tile,
                pl.BlockSpec((lanes, TILE), lambda i, n: (0, i)),
                pl.BlockSpec((2, TILE), lambda i, n: (0, i)),
                pl.BlockSpec((1, TILE), lambda i, n: (0, i)),
            ],
            out_specs=[tile, full, full],
            scratch_shapes=[
                pltpu.VMEM((length, lanes), F32),
                pltpu.VMEM((length, lanes), F32),
                pltpu.VMEM((lanes, length), BF),
            ],
        ),
        out_shape=(jax.ShapeDtypeStruct((length, lanes), BF),) * 3,
        compiler_params=params(False),
    )(numbers, query, key, value, grad, mixed, logs, start_row)


ROOT = math.sqrt(2.0 / math.pi)
CUBIC = 0.044715
CONTRACT_FIRST = (((0,), (0,)), ((), ()))
CONTRACT_LAST = (((1,), (1,)), ((), ()))


def statistics(value):
    row_mean = jnp.mean(value, axis=1, keepdims=True)
    centred = value - row_mean
    inverse = lax.rsqrt(jnp.mean(centred * centred, axis=1, keepdims=True) + EPS)
    return centred * inverse, inverse


def stacked(value):
    return value.reshape(-1, value.shape[-1])


def experts_exchange(by_head, out_proj, tokens, dispatch, gain, cotangent, grads, first_proj, second_proj):
    count = lax.axis_size("ctx")
    half_rows, lanes = by_head.shape[1:]
    rows, width = tokens.shape
    number, _, units = first_proj.shape
    cap = CAP
    total_rows = 4 * count * cap
    quarter = width // 4
    splits = 2
    part_units = units // splits

    def kernel(
        a_ref, w0_ref, w1_ref, w2_ref, w3_ref, x_ref, d_ref, g_ref, c_ref, g0_ref, g1_ref, g2_ref, g3_ref, first_ref, second_ref,
        mixed, middle, rows_out, active_out, hidden_out, own_out, far_out, heads, grad_middle, gain_out, shard,
        routed, slots, rows_v, g_buf, first_buf, second_buf, active_v, hidden_v, back_v, back_near, back_far, back_got,
        out_v, out_near, own_v, far_v, summed, home_got, back, shard_near, shard_far, shard_got,
        ss_m, rs_m, ss_1, rs_1, ss_x, rs_x, ss_s, rs_s, ss_f, rs_f, ss_bn, rs_bn, ss_bf, rs_bf, ss_on, rs_on, ss_h, rs_h,
        ss_t, rs_t, ss_n, rs_n, ss_w, rs_w, l_first, l_second, l_g, st_r, st_a, st_h, st_o, st_f,
    ):
        c, f, z, y, x, k = place()
        sib = (c, f + 1 - 2 * k)
        xn = (c, (f + 2) % 4)
        pair = 2 * z + k
        target = 2 * x + y

        def load_first(e, u):
            cols = pl.ds(u * part_units, part_units)
            return pltpu.make_async_copy(first_ref.at[e, :, cols], first_buf.at[u], l_first.at[u])

        def load_second(e, u):
            part = pl.ds(u * part_units, part_units)
            return pltpu.make_async_copy(second_ref.at[e, part], second_buf.at[u], l_second.at[u])

        def load_grads(e, slot):
            refs = (g0_ref, g1_ref, g2_ref, g3_ref)
            return [pltpu.make_async_copy(ref.at[:, e], g_buf.at[slot, j], l_g.at[slot, j]) for j, ref in enumerate(refs)]

        def there(half):
            column = (2 * relative(z, target) + k) * lanes
            return mixed.at[half, :, pl.ds(pl.multiple_of(column, lanes), lanes)]

        def send(i, half):
            ct = (c + i) % count
            return remote(
                a_ref.at[block_at(ct, half, count)], there(half), ss_m.at[i, half], rs_m.at[pair, half], (ct, target)
            )

        def keep(half):
            return pltpu.make_async_copy(a_ref.at[block_at(c, half, count)], there(half), rs_m.at[pair, half])

        for half in range(2):
            for i in range(1, count):
                send(i, half).start()

            @pl.when(k == y)
            def _(half=half):
                keep(half).start()

            @pl.when(k != y)
            def _(half=half):
                send(0, half).start()

        for u in range(splits):
            load_first(0, u).start()
            load_second(0, u).start()
        for load in load_grads(0, 0):
            load.start()

        for half in range(2):
            for other in range(count):
                column = (2 * relative(other // 2, f) + other % 2) * lanes
                cols = pl.ds(pl.multiple_of(column, lanes), lanes)
                remote(a_ref.at[0], mixed.at[half, :, cols], ss_m.at[0, half], rs_m.at[other, half], sib).wait_recv()
            here = pl.ds(half * half_rows, half_rows)
            value = x_ref[here, :].astype(F32)
            for j, w_ref in enumerate((w0_ref, w1_ref, w2_ref, w3_ref)):
                cols = pl.ds(j * quarter, quarter)
                value += jnp.dot(mixed[half, :, cols], w_ref[...], preferred_element_type=F32)
            middle[here, :] = value
            hat, _ = statistics(value)
            routed[here, :] = (hat * g_ref[...]).astype(BF)
        slots[...] = jnp.dot(d_ref[...], routed[...], preferred_element_type=F32).astype(BF).reshape(slots.shape)

        def rows_first(e, i):
            owner = (c + i) % count
            return remote(slots.at[owner, e], rows_v.at[0, e, c], ss_1.at[e], rs_1.at[e], (owner, f))

        def hop(e, rel, dst, send_sem, recv_sem, dev):
            return remote(rows_v.at[rel, e], rows_v.at[dst, e], send_sem.at[e], recv_sem.at[e], dev)

        def rows_across(e):
            return hop(e, 0, 2, ss_x, rs_x, xn)

        def rows_share(e):
            return hop(e, 0, 1, ss_s, rs_s, sib)

        def rows_share_far(e):
            return hop(e, 2, 3, ss_f, rs_f, sib)

        def start_rows(e, carry):
            for i in range(1, count):
                rows_first(e, i).start()
            pltpu.make_async_copy(slots.at[c, e], rows_v.at[0, e, c], rs_1.at[e]).start()
            return carry

        lax.fori_loop(0, number, start_rows, 0)

        def forward(e):
            remote(rows_v.at[0, e], rows_v.at[0, e], ss_x.at[e], rs_1.at[e], sib).wait_recv()
            rows_across(e).start()
            rows_share(e).start()

        def forward_far(e):
            rows_across(e).wait_recv()
            rows_share_far(e).start()

        def near_send(e, j):
            return remote(back_v.at[2 * j + 1, e], back_near.at[j, e], ss_bn.at[e, j], rs_bn.at[e, j], sib)

        def near_out(e, j):
            return remote(out_v.at[2 * j + 1, e], out_near.at[j, e], ss_on.at[e, j], rs_on.at[e, j], sib)

        def far_send(e):
            return remote(back_far.at[e], back_got.at[e], ss_bf.at[e], rs_bf.at[e], xn)

        def store_own(e):
            return pltpu.make_async_copy(own_v.at[e], own_out.at[:, e], st_o.at[e])

        def store_far(e):
            return pltpu.make_async_copy(far_v.at[e], far_out.at[:, e], st_f.at[e])

        def store_rows(e):
            return pltpu.make_async_copy(rows_v.at[:, e], rows_out.at[:, e], st_r.at[e])

        def store_active(e, slot):
            return pltpu.make_async_copy(active_v.at[slot], active_out.at[e], st_a.at[slot])

        def store_hidden(e, slot):
            return pltpu.make_async_copy(hidden_v.at[slot], hidden_out.at[e], st_h.at[slot])

        def sum_far(e):
            near_send(e, 1).wait_recv()
            back_far[e] = (back_v[2, e].astype(F32) + back_near[1, e].astype(F32)).astype(BF)
            far_send(e).start()

        def sum_outputs(e):
            for j in range(2):
                near_out(e, j).wait_recv()
            own_v[e] = (out_v[0, e].astype(F32) + out_near[0, e].astype(F32)).astype(BF)
            far_v[e] = (out_v[2, e].astype(F32) + out_near[1, e].astype(F32)).astype(BF)
            store_own(e).start()
            store_far(e).start()

        def home(e, i):
            ct = (c + i) % count
            return remote(summed.at[e, ct], home_got.at[c, e], ss_h.at[e], rs_h, (ct, f))

        def go_home(e):
            near_send(e, 0).wait_recv()
            far_send(e).wait_recv()
            summed[e] = (
                back_v[0, e].astype(F32) + back_near[0, e].astype(F32) + back_got[e].astype(F32)
            ).astype(BF)
            for i in range(1, count):
                home(e, i).start()
            pltpu.make_async_copy(summed.at[e, c], home_got.at[c, e], rs_h).start()

        def expert(e, carry):
            slot = e % 2

            @pl.when(e + 1 < number)
            def _():
                for load in load_grads(e + 1, 1 - slot):
                    load.start()

            @pl.when(e + 2 < number)
            def _():
                forward(e + 2)

            @pl.when(e + 1 < number)
            def _():
                forward_far(e + 1)

            rows_share(e).wait_recv()
            rows_share_far(e).wait_recv()
            store_rows(e).start()
            for load in load_grads(e, slot):
                load.wait()

            @pl.when(e >= 2)
            def _():
                store_active(e, slot).wait()
                store_hidden(e, slot).wait()

            row = rows_v[:, e].reshape(total_rows, width)
            grad = g_buf[slot].reshape(total_rows, width)
            term = jnp.zeros((total_rows, width), F32)
            firsts, seconds = [], []
            for u in range(splits):
                load_first(e, u).wait()
                load_second(e, u).wait()
                first = first_buf[u].astype(BF)
                second = second_buf[u].astype(BF)
                seconds.append(second)
                hidden = jnp.dot(row, first, preferred_element_type=F32)
                upstream = lax.dot_general(grad, second, CONTRACT_LAST, preferred_element_type=F32)
                bent = jnp.tanh(ROOT * (hidden + CUBIC * hidden * hidden * hidden))
                cols = pl.ds(u * part_units, part_units)
                active_v[slot, :, cols] = (0.5 * hidden * (1.0 + bent)).astype(BF)
                slope = 0.5 * (1.0 + bent) + 0.5 * hidden * (1.0 - bent * bent) * (
                    ROOT * (1.0 + 3.0 * CUBIC * hidden * hidden)
                )
                grad_hidden = (upstream * slope).astype(BF)
                hidden_v[slot, :, cols] = grad_hidden
                term += lax.dot_general(grad_hidden, first, CONTRACT_LAST, preferred_element_type=F32)
            back_v[:, e] = term.astype(BF).reshape(4, count, cap, width)
            near_send(e, 1).start()
            near_send(e, 0).start()
            result = jnp.zeros((total_rows, width), F32)
            for u in range(splits):
                cols = pl.ds(u * part_units, part_units)
                result += jnp.dot(active_v[slot, :, cols], seconds[u], preferred_element_type=F32)
            out_v[:, e] = result.astype(BF).reshape(4, count, cap, width)
            near_out(e, 1).start()
            near_out(e, 0).start()

            @pl.when(e + 1 < number)
            def _():
                for u in range(splits):
                    load_first(e + 1, u).start()
                    load_second(e + 1, u).start()

            store_active(e, slot).start()
            store_hidden(e, slot).start()

            @pl.when(e >= 1)
            def _():
                sum_far(e - 1)
                sum_outputs(e - 1)

            @pl.when(e >= 3)
            def _():
                go_home(e - 3)

            return carry

        forward(0)
        forward(1)
        forward_far(0)
        lax.fori_loop(0, number, expert, 0)
        sum_far(number - 1)
        sum_outputs(number - 1)
        for e in range(number - 3, number):
            go_home(e)
        hat, inverse = statistics(middle[...])
        remote(home_got, home_got, ss_h.at[0], rs_h, sib).wait_recv()

        returned = lax.dot_general(d_ref[...], home_got[...].reshape(-1, width), CONTRACT_FIRST, preferred_element_type=F32)
        scaled = returned * g_ref[...]
        mean_grad = jnp.mean(scaled, axis=1, keepdims=True)
        mean_proj = jnp.mean(scaled * hat, axis=1, keepdims=True)
        gain_out[...] = jnp.sum(returned * hat, axis=0, keepdims=True)
        gradient = c_ref[...].astype(F32) + inverse * (scaled - mean_grad - hat * mean_proj)
        grad_middle[...] = gradient
        low = gradient.astype(BF)
        for j, w_ref in enumerate((w0_ref, w1_ref, w2_ref, w3_ref)):
            back[:, :, j * quarter : (j + 1) * quarter] = (
                lax.dot_general(low, w_ref[...], CONTRACT_LAST, preferred_element_type=F32)
                .astype(BF)
                .reshape(2, half_rows, quarter)
            )

        def part(half, number_of_pair):
            column = (2 * relative(number_of_pair // 2, f) + number_of_pair % 2) * lanes
            return back.at[half, :, pl.ds(pl.multiple_of(column, lanes), lanes)]

        def send_heads(i, half):
            other = (2 * z + k + i) % count
            b = block_at(c, half, count)
            dev = (2 * (other // 2) + k, 2 * x + other % 2)
            return remote(part(half, other), heads.at[b], ss_t.at[i, half], rs_t.at[b], dev)

        for i in range(1, count):
            for half in range(2):
                send_heads(i, half).start()

        @pl.when(k == y)
        def _():
            for half in range(2):
                b = block_at(c, half, count)
                pltpu.make_async_copy(part(half, 2 * z + k), heads.at[b], rs_t.at[b]).start()

        @pl.when(k != y)
        def _():
            for half in range(2):
                send_heads(0, half).start()

        for e in range(number):
            for j in range(2):
                near_send(e, j).wait_send()

        def term_place(j):
            return back_v.at[j, 0 : quarter // (count * cap)]

        def shard_term(j):
            half_quarter = quarter // 2
            mixed_part = [mixed[half, :, j * quarter : (j + 1) * quarter] for half in range(2)]
            value = sum(
                lax.dot_general(
                    mixed_part[half], low[half * half_rows : (half + 1) * half_rows], CONTRACT_FIRST, preferred_element_type=F32
                )
                for half in range(2)
            )
            return value.astype(BF).reshape(shard_far.shape)

        def core_send(j):
            return remote(term_place(2 * j + 1), shard_near.at[j], ss_n.at[j], rs_n.at[j], sib)

        across = remote(shard_far, shard_got, ss_w, rs_w, xn)
        for j in (1, 0):
            back_v[2 * j + 1, 0 : quarter // (count * cap)] = shard_term(2 * j + 1)
            core_send(j).start()
        own_far = shard_term(2)
        core_send(1).wait_recv()
        shard_far[...] = (own_far.astype(F32) + shard_near[1].astype(F32)).astype(BF)
        across.start()
        own_near = shard_term(0)
        core_send(0).wait_recv()
        across.wait_recv()
        shard[...] = (
            (own_near.astype(F32) + shard_near[0].astype(F32) + shard_got[...].astype(F32)).astype(BF).reshape(shard.shape)
        )

        for b in range(2 * count):
            remote(part(0, 0), heads.at[b], ss_t.at[0, 0], rs_t.at[b], sib).wait_recv()

        def leave(e, carry):
            sent = pl.ds(0, count - 1)
            remote(slots.at[sent, e], rows_v.at[0, e, sent], ss_1.at[e], rs_1.at[e], sib).wait_send()
            remote(summed.at[e, sent], home_got.at[sent, e], ss_h.at[e], rs_h, sib).wait_send()
            rows_across(e).wait_send()
            rows_share(e).wait_send()
            rows_share_far(e).wait_send()
            far_send(e).wait_send()
            for j in range(2):
                near_out(e, j).wait_send()
            store_own(e).wait()
            store_far(e).wait()
            store_rows(e).wait()
            return carry

        lax.fori_loop(0, number, leave, 0)
        for e in (number - 2, number - 1):
            store_active(e, e % 2).wait()
            store_hidden(e, e % 2).wait()
        for i in range(1, count):
            for half in range(2):
                send(i, half).wait_send()
                send_heads(i, half).wait_send()

        @pl.when(k != y)
        def _():
            for half in range(2):
                send(0, half).wait_send()
                send_heads(0, half).wait_send()

        core_send(0).wait_send()
        core_send(1).wait_send()
        across.wait_send()

    vmem = pl.BlockSpec(memory_space=pltpu.VMEM)
    block = (count, cap, width)
    low = lambda *shape: pltpu.VMEM(shape, BF)
    fold = (quarter // (count * cap),) + block
    return pl.pallas_call(
        kernel,
        name="experts_exchange",
        cost_estimate=lasting(100),
        out_shape=(
            jax.ShapeDtypeStruct((2, half_rows, width), BF),
            jax.ShapeDtypeStruct((rows, width), F32),
            jax.ShapeDtypeStruct((4, number) + block, BF),
            jax.ShapeDtypeStruct((number, total_rows, units), BF),
            jax.ShapeDtypeStruct((number, total_rows, units), BF),
            jax.ShapeDtypeStruct((count, number, cap, width), BF),
            jax.ShapeDtypeStruct((count, number, cap, width), BF),
            jax.ShapeDtypeStruct((2 * count, half_rows, lanes), BF),
            jax.ShapeDtypeStruct((rows, width), F32),
            jax.ShapeDtypeStruct((1, width), F32),
            jax.ShapeDtypeStruct((quarter, width), BF),
        ),
        in_specs=[ANY] + [vmem] * 8 + [ANY] * 6,
        out_specs=(vmem, vmem, ANY, ANY, ANY, ANY, ANY, ANY, vmem, vmem, vmem),
        scratch_shapes=[
            low(rows, width), low(count, number, cap, width), low(4, number, *block), low(2, 4, *block),
            pltpu.VMEM((splits, width, part_units), F32), pltpu.VMEM((splits, part_units, width), F32),
            low(2, total_rows, units), low(2, total_rows, units),
            low(4, number, *block), low(2, number, *block), low(number, *block), low(number, *block),
            low(4, number, *block), low(2, number, *block), low(number, *block), low(number, *block),
            low(number, *block), low(count, number, cap, width), low(2, half_rows, width),
            low(2, *fold), low(*fold), low(*fold),
            DMA((count, 2)), DMA((count, 2)), DMA((number,)), DMA((number,)), DMA((number,)), DMA((number,)),
            DMA((number,)), DMA((number,)), DMA((number,)), DMA((number,)), DMA((number, 2)), DMA((number, 2)),
            DMA((number,)), DMA((number,)), DMA((number, 2)), DMA((number, 2)), DMA((number,)), DMA,
            DMA((count, 2)), DMA((2 * count,)), DMA((2,)), DMA((2,)), DMA, DMA,
            DMA((splits,)), DMA((splits,)), DMA((2, 4)), DMA((number,)), DMA((2,)), DMA((2,)), DMA((number,)), DMA((number,)),
        ],
        compiler_params=pltpu.CompilerParams(has_side_effects=True, vmem_limit_bytes=60 << 20),
    )(by_head, *out_proj, tokens, dispatch, gain, cotangent, *grads, first_proj, second_proj)


def experts_weights(rows, grads, active, grad_hidden):
    _, number, count, cap, width = rows.shape
    total, units = active.shape[1:]

    def kernel(r_ref, g0_ref, g1_ref, g2_ref, g3_ref, a_ref, h_ref, da, db, done):
        done[...] = jnp.zeros_like(done)
        grad = jnp.concatenate([stacked(ref[...]) for ref in (g0_ref, g1_ref, g2_ref, g3_ref)], axis=0)
        da[0] = lax.dot_general(stacked(r_ref[...]), h_ref[0], CONTRACT_FIRST, preferred_element_type=F32)
        db[0] = lax.dot_general(a_ref[0], grad, CONTRACT_FIRST, preferred_element_type=F32)

    parts = pl.BlockSpec((4, 1, count, cap, width), lambda e: (0, e, 0, 0, 0))
    quarter = pl.BlockSpec((count, 1, cap, width), lambda e: (0, e, 0, 0))
    wide = pl.BlockSpec((1, total, units), lambda e: (e, 0, 0))
    return pl.pallas_call(
        kernel,
        name="experts_weights",
        grid=(number,),
        in_specs=[parts, quarter, quarter, quarter, quarter, wide, wide],
        out_specs=[
            pl.BlockSpec((1, width, units), lambda e: (e, 0, 0)),
            pl.BlockSpec((1, units, width), lambda e: (e, 0, 0)),
            pl.BlockSpec((8, 128), lambda e: (0, 0)),
        ],
        out_shape=(
            jax.ShapeDtypeStruct((number, width, units), F32),
            jax.ShapeDtypeStruct((number, units, width), F32),
            jax.ShapeDtypeStruct((8, 128), F32),
        ),
        cost_estimate=pl.CostEstimate(
            flops=4 * number * total * units * width, bytes_accessed=12 * number * units * width, transcendentals=0
        ),
        compiler_params=params(False),
    )(rows, *grads, active, grad_hidden)


def after(value, *others):
    return lax.optimization_barrier((value,) + others)[0]


def finish_exchange(arrays, parts, out_slab, gain_part, weight):
    count = lax.axis_size("ctx")
    depth = count // 2
    number = len(arrays)
    lanes = arrays[0].shape[2]
    width = count * lanes
    _, rows, wide = parts.shape
    slab = rows // count
    pieces_w = 4
    piece_w = rows // pieces_w

    def kernel(*refs):
        ins, (p_ref, o_ref, g_ref, w_ref), (tok_out, w_out, o_out, g_out, w_all) = (
            refs[:number],
            refs[number : number + 4],
            refs[number + 4 : number + 9],
        )
        (
            got, held, got_g, sum_g, got_gc,
            ss, rs, ss_r, rs_r, ss_up, ss_dn, rs_z, ss_a, ss_b, rs_o,
            ss_of, rs_of, ss_g, rs_g, ss_gc, rs_gc, ss_wx, rs_wx, ss_ws, rs_ws, ss_wf, rs_wf, loc,
        ) = refs[number + 9 :]
        c, f, z, y, x, k = place()
        pair = 2 * z + k
        target = 2 * x + y
        sib = (c, f + 1 - 2 * k)
        xn = (c, (f + 2) % 4)
        up = (c + 2, f)
        down = (c - 2, f)

        def gain_send(j):
            return remote(sum_g.at[j], got_g.at[j], ss_g.at[j], rs_g.at[j], sib if j == 0 else xn)

        sum_g[0] = g_ref[...]
        gain_send(0).start()

        def slab_spread(i):
            return remote(o_ref, o_out.at[c], ss_of.at[i], rs_of.at[c], ((c + i) % count, f))

        slab_own = pltpu.make_async_copy(o_ref, o_out.at[c], rs_of.at[c])

        def weight_part(shard, i):
            return w_all.at[shard, pl.ds(i * piece_w, piece_w)]

        def weight_across(i):
            return remote(w_ref.at[pl.ds(i * piece_w, piece_w)], weight_part(f, i), ss_wx.at[i], rs_wx.at[i], xn)

        def weight_on(i, shard):
            return remote(weight_part(shard, i), weight_part(shard, i), ss_wf.at[i], rs_wf.at[i], sib)

        weight_share = remote(w_ref, w_all.at[f], ss_ws, rs_ws, sib)
        weight_own = pltpu.make_async_copy(w_ref, w_all.at[f], loc)

        peers = [
            (2 * z + 1 - y, f, 2 * x + 1 - y),
            (c, (f + 2) % 4, 2 * (1 - x) + y),
            (2 * z + 1 - y, (f + 2) % 4, 2 * (1 - x) + 1 - y),
        ]

        def third(ref, j):
            return ref.at[:, pl.ds(j * lanes, lanes)]

        def scatter(d, j):
            cp, fp, shard = peers[d]
            return remote(third(p_ref.at[shard], j), third(got.at[d], j), ss_r.at[d, j], rs_r.at[d, j], (cp, fp))

        for j in range(3):
            for d in (2, 1, 0):
                scatter(d, j).start()

        def there(half, a):
            return tok_out.at[half, :, pl.ds(pl.multiple_of(a * width + pair * lanes, lanes), lanes)]

        def send(i, half, a):
            ct = (c + i) % count
            return remote(
                ins[a].at[block_at(ct, half, count)], there(half, a), ss.at[i, half, a], rs.at[pair, half, a], (ct, target)
            )

        def own(half, a):
            return pltpu.make_async_copy(ins[a].at[block_at(c, half, count)], there(half, a), rs.at[pair, half, a])

        pieces = [(half, a) for a in range(number) for half in range(2)]
        def send_all(numbers):
            for i in numbers:
                for half, a in pieces:
                    send(i, half, a).start()

        send_all(range(2, count, 2))

        @pl.when(k == y)
        def _():
            for half, a in pieces:
                own(half, a).start()

        @pl.when(k != y)
        def _():
            for half, a in pieces:
                send(0, half, a).start()

        for i in range(pieces_w):
            weight_across(i).start()
        weight_share.start()
        weight_own.start()
        slab_own.start()
        gain_send(0).wait_recv()
        sum_g[1] = sum_g[0] + got_g[0]
        gain_send(1).start()

        def chain(zb, j, sem, dev):
            return remote(third(held.at[zb], j), third(held.at[zb], j), sem.at[j], rs_z.at[zb, j], dev)

        def goal(zb, j):
            return w_out.at[:, pl.ds(pl.multiple_of(j * width + (2 * zb + k) * lanes, lanes), lanes)]

        def own_column(zb, j):
            return remote(third(held.at[zb], j), goal(zb, j), ss_a.at[zb, j], rs_o.at[2 * zb + k, j], (c, target))

        def own_local(zb, j):
            return pltpu.make_async_copy(third(held.at[zb], j), goal(zb, j), rs_o.at[2 * zb + k, j])

        def next_column(zb, j):
            return remote(
                third(held.at[zb], j), goal(zb, j), ss_b.at[zb, j], rs_o.at[2 * zb + k, j], (2 * z + 1 - y, target)
            )

        def spread(zb, j):
            next_column(zb, j).start()

            @pl.when(k == y)
            def _():
                own_local(zb, j).start()

            @pl.when(k != y)
            def _():
                own_column(zb, j).start()

        for j in range(3):
            at = pl.ds(j * lanes, lanes)
            total = p_ref[2 * x + y, :, at].astype(F32)
            for d in range(3):
                scatter(d, j).wait_recv()
                total += got[d, :, at].astype(F32)
            held[z, :, at] = total.astype(BF)

            @pl.when(z < depth - 1)
            def _(j=j):
                chain(z, j, ss_up.at[0], up).start()

            @pl.when(z > 0)
            def _(j=j):
                chain(z, j, ss_dn.at[0], down).start()

            spread(z, j)
        send_all(range(1, count, 2))

        gain_send(1).wait_recv()
        sum_g[2] = sum_g[1] + got_g[1]

        def gain_spread(i):
            return remote(sum_g.at[2], got_gc.at[c], ss_gc.at[i], rs_gc.at[c], ((c + i) % count, f))

        for i in range(1, count):
            gain_spread(i).start()
            slab_spread(i).start()

        def weight_pass(i):
            shard = (f + 2) % 4
            remote(weight_part(shard, i), weight_part(shard, i), ss_wf.at[i], rs_wx.at[i], sib).wait_recv()
            weight_on(i, shard).start()

        for hop in range(1, depth):
            for j in range(3):

                @pl.when(z - hop >= 0)
                def _(hop=hop, j=j):
                    chain(z - hop, j, ss_up.at[hop], sib).wait_recv()

                    @pl.when(z < depth - 1)
                    def _():
                        chain(z - hop, j, ss_up.at[hop], up).start()

                    spread(z - hop, j)

                @pl.when(z + hop <= depth - 1)
                def _(hop=hop, j=j):
                    chain(z + hop, j, ss_dn.at[hop], sib).wait_recv()

                    @pl.when(z > 0)
                    def _():
                        chain(z + hop, j, ss_dn.at[hop], down).start()

                    spread(z + hop, j)

            weight_pass(hop - 1)
        for i in range(depth - 1, pieces_w):
            weight_pass(i)

        total_g = sum_g[2]
        for i in range(1, count):
            cs = (c + i) % count
            remote(sum_g.at[2], got_gc.at[cs], ss_gc.at[i], rs_gc.at[cs], sib).wait_recv()
            total_g += got_gc[cs]
        g_out[...] = total_g

        gain_send(0).wait_send()
        gain_send(1).wait_send()
        for i in range(pieces_w):
            weight_across(i).wait_send()
            weight_on(i, (f + 2) % 4).wait_send()
            remote(weight_part(0, i), weight_part(0, i), ss_wf.at[i], rs_wf.at[i], sib).wait_recv()
        weight_share.wait()
        weight_own.wait()
        for d in range(3):
            for j in range(3):
                scatter(d, j).wait_send()
        for half, a in pieces:
            for other in range(count):
                cols = pl.ds(a * width + other * lanes, lanes)
                remote(ins[a].at[0], tok_out.at[half, :, cols], ss.at[0, half, a], rs.at[other, half, a], sib).wait_recv()
        for i in range(1, count):
            for half, a in pieces:
                send(i, half, a).wait_send()
            gain_spread(i).wait_send()
            slab_spread(i).wait_send()
            cs = (c + i) % count
            remote(o_ref, o_out.at[cs], ss_of.at[i], rs_of.at[cs], sib).wait_recv()
        slab_own.wait()

        @pl.when(k != y)
        def _():
            for half, a in pieces:
                send(0, half, a).wait_send()
            for zb in range(depth):
                for j in range(3):
                    own_column(zb, j).wait_send()

        for other in range(count):
            for j in range(3):
                remote(
                    third(held.at[0], j), third(w_out, j * count + other), ss_a.at[0, j], rs_o.at[other, j], sib
                ).wait_recv()
        for hop in range(depth):

            @pl.when((z < depth - 1) & (z - hop >= 0))
            def _(hop=hop):
                for j in range(3):
                    chain(z - hop, j, ss_up.at[hop], up).wait_send()

            @pl.when((z > 0) & (z + hop <= depth - 1))
            def _(hop=hop):
                for j in range(3):
                    chain(z + hop, j, ss_dn.at[hop], down).wait_send()

        for zb in range(depth):
            for j in range(3):
                next_column(zb, j).wait_send()

    vmem = pl.BlockSpec(memory_space=pltpu.VMEM)
    eighth = gain_part.shape
    return pl.pallas_call(
        kernel,
        name="finish_exchange",
        cost_estimate=lasting(70),
        out_shape=(
            jax.ShapeDtypeStruct((2, arrays[0].shape[1], number * width), BF),
            jax.ShapeDtypeStruct((rows, 3 * width), BF),
            jax.ShapeDtypeStruct((count, slab, width), BF),
            jax.ShapeDtypeStruct(eighth, F32),
            jax.ShapeDtypeStruct((4,) + weight.shape, BF),
        ),
        in_specs=[ANY] * number + [vmem, ANY, vmem, ANY],
        out_specs=(ANY, ANY, ANY, vmem, ANY),
        scratch_shapes=[
            pltpu.VMEM((3, rows, wide), BF),
            pltpu.VMEM((depth, rows, wide), BF),
            pltpu.VMEM((2,) + eighth, F32),
            pltpu.VMEM((3,) + eighth, F32),
            pltpu.VMEM((count,) + eighth, F32),
            DMA((count, 2, number)), DMA((count, 2, number)),
            DMA((3, 3)), DMA((3, 3)), DMA((depth, 3)), DMA((depth, 3)), DMA((depth, 3)),
            DMA((depth, 3)), DMA((depth, 3)), DMA((count, 3)),
            DMA((count,)), DMA((count,)), DMA((2,)), DMA((2,)), DMA((count,)), DMA((count,)),
            DMA((pieces_w,)), DMA((pieces_w,)), DMA, DMA, DMA((pieces_w,)), DMA((pieces_w,)), DMA,
        ],
        compiler_params=params(),
    )(*arrays, parts, out_slab, gain_part, weight)


def slots_of(routes):
    tokens = routes.shape[0]
    chosen = routes[:, None] == jnp.arange(EXPERTS, dtype=jnp.int32)[None, :]
    earlier = (jnp.arange(tokens)[:, None] >= jnp.arange(tokens)[None, :]).astype(BF)
    running = jnp.dot(earlier, chosen.astype(BF), preferred_element_type=F32)
    rank = jnp.sum(jnp.where(chosen, running, 0.0), axis=1).astype(jnp.int32) - 1
    slot = routes * CAP + rank
    return (jnp.arange(EXPERTS * CAP, dtype=jnp.int32)[:, None] == slot[None, :]).astype(BF)


def by_head_pairs(
    tokens, doc_starts, expert_ids, query_key_value_weight, output_weight_matrix, expert_in, expert_out, gain_one, gain_two, grad_output
):
    half_rows = tokens.shape[3]
    width = tokens.shape[4]
    count = lax.axis_size("ctx")
    rows = 2 * half_rows
    length = count * rows
    scale = (width // HEADS) ** (-0.5)
    f = lax.axis_index("fsdp")
    lanes = 2 * (width // HEADS)
    shard_rows = width // 4
    pick = (((0,), (0,)), ((), ()))
    turn = (((1,), (1,)), ((), ()))
    start_x = tokens.reshape(rows, width).astype(F32)
    cotangent = grad_output.reshape(rows, width)
    qkv_low = query_key_value_weight.astype(BF)
    first_normed, hat_one, inverse_one = norm_forward(start_x, gain_one)
    normed = first_normed.astype(BF)
    stream, starts, columns = gather_stream(
        normed.reshape(2, half_rows, width), doc_starts.reshape(2, half_rows), qkv_low
    )
    dispatch = slots_of(expert_ids.reshape(rows))
    own_experts = EXPERTS // count
    shape = (count, own_experts, CAP, width)
    send_grads = jnp.dot(dispatch, cotangent, preferred_element_type=F32).astype(BF).reshape(shape)
    grads_near = lax.all_to_all(send_grads, "ctx", split_axis=0, concat_axis=0, tiled=True)
    grads_near = after(grads_near, stream)
    out_own = output_weight_matrix.astype(BF)
    grads_far = swap(grads_near, "fsdp", 2)
    out_far = swap(out_own, "fsdp", 2)
    out_far = after(out_far, stream)
    out_beside = [swap(after(out_own, stream), "fsdp", 1), swap(out_far, "fsdp", 1)]
    stream = stream.reshape(length, width)
    start_row = jnp.concatenate([starts[:, 0].reshape(-1), starts[::-1, 1].reshape(-1)])[None]
    numbers = jnp.min(start_row.reshape(-1, TILE), axis=1) // TILE
    query, key, value, mixed16, mixed32, logs = attend_forward(stream, columns, start_row, numbers, scale)
    grads_far = after(grads_far, mixed16)
    grads_beside = [swap(grads_near, "fsdp", 1), swap(grads_far, "fsdp", 1)]
    out_proj = [out_own, out_beside[0], out_far, out_beside[1]]
    gain_row = gain_two.reshape(1, width)
    all_grads = [grads_near, grads_beside[0], grads_far, grads_beside[1]]
    (
        mixed, middle, all_rows, active, grad_hidden, out_own, out_send, grad_heads, grad_middle, grad_gain_two, out_shard,
    ) = experts_exchange(
        mixed16.reshape(2 * count, half_rows, lanes), out_proj, tokens.reshape(rows, width), dispatch, gain_row, cotangent,
        all_grads, expert_in, expert_out,
    )
    slots = (EXPERTS * CAP, width)
    out_got = swap(out_send, "fsdp", 2)
    grad_in, grad_outw, done = experts_weights(after(all_rows, out_send), all_grads, active, grad_hidden)
    out_sum = (out_own.astype(F32) + out_got.astype(F32) + done[0, 0]).astype(BF)
    slab_rows = shard_rows // count
    both_send = jnp.concatenate([out_shard.reshape(count, slab_rows, width), out_sum.reshape(count, -1, width)], axis=1)
    both = lax.all_to_all(both_send, "ctx", split_axis=0, concat_axis=0, tiled=True)
    grad_q, grad_k, grad_v = attend_backward(
        query, key, value, after(grad_heads, both_send).reshape(length, lanes), mixed32, logs, start_row, numbers, scale
    )
    both = after(both, grad_q)
    out_slab = jnp.sum(both[:, :slab_rows].astype(F32), axis=0).astype(BF)
    back_rows = both[:, slab_rows:]
    blocks = (2 * count, half_rows, lanes)
    own_grads = jnp.concatenate([grad_q, grad_k, grad_v], axis=1)
    parts = lax.dot_general(stream, own_grads, pick, preferred_element_type=F32).astype(BF)
    grad_projected, weight_grad, shard_out, gain_sum, projection = finish_exchange(
        [grad_q.reshape(blocks), grad_k.reshape(blocks), grad_v.reshape(blocks)],
        parts.reshape(4, shard_rows, 3 * lanes),
        out_slab,
        grad_gain_two,
        qkv_low,
    )
    grad_projected = grad_projected.reshape(rows, 3 * width)
    projection = projection.reshape(width, 3 * width)
    back_rows = after(back_rows, weight_grad)
    expert_sum = lax.dot_general(dispatch, back_rows.reshape(slots), pick, preferred_element_type=F32)
    block_out = (middle + expert_sum).astype(BF)
    weight_grad = weight_grad.astype(F32)
    shard_out = shard_out.reshape(shard_rows, width).astype(F32)
    grad_normed = lax.dot_general(grad_projected, projection, turn, preferred_element_type=F32)
    grad_in_norm, _ = norm_backward(grad_normed[None], hat_one[None], inverse_one[None], gain_one)
    grad_start = grad_middle + grad_in_norm[0]
    own_gain = lax.dynamic_slice(gain_one, (f * shard_rows,), (shard_rows,))
    shard_gain_one = jnp.sum(weight_grad * qkv_low.astype(F32), axis=1) / own_gain
    shard_gain_two = lax.dynamic_slice(gain_sum.reshape(width), (f * shard_rows,), (shard_rows,))
    return (
        block_out.reshape(tokens.shape),
        grad_start.reshape(tokens.shape),
        weight_grad,
        shard_out,
        grad_in,
        grad_outw,
        shard_gain_one,
        shard_gain_two,
    )


def solution(mesh):
    pairs = mesh.shape["ctx"] * 2 == HEADS and mesh.shape["fsdp"] == 4
    return jax.shard_map(
        by_head_pairs if pairs else shards,
        mesh=mesh,
        in_specs=(
            P("fsdp", "ctx", None, None, None),
            P("fsdp", "ctx", None, None),
            P("fsdp", "ctx", None, None, None),
            P("fsdp", None),
            P("fsdp", None),
            P("ctx", None, "fsdp"),
            P("ctx", "fsdp", None),
            P(),
            P(),
            P("fsdp", "ctx", None, None, None),
        ),
        out_specs=(
            P("fsdp", "ctx", None, None, None),
            P("fsdp", "ctx", None, None, None),
            P("fsdp", None),
            P("fsdp", None),
            P("ctx", None, "fsdp"),
            P("ctx", "fsdp", None),
            P("fsdp"),
            P("fsdp"),
        ),
        check_vma=False,
    )
```

```python
import math

import jax
import jax.numpy as jnp
from jax import lax
from jax.experimental import pallas as pl
from jax.experimental.pallas import tpu as pltpu
from jax.sharding import PartitionSpec as P

HEADS = 16
EXPERTS = 64
CAP = 8


EPS = 1e-05
NEGATIVE = -1e30


def position_of(row_ids, ctx_count, half_rows):
    device = row_ids // (2 * half_rows)
    upper_half = row_ids // half_rows % 2
    offset = row_ids % half_rows
    return jnp.where(
        upper_half == 0,
        device * half_rows + offset,
        (2 * ctx_count - 1 - device) * half_rows + offset,
    )


def norm_forward(value, gain):
    row_mean = jnp.mean(value, axis=-1, keepdims=True)
    centred = value - row_mean
    inverse = lax.rsqrt(jnp.mean(centred * centred, axis=-1, keepdims=True) + EPS)
    normed = centred * inverse
    return (normed * gain, normed, inverse)


def norm_backward(gradient, normed, inverse, gain):
    scaled = gradient * gain
    mean_grad = jnp.mean(scaled, axis=-1, keepdims=True)
    mean_proj = jnp.mean(scaled * normed, axis=-1, keepdims=True)
    return (
        inverse * (scaled - mean_grad - normed * mean_proj),
        jnp.sum(gradient * normed, axis=(0, 1)),
    )


def scores(query, keys, query_pos, key_pos, query_start, score_scale):
    raw_scores = (
        jnp.einsum("qshe,kshe->shqk", query, keys, preferred_element_type=jnp.float32) * score_scale
    )
    visible = (key_pos[None, None, None, :] <= query_pos[None, None, :, None]) & (
        key_pos[None, None, None, :] >= query_start.T[:, None, :, None]
    )
    return jnp.where(visible, raw_scores, NEGATIVE)


def log_totals(query, keys, query_pos, query_start, score_scale, ctx_count, half_rows, key_block):
    block_count = keys.shape[0] // key_block
    carry_shape = (query.shape[1], query.shape[2], query.shape[0])

    def log_one_block(block_index, carried):
        running_max, running = carried
        first_row = block_index * key_block
        key_piece = lax.dynamic_slice_in_dim(keys, first_row, key_block, 0)
        key_pos = position_of(
            first_row + jnp.arange(key_block, dtype=jnp.int32), ctx_count, half_rows
        )
        score_rows = scores(query, key_piece, query_pos, key_pos, query_start, score_scale)
        new_max = jnp.maximum(running_max, jnp.max(score_rows, axis=-1))
        running = running * jnp.exp(running_max - new_max) + jnp.sum(
            jnp.exp(score_rows - new_max[..., None]), axis=-1
        )
        return (new_max, running)

    running_max, running = lax.fori_loop(
        0,
        block_count,
        log_one_block,
        (jnp.full(carry_shape, NEGATIVE, jnp.float32), jnp.zeros(carry_shape, jnp.float32)),
    )
    return running_max + jnp.log(running)


def attend(
    query,
    keys,
    values,
    query_pos,
    query_start,
    log_total,
    score_scale,
    ctx_count,
    half_rows,
    key_block,
):
    block_count = keys.shape[0] // key_block
    zeros_init = jnp.zeros(query.shape, jnp.float32)

    def attend_one_block(block_index, carried):
        output, remainder = carried
        first_row = block_index * key_block
        key_piece = lax.dynamic_slice_in_dim(keys, first_row, key_block, 0)
        value_piece = lax.dynamic_slice_in_dim(values, first_row, key_block, 0)
        key_pos = position_of(
            first_row + jnp.arange(key_block, dtype=jnp.int32), ctx_count, half_rows
        )
        weights = jnp.exp(
            scores(query, key_piece, query_pos, key_pos, query_start, score_scale)
            - log_total[..., None]
        )
        rounded = weights.astype(jnp.bfloat16)
        leftover = (weights - rounded.astype(jnp.float32)).astype(jnp.bfloat16)
        output = output + jnp.einsum(
            "shqk,kshe->qshe", rounded, value_piece, preferred_element_type=jnp.float32
        )
        remainder = remainder + jnp.einsum(
            "shqk,kshe->qshe", leftover, value_piece, preferred_element_type=jnp.float32
        )
        return (output, remainder)

    return lax.fori_loop(0, block_count, attend_one_block, (zeros_init, zeros_init))


def query_grads(
    query,
    keys,
    values,
    grad_heads,
    query_pos,
    query_start,
    log_total,
    row_delta,
    score_scale,
    ctx_count,
    half_rows,
    key_block,
):
    block_count = keys.shape[0] // key_block

    def query_one_block(block_index, running):
        first_row = block_index * key_block
        key_piece = lax.dynamic_slice_in_dim(keys, first_row, key_block, 0)
        value_piece = lax.dynamic_slice_in_dim(values, first_row, key_block, 0)
        key_pos = position_of(
            first_row + jnp.arange(key_block, dtype=jnp.int32), ctx_count, half_rows
        )
        weights = jnp.exp(
            scores(query, key_piece, query_pos, key_pos, query_start, score_scale)
            - log_total[..., None]
        )
        grad_weight = jnp.einsum(
            "qshe,kshe->shqk", grad_heads, value_piece, preferred_element_type=jnp.float32
        )
        grad_score = (weights * (grad_weight - row_delta[..., None])).astype(jnp.bfloat16)
        return running + jnp.einsum(
            "shqk,kshe->qshe", grad_score, key_piece, preferred_element_type=jnp.float32
        )

    return (
        lax.fori_loop(0, block_count, query_one_block, jnp.zeros(query.shape, jnp.float32))
        * score_scale
    )


def key_grads(
    query,
    grad_heads,
    query_pos,
    query_start,
    log_total,
    row_delta,
    key_piece,
    value_piece,
    key_pos,
    score_scale,
):
    weights = jnp.exp(
        scores(query, key_piece, query_pos, key_pos, query_start, score_scale)
        - log_total[..., None]
    )
    grad_weight = jnp.einsum(
        "qshe,kshe->shqk", grad_heads, value_piece, preferred_element_type=jnp.float32
    )
    grad_score = (weights * (grad_weight - row_delta[..., None])).astype(jnp.bfloat16)
    key_part = (
        jnp.einsum("shqk,qshe->kshe", grad_score, query, preferred_element_type=jnp.float32)
        * score_scale
    )
    value_part = jnp.einsum(
        "shqk,qshe->kshe",
        weights.astype(jnp.bfloat16),
        grad_heads,
        preferred_element_type=jnp.float32,
    )
    return (key_part, value_part)


def shards(
    tokens,
    doc_starts,
    expert_ids,
    query_key_value_weight,
    output_weight_matrix,
    expert_in,
    expert_out,
    gain_one,
    gain_two,
    grad_output,
):
    seq_dev = tokens.shape[0]
    half_rows = tokens.shape[3]
    model_width = tokens.shape[4]
    local_rows = 2 * half_rows
    ctx_count = lax.axis_size("ctx")
    head_count = HEADS
    head_size = model_width // head_count
    score_scale = head_size ** (-0.5)
    keys_total = ctx_count * local_rows
    key_block = min(512, keys_total)
    own_rows = lax.axis_index("ctx") * local_rows + jnp.arange(local_rows, dtype=jnp.int32)
    query_pos = position_of(own_rows, ctx_count, half_rows)
    query_start = doc_starts.reshape(seq_dev, local_rows).T
    routes_local = expert_ids.reshape(seq_dev, local_rows).T
    start_x = (
        tokens.reshape(seq_dev, local_rows, model_width).transpose(1, 0, 2).astype(jnp.float32)
    )
    cotangent = grad_output.reshape(seq_dev, local_rows, model_width).transpose(1, 0, 2)
    projection, out_proj = (
        lax.all_gather(query_key_value_weight.astype(jnp.bfloat16), "fsdp", axis=0, tiled=True),
        lax.all_gather(output_weight_matrix.astype(jnp.bfloat16), "fsdp", axis=0, tiled=True),
    )
    first_normed_rows, hat_one, inverse_one = norm_forward(start_x, gain_one)
    normed_low = first_normed_rows.astype(jnp.bfloat16)
    projected_rows = jnp.einsum(
        "tsd,de->tse", normed_low, projection, preferred_element_type=jnp.float32
    ).astype(jnp.bfloat16)
    query = projected_rows[..., :model_width]
    keys = projected_rows[..., model_width : 2 * model_width]
    values = projected_rows[..., 2 * model_width :]
    key_all, value_all = (
        lax.all_gather(keys, "ctx", axis=0, tiled=True),
        lax.all_gather(values, "ctx", axis=0, tiled=True),
    )
    query_heads = query.reshape(local_rows, seq_dev, head_count, head_size)
    key_heads = key_all.reshape(keys_total, seq_dev, head_count, head_size)
    value_heads = value_all.reshape(keys_total, seq_dev, head_count, head_size)
    log_total = log_totals(
        query_heads, key_heads, query_pos, query_start, score_scale, ctx_count, half_rows, key_block
    )
    mixed_heads_out, remainder = attend(
        query_heads,
        key_heads,
        value_heads,
        query_pos,
        query_start,
        log_total,
        score_scale,
        ctx_count,
        half_rows,
        key_block,
    )
    mixed_low = mixed_heads_out.astype(jnp.bfloat16).reshape(local_rows, seq_dev, model_width)
    attention_rows_out = jnp.einsum(
        "tsd,de->tse", mixed_low, out_proj, preferred_element_type=jnp.float32
    )
    middle = start_x + attention_rows_out
    normed_two, hat_two, inverse_two = norm_forward(middle, gain_two)
    routed = normed_two.astype(jnp.bfloat16)
    slot_count = EXPERTS * CAP
    per_owner = EXPERTS // ctx_count
    chosen = (routes_local[..., None] == jnp.arange(EXPERTS, dtype=jnp.int32)).astype(jnp.int32)
    earlier = (
        jnp.arange(local_rows)[:, None] >= jnp.arange(local_rows)[None, :]
    ).astype(jnp.bfloat16)
    running = jnp.einsum(
        "tu,use->tse", earlier, chosen.astype(jnp.bfloat16), preferred_element_type=jnp.float32
    )
    rank_within = jnp.sum(chosen * running.astype(jnp.int32), axis=-1) - 1
    slot_index = routes_local * CAP + rank_within
    dispatch = (
        slot_index.T[:, None, :] == jnp.arange(slot_count, dtype=jnp.int32)[None, :, None]
    ).astype(jnp.bfloat16)
    dispatch = dispatch.reshape(seq_dev, ctx_count, per_owner, CAP, local_rows)
    send_rows = jnp.einsum(
        "snect,tsd->nescd", dispatch, routed, preferred_element_type=jnp.float32
    ).astype(jnp.bfloat16)
    send_grads = jnp.einsum(
        "snect,tsd->nescd", dispatch, cotangent, preferred_element_type=jnp.float32
    ).astype(jnp.bfloat16)
    got_rows, got_grads = (
        lax.all_to_all(send_rows, "ctx", split_axis=0, concat_axis=0, tiled=True),
        lax.all_to_all(send_grads, "ctx", split_axis=0, concat_axis=0, tiled=True),
    )
    in_low = expert_in.astype(jnp.bfloat16)
    out_low = expert_out.astype(jnp.bfloat16)
    all_rows, all_grads = (
        lax.all_gather(got_rows, "fsdp", axis=2, tiled=True),
        lax.all_gather(got_grads, "fsdp", axis=2, tiled=True),
    )
    hidden = jnp.einsum("nercd,edf->nercf", all_rows, in_low, preferred_element_type=jnp.float32)
    active = jax.nn.gelu(hidden).astype(jnp.bfloat16)
    partial_rows = jnp.einsum(
        "nercf,efd->nercd", active, out_low, preferred_element_type=jnp.float32
    )
    result = lax.psum_scatter(
        partial_rows.astype(jnp.bfloat16), "fsdp", scatter_dimension=2, tiled=True
    )
    upstream = jnp.einsum(
        "nercd,efd->nercf", all_grads, out_low, preferred_element_type=jnp.float32
    )
    unused, gelu_back = jax.vjp(jax.nn.gelu, hidden)
    grad_hidden = gelu_back(upstream)[0].astype(jnp.bfloat16)
    grad_in = jnp.einsum(
        "nercd,nercf->edf", all_rows, grad_hidden, preferred_element_type=jnp.float32
    )
    grad_outw = jnp.einsum(
        "nercf,nercd->efd", active, all_grads, preferred_element_type=jnp.float32
    )
    row_part = jnp.einsum(
        "nercf,edf->nercd", grad_hidden, in_low, preferred_element_type=jnp.float32
    )
    row_grad = lax.psum_scatter(row_part, "fsdp", scatter_dimension=2, tiled=True).astype(
        jnp.bfloat16
    )
    back_rows = lax.all_to_all(result, "ctx", split_axis=0, concat_axis=0, tiled=True)
    expert_sum = jnp.einsum(
        "snect,nescd->tsd", dispatch, back_rows, preferred_element_type=jnp.float32
    )
    output_rows = middle + expert_sum
    returned = lax.all_to_all(row_grad, "ctx", split_axis=0, concat_axis=0, tiled=True)
    grad_routed = jnp.einsum(
        "snect,nescd->tsd", dispatch, returned, preferred_element_type=jnp.float32
    )
    grad_mid_norm, grad_gain_two = norm_backward(grad_routed, hat_two, inverse_two, gain_two)
    grad_middle = cotangent.astype(jnp.float32) + grad_mid_norm
    grad_attn = grad_middle.astype(jnp.bfloat16)
    grad_outproj = jnp.einsum(
        "tsd,tse->de", mixed_low, grad_attn, preferred_element_type=jnp.float32
    )
    grad_mixed = jnp.einsum(
        "tse,de->tsd", grad_attn, out_proj, preferred_element_type=jnp.float32
    ).astype(jnp.bfloat16)
    grad_heads = grad_mixed.reshape(local_rows, seq_dev, head_count, head_size)
    full_mixed = mixed_heads_out + remainder
    row_delta = jnp.sum(grad_heads.astype(jnp.float32) * full_mixed, axis=-1).transpose(1, 2, 0)
    grad_query = query_grads(
        query_heads,
        key_heads,
        value_heads,
        grad_heads,
        query_pos,
        query_start,
        log_total,
        row_delta,
        score_scale,
        ctx_count,
        half_rows,
        key_block,
    ).astype(jnp.bfloat16)
    sub_rows = math.gcd(local_rows * lax.axis_size("ctx"), key_block)

    def one_piece(piece_index):
        piece_start = piece_index * sub_rows
        key_piece = lax.dynamic_slice_in_dim(key_heads, piece_start, sub_rows, 0)
        value_piece = lax.dynamic_slice_in_dim(value_heads, piece_start, sub_rows, 0)
        key_pos = position_of(
            piece_start + jnp.arange(sub_rows, dtype=jnp.int32), ctx_count, half_rows
        )
        key_part, value_part = key_grads(
            query_heads,
            grad_heads,
            query_pos,
            query_start,
            log_total,
            row_delta,
            key_piece,
            value_piece,
            key_pos,
            score_scale,
        )
        return jnp.concatenate(
            [
                key_part.reshape(sub_rows, seq_dev, model_width),
                value_part.reshape(sub_rows, seq_dev, model_width),
            ],
            axis=-1,
        )

    summed = lax.psum_scatter(
        lax.map(
            one_piece, jnp.arange(local_rows * lax.axis_size("ctx") // sub_rows, dtype=jnp.int32)
        ).reshape(local_rows * lax.axis_size("ctx"), seq_dev, 2 * model_width),
        "ctx",
        scatter_dimension=0,
        tiled=True,
    )
    grad_key = summed[..., :model_width].astype(jnp.bfloat16)
    grad_value = summed[..., model_width:].astype(jnp.bfloat16)
    grad_projected = jnp.concatenate(
        [grad_query.reshape(local_rows, seq_dev, model_width), grad_key, grad_value], axis=-1
    )
    grad_projection = jnp.einsum(
        "tsd,tse->de", normed_low, grad_projected, preferred_element_type=jnp.float32
    )
    grad_normed = jnp.einsum(
        "tse,de->tsd", grad_projected, projection, preferred_element_type=jnp.float32
    )
    grad_in_norm, grad_gain_one = norm_backward(grad_normed, hat_one, inverse_one, gain_one)
    grad_start = grad_middle + grad_in_norm
    shard_proj, shard_outproj, shard_gain_one, shard_gain_two = (
        lax.psum_scatter(
            grad_projection.astype(jnp.bfloat16), "fsdp", scatter_dimension=0, tiled=True
        ).astype(jnp.float32),
        lax.psum_scatter(
            grad_outproj.astype(jnp.bfloat16), "fsdp", scatter_dimension=0, tiled=True
        ).astype(jnp.float32),
        lax.psum_scatter(
            grad_gain_one.astype(jnp.bfloat16), "fsdp", scatter_dimension=0, tiled=True
        ).astype(jnp.float32),
        lax.psum_scatter(
            grad_gain_two.astype(jnp.bfloat16), "fsdp", scatter_dimension=0, tiled=True
        ).astype(jnp.float32),
    )
    shard_proj, shard_outproj, shard_gain_one, shard_gain_two = (
        lax.psum(shard_proj.astype(jnp.bfloat16), "ctx").astype(jnp.float32),
        lax.psum(shard_outproj.astype(jnp.bfloat16), "ctx").astype(jnp.float32),
        lax.psum(shard_gain_one.astype(jnp.bfloat16), "ctx").astype(jnp.float32),
        lax.psum(shard_gain_two.astype(jnp.bfloat16), "ctx").astype(jnp.float32),
    )
    block_out = output_rows.transpose(1, 0, 2).reshape(tokens.shape).astype(jnp.bfloat16)
    grad_tokens = grad_start.transpose(1, 0, 2).reshape(tokens.shape)
    return (
        block_out,
        grad_tokens,
        shard_proj,
        shard_outproj,
        grad_in,
        grad_outw,
        shard_gain_one,
        shard_gain_two,
    )


BF = jnp.bfloat16
F32 = jnp.float32
CONTRACT_FIRST = (((0,), (0,)), ((), ()))
CONTRACT_LAST = (((1,), (1,)), ((), ()))
MESH_ID = pl.DeviceIdType.MESH
ANY = pl.BlockSpec(memory_space=pl.ANY)
DMA = pltpu.SemaphoreType.DMA
VMEM_CAP = 56 << 20


def place():
    c = lax.axis_index("ctx")
    f = lax.axis_index("fsdp")
    return c, f, c // 2, c % 2, f // 2, f % 2


def remote(src, dst, send, recv, device):
    return pltpu.make_async_remote_copy(
        src_ref=src, dst_ref=dst, send_sem=send, recv_sem=recv, device_id=device, device_id_type=MESH_ID
    )


def block_at(c, half, count):
    return c if half == 0 else 2 * count - 1 - c


def statistics(value):
    row_mean = jnp.mean(value, axis=1, keepdims=True)
    centred = value - row_mean
    inverse = lax.rsqrt(jnp.mean(centred * centred, axis=1, keepdims=True) + EPS)
    return centred * inverse, inverse


def stacked(value):
    return value.reshape(-1, value.shape[-1])


def relative(a, b):
    return (a // 2 + b // 2) % 2 * 2 + (a + b) % 2


def swap(value, axis, bit):
    size = lax.axis_size(axis)
    return lax.ppermute(value, axis, [(i, i ^ bit) for i in range(size)])


def lasting(microseconds):
    return pl.CostEstimate(flops=0, bytes_accessed=int(microseconds * 3.3e6), transcendentals=0)


def params(side=True):
    return pltpu.CompilerParams(has_side_effects=side, vmem_limit_bytes=VMEM_CAP)


def gather_stream(tokens, gain, routes, cotangent, starts, weight, matrix):
    count = lax.axis_size("ctx")
    depth = count // 2
    rows, wide = weight.shape
    part = wide // count
    lanes = part // 3
    half_rows, width = tokens.shape[1:]
    own_rows = 2 * half_rows
    own_experts = EXPERTS // count

    def kernel(
        x_ref, g_ref, e_ref, c_ref, s_ref, wf_ref, of_ref, tok, st, cols, beside, far, diagonal, got, w_ref, o_ref, hot,
        n_ref, d_ref, rs_t, ss_p, ss_up, ss_dn, ss_sib, rs_s, ss_s, rs_w, ss_w, ss_o, rs_o, ss_d, rs_d,
    ):
        c, f, z, y, x, k = place()
        sib = (c, f + 1 - 2 * k)
        partner = (c + 1 - 2 * y, f + 1 - 2 * k)
        up = (c + 2, f)
        down = (c - 2, f)
        holder = k == y
        for h in range(2):
            hat, _ = statistics(x_ref[h].astype(F32))
            n_ref[h] = (hat * g_ref[...]).astype(BF)

        def send_in(h):
            b = block_at(c, h, count)
            return remote(n_ref.at[h], tok.at[b], ss_p.at[h], rs_t.at[b], partner)

        def local_in(h):
            b = block_at(c, h, count)
            return pltpu.make_async_copy(n_ref.at[h], tok.at[b], rs_t.at[b])

        @pl.when(holder)
        def _():
            for h in range(2):
                local_in(h).start()

        @pl.when(jnp.logical_not(holder))
        def _():
            for h in range(2):
                send_in(h).start()

        for zt in range(depth):
            for kt in range(2):
                mine = holder & (z == zt) & (k == kt)

                @pl.when(mine)
                def _():
                    pltpu.make_async_copy(s_ref, st.at[c], rs_s.at[c]).start()

                @pl.when(jnp.logical_not(mine))
                def _(zt=zt, kt=kt):
                    remote(s_ref, st.at[c], ss_s.at[2 * zt + kt], rs_s.at[c], (2 * zt + k, 2 * x + kt)).start()

        goals = [(2 * z + k, (c, (f + 2) % 4)), (2 * z + 1 - k, (c, (sib[1] + 2) % 4)), (2 * z + 1 - k, sib)]

        def columns(pair):
            return w_ref.at[:, pl.ds(pl.multiple_of(pair * part, part), part)]

        def weight_place(shard):
            return cols.at[pl.ds(pl.multiple_of(shard * rows, rows), rows)]

        def weight_send(t):
            pair, dev = goals[t]
            return remote(columns(pair), weight_place(f), ss_w.at[t], rs_w.at[f], dev)

        for number in range(count):
            for j in range(3):
                at = number * part + j * lanes
                w_ref[:, at : at + lanes] = wf_ref[:, j * count * lanes + number * lanes :][:, :lanes].astype(BF)
        for t in range(3):
            weight_send(t).start()
        pltpu.make_async_copy(columns(2 * z + k), weight_place(f), rs_w.at[f]).start()
        o_ref[...] = of_ref[...].astype(BF)
        matrix_far = remote(o_ref, far, ss_o.at[0], rs_o.at[0], goals[0][1])
        matrix_beside = remote(o_ref, beside, ss_o.at[1], rs_o.at[1], sib)
        matrix_on = remote(far, diagonal, ss_o.at[2], rs_o.at[2], sib)
        matrix_far.start()
        matrix_beside.start()

        def slots_send(i):
            ct = (c + i) % count
            return remote(d_ref.at[ct], got.at[c], ss_d.at[i], rs_d.at[c], (ct, f))

        def copy_block(zb, h, ss, dev):
            b = block_at(2 * zb + k, h, count)
            return remote(tok.at[b], tok.at[b], ss, rs_t.at[b], dev)

        for j in range(depth):
            for h in range(2):
                if j == 0:
                    copy_block(z, h, ss_p.at[h], sib).wait_recv()

                    @pl.when(z < depth - 1)
                    def _(h=h):
                        copy_block(z, h, ss_up.at[0, h], up).start()

                    @pl.when(z > 0)
                    def _(h=h):
                        copy_block(z, h, ss_dn.at[0, h], down).start()

                    copy_block(z, h, ss_sib.at[z, h], sib).start()
                    if h == 1:
                        expert = lax.broadcasted_iota(jnp.int32, (EXPERTS, own_rows), 0)
                        chosen = expert == e_ref[...]
                        earlier = lax.broadcasted_iota(jnp.int32, (own_rows, own_rows), 0) <= lax.broadcasted_iota(
                            jnp.int32, (own_rows, own_rows), 1
                        )
                        running = jnp.dot(
                            jnp.where(chosen, 1.0, 0.0).astype(BF),
                            jnp.where(earlier, 1.0, 0.0).astype(BF),
                            preferred_element_type=F32,
                        )
                        rank = jnp.sum(jnp.where(chosen, running, 0.0), axis=0, keepdims=True).astype(jnp.int32) - 1
                        slot = e_ref[...] * CAP + rank
                        index = lax.broadcasted_iota(jnp.int32, (EXPERTS * CAP, own_rows), 0)
                        hot[...] = jnp.where(index == slot, 1.0, 0.0).astype(BF)
                        d_ref[...] = (
                            jnp.dot(hot[...], c_ref[...], preferred_element_type=F32).astype(BF).reshape(d_ref.shape)
                        )
                        for i in range(1, count):
                            slots_send(i).start()
                        pltpu.make_async_copy(d_ref.at[c], got.at[c], rs_d.at[c]).start()
                    continue

                @pl.when(z - j >= 0)
                def _(j=j, h=h):
                    copy_block(z - j, h, ss_p.at[h], sib).wait_recv()

                    @pl.when(z < depth - 1)
                    def _():
                        copy_block(z - j, h, ss_up.at[j, h], up).start()

                    copy_block(z - j, h, ss_sib.at[z - j, h], sib).start()

                @pl.when(z + j <= depth - 1)
                def _(j=j, h=h):
                    copy_block(z + j, h, ss_p.at[h], sib).wait_recv()

                    @pl.when(z > 0)
                    def _():
                        copy_block(z + j, h, ss_dn.at[j, h], down).start()

                    copy_block(z + j, h, ss_sib.at[z + j, h], sib).start()

        matrix_far.wait_recv()
        matrix_on.start()
        for zt in range(depth):
            for h in range(2):
                b = block_at(2 * zt + 1 - k, h, count)
                remote(tok.at[b], tok.at[b], ss_p.at[h], rs_t.at[b], sib).wait_recv()
                copy_block(zt, h, ss_sib.at[zt, h], sib).wait_send()
        for ct in range(count):
            remote(s_ref, st.at[ct], ss_s.at[0], rs_s.at[ct], sib).wait_recv()
        for shard in range(4):
            remote(columns(0), weight_place(shard), ss_w.at[0], rs_w.at[shard], sib).wait_recv()
        for t in range(3):
            weight_send(t).wait_send()
        matrix_far.wait_send()
        matrix_beside.wait()
        matrix_on.wait()
        for i in range(count):
            if i:
                slots_send(i).wait_send()
            remote(d_ref.at[i], got.at[i], ss_d.at[i], rs_d.at[i], sib).wait_recv()

        @pl.when(jnp.logical_not(holder))
        def _():
            for h in range(2):
                send_in(h).wait_send()

        for j in range(depth):

            @pl.when((z < depth - 1) & (z - j >= 0))
            def _(j=j):
                for h in range(2):
                    copy_block(z - j, h, ss_up.at[j, h], up).wait_send()

            @pl.when((z > 0) & (z + j <= depth - 1))
            def _(j=j):
                for h in range(2):
                    copy_block(z + j, h, ss_dn.at[j, h], down).wait_send()

        for zt in range(depth):
            for kt in range(2):
                mine = holder & (z == zt) & (k == kt)

                @pl.when(jnp.logical_not(mine))
                def _(zt=zt, kt=kt):
                    remote(s_ref, st.at[c], ss_s.at[2 * zt + kt], rs_s.at[c], sib).wait_send()

    return pl.pallas_call(
        kernel,
        name="gather_stream",
        cost_estimate=lasting(50),
        out_shape=(
            jax.ShapeDtypeStruct((2 * count, half_rows, width), BF),
            jax.ShapeDtypeStruct((count,) + starts.shape, starts.dtype),
            jax.ShapeDtypeStruct((4 * rows, part), BF),
            *[jax.ShapeDtypeStruct(matrix.shape, BF)] * 3,
            jax.ShapeDtypeStruct((count, own_experts, CAP, width), BF),
            jax.ShapeDtypeStruct((rows, wide), BF),
            jax.ShapeDtypeStruct(matrix.shape, BF),
            jax.ShapeDtypeStruct((EXPERTS * CAP, own_rows), BF),
        ),
        in_specs=[pl.BlockSpec(memory_space=pltpu.VMEM)] * 7,
        out_specs=(ANY,) * 7 + (pl.BlockSpec(memory_space=pltpu.VMEM),) * 3,
        scratch_shapes=[
            pltpu.VMEM((2, half_rows, width), BF), pltpu.VMEM((count, own_experts, CAP, width), BF),
            DMA((2 * count,)), DMA((2,)), DMA((depth, 2)), DMA((depth, 2)), DMA((depth, 2)),
            DMA((count,)), DMA((count,)), DMA((4,)), DMA((3,)), DMA((3,)), DMA((3,)), DMA((count,)), DMA((count,)),
        ],
        compiler_params=params(),
    )(tokens, gain, routes, cotangent, starts, weight, matrix)


TILE = 256


def halves(value, axis):
    size = value.shape[axis] // 2
    at = lax.broadcasted_iota(jnp.int32, value.shape, axis)
    zero = jnp.zeros_like(value)
    return [jnp.where(at < size, value, zero), jnp.where(at >= size, value, zero)]


def attend_forward(stream, columns, start_row, numbers, scale):
    length, width = stream.shape
    tiles = length // TILE
    lanes = 128
    size = lanes // 2

    def kernel(first, x_ref, w_ref, s_ref, out, m16, m32, lse, k_rows, v_turned):
        i = pl.program_id(0)
        own = pl.ds(pl.multiple_of(i * TILE, TILE), TILE)
        rows = x_ref[...]
        projected = jnp.dot(rows, w_ref[...], preferred_element_type=F32).astype(BF)
        out[...] = projected
        query, key, value = [projected[:, j * lanes : (j + 1) * lanes] for j in range(3)]
        k_rows[own, :] = key
        v_turned[:, own] = value.T
        queries = halves((query * scale).T, 0)
        start = s_ref[...]
        key_row = lax.broadcasted_iota(jnp.int32, (TILE, TILE), 0)
        query_column = i * TILE + lax.broadcasted_iota(jnp.int32, (TILE, TILE), 1)

        def step(j, carried):
            at = pl.multiple_of(j * TILE, TILE)
            keys = k_rows[pl.ds(at, TILE), :]
            seen = (key_row + at <= query_column) & (key_row + at >= start)
            out = []
            for h in range(2):
                top, total, mixed = carried[h]
                score = jnp.where(seen, jnp.dot(keys, queries[h], preferred_element_type=F32), NEGATIVE)
                new_top = jnp.maximum(top, jnp.max(score, axis=0, keepdims=True))
                weight = jnp.exp(score - new_top)
                shrink = jnp.exp(top - new_top)
                total = total * shrink + jnp.sum(weight, axis=0, keepdims=True)
                values = v_turned[h * size : (h + 1) * size, pl.ds(at, TILE)]
                mixed = mixed * shrink + jnp.dot(values, weight.astype(BF), preferred_element_type=F32)
                out.append((new_top, total, mixed))
            return tuple(out)

        begin = (
            jnp.full((1, TILE), NEGATIVE, F32),
            jnp.zeros((1, TILE), F32),
            jnp.zeros((size, TILE), F32),
        )
        done = lax.fori_loop(first[i], i + 1, step, (begin, begin))
        mixed = jnp.concatenate([part / total for _, total, part in done], axis=0)
        m32[...] = mixed
        m16[...] = mixed.T.astype(BF)
        lse[...] = jnp.concatenate([top + jnp.log(total) for top, total, _ in done], axis=0)

    tile = pl.BlockSpec((TILE, lanes), lambda i, n: (i, 0))
    turned = pl.BlockSpec((lanes, TILE), lambda i, n: (0, i))
    return pl.pallas_call(
        kernel,
        name="attend_forward",
        cost_estimate=lasting(22),
        grid_spec=pltpu.PrefetchScalarGridSpec(
            num_scalar_prefetch=1,
            grid=(tiles,),
            in_specs=[
                pl.BlockSpec((TILE, width), lambda i, n: (i, 0)),
                pl.BlockSpec((width, 3 * lanes), lambda i, n: (0, 0)),
                pl.BlockSpec((1, TILE), lambda i, n: (0, i)),
            ],
            out_specs=[
                pl.BlockSpec((TILE, 3 * lanes), lambda i, n: (i, 0)),
                tile,
                turned,
                pl.BlockSpec((2, TILE), lambda i, n: (0, i)),
            ],
            scratch_shapes=[pltpu.VMEM((length, lanes), BF), pltpu.VMEM((lanes, length), BF)],
        ),
        out_shape=(
            jax.ShapeDtypeStruct((length, 3 * lanes), BF),
            jax.ShapeDtypeStruct((length, lanes), BF),
            jax.ShapeDtypeStruct((lanes, length), F32),
            jax.ShapeDtypeStruct((2, length), F32),
        ),
        compiler_params=params(False),
    )(numbers, stream, columns, start_row)


def backward_local(qkv, grad, mixed, logs, start_row, numbers, scale, stream, rows, cotangents, active, grad_hidden):
    length = qkv.shape[0]
    lanes = 128
    tiles = length // TILE
    size = lanes // 2
    _, number, count, cap, width = rows.shape
    total_rows, units = active.shape[1:]
    assert tiles == number

    def kernel(
        first, q_ref, k_ref, v_ref, g_ref, m_ref, l_ref, s_ref, x_ref, r_ref, g0_ref, g1_ref, g2_ref, g3_ref, a_ref, h_ref,
        out, weight, da, db, acc_k, acc_v, k_turned,
    ):
        i = pl.program_id(0)
        gradient = jnp.concatenate([stacked(ref[...]) for ref in (g0_ref, g1_ref, g2_ref, g3_ref)], axis=0)
        da[0] = lax.dot_general(stacked(r_ref[...]), h_ref[0], CONTRACT_FIRST, preferred_element_type=F32)
        db[0] = lax.dot_general(a_ref[0], gradient, CONTRACT_FIRST, preferred_element_type=F32)

        @pl.when(i == 0)
        def _():
            acc_k[...] = jnp.zeros_like(acc_k)
            acc_v[...] = jnp.zeros_like(acc_v)
            for t in range(tiles):
                k_turned[:, t * TILE : (t + 1) * TILE] = k_ref[t * TILE : (t + 1) * TILE, :].T

        scaled = q_ref[...] * scale
        grads = g_ref[...]
        turned = grads.T
        queries, queries_turned = halves(scaled, 1), halves(scaled.T, 0)
        grad_rows, grads_turned = halves(grads, 1), halves(turned, 0)
        product = turned.astype(F32) * m_ref[...]
        deltas = [jnp.sum(product[h * size : (h + 1) * size], axis=0, keepdims=True) for h in range(2)]
        logs_row = [l_ref[h : h + 1, :] for h in range(2)]
        start = s_ref[...]
        key_row = lax.broadcasted_iota(jnp.int32, (TILE, TILE), 0)
        query_column = i * TILE + lax.broadcasted_iota(jnp.int32, (TILE, TILE), 1)

        def step(j, running):
            at = pl.multiple_of(j * TILE, TILE)
            keys = k_ref[pl.ds(at, TILE), :]
            values = v_ref[pl.ds(at, TILE), :]
            seen = (key_row + at <= query_column) & (key_row + at >= start)
            key_sum = jnp.zeros((TILE, lanes), F32)
            value_sum = jnp.zeros((TILE, lanes), F32)
            out = []
            for h in range(2):
                score = jnp.dot(keys, queries_turned[h], preferred_element_type=F32)
                weight = jnp.exp(jnp.where(seen, score - logs_row[h], NEGATIVE))
                grad_weight = jnp.dot(values, grads_turned[h], preferred_element_type=F32)
                grad_score = (weight * (grad_weight - deltas[h])).astype(BF)
                value_sum += jnp.dot(weight.astype(BF), grad_rows[h], preferred_element_type=F32)
                key_sum += jnp.dot(grad_score, queries[h], preferred_element_type=F32)
                part = k_turned[h * size : (h + 1) * size, pl.ds(at, TILE)]
                out.append(running[h] + jnp.dot(part, grad_score, preferred_element_type=F32))
            acc_k[pl.ds(at, TILE), :] += key_sum
            acc_v[pl.ds(at, TILE), :] += value_sum
            return tuple(out)

        zero = jnp.zeros((size, TILE), F32)
        total = lax.fori_loop(first[i], i + 1, step, (zero, zero))
        own = pl.ds(pl.multiple_of(i * TILE, TILE), TILE)
        out[own, 0:lanes] = (jnp.concatenate(total, axis=0) * scale).T.astype(BF)

        @pl.when(i == tiles - 1)
        def _():
            out[:, lanes : 2 * lanes] = acc_k[...].astype(BF)
            out[:, 2 * lanes : 3 * lanes] = acc_v[...].astype(BF)
            weight[...] = lax.dot_general(x_ref[...], out[...], CONTRACT_FIRST, preferred_element_type=F32).astype(BF)

    tile = pl.BlockSpec((TILE, lanes), lambda i, n: (i, 0))
    quarter = pl.BlockSpec((count, 1, cap, width), lambda i, n: (0, i, 0, 0))
    wide = pl.BlockSpec((1, total_rows, units), lambda i, n: (i, 0, 0))
    return pl.pallas_call(
        kernel,
        name="backward_local",
        cost_estimate=lasting(30),
        grid_spec=pltpu.PrefetchScalarGridSpec(
            num_scalar_prefetch=1,
            grid=(tiles,),
            in_specs=[
                tile,
                pl.BlockSpec((length, lanes), lambda i, n: (0, 1)),
                pl.BlockSpec((length, lanes), lambda i, n: (0, 2)),
                tile,
                pl.BlockSpec((lanes, TILE), lambda i, n: (0, i)),
                pl.BlockSpec((2, TILE), lambda i, n: (0, i)),
                pl.BlockSpec((1, TILE), lambda i, n: (0, i)),
                pl.BlockSpec((length, width), lambda i, n: (0, 0), pipeline_mode=pl.Buffered(1)),
                pl.BlockSpec((4, 1, count, cap, width), lambda i, n: (0, i, 0, 0, 0)),
                quarter,
                quarter,
                quarter,
                quarter,
                wide,
                wide,
            ],
            out_specs=[
                pl.BlockSpec((length, 3 * lanes), lambda i, n: (0, 0)),
                pl.BlockSpec((width, 3 * lanes), lambda i, n: (0, 0)),
                pl.BlockSpec((1, width, units), lambda i, n: (i, 0, 0)),
                pl.BlockSpec((1, units, width), lambda i, n: (i, 0, 0)),
            ],
            scratch_shapes=[
                pltpu.VMEM((length, lanes), F32),
                pltpu.VMEM((length, lanes), F32),
                pltpu.VMEM((lanes, length), BF),
            ],
        ),
        out_shape=(
            jax.ShapeDtypeStruct((length, 3 * lanes), BF),
            jax.ShapeDtypeStruct((width, 3 * lanes), BF),
            jax.ShapeDtypeStruct((number, width, units), F32),
            jax.ShapeDtypeStruct((number, units, width), F32),
        ),
        compiler_params=params(False),
    )(numbers, qkv, qkv, qkv, grad, mixed, logs, start_row, stream, rows, *cotangents, active, grad_hidden)


ROOT = math.sqrt(2.0 / math.pi)
CUBIC = 0.044715


def experts_exchange(by_head, out_proj, tokens, dispatch, gain, cotangent, grads, first_proj, second_proj):
    count = lax.axis_size("ctx")
    half_rows, lanes = by_head.shape[1:]
    rows, width = tokens.shape
    number, _, units = first_proj.shape
    cap = CAP
    total_rows = 4 * count * cap
    quarter = width // 4
    slab = quarter // count
    splits = 2
    part_units = units // splits

    def kernel(
        a_ref, w0_ref, w1_ref, w2_ref, w3_ref, x_ref, d_ref, g_ref, c_ref, g0_ref, g1_ref, g2_ref, g3_ref, first_ref, second_ref,
        mixed, middle, rows_out, active_out, hidden_out, heads, grad_middle, gain_out, later,
        routed, slots, rows_v, g_buf, first_buf, second_buf, active_v, hidden_v, back_v, back_near, back_far, back_got,
        out_v, out_near, own_v, far_v, out_got, summed, home_got, back, shard_near, shard_far, shard_got, shard_v,
        ss_m, rs_m, ss_1, rs_1, ss_x, rs_x, ss_s, rs_s, ss_f, rs_f, ss_bn, rs_bn, ss_bf, rs_bf, ss_on, rs_on, ss_h, rs_h,
        ss_t, rs_t, ss_n, rs_n, ss_w, rs_w, l_first, l_second, l_g, st_r, st_a, st_h, st_o, ss_of, rs_of, st_w,
    ):
        c, f, z, y, x, k = place()
        sib = (c, f + 1 - 2 * k)
        xn = (c, (f + 2) % 4)
        pair = 2 * z + k
        target = 2 * x + y

        def load_first(e, u):
            cols = pl.ds(u * part_units, part_units)
            return pltpu.make_async_copy(first_ref.at[e, :, cols], first_buf.at[u], l_first.at[u])

        def load_second(e, u):
            part = pl.ds(u * part_units, part_units)
            return pltpu.make_async_copy(second_ref.at[e, part], second_buf.at[u], l_second.at[u])

        def load_grads(e, slot):
            refs = (g0_ref, g1_ref, g2_ref, g3_ref)
            return [pltpu.make_async_copy(ref.at[:, e], g_buf.at[slot, j], l_g.at[slot, j]) for j, ref in enumerate(refs)]

        def there(half):
            column = (2 * relative(z, target) + k) * lanes
            return mixed.at[half, :, pl.ds(pl.multiple_of(column, lanes), lanes)]

        def send(i, half):
            ct = (c + i) % count
            return remote(
                a_ref.at[block_at(ct, half, count)], there(half), ss_m.at[i, half], rs_m.at[pair, half], (ct, target)
            )

        def keep(half):
            return pltpu.make_async_copy(a_ref.at[block_at(c, half, count)], there(half), rs_m.at[pair, half])

        for half in range(2):
            for i in range(1, count):
                send(i, half).start()

            @pl.when(k == y)
            def _(half=half):
                keep(half).start()

            @pl.when(k != y)
            def _(half=half):
                send(0, half).start()

        for u in range(splits):
            load_first(0, u).start()
            load_second(0, u).start()
        for load in load_grads(0, 0):
            load.start()

        for half in range(2):
            for other in range(count):
                column = (2 * relative(other // 2, f) + other % 2) * lanes
                cols = pl.ds(pl.multiple_of(column, lanes), lanes)
                remote(a_ref.at[0], mixed.at[half, :, cols], ss_m.at[0, half], rs_m.at[other, half], sib).wait_recv()
            here = pl.ds(half * half_rows, half_rows)
            value = x_ref[here, :].astype(F32)
            for j, w_ref in enumerate((w0_ref, w1_ref, w2_ref, w3_ref)):
                cols = pl.ds(j * quarter, quarter)
                value += jnp.dot(mixed[half, :, cols], w_ref[...], preferred_element_type=F32)
            middle[here, :] = value
            hat, _ = statistics(value)
            routed[here, :] = (hat * g_ref[...]).astype(BF)
        slots[...] = jnp.dot(d_ref[...], routed[...], preferred_element_type=F32).astype(BF).reshape(slots.shape)

        def rows_first(e, i):
            owner = (c + i) % count
            return remote(slots.at[owner, e], rows_v.at[0, e, c], ss_1.at[e], rs_1.at[e], (owner, f))

        def hop(e, rel, dst, send_sem, recv_sem, dev):
            return remote(rows_v.at[rel, e], rows_v.at[dst, e], send_sem.at[e], recv_sem.at[e], dev)

        def rows_across(e):
            return hop(e, 0, 2, ss_x, rs_x, xn)

        def rows_share(e):
            return hop(e, 0, 1, ss_s, rs_s, sib)

        def rows_share_far(e):
            return hop(e, 2, 3, ss_f, rs_f, sib)

        def start_rows(e, carry):
            for i in range(1, count):
                rows_first(e, i).start()
            pltpu.make_async_copy(slots.at[c, e], rows_v.at[0, e, c], rs_1.at[e]).start()
            return carry

        lax.fori_loop(0, number, start_rows, 0)

        def forward(e):
            remote(rows_v.at[0, e], rows_v.at[0, e], ss_x.at[e], rs_1.at[e], sib).wait_recv()
            rows_across(e).start()
            rows_share(e).start()

        def forward_far(e):
            rows_across(e).wait_recv()
            rows_share_far(e).start()

        def near_send(e, j):
            return remote(back_v.at[2 * j + 1, e], back_near.at[j, e], ss_bn.at[e, j], rs_bn.at[e, j], sib)

        def near_out(e, j):
            return remote(out_v.at[2 * j + 1, e], out_near.at[j, e], ss_on.at[e, j], rs_on.at[e, j], sib)

        def far_send(e):
            return remote(back_far.at[e], back_got.at[e], ss_bf.at[e], rs_bf.at[e], xn)

        def store_own(e):
            return pltpu.make_async_copy(own_v.at[e], later.at[:, pl.ds(pl.multiple_of(slab + e * cap, cap), cap)], st_o.at[e])

        def far_out(e):
            return remote(far_v.at[e], out_got.at[e], ss_of.at[e], rs_of.at[e], xn)

        def store_rows(e):
            return pltpu.make_async_copy(rows_v.at[:, e], rows_out.at[:, e], st_r.at[e])

        def store_active(e, slot):
            return pltpu.make_async_copy(active_v.at[slot], active_out.at[e], st_a.at[slot])

        def store_hidden(e, slot):
            return pltpu.make_async_copy(hidden_v.at[slot], hidden_out.at[e], st_h.at[slot])

        def sum_far(e):
            near_send(e, 1).wait_recv()
            back_far[e] = (back_v[2, e].astype(F32) + back_near[1, e].astype(F32)).astype(BF)
            far_send(e).start()

        def sum_outputs(e):
            for j in range(2):
                near_out(e, j).wait_recv()
            own_v[e] = (out_v[0, e].astype(F32) + out_near[0, e].astype(F32)).astype(BF)
            far_v[e] = (out_v[2, e].astype(F32) + out_near[1, e].astype(F32)).astype(BF)

        def home(e, i):
            ct = (c + i) % count
            return remote(summed.at[e, ct], home_got.at[c, e], ss_h.at[e], rs_h, (ct, f))

        def go_home(e):
            near_send(e, 0).wait_recv()
            far_send(e).wait_recv()
            summed[e] = (
                back_v[0, e].astype(F32) + back_near[0, e].astype(F32) + back_got[e].astype(F32)
            ).astype(BF)
            for i in range(1, count):
                home(e, i).start()
            pltpu.make_async_copy(summed.at[e, c], home_got.at[c, e], rs_h).start()

        def expert(e, carry):
            slot = e % 2

            @pl.when(e + 1 < number)
            def _():
                for load in load_grads(e + 1, 1 - slot):
                    load.start()

            @pl.when(e + 2 < number)
            def _():
                forward(e + 2)

            @pl.when(e + 1 < number)
            def _():
                forward_far(e + 1)

            rows_share(e).wait_recv()
            rows_share_far(e).wait_recv()
            store_rows(e).start()
            for load in load_grads(e, slot):
                load.wait()

            @pl.when(e >= 2)
            def _():
                store_active(e, slot).wait()
                store_hidden(e, slot).wait()

            row = rows_v[:, e].reshape(total_rows, width)
            grad = g_buf[slot].reshape(total_rows, width)
            term = jnp.zeros((total_rows, width), F32)
            firsts, seconds = [], []
            for u in range(splits):
                load_first(e, u).wait()
                load_second(e, u).wait()
                first = first_buf[u].astype(BF)
                second = second_buf[u].astype(BF)
                seconds.append(second)
                hidden = jnp.dot(row, first, preferred_element_type=F32)
                upstream = lax.dot_general(grad, second, CONTRACT_LAST, preferred_element_type=F32)
                bent = jnp.tanh(ROOT * (hidden + CUBIC * hidden * hidden * hidden))
                cols = pl.ds(u * part_units, part_units)
                active_v[slot, :, cols] = (0.5 * hidden * (1.0 + bent)).astype(BF)
                slope = 0.5 * (1.0 + bent) + 0.5 * hidden * (1.0 - bent * bent) * (
                    ROOT * (1.0 + 3.0 * CUBIC * hidden * hidden)
                )
                grad_hidden = (upstream * slope).astype(BF)
                hidden_v[slot, :, cols] = grad_hidden
                term += lax.dot_general(grad_hidden, first, CONTRACT_LAST, preferred_element_type=F32)
            back_v[:, e] = term.astype(BF).reshape(4, count, cap, width)
            near_send(e, 1).start()
            near_send(e, 0).start()
            result = jnp.zeros((total_rows, width), F32)
            for u in range(splits):
                cols = pl.ds(u * part_units, part_units)
                result += jnp.dot(active_v[slot, :, cols], seconds[u], preferred_element_type=F32)
            out_v[:, e] = result.astype(BF).reshape(4, count, cap, width)
            near_out(e, 1).start()
            near_out(e, 0).start()

            @pl.when(e + 1 < number)
            def _():
                for u in range(splits):
                    load_first(e + 1, u).start()
                    load_second(e + 1, u).start()

            store_active(e, slot).start()
            store_hidden(e, slot).start()

            @pl.when(e >= 1)
            def _():
                sum_far(e - 1)
                sum_outputs(e - 1)

            @pl.when(e >= 3)
            def _():
                go_home(e - 3)

            return carry

        forward(0)
        forward(1)
        forward_far(0)
        lax.fori_loop(0, number, expert, 0)
        sum_far(number - 1)
        sum_outputs(number - 1)
        for e in range(number):
            far_out(e).start()
        for e in range(number - 3, number):
            go_home(e)
        hat, inverse = statistics(middle[...])
        remote(home_got, home_got, ss_h.at[0], rs_h, sib).wait_recv()

        returned = lax.dot_general(d_ref[...], home_got[...].reshape(-1, width), CONTRACT_FIRST, preferred_element_type=F32)
        scaled = returned * g_ref[...]
        mean_grad = jnp.mean(scaled, axis=1, keepdims=True)
        mean_proj = jnp.mean(scaled * hat, axis=1, keepdims=True)
        gain_out[...] = jnp.sum(returned * hat, axis=0, keepdims=True)
        gradient = c_ref[...].astype(F32) + inverse * (scaled - mean_grad - hat * mean_proj)
        grad_middle[...] = gradient
        low = gradient.astype(BF)
        for j, w_ref in enumerate((w0_ref, w1_ref, w2_ref, w3_ref)):
            back[:, :, j * quarter : (j + 1) * quarter] = (
                lax.dot_general(low, w_ref[...], CONTRACT_LAST, preferred_element_type=F32)
                .astype(BF)
                .reshape(2, half_rows, quarter)
            )

        def part(half, number_of_pair):
            column = (2 * relative(number_of_pair // 2, f) + number_of_pair % 2) * lanes
            return back.at[half, :, pl.ds(pl.multiple_of(column, lanes), lanes)]

        def send_heads(i, half):
            other = (2 * z + k + i) % count
            b = block_at(c, half, count)
            dev = (2 * (other // 2) + k, 2 * x + other % 2)
            return remote(part(half, other), heads.at[b], ss_t.at[i, half], rs_t.at[b], dev)

        for i in range(1, count):
            for half in range(2):
                send_heads(i, half).start()

        @pl.when(k == y)
        def _():
            for half in range(2):
                b = block_at(c, half, count)
                pltpu.make_async_copy(part(half, 2 * z + k), heads.at[b], rs_t.at[b]).start()

        @pl.when(k != y)
        def _():
            for half in range(2):
                send_heads(0, half).start()

        for e in range(number):
            for j in range(2):
                near_send(e, j).wait_send()

        def term_place(j):
            return back_v.at[j, 0 : quarter // (count * cap)]

        def shard_term(j):
            half_quarter = quarter // 2
            mixed_part = [mixed[half, :, j * quarter : (j + 1) * quarter] for half in range(2)]
            value = sum(
                lax.dot_general(
                    mixed_part[half], low[half * half_rows : (half + 1) * half_rows], CONTRACT_FIRST, preferred_element_type=F32
                )
                for half in range(2)
            )
            return value.astype(BF).reshape(shard_far.shape)

        def core_send(j):
            return remote(term_place(2 * j + 1), shard_near.at[j], ss_n.at[j], rs_n.at[j], sib)

        across = remote(shard_far, shard_got, ss_w, rs_w, xn)
        for j in (1, 0):
            back_v[2 * j + 1, 0 : quarter // (count * cap)] = shard_term(2 * j + 1)
            core_send(j).start()
        own_far = shard_term(2)
        core_send(1).wait_recv()
        shard_far[...] = (own_far.astype(F32) + shard_near[1].astype(F32)).astype(BF)
        across.start()
        own_near = shard_term(0)
        core_send(0).wait_recv()

        def finish_output(e, carry):
            far_out(e).wait_recv()
            own_v[e] = (own_v[e].astype(F32) + out_got[e].astype(F32)).astype(BF)
            store_own(e).start()
            return carry

        lax.fori_loop(0, number, finish_output, 0)
        across.wait_recv()
        shard_v[...] = (
            (own_near.astype(F32) + shard_near[0].astype(F32) + shard_got[...].astype(F32)).astype(BF).reshape(shard_v.shape)
        )
        store_shard = pltpu.make_async_copy(shard_v, later.at[:, pl.ds(0, slab)], st_w)
        store_shard.start()

        for b in range(2 * count):
            remote(part(0, 0), heads.at[b], ss_t.at[0, 0], rs_t.at[b], sib).wait_recv()

        def leave(e, carry):
            sent = pl.ds(0, count - 1)
            remote(slots.at[sent, e], rows_v.at[0, e, sent], ss_1.at[e], rs_1.at[e], sib).wait_send()
            remote(summed.at[e, sent], home_got.at[sent, e], ss_h.at[e], rs_h, sib).wait_send()
            rows_across(e).wait_send()
            rows_share(e).wait_send()
            rows_share_far(e).wait_send()
            far_send(e).wait_send()
            for j in range(2):
                near_out(e, j).wait_send()
            store_own(e).wait()
            far_out(e).wait_send()
            store_rows(e).wait()
            return carry

        lax.fori_loop(0, number, leave, 0)
        store_shard.wait()
        for e in (number - 2, number - 1):
            store_active(e, e % 2).wait()
            store_hidden(e, e % 2).wait()
        for i in range(1, count):
            for half in range(2):
                send(i, half).wait_send()
                send_heads(i, half).wait_send()

        @pl.when(k != y)
        def _():
            for half in range(2):
                send(0, half).wait_send()
                send_heads(0, half).wait_send()

        core_send(0).wait_send()
        core_send(1).wait_send()
        across.wait_send()

    vmem = pl.BlockSpec(memory_space=pltpu.VMEM)
    block = (count, cap, width)
    low = lambda *shape: pltpu.VMEM(shape, BF)
    fold = (quarter // (count * cap),) + block
    return pl.pallas_call(
        kernel,
        name="experts_exchange",
        cost_estimate=lasting(100),
        out_shape=(
            jax.ShapeDtypeStruct((2, half_rows, width), BF),
            jax.ShapeDtypeStruct((rows, width), F32),
            jax.ShapeDtypeStruct((4, number) + block, BF),
            jax.ShapeDtypeStruct((number, total_rows, units), BF),
            jax.ShapeDtypeStruct((number, total_rows, units), BF),
            jax.ShapeDtypeStruct((2 * count, half_rows, lanes), BF),
            jax.ShapeDtypeStruct((rows, width), F32),
            jax.ShapeDtypeStruct((1, width), F32),
            jax.ShapeDtypeStruct((count, slab + number * cap, width), BF),
        ),
        in_specs=[ANY] + [vmem] * 8 + [ANY] * 6,
        out_specs=(vmem, vmem, ANY, ANY, ANY, ANY, vmem, vmem, ANY),
        scratch_shapes=[
            low(rows, width), low(count, number, cap, width), low(4, number, *block), low(2, 4, *block),
            pltpu.VMEM((splits, width, part_units), F32), pltpu.VMEM((splits, part_units, width), F32),
            low(2, total_rows, units), low(2, total_rows, units),
            low(4, number, *block), low(2, number, *block), low(number, *block), low(number, *block),
            low(4, number, *block), low(2, number, *block), low(number, *block), low(number, *block), low(number, *block),
            low(number, *block), low(count, number, cap, width), low(2, half_rows, width),
            low(2, *fold), low(*fold), low(*fold), low(count, slab, width),
            DMA((count, 2)), DMA((count, 2)), DMA((number,)), DMA((number,)), DMA((number,)), DMA((number,)),
            DMA((number,)), DMA((number,)), DMA((number,)), DMA((number,)), DMA((number, 2)), DMA((number, 2)),
            DMA((number,)), DMA((number,)), DMA((number, 2)), DMA((number, 2)), DMA((number,)), DMA,
            DMA((count, 2)), DMA((2 * count,)), DMA((2,)), DMA((2,)), DMA, DMA,
            DMA((splits,)), DMA((splits,)), DMA((2, 4)), DMA((number,)), DMA((2,)), DMA((2,)), DMA((number,)), DMA((number,)), DMA((number,)), DMA,
        ],
        compiler_params=pltpu.CompilerParams(has_side_effects=True, vmem_limit_bytes=60 << 20),
    )(by_head, *out_proj, tokens, dispatch, gain, cotangent, *grads, first_proj, second_proj)


def after(value, *others):
    return lax.optimization_barrier((value,) + others)[0]


def finish_exchange(grads, parts, out_slab, gain_part, weight):
    count = lax.axis_size("ctx")
    depth = count // 2
    part = grads.shape[2]
    half_rows = grads.shape[1]
    _, rows, _ = parts.shape
    pieces = 4
    piece = rows // pieces

    def kernel(
        a_ref, p_ref, o_ref, g_ref, w_ref, tok_out, w_out, o_out, g_out, w_all, got, held, got_g, sum_g, got_gc,
        ss, rs, ss_r, rs_r, ss_up, ss_dn, rs_z, ss_a, ss_b, rs_o,
        ss_of, rs_of, ss_g, rs_g, ss_gc, rs_gc, ss_wx, rs_wx, ss_ws, rs_ws, ss_wf, rs_wf, loc,
    ):
        c, f, z, y, x, k = place()
        pair = 2 * z + k
        target = 2 * x + y
        sib = (c, f + 1 - 2 * k)
        xn = (c, (f + 2) % 4)
        up = (c + 2, f)
        down = (c - 2, f)

        def columns(ref, number):
            return ref.at[:, pl.ds(pl.multiple_of(number * part, part), part)]

        peers = [
            (2 * z + 1 - y, f, 2 * x + 1 - y),
            (c, (f + 2) % 4, 2 * (1 - x) + y),
            (2 * z + 1 - y, (f + 2) % 4, 2 * (1 - x) + 1 - y),
        ]

        def scatter(d):
            cp, fp, shard = peers[d]
            return remote(p_ref.at[shard], got.at[d], ss_r.at[d], rs_r.at[d], (cp, fp))

        for d in (2, 1, 0):
            scatter(d).start()

        def weight_part(shard, i):
            return w_all.at[shard, pl.ds(i * piece, piece)]

        def weight_across(i):
            return remote(w_ref.at[pl.ds(i * piece, piece)], weight_part(f, i), ss_wx.at[i], rs_wx.at[i], xn)

        def weight_on(i, shard):
            return remote(weight_part(shard, i), weight_part(shard, i), ss_wf.at[i], rs_wf.at[i], sib)

        def weight_pass(i):
            shard = (f + 2) % 4
            remote(weight_part(shard, i), weight_part(shard, i), ss_wf.at[i], rs_wx.at[i], sib).wait_recv()
            weight_on(i, shard).start()

        weight_share = remote(w_ref, w_all.at[f], ss_ws, rs_ws, sib)
        weight_own = pltpu.make_async_copy(w_ref, w_all.at[f], loc)
        for i in range(pieces):
            weight_across(i).start()

        def there(half):
            return columns(tok_out.at[half], pair)

        def send(i, half):
            ct = (c + i) % count
            return remote(a_ref.at[block_at(ct, half, count)], there(half), ss.at[i, half], rs.at[pair, half], (ct, target))

        def send_all(numbers):
            for i in numbers:
                for half in range(2):
                    send(i, half).start()

        send_all(range(2, count, 2))

        def gain_send(j):
            return remote(sum_g.at[j], got_g.at[j], ss_g.at[j], rs_g.at[j], sib if j == 0 else xn)

        sum_g[0] = g_ref[...]
        gain_send(0).start()

        def chain(zb, sem, dev):
            return remote(held.at[zb], held.at[zb], sem, rs_z.at[zb], dev)

        def own_column(zb):
            return remote(held.at[zb], columns(w_out, 2 * zb + k), ss_a.at[zb], rs_o.at[2 * zb + k], (c, target))

        def own_local(zb):
            return pltpu.make_async_copy(held.at[zb], columns(w_out, 2 * zb + k), rs_o.at[2 * zb + k])

        def next_column(zb):
            return remote(
                held.at[zb], columns(w_out, 2 * zb + k), ss_b.at[zb], rs_o.at[2 * zb + k], (2 * z + 1 - y, target)
            )

        def spread(zb):
            next_column(zb).start()

            @pl.when(k == y)
            def _():
                own_local(zb).start()

            @pl.when(k != y)
            def _():
                own_column(zb).start()

        total = p_ref[2 * x + y].astype(F32)
        for d in range(3):
            scatter(d).wait_recv()
            total += got[d].astype(F32)
        held[z] = total.astype(BF)

        @pl.when(z < depth - 1)
        def _():
            chain(z, ss_up.at[0], up).start()

        @pl.when(z > 0)
        def _():
            chain(z, ss_dn.at[0], down).start()

        spread(z)
        send_all(range(1, count, 2))

        @pl.when(k == y)
        def _():
            for half in range(2):
                pltpu.make_async_copy(a_ref.at[block_at(c, half, count)], there(half), rs.at[pair, half]).start()

        @pl.when(k != y)
        def _():
            for half in range(2):
                send(0, half).start()

        weight_share.start()
        weight_own.start()
        gain_send(0).wait_recv()
        sum_g[1] = sum_g[0] + got_g[0]
        gain_send(1).start()

        def slab_spread(i):
            return remote(o_ref, o_out.at[c], ss_of.at[i], rs_of.at[c], ((c + i) % count, f))

        def gain_spread(i):
            return remote(sum_g.at[2], got_gc.at[c], ss_gc.at[i], rs_gc.at[c], ((c + i) % count, f))

        slab_own = pltpu.make_async_copy(o_ref, o_out.at[c], rs_of.at[c])
        slab_own.start()
        for hop in range(1, depth):

            @pl.when(z - hop >= 0)
            def _(hop=hop):
                chain(z - hop, ss_up.at[hop], sib).wait_recv()

                @pl.when(z < depth - 1)
                def _():
                    chain(z - hop, ss_up.at[hop], up).start()

                spread(z - hop)

            @pl.when(z + hop <= depth - 1)
            def _(hop=hop):
                chain(z + hop, ss_dn.at[hop], sib).wait_recv()

                @pl.when(z > 0)
                def _():
                    chain(z + hop, ss_dn.at[hop], down).start()

                spread(z + hop)

            weight_pass(hop - 1)
            if hop == 1:
                gain_send(1).wait_recv()
                sum_g[2] = sum_g[1] + got_g[1]
                for i in range(1, count):
                    gain_spread(i).start()
                    slab_spread(i).start()
        for i in range(depth - 1, pieces):
            weight_pass(i)
        total_g = sum_g[2]
        for i in range(1, count):
            cs = (c + i) % count
            remote(sum_g.at[2], got_gc.at[cs], ss_gc.at[i], rs_gc.at[cs], sib).wait_recv()
            total_g += got_gc[cs]
        g_out[...] = total_g

        gain_send(0).wait_send()
        gain_send(1).wait_send()
        for i in range(pieces):
            weight_across(i).wait_send()
            weight_on(i, (f + 2) % 4).wait_send()
            remote(weight_part(0, i), weight_part(0, i), ss_wf.at[i], rs_wf.at[i], sib).wait_recv()
        weight_share.wait()
        weight_own.wait()
        for d in range(3):
            scatter(d).wait_send()
        for other in range(count):
            for half in range(2):
                remote(a_ref.at[0], columns(tok_out.at[half], other), ss.at[0, half], rs.at[other, half], sib).wait_recv()
            remote(held.at[0], columns(w_out, other), ss_a.at[0], rs_o.at[other], sib).wait_recv()
        for i in range(1, count):
            for half in range(2):
                send(i, half).wait_send()
            gain_spread(i).wait_send()
            slab_spread(i).wait_send()
            cs = (c + i) % count
            remote(o_ref, o_out.at[cs], ss_of.at[i], rs_of.at[cs], sib).wait_recv()
        slab_own.wait()

        @pl.when(k != y)
        def _():
            for half in range(2):
                send(0, half).wait_send()
            for zb in range(depth):
                own_column(zb).wait_send()

        for zb in range(depth):
            next_column(zb).wait_send()
        for hop in range(depth):

            @pl.when((z < depth - 1) & (z - hop >= 0))
            def _(hop=hop):
                chain(z - hop, ss_up.at[hop], up).wait_send()

            @pl.when((z > 0) & (z + hop <= depth - 1))
            def _(hop=hop):
                chain(z + hop, ss_dn.at[hop], down).wait_send()

    vmem = pl.BlockSpec(memory_space=pltpu.VMEM)
    eighth = gain_part.shape
    return pl.pallas_call(
        kernel,
        name="finish_exchange",
        cost_estimate=lasting(60),
        out_shape=(
            jax.ShapeDtypeStruct((2, half_rows, count * part), BF),
            jax.ShapeDtypeStruct((rows, count * part), BF),
            jax.ShapeDtypeStruct((count,) + out_slab.shape, BF),
            jax.ShapeDtypeStruct(eighth, F32),
            jax.ShapeDtypeStruct((4,) + weight.shape, BF),
        ),
        in_specs=[vmem] * 5,
        out_specs=(ANY, ANY, ANY, vmem, ANY),
        scratch_shapes=[
            pltpu.VMEM((3, rows, part), BF),
            pltpu.VMEM((depth, rows, part), BF),
            pltpu.VMEM((2,) + eighth, F32),
            pltpu.VMEM((3,) + eighth, F32),
            pltpu.VMEM((count,) + eighth, F32),
            DMA((count, 2)), DMA((count, 2)), DMA((3,)), DMA((3,)), DMA((depth,)), DMA((depth,)), DMA((depth,)),
            DMA((depth,)), DMA((depth,)), DMA((count,)),
            DMA((count,)), DMA((count,)), DMA((2,)), DMA((2,)), DMA((count,)), DMA((count,)),
            DMA((pieces,)), DMA((pieces,)), DMA, DMA, DMA((pieces,)), DMA((pieces,)), DMA,
        ],
        compiler_params=params(),
    )(grads, parts, out_slab, gain_part, weight)


def finish_local(
    grad_projected, projection, tokens, gain, grad_middle, middle, dispatch, expert_rows, weight_grad, weight, own_gain, out_slabs
):
    rows, width = tokens.shape
    quarter, wide = weight.shape
    lanes = 128
    part = 3 * lanes
    count = wide // part

    def kernel(p_ref, w_ref, x_ref, g_ref, m_ref, mid_ref, d_ref, e_ref, wg_ref, wl_ref, og_ref, o_ref, block, token, wout, gout, oout, acc):
        j = pl.program_id(0)
        acc[j] = lax.dot_general(p_ref[...], w_ref[0], CONTRACT_LAST, preferred_element_type=F32)

        @pl.when(j == 0)
        def _():
            summed = lax.dot_general(d_ref[...], e_ref[...], CONTRACT_FIRST, preferred_element_type=F32)
            block[...] = (mid_ref[...] + summed).astype(BF)
            oout[...] = o_ref[...].astype(F32)

        @pl.when(j == 1)
        def _():
            total = jnp.zeros((quarter, 1), F32)
            for number in range(count):
                for kind in range(3):
                    at = number * part + kind * lanes
                    value = wg_ref[:, at : at + lanes].astype(F32)
                    to = (kind * count + number) * lanes
                    wout[:, to : to + lanes] = value
                    total += jnp.sum(value * wl_ref[:, at : at + lanes].astype(F32), axis=1, keepdims=True)
            gout[...] = total / og_ref[...]

        @pl.when(j == 3)
        def _():
            hat, inverse = statistics(x_ref[...].astype(F32))
            scaled = jnp.concatenate([acc[i] for i in range(4)], axis=1) * g_ref[...]
            mean_grad = jnp.mean(scaled, axis=1, keepdims=True)
            mean_proj = jnp.mean(scaled * hat, axis=1, keepdims=True)
            token[...] = m_ref[...] + inverse * (scaled - mean_grad - hat * mean_proj)

    def whole(value):
        return pl.BlockSpec(value.shape, lambda j: (0,) * value.ndim)

    shapes = (
        jax.ShapeDtypeStruct((rows, width), BF),
        jax.ShapeDtypeStruct((rows, width), F32),
        jax.ShapeDtypeStruct((quarter, wide), F32),
        jax.ShapeDtypeStruct((quarter, 1), F32),
        jax.ShapeDtypeStruct((quarter, width), F32),
    )
    rest = (tokens, gain, grad_middle, middle, dispatch, expert_rows, weight_grad, weight, own_gain, out_slabs)
    return pl.pallas_call(
        kernel,
        name="finish_local",
        cost_estimate=lasting(9),
        grid=(4,),
        in_specs=[whole(grad_projected), pl.BlockSpec((1, quarter, wide), lambda j: (j, 0, 0))] + [whole(v) for v in rest],
        out_specs=[whole(v) for v in shapes],
        out_shape=shapes,
        scratch_shapes=[pltpu.VMEM((4, rows, quarter), F32)],
        compiler_params=params(False),
    )(grad_projected, projection, *rest)


def by_head_pairs(
    tokens, doc_starts, expert_ids, query_key_value_weight, output_weight_matrix, expert_in, expert_out, gain_one, gain_two, grad_output
):
    half_rows = tokens.shape[3]
    width = tokens.shape[4]
    count = lax.axis_size("ctx")
    rows = 2 * half_rows
    length = count * rows
    scale = (width // HEADS) ** (-0.5)
    f = lax.axis_index("fsdp")
    lanes = 2 * (width // HEADS)
    shard_rows = width // 4
    own_tokens = tokens.reshape(rows, width)
    cotangent = grad_output.reshape(rows, width)
    gain_row = gain_one.reshape(1, width)
    stream, starts, columns, out_beside, out_far, out_diagonal, grads_near, qkv_low, out_own, dispatch = gather_stream(
        own_tokens.reshape(2, half_rows, width),
        gain_row,
        expert_ids.reshape(1, rows),
        cotangent,
        doc_starts.reshape(2, half_rows),
        query_key_value_weight,
        output_weight_matrix,
    )
    grads_far = swap(grads_near, "fsdp", 2)
    stream = stream.reshape(length, width)
    start_row = jnp.concatenate([starts[:, 0].reshape(-1), starts[::-1, 1].reshape(-1)])[None]
    numbers = jnp.min(start_row.reshape(-1, TILE), axis=1) // TILE
    qkv, mixed16, mixed32, logs = attend_forward(stream, columns, start_row, numbers, scale)
    grads_far = after(grads_far, mixed16)
    all_grads = [grads_near, swap(grads_near, "fsdp", 1), grads_far, swap(grads_far, "fsdp", 1)]
    mixed, middle, all_rows, active, grad_hidden, grad_heads, grad_middle, grad_gain_two, later = experts_exchange(
        mixed16.reshape(2 * count, half_rows, lanes),
        [out_own, out_beside, out_far, out_diagonal],
        own_tokens,
        dispatch,
        gain_two.reshape(1, width),
        cotangent,
        all_grads,
        expert_in,
        expert_out,
    )
    home = lax.all_to_all(later, "ctx", split_axis=0, concat_axis=0, tiled=True)
    own_grads, parts, grad_in, grad_outw = backward_local(
        qkv,
        after(grad_heads, later).reshape(length, lanes),
        mixed32,
        logs,
        start_row,
        numbers,
        scale,
        stream,
        all_rows,
        all_grads,
        active,
        grad_hidden,
    )
    home = after(home, own_grads)
    slab_rows = shard_rows // count
    out_slab = jnp.sum(home[:, :slab_rows].astype(F32), axis=0).astype(BF)
    back_rows = home[:, slab_rows:]
    grad_projected, weight_grad, shard_out, gain_sum, projection = finish_exchange(
        own_grads.reshape(2 * count, half_rows, 3 * lanes),
        parts.reshape(4, shard_rows, 3 * lanes),
        out_slab,
        grad_gain_two,
        qkv_low,
    )
    own_gain = lax.dynamic_slice(gain_one, (f * shard_rows,), (shard_rows,)).reshape(shard_rows, 1)
    block_out, grad_start, weight_grad, shard_gain_one, shard_out = finish_local(
        grad_projected.reshape(rows, 3 * width),
        projection,
        own_tokens,
        gain_row,
        grad_middle,
        middle,
        dispatch,
        back_rows.reshape(EXPERTS * CAP, width),
        weight_grad,
        qkv_low,
        own_gain,
        shard_out.reshape(shard_rows, width),
    )
    shard_gain_one = shard_gain_one.reshape(shard_rows)
    shard_gain_two = lax.dynamic_slice(gain_sum.reshape(width), (f * shard_rows,), (shard_rows,))
    return (
        block_out.reshape(tokens.shape),
        grad_start.reshape(tokens.shape),
        weight_grad,
        shard_out,
        grad_in,
        grad_outw,
        shard_gain_one,
        shard_gain_two,
    )


def solution(mesh):
    pairs = mesh.shape["ctx"] * 2 == HEADS and mesh.shape["fsdp"] == 4
    return jax.shard_map(
        by_head_pairs if pairs else shards,
        mesh=mesh,
        in_specs=(
            P("fsdp", "ctx", None, None, None),
            P("fsdp", "ctx", None, None),
            P("fsdp", "ctx", None, None, None),
            P("fsdp", None),
            P("fsdp", None),
            P("ctx", None, "fsdp"),
            P("ctx", "fsdp", None),
            P(),
            P(),
            P("fsdp", "ctx", None, None, None),
        ),
        out_specs=(
            P("fsdp", "ctx", None, None, None),
            P("fsdp", "ctx", None, None, None),
            P("fsdp", None),
            P("fsdp", None),
            P("ctx", None, "fsdp"),
            P("ctx", "fsdp", None),
            P("fsdp"),
            P("fsdp"),
        ),
        check_vma=False,
    )
```

```python
import math

import jax
import jax.numpy as jnp
from jax import lax
from jax.experimental import pallas as pl
from jax.experimental.pallas import tpu as pltpu
from jax.sharding import PartitionSpec as P

HEADS = 16
EXPERTS = 64
CAP = 8


EPS = 1e-05
NEGATIVE = -1e30


def position_of(row_ids, ctx_count, half_rows):
    device = row_ids // (2 * half_rows)
    upper_half = row_ids // half_rows % 2
    offset = row_ids % half_rows
    return jnp.where(
        upper_half == 0,
        device * half_rows + offset,
        (2 * ctx_count - 1 - device) * half_rows + offset,
    )


def norm_forward(value, gain):
    row_mean = jnp.mean(value, axis=-1, keepdims=True)
    centred = value - row_mean
    inverse = lax.rsqrt(jnp.mean(centred * centred, axis=-1, keepdims=True) + EPS)
    normed = centred * inverse
    return (normed * gain, normed, inverse)


def norm_backward(gradient, normed, inverse, gain):
    scaled = gradient * gain
    mean_grad = jnp.mean(scaled, axis=-1, keepdims=True)
    mean_proj = jnp.mean(scaled * normed, axis=-1, keepdims=True)
    return (
        inverse * (scaled - mean_grad - normed * mean_proj),
        jnp.sum(gradient * normed, axis=(0, 1)),
    )


def scores(query, keys, query_pos, key_pos, query_start, score_scale):
    raw_scores = (
        jnp.einsum("qshe,kshe->shqk", query, keys, preferred_element_type=jnp.float32) * score_scale
    )
    visible = (key_pos[None, None, None, :] <= query_pos[None, None, :, None]) & (
        key_pos[None, None, None, :] >= query_start.T[:, None, :, None]
    )
    return jnp.where(visible, raw_scores, NEGATIVE)


def log_totals(query, keys, query_pos, query_start, score_scale, ctx_count, half_rows, key_block):
    block_count = keys.shape[0] // key_block
    carry_shape = (query.shape[1], query.shape[2], query.shape[0])

    def log_one_block(block_index, carried):
        running_max, running = carried
        first_row = block_index * key_block
        key_piece = lax.dynamic_slice_in_dim(keys, first_row, key_block, 0)
        key_pos = position_of(
            first_row + jnp.arange(key_block, dtype=jnp.int32), ctx_count, half_rows
        )
        score_rows = scores(query, key_piece, query_pos, key_pos, query_start, score_scale)
        new_max = jnp.maximum(running_max, jnp.max(score_rows, axis=-1))
        running = running * jnp.exp(running_max - new_max) + jnp.sum(
            jnp.exp(score_rows - new_max[..., None]), axis=-1
        )
        return (new_max, running)

    running_max, running = lax.fori_loop(
        0,
        block_count,
        log_one_block,
        (jnp.full(carry_shape, NEGATIVE, jnp.float32), jnp.zeros(carry_shape, jnp.float32)),
    )
    return running_max + jnp.log(running)


def attend(
    query,
    keys,
    values,
    query_pos,
    query_start,
    log_total,
    score_scale,
    ctx_count,
    half_rows,
    key_block,
):
    block_count = keys.shape[0] // key_block
    zeros_init = jnp.zeros(query.shape, jnp.float32)

    def attend_one_block(block_index, carried):
        output, remainder = carried
        first_row = block_index * key_block
        key_piece = lax.dynamic_slice_in_dim(keys, first_row, key_block, 0)
        value_piece = lax.dynamic_slice_in_dim(values, first_row, key_block, 0)
        key_pos = position_of(
            first_row + jnp.arange(key_block, dtype=jnp.int32), ctx_count, half_rows
        )
        weights = jnp.exp(
            scores(query, key_piece, query_pos, key_pos, query_start, score_scale)
            - log_total[..., None]
        )
        rounded = weights.astype(jnp.bfloat16)
        leftover = (weights - rounded.astype(jnp.float32)).astype(jnp.bfloat16)
        output = output + jnp.einsum(
            "shqk,kshe->qshe", rounded, value_piece, preferred_element_type=jnp.float32
        )
        remainder = remainder + jnp.einsum(
            "shqk,kshe->qshe", leftover, value_piece, preferred_element_type=jnp.float32
        )
        return (output, remainder)

    return lax.fori_loop(0, block_count, attend_one_block, (zeros_init, zeros_init))


def query_grads(
    query,
    keys,
    values,
    grad_heads,
    query_pos,
    query_start,
    log_total,
    row_delta,
    score_scale,
    ctx_count,
    half_rows,
    key_block,
):
    block_count = keys.shape[0] // key_block

    def query_one_block(block_index, running):
        first_row = block_index * key_block
        key_piece = lax.dynamic_slice_in_dim(keys, first_row, key_block, 0)
        value_piece = lax.dynamic_slice_in_dim(values, first_row, key_block, 0)
        key_pos = position_of(
            first_row + jnp.arange(key_block, dtype=jnp.int32), ctx_count, half_rows
        )
        weights = jnp.exp(
            scores(query, key_piece, query_pos, key_pos, query_start, score_scale)
            - log_total[..., None]
        )
        grad_weight = jnp.einsum(
            "qshe,kshe->shqk", grad_heads, value_piece, preferred_element_type=jnp.float32
        )
        grad_score = (weights * (grad_weight - row_delta[..., None])).astype(jnp.bfloat16)
        return running + jnp.einsum(
            "shqk,kshe->qshe", grad_score, key_piece, preferred_element_type=jnp.float32
        )

    return (
        lax.fori_loop(0, block_count, query_one_block, jnp.zeros(query.shape, jnp.float32))
        * score_scale
    )


def key_grads(
    query,
    grad_heads,
    query_pos,
    query_start,
    log_total,
    row_delta,
    key_piece,
    value_piece,
    key_pos,
    score_scale,
):
    weights = jnp.exp(
        scores(query, key_piece, query_pos, key_pos, query_start, score_scale)
        - log_total[..., None]
    )
    grad_weight = jnp.einsum(
        "qshe,kshe->shqk", grad_heads, value_piece, preferred_element_type=jnp.float32
    )
    grad_score = (weights * (grad_weight - row_delta[..., None])).astype(jnp.bfloat16)
    key_part = (
        jnp.einsum("shqk,qshe->kshe", grad_score, query, preferred_element_type=jnp.float32)
        * score_scale
    )
    value_part = jnp.einsum(
        "shqk,qshe->kshe",
        weights.astype(jnp.bfloat16),
        grad_heads,
        preferred_element_type=jnp.float32,
    )
    return (key_part, value_part)


def shards(
    tokens,
    doc_starts,
    expert_ids,
    query_key_value_weight,
    output_weight_matrix,
    expert_in,
    expert_out,
    gain_one,
    gain_two,
    grad_output,
):
    seq_dev = tokens.shape[0]
    half_rows = tokens.shape[3]
    model_width = tokens.shape[4]
    local_rows = 2 * half_rows
    ctx_count = lax.axis_size("ctx")
    head_count = HEADS
    head_size = model_width // head_count
    score_scale = head_size ** (-0.5)
    keys_total = ctx_count * local_rows
    key_block = min(512, keys_total)
    own_rows = lax.axis_index("ctx") * local_rows + jnp.arange(local_rows, dtype=jnp.int32)
    query_pos = position_of(own_rows, ctx_count, half_rows)
    query_start = doc_starts.reshape(seq_dev, local_rows).T
    routes_local = expert_ids.reshape(seq_dev, local_rows).T
    start_x = (
        tokens.reshape(seq_dev, local_rows, model_width).transpose(1, 0, 2).astype(jnp.float32)
    )
    cotangent = grad_output.reshape(seq_dev, local_rows, model_width).transpose(1, 0, 2)
    projection, out_proj = (
        lax.all_gather(query_key_value_weight.astype(jnp.bfloat16), "fsdp", axis=0, tiled=True),
        lax.all_gather(output_weight_matrix.astype(jnp.bfloat16), "fsdp", axis=0, tiled=True),
    )
    first_normed_rows, hat_one, inverse_one = norm_forward(start_x, gain_one)
    normed_low = first_normed_rows.astype(jnp.bfloat16)
    projected_rows = jnp.einsum(
        "tsd,de->tse", normed_low, projection, preferred_element_type=jnp.float32
    ).astype(jnp.bfloat16)
    query = projected_rows[..., :model_width]
    keys = projected_rows[..., model_width : 2 * model_width]
    values = projected_rows[..., 2 * model_width :]
    key_all, value_all = (
        lax.all_gather(keys, "ctx", axis=0, tiled=True),
        lax.all_gather(values, "ctx", axis=0, tiled=True),
    )
    query_heads = query.reshape(local_rows, seq_dev, head_count, head_size)
    key_heads = key_all.reshape(keys_total, seq_dev, head_count, head_size)
    value_heads = value_all.reshape(keys_total, seq_dev, head_count, head_size)
    log_total = log_totals(
        query_heads, key_heads, query_pos, query_start, score_scale, ctx_count, half_rows, key_block
    )
    mixed_heads_out, remainder = attend(
        query_heads,
        key_heads,
        value_heads,
        query_pos,
        query_start,
        log_total,
        score_scale,
        ctx_count,
        half_rows,
        key_block,
    )
    mixed_low = mixed_heads_out.astype(jnp.bfloat16).reshape(local_rows, seq_dev, model_width)
    attention_rows_out = jnp.einsum(
        "tsd,de->tse", mixed_low, out_proj, preferred_element_type=jnp.float32
    )
    middle = start_x + attention_rows_out
    normed_two, hat_two, inverse_two = norm_forward(middle, gain_two)
    routed = normed_two.astype(jnp.bfloat16)
    slot_count = EXPERTS * CAP
    per_owner = EXPERTS // ctx_count
    chosen = (routes_local[..., None] == jnp.arange(EXPERTS, dtype=jnp.int32)).astype(jnp.int32)
    earlier = (
        jnp.arange(local_rows)[:, None] >= jnp.arange(local_rows)[None, :]
    ).astype(jnp.bfloat16)
    running = jnp.einsum(
        "tu,use->tse", earlier, chosen.astype(jnp.bfloat16), preferred_element_type=jnp.float32
    )
    rank_within = jnp.sum(chosen * running.astype(jnp.int32), axis=-1) - 1
    slot_index = routes_local * CAP + rank_within
    dispatch = (
        slot_index.T[:, None, :] == jnp.arange(slot_count, dtype=jnp.int32)[None, :, None]
    ).astype(jnp.bfloat16)
    dispatch = dispatch.reshape(seq_dev, ctx_count, per_owner, CAP, local_rows)
    send_rows = jnp.einsum(
        "snect,tsd->nescd", dispatch, routed, preferred_element_type=jnp.float32
    ).astype(jnp.bfloat16)
    send_grads = jnp.einsum(
        "snect,tsd->nescd", dispatch, cotangent, preferred_element_type=jnp.float32
    ).astype(jnp.bfloat16)
    got_rows, got_grads = (
        lax.all_to_all(send_rows, "ctx", split_axis=0, concat_axis=0, tiled=True),
        lax.all_to_all(send_grads, "ctx", split_axis=0, concat_axis=0, tiled=True),
    )
    in_low = expert_in.astype(jnp.bfloat16)
    out_low = expert_out.astype(jnp.bfloat16)
    all_rows, all_grads = (
        lax.all_gather(got_rows, "fsdp", axis=2, tiled=True),
        lax.all_gather(got_grads, "fsdp", axis=2, tiled=True),
    )
    hidden = jnp.einsum("nercd,edf->nercf", all_rows, in_low, preferred_element_type=jnp.float32)
    active = jax.nn.gelu(hidden).astype(jnp.bfloat16)
    partial_rows = jnp.einsum(
        "nercf,efd->nercd", active, out_low, preferred_element_type=jnp.float32
    )
    result = lax.psum_scatter(
        partial_rows.astype(jnp.bfloat16), "fsdp", scatter_dimension=2, tiled=True
    )
    upstream = jnp.einsum(
        "nercd,efd->nercf", all_grads, out_low, preferred_element_type=jnp.float32
    )
    unused, gelu_back = jax.vjp(jax.nn.gelu, hidden)
    grad_hidden = gelu_back(upstream)[0].astype(jnp.bfloat16)
    grad_in = jnp.einsum(
        "nercd,nercf->edf", all_rows, grad_hidden, preferred_element_type=jnp.float32
    )
    grad_outw = jnp.einsum(
        "nercf,nercd->efd", active, all_grads, preferred_element_type=jnp.float32
    )
    row_part = jnp.einsum(
        "nercf,edf->nercd", grad_hidden, in_low, preferred_element_type=jnp.float32
    )
    row_grad = lax.psum_scatter(row_part, "fsdp", scatter_dimension=2, tiled=True).astype(
        jnp.bfloat16
    )
    back_rows = lax.all_to_all(result, "ctx", split_axis=0, concat_axis=0, tiled=True)
    expert_sum = jnp.einsum(
        "snect,nescd->tsd", dispatch, back_rows, preferred_element_type=jnp.float32
    )
    output_rows = middle + expert_sum
    returned = lax.all_to_all(row_grad, "ctx", split_axis=0, concat_axis=0, tiled=True)
    grad_routed = jnp.einsum(
        "snect,nescd->tsd", dispatch, returned, preferred_element_type=jnp.float32
    )
    grad_mid_norm, grad_gain_two = norm_backward(grad_routed, hat_two, inverse_two, gain_two)
    grad_middle = cotangent.astype(jnp.float32) + grad_mid_norm
    grad_attn = grad_middle.astype(jnp.bfloat16)
    grad_outproj = jnp.einsum(
        "tsd,tse->de", mixed_low, grad_attn, preferred_element_type=jnp.float32
    )
    grad_mixed = jnp.einsum(
        "tse,de->tsd", grad_attn, out_proj, preferred_element_type=jnp.float32
    ).astype(jnp.bfloat16)
    grad_heads = grad_mixed.reshape(local_rows, seq_dev, head_count, head_size)
    full_mixed = mixed_heads_out + remainder
    row_delta = jnp.sum(grad_heads.astype(jnp.float32) * full_mixed, axis=-1).transpose(1, 2, 0)
    grad_query = query_grads(
        query_heads,
        key_heads,
        value_heads,
        grad_heads,
        query_pos,
        query_start,
        log_total,
        row_delta,
        score_scale,
        ctx_count,
        half_rows,
        key_block,
    ).astype(jnp.bfloat16)
    sub_rows = math.gcd(local_rows * lax.axis_size("ctx"), key_block)

    def one_piece(piece_index):
        piece_start = piece_index * sub_rows
        key_piece = lax.dynamic_slice_in_dim(key_heads, piece_start, sub_rows, 0)
        value_piece = lax.dynamic_slice_in_dim(value_heads, piece_start, sub_rows, 0)
        key_pos = position_of(
            piece_start + jnp.arange(sub_rows, dtype=jnp.int32), ctx_count, half_rows
        )
        key_part, value_part = key_grads(
            query_heads,
            grad_heads,
            query_pos,
            query_start,
            log_total,
            row_delta,
            key_piece,
            value_piece,
            key_pos,
            score_scale,
        )
        return jnp.concatenate(
            [
                key_part.reshape(sub_rows, seq_dev, model_width),
                value_part.reshape(sub_rows, seq_dev, model_width),
            ],
            axis=-1,
        )

    summed = lax.psum_scatter(
        lax.map(
            one_piece, jnp.arange(local_rows * lax.axis_size("ctx") // sub_rows, dtype=jnp.int32)
        ).reshape(local_rows * lax.axis_size("ctx"), seq_dev, 2 * model_width),
        "ctx",
        scatter_dimension=0,
        tiled=True,
    )
    grad_key = summed[..., :model_width].astype(jnp.bfloat16)
    grad_value = summed[..., model_width:].astype(jnp.bfloat16)
    grad_projected = jnp.concatenate(
        [grad_query.reshape(local_rows, seq_dev, model_width), grad_key, grad_value], axis=-1
    )
    grad_projection = jnp.einsum(
        "tsd,tse->de", normed_low, grad_projected, preferred_element_type=jnp.float32
    )
    grad_normed = jnp.einsum(
        "tse,de->tsd", grad_projected, projection, preferred_element_type=jnp.float32
    )
    grad_in_norm, grad_gain_one = norm_backward(grad_normed, hat_one, inverse_one, gain_one)
    grad_start = grad_middle + grad_in_norm
    shard_proj, shard_outproj, shard_gain_one, shard_gain_two = (
        lax.psum_scatter(
            grad_projection.astype(jnp.bfloat16), "fsdp", scatter_dimension=0, tiled=True
        ).astype(jnp.float32),
        lax.psum_scatter(
            grad_outproj.astype(jnp.bfloat16), "fsdp", scatter_dimension=0, tiled=True
        ).astype(jnp.float32),
        lax.psum_scatter(
            grad_gain_one.astype(jnp.bfloat16), "fsdp", scatter_dimension=0, tiled=True
        ).astype(jnp.float32),
        lax.psum_scatter(
            grad_gain_two.astype(jnp.bfloat16), "fsdp", scatter_dimension=0, tiled=True
        ).astype(jnp.float32),
    )
    shard_proj, shard_outproj, shard_gain_one, shard_gain_two = (
        lax.psum(shard_proj.astype(jnp.bfloat16), "ctx").astype(jnp.float32),
        lax.psum(shard_outproj.astype(jnp.bfloat16), "ctx").astype(jnp.float32),
        lax.psum(shard_gain_one.astype(jnp.bfloat16), "ctx").astype(jnp.float32),
        lax.psum(shard_gain_two.astype(jnp.bfloat16), "ctx").astype(jnp.float32),
    )
    block_out = output_rows.transpose(1, 0, 2).reshape(tokens.shape).astype(jnp.bfloat16)
    grad_tokens = grad_start.transpose(1, 0, 2).reshape(tokens.shape)
    return (
        block_out,
        grad_tokens,
        shard_proj,
        shard_outproj,
        grad_in,
        grad_outw,
        shard_gain_one,
        shard_gain_two,
    )


BF = jnp.bfloat16
F32 = jnp.float32
CONTRACT_FIRST = (((0,), (0,)), ((), ()))
CONTRACT_LAST = (((1,), (1,)), ((), ()))
MESH_ID = pl.DeviceIdType.MESH
ANY = pl.BlockSpec(memory_space=pl.ANY)
DMA = pltpu.SemaphoreType.DMA
VMEM_CAP = 56 << 20


def place():
    c = lax.axis_index("ctx")
    f = lax.axis_index("fsdp")
    return c, f, c // 2, c % 2, f // 2, f % 2


def remote(src, dst, send, recv, device):
    return pltpu.make_async_remote_copy(
        src_ref=src, dst_ref=dst, send_sem=send, recv_sem=recv, device_id=device, device_id_type=MESH_ID
    )


def block_at(c, half, count):
    return c if half == 0 else 2 * count - 1 - c


def statistics(value):
    row_mean = jnp.mean(value, axis=1, keepdims=True)
    centred = value - row_mean
    inverse = lax.rsqrt(jnp.mean(centred * centred, axis=1, keepdims=True) + EPS)
    return centred * inverse, inverse


def stacked(value):
    return value.reshape(-1, value.shape[-1])


def relative(a, b):
    return (a // 2 + b // 2) % 2 * 2 + (a + b) % 2


def swap(value, axis, bit):
    size = lax.axis_size(axis)
    return lax.ppermute(value, axis, [(i, i ^ bit) for i in range(size)])


def lasting(microseconds):
    return pl.CostEstimate(flops=0, bytes_accessed=int(microseconds * 3.3e6), transcendentals=0)


def params(side=True):
    return pltpu.CompilerParams(has_side_effects=side, vmem_limit_bytes=VMEM_CAP)


def gather_stream(tokens, gain, routes, cotangent, starts, weight, matrix):
    count = lax.axis_size("ctx")
    depth = count // 2
    rows, wide = weight.shape
    part = wide // count
    lanes = part // 3
    half_rows, width = tokens.shape[1:]
    own_rows = 2 * half_rows
    own_experts = EXPERTS // count

    def kernel(
        x_ref, g_ref, e_ref, c_ref, s_ref, wf_ref, of_ref, tok, st, cols, beside, far, diagonal, d_ref, w_ref, o_ref, hot,
        n_ref, rs_t, ss_p, ss_up, ss_dn, ss_sib, rs_s, ss_s, rs_w, ss_w, ss_o, rs_o,
    ):
        c, f, z, y, x, k = place()
        sib = (c, f + 1 - 2 * k)
        partner = (c + 1 - 2 * y, f + 1 - 2 * k)
        up = (c + 2, f)
        down = (c - 2, f)
        holder = k == y
        for h in range(2):
            hat, _ = statistics(x_ref[h].astype(F32))
            n_ref[h] = (hat * g_ref[...]).astype(BF)

        def send_in(h):
            b = block_at(c, h, count)
            return remote(n_ref.at[h], tok.at[b], ss_p.at[h], rs_t.at[b], partner)

        def local_in(h):
            b = block_at(c, h, count)
            return pltpu.make_async_copy(n_ref.at[h], tok.at[b], rs_t.at[b])

        @pl.when(holder)
        def _():
            for h in range(2):
                local_in(h).start()

        @pl.when(jnp.logical_not(holder))
        def _():
            for h in range(2):
                send_in(h).start()

        for zt in range(depth):
            for kt in range(2):
                mine = holder & (z == zt) & (k == kt)

                @pl.when(mine)
                def _():
                    pltpu.make_async_copy(s_ref, st.at[c], rs_s.at[c]).start()

                @pl.when(jnp.logical_not(mine))
                def _(zt=zt, kt=kt):
                    remote(s_ref, st.at[c], ss_s.at[2 * zt + kt], rs_s.at[c], (2 * zt + k, 2 * x + kt)).start()

        goals = [(2 * z + k, (c, (f + 2) % 4)), (2 * z + 1 - k, (c, (sib[1] + 2) % 4)), (2 * z + 1 - k, sib)]

        def columns(pair):
            return w_ref.at[:, pl.ds(pl.multiple_of(pair * part, part), part)]

        def weight_place(shard):
            return cols.at[pl.ds(pl.multiple_of(shard * rows, rows), rows)]

        def weight_send(t):
            pair, dev = goals[t]
            return remote(columns(pair), weight_place(f), ss_w.at[t], rs_w.at[f], dev)

        for number in range(count):
            for j in range(3):
                at = number * part + j * lanes
                w_ref[:, at : at + lanes] = wf_ref[:, j * count * lanes + number * lanes :][:, :lanes].astype(BF)
        for t in range(3):
            weight_send(t).start()
        pltpu.make_async_copy(columns(2 * z + k), weight_place(f), rs_w.at[f]).start()
        o_ref[...] = of_ref[...].astype(BF)
        matrix_far = remote(o_ref, far, ss_o.at[0], rs_o.at[0], goals[0][1])
        matrix_beside = remote(o_ref, beside, ss_o.at[1], rs_o.at[1], sib)
        matrix_on = remote(far, diagonal, ss_o.at[2], rs_o.at[2], sib)
        matrix_far.start()
        matrix_beside.start()

        def copy_block(zb, h, ss, dev):
            b = block_at(2 * zb + k, h, count)
            return remote(tok.at[b], tok.at[b], ss, rs_t.at[b], dev)

        for j in range(depth):
            for h in range(2):
                if j == 0:
                    copy_block(z, h, ss_p.at[h], sib).wait_recv()

                    @pl.when(z < depth - 1)
                    def _(h=h):
                        copy_block(z, h, ss_up.at[0, h], up).start()

                    @pl.when(z > 0)
                    def _(h=h):
                        copy_block(z, h, ss_dn.at[0, h], down).start()

                    copy_block(z, h, ss_sib.at[z, h], sib).start()
                    if h == 1:
                        expert = lax.broadcasted_iota(jnp.int32, (EXPERTS, own_rows), 0)
                        chosen = expert == e_ref[...]
                        earlier = lax.broadcasted_iota(jnp.int32, (own_rows, own_rows), 0) <= lax.broadcasted_iota(
                            jnp.int32, (own_rows, own_rows), 1
                        )
                        running = jnp.dot(
                            jnp.where(chosen, 1.0, 0.0).astype(BF),
                            jnp.where(earlier, 1.0, 0.0).astype(BF),
                            preferred_element_type=F32,
                        )
                        rank = jnp.sum(jnp.where(chosen, running, 0.0), axis=0, keepdims=True).astype(jnp.int32) - 1
                        slot = e_ref[...] * CAP + rank
                        index = lax.broadcasted_iota(jnp.int32, (EXPERTS * CAP, own_rows), 0)
                        hot[...] = jnp.where(index == slot, 1.0, 0.0).astype(BF)
                        d_ref[...] = (
                            jnp.dot(hot[...], c_ref[...], preferred_element_type=F32).astype(BF).reshape(d_ref.shape)
                        )
                    continue

                @pl.when(z - j >= 0)
                def _(j=j, h=h):
                    copy_block(z - j, h, ss_p.at[h], sib).wait_recv()

                    @pl.when(z < depth - 1)
                    def _():
                        copy_block(z - j, h, ss_up.at[j, h], up).start()

                    copy_block(z - j, h, ss_sib.at[z - j, h], sib).start()

                @pl.when(z + j <= depth - 1)
                def _(j=j, h=h):
                    copy_block(z + j, h, ss_p.at[h], sib).wait_recv()

                    @pl.when(z > 0)
                    def _():
                        copy_block(z + j, h, ss_dn.at[j, h], down).start()

                    copy_block(z + j, h, ss_sib.at[z + j, h], sib).start()

        matrix_far.wait_recv()
        matrix_on.start()
        for zt in range(depth):
            for h in range(2):
                b = block_at(2 * zt + 1 - k, h, count)
                remote(tok.at[b], tok.at[b], ss_p.at[h], rs_t.at[b], sib).wait_recv()
                copy_block(zt, h, ss_sib.at[zt, h], sib).wait_send()
        for ct in range(count):
            remote(s_ref, st.at[ct], ss_s.at[0], rs_s.at[ct], sib).wait_recv()
        for shard in range(4):
            remote(columns(0), weight_place(shard), ss_w.at[0], rs_w.at[shard], sib).wait_recv()
        for t in range(3):
            weight_send(t).wait_send()
        matrix_far.wait_send()
        matrix_beside.wait()
        matrix_on.wait()

        @pl.when(jnp.logical_not(holder))
        def _():
            for h in range(2):
                send_in(h).wait_send()

        for j in range(depth):

            @pl.when((z < depth - 1) & (z - j >= 0))
            def _(j=j):
                for h in range(2):
                    copy_block(z - j, h, ss_up.at[j, h], up).wait_send()

            @pl.when((z > 0) & (z + j <= depth - 1))
            def _(j=j):
                for h in range(2):
                    copy_block(z + j, h, ss_dn.at[j, h], down).wait_send()

        for zt in range(depth):
            for kt in range(2):
                mine = holder & (z == zt) & (k == kt)

                @pl.when(jnp.logical_not(mine))
                def _(zt=zt, kt=kt):
                    remote(s_ref, st.at[c], ss_s.at[2 * zt + kt], rs_s.at[c], sib).wait_send()

    return pl.pallas_call(
        kernel,
        name="gather_stream",
        cost_estimate=lasting(50),
        out_shape=(
            jax.ShapeDtypeStruct((2 * count, half_rows, width), BF),
            jax.ShapeDtypeStruct((count,) + starts.shape, starts.dtype),
            jax.ShapeDtypeStruct((4 * rows, part), BF),
            *[jax.ShapeDtypeStruct(matrix.shape, BF)] * 3,
            jax.ShapeDtypeStruct((count, own_experts, CAP, width), BF),
            jax.ShapeDtypeStruct((rows, wide), BF),
            jax.ShapeDtypeStruct(matrix.shape, BF),
            jax.ShapeDtypeStruct((EXPERTS * CAP, own_rows), BF),
        ),
        in_specs=[pl.BlockSpec(memory_space=pltpu.VMEM)] * 7,
        out_specs=(ANY,) * 6 + (pl.BlockSpec(memory_space=pltpu.VMEM),) * 4,
        scratch_shapes=[
            pltpu.VMEM((2, half_rows, width), BF),
            DMA((2 * count,)), DMA((2,)), DMA((depth, 2)), DMA((depth, 2)), DMA((depth, 2)),
            DMA((count,)), DMA((count,)), DMA((4,)), DMA((3,)), DMA((3,)), DMA((3,)),
        ],
        compiler_params=params(),
    )(tokens, gain, routes, cotangent, starts, weight, matrix)


TILE = 256


def halves(value, axis):
    size = value.shape[axis] // 2
    at = lax.broadcasted_iota(jnp.int32, value.shape, axis)
    zero = jnp.zeros_like(value)
    return [jnp.where(at < size, value, zero), jnp.where(at >= size, value, zero)]


def attend_forward(stream, columns, start_row, numbers, scale):
    length, width = stream.shape
    tiles = length // TILE
    lanes = 128
    size = lanes // 2

    def kernel(first, x_ref, w_ref, s_ref, out, m16, m32, lse, k_rows, v_turned):
        i = pl.program_id(0)
        own = pl.ds(pl.multiple_of(i * TILE, TILE), TILE)
        rows = x_ref[...]
        projected = jnp.dot(rows, w_ref[...], preferred_element_type=F32).astype(BF)
        out[...] = projected
        query, key, value = [projected[:, j * lanes : (j + 1) * lanes] for j in range(3)]
        k_rows[own, :] = key
        v_turned[:, own] = value.T
        queries = halves((query * scale).T, 0)
        start = s_ref[...]
        key_row = lax.broadcasted_iota(jnp.int32, (TILE, TILE), 0)
        query_column = i * TILE + lax.broadcasted_iota(jnp.int32, (TILE, TILE), 1)

        def step(j, carried):
            at = pl.multiple_of(j * TILE, TILE)
            keys = k_rows[pl.ds(at, TILE), :]
            seen = (key_row + at <= query_column) & (key_row + at >= start)
            out = []
            for h in range(2):
                top, total, mixed = carried[h]
                score = jnp.where(seen, jnp.dot(keys, queries[h], preferred_element_type=F32), NEGATIVE)
                new_top = jnp.maximum(top, jnp.max(score, axis=0, keepdims=True))
                weight = jnp.exp(score - new_top)
                shrink = jnp.exp(top - new_top)
                total = total * shrink + jnp.sum(weight, axis=0, keepdims=True)
                values = v_turned[h * size : (h + 1) * size, pl.ds(at, TILE)]
                mixed = mixed * shrink + jnp.dot(values, weight.astype(BF), preferred_element_type=F32)
                out.append((new_top, total, mixed))
            return tuple(out)

        begin = (
            jnp.full((1, TILE), NEGATIVE, F32),
            jnp.zeros((1, TILE), F32),
            jnp.zeros((size, TILE), F32),
        )
        done = lax.fori_loop(first[i], i + 1, step, (begin, begin))
        mixed = jnp.concatenate([part / total for _, total, part in done], axis=0)
        m32[...] = mixed
        m16[...] = mixed.T.astype(BF)
        lse[...] = jnp.concatenate([top + jnp.log(total) for top, total, _ in done], axis=0)

    tile = pl.BlockSpec((TILE, lanes), lambda i, n: (i, 0))
    turned = pl.BlockSpec((lanes, TILE), lambda i, n: (0, i))
    return pl.pallas_call(
        kernel,
        name="attend_forward",
        cost_estimate=lasting(22),
        grid_spec=pltpu.PrefetchScalarGridSpec(
            num_scalar_prefetch=1,
            grid=(tiles,),
            in_specs=[
                pl.BlockSpec((TILE, width), lambda i, n: (i, 0)),
                pl.BlockSpec((width, 3 * lanes), lambda i, n: (0, 0)),
                pl.BlockSpec((1, TILE), lambda i, n: (0, i)),
            ],
            out_specs=[
                pl.BlockSpec((TILE, 3 * lanes), lambda i, n: (i, 0)),
                tile,
                turned,
                pl.BlockSpec((2, TILE), lambda i, n: (0, i)),
            ],
            scratch_shapes=[pltpu.VMEM((length, lanes), BF), pltpu.VMEM((lanes, length), BF)],
        ),
        out_shape=(
            jax.ShapeDtypeStruct((length, 3 * lanes), BF),
            jax.ShapeDtypeStruct((length, lanes), BF),
            jax.ShapeDtypeStruct((lanes, length), F32),
            jax.ShapeDtypeStruct((2, length), F32),
        ),
        compiler_params=params(False),
    )(numbers, stream, columns, start_row)


def backward_local(qkv, grad, mixed, logs, start_row, numbers, scale, stream, rows, cotangents, active, grad_hidden):
    length = qkv.shape[0]
    lanes = 128
    tiles = length // TILE
    size = lanes // 2
    _, number, count, cap, width = rows.shape
    total_rows, units = active.shape[1:]
    assert tiles == number

    def kernel(
        first, q_ref, k_ref, v_ref, g_ref, m_ref, l_ref, s_ref, x_ref, r_ref, g0_ref, g1_ref, g2_ref, g3_ref, a_ref, h_ref,
        out, weight, da, db, acc_k, acc_v, k_turned,
    ):
        i = pl.program_id(0)
        gradient = jnp.concatenate([stacked(ref[...]) for ref in (g0_ref, g1_ref, g2_ref, g3_ref)], axis=0)
        da[0] = lax.dot_general(stacked(r_ref[...]), h_ref[0], CONTRACT_FIRST, preferred_element_type=F32)
        db[0] = lax.dot_general(a_ref[0], gradient, CONTRACT_FIRST, preferred_element_type=F32)

        @pl.when(i == 0)
        def _():
            acc_k[...] = jnp.zeros_like(acc_k)
            acc_v[...] = jnp.zeros_like(acc_v)
            for t in range(tiles):
                k_turned[:, t * TILE : (t + 1) * TILE] = k_ref[t * TILE : (t + 1) * TILE, :].T

        scaled = q_ref[...] * scale
        grads = g_ref[...]
        turned = grads.T
        queries, queries_turned = halves(scaled, 1), halves(scaled.T, 0)
        grad_rows, grads_turned = halves(grads, 1), halves(turned, 0)
        product = turned.astype(F32) * m_ref[...]
        deltas = [jnp.sum(product[h * size : (h + 1) * size], axis=0, keepdims=True) for h in range(2)]
        logs_row = [l_ref[h : h + 1, :] for h in range(2)]
        start = s_ref[...]
        key_row = lax.broadcasted_iota(jnp.int32, (TILE, TILE), 0)
        query_column = i * TILE + lax.broadcasted_iota(jnp.int32, (TILE, TILE), 1)

        def step(j, running):
            at = pl.multiple_of(j * TILE, TILE)
            keys = k_ref[pl.ds(at, TILE), :]
            values = v_ref[pl.ds(at, TILE), :]
            seen = (key_row + at <= query_column) & (key_row + at >= start)
            key_sum = jnp.zeros((TILE, lanes), F32)
            value_sum = jnp.zeros((TILE, lanes), F32)
            out = []
            for h in range(2):
                score = jnp.dot(keys, queries_turned[h], preferred_element_type=F32)
                weight = jnp.exp(jnp.where(seen, score - logs_row[h], NEGATIVE))
                grad_weight = jnp.dot(values, grads_turned[h], preferred_element_type=F32)
                grad_score = (weight * (grad_weight - deltas[h])).astype(BF)
                value_sum += jnp.dot(weight.astype(BF), grad_rows[h], preferred_element_type=F32)
                key_sum += jnp.dot(grad_score, queries[h], preferred_element_type=F32)
                part = k_turned[h * size : (h + 1) * size, pl.ds(at, TILE)]
                out.append(running[h] + jnp.dot(part, grad_score, preferred_element_type=F32))
            acc_k[pl.ds(at, TILE), :] += key_sum
            acc_v[pl.ds(at, TILE), :] += value_sum
            return tuple(out)

        zero = jnp.zeros((size, TILE), F32)
        total = lax.fori_loop(first[i], i + 1, step, (zero, zero))
        own = pl.ds(pl.multiple_of(i * TILE, TILE), TILE)
        out[own, 0:lanes] = (jnp.concatenate(total, axis=0) * scale).T.astype(BF)

        @pl.when(i == tiles - 1)
        def _():
            out[:, lanes : 2 * lanes] = acc_k[...].astype(BF)
            out[:, 2 * lanes : 3 * lanes] = acc_v[...].astype(BF)
            weight[...] = lax.dot_general(x_ref[...], out[...], CONTRACT_FIRST, preferred_element_type=F32).astype(BF)

    tile = pl.BlockSpec((TILE, lanes), lambda i, n: (i, 0))
    quarter = pl.BlockSpec((count, 1, cap, width), lambda i, n: (0, i, 0, 0))
    wide = pl.BlockSpec((1, total_rows, units), lambda i, n: (i, 0, 0))
    return pl.pallas_call(
        kernel,
        name="backward_local",
        cost_estimate=lasting(30),
        grid_spec=pltpu.PrefetchScalarGridSpec(
            num_scalar_prefetch=1,
            grid=(tiles,),
            in_specs=[
                tile,
                pl.BlockSpec((length, lanes), lambda i, n: (0, 1)),
                pl.BlockSpec((length, lanes), lambda i, n: (0, 2)),
                tile,
                pl.BlockSpec((lanes, TILE), lambda i, n: (0, i)),
                pl.BlockSpec((2, TILE), lambda i, n: (0, i)),
                pl.BlockSpec((1, TILE), lambda i, n: (0, i)),
                pl.BlockSpec((length, width), lambda i, n: (0, 0), pipeline_mode=pl.Buffered(1)),
                pl.BlockSpec((4, 1, count, cap, width), lambda i, n: (0, i, 0, 0, 0)),
                quarter,
                quarter,
                quarter,
                quarter,
                wide,
                wide,
            ],
            out_specs=[
                pl.BlockSpec((length, 3 * lanes), lambda i, n: (0, 0)),
                pl.BlockSpec((width, 3 * lanes), lambda i, n: (0, 0)),
                pl.BlockSpec((1, width, units), lambda i, n: (i, 0, 0)),
                pl.BlockSpec((1, units, width), lambda i, n: (i, 0, 0)),
            ],
            scratch_shapes=[
                pltpu.VMEM((length, lanes), F32),
                pltpu.VMEM((length, lanes), F32),
                pltpu.VMEM((lanes, length), BF),
            ],
        ),
        out_shape=(
            jax.ShapeDtypeStruct((length, 3 * lanes), BF),
            jax.ShapeDtypeStruct((width, 3 * lanes), BF),
            jax.ShapeDtypeStruct((number, width, units), F32),
            jax.ShapeDtypeStruct((number, units, width), F32),
        ),
        compiler_params=params(False),
    )(numbers, qkv, qkv, qkv, grad, mixed, logs, start_row, stream, rows, *cotangents, active, grad_hidden)


ROOT = math.sqrt(2.0 / math.pi)
CUBIC = 0.044715


def experts_exchange(by_head, out_proj, tokens, dispatch, gain, cotangent, near, first_proj, second_proj):
    count = lax.axis_size("ctx")
    half_rows, lanes = by_head.shape[1:]
    rows, width = tokens.shape
    number, _, units = first_proj.shape
    cap = CAP
    total_rows = 4 * count * cap
    quarter = width // 4
    slab = quarter // count
    splits = 2
    part_units = units // splits

    def kernel(
        a_ref, w0_ref, w1_ref, w2_ref, w3_ref, x_ref, d_ref, g_ref, c_ref, g0_ref, first_ref, second_ref,
        mixed, middle, rows_out, g1_ref, g2_ref, g3_ref, active_out, hidden_out, heads, grad_middle, gain_out, later,
        routed, slots, rows_v, g_buf, first_buf, second_buf, active_v, hidden_v, back_v, back_near, back_far, back_got,
        out_v, out_near, own_v, far_v, out_got, summed, home_got, back, shard_near, shard_far, shard_got, shard_v,
        ss_m, rs_m, ss_1, rs_1, ss_x, rs_x, ss_s, rs_s, ss_f, rs_f, ss_bn, rs_bn, ss_bf, rs_bf, ss_on, rs_on, ss_h, rs_h,
        ss_t, rs_t, ss_n, rs_n, ss_w, rs_w, ss_g, rs_g, l_first, l_second, l_g, st_r, st_a, st_h, st_o, ss_of, rs_of, st_w,
    ):
        c, f, z, y, x, k = place()
        sib = (c, f + 1 - 2 * k)
        xn = (c, (f + 2) % 4)
        pair = 2 * z + k
        target = 2 * x + y

        def load_first(e, u):
            cols = pl.ds(u * part_units, part_units)
            return pltpu.make_async_copy(first_ref.at[e, :, cols], first_buf.at[u], l_first.at[u])

        def load_second(e, u):
            part = pl.ds(u * part_units, part_units)
            return pltpu.make_async_copy(second_ref.at[e, part], second_buf.at[u], l_second.at[u])

        def load_grads(e, slot):
            refs = (g0_ref, g1_ref, g2_ref, g3_ref)
            return [pltpu.make_async_copy(ref.at[:, e], g_buf.at[slot, j], l_g.at[slot, j]) for j, ref in enumerate(refs)]

        def grads_across(e):
            return remote(g0_ref.at[:, e], g2_ref.at[:, e], ss_g.at[0, e], rs_g.at[0, e], xn)

        def grads_share(e):
            return remote(g0_ref.at[:, e], g1_ref.at[:, e], ss_g.at[1, e], rs_g.at[1, e], sib)

        def grads_share_far(e):
            return remote(g2_ref.at[:, e], g3_ref.at[:, e], ss_g.at[2, e], rs_g.at[2, e], sib)

        def forward_grads(e):
            grads_across(e).wait_recv()
            grads_share_far(e).start()

        def start_load_grads(e, slot):
            grads_share(e).wait_recv()
            grads_share_far(e).wait_recv()
            for load in load_grads(e, slot):
                load.start()

        def there(half):
            column = (2 * relative(z, target) + k) * lanes
            return mixed.at[half, :, pl.ds(pl.multiple_of(column, lanes), lanes)]

        def send(i, half):
            ct = (c + i) % count
            return remote(
                a_ref.at[block_at(ct, half, count)], there(half), ss_m.at[i, half], rs_m.at[pair, half], (ct, target)
            )

        def keep(half):
            return pltpu.make_async_copy(a_ref.at[block_at(c, half, count)], there(half), rs_m.at[pair, half])

        for half in range(2):
            for i in range(1, count):
                send(i, half).start()

            @pl.when(k == y)
            def _(half=half):
                keep(half).start()

            @pl.when(k != y)
            def _(half=half):
                send(0, half).start()

        for u in range(splits):
            load_first(0, u).start()
            load_second(0, u).start()

        def start_grads(e, carry):
            grads_across(e).start()
            grads_share(e).start()
            return carry

        lax.fori_loop(0, number, start_grads, 0)
        for half in range(2):
            for other in range(count):
                column = (2 * relative(other // 2, f) + other % 2) * lanes
                cols = pl.ds(pl.multiple_of(column, lanes), lanes)
                remote(a_ref.at[0], mixed.at[half, :, cols], ss_m.at[0, half], rs_m.at[other, half], sib).wait_recv()
            here = pl.ds(half * half_rows, half_rows)
            value = x_ref[here, :].astype(F32)
            for j, w_ref in enumerate((w0_ref, w1_ref, w2_ref, w3_ref)):
                cols = pl.ds(j * quarter, quarter)
                value += jnp.dot(mixed[half, :, cols], w_ref[...], preferred_element_type=F32)
            middle[here, :] = value
            hat, _ = statistics(value)
            routed[here, :] = (hat * g_ref[...]).astype(BF)
        slots[...] = jnp.dot(d_ref[...], routed[...], preferred_element_type=F32).astype(BF).reshape(slots.shape)

        def rows_first(e, i):
            owner = (c + i) % count
            return remote(slots.at[owner, e], rows_v.at[0, e, c], ss_1.at[e], rs_1.at[e], (owner, f))

        def hop(e, rel, dst, send_sem, recv_sem, dev):
            return remote(rows_v.at[rel, e], rows_v.at[dst, e], send_sem.at[e], recv_sem.at[e], dev)

        def rows_across(e):
            return hop(e, 0, 2, ss_x, rs_x, xn)

        def rows_share(e):
            return hop(e, 0, 1, ss_s, rs_s, sib)

        def rows_share_far(e):
            return hop(e, 2, 3, ss_f, rs_f, sib)

        def start_rows(e, carry):
            for i in range(1, count):
                rows_first(e, i).start()
            pltpu.make_async_copy(slots.at[c, e], rows_v.at[0, e, c], rs_1.at[e]).start()
            return carry

        lax.fori_loop(0, number, start_rows, 0)

        def forward(e):
            remote(rows_v.at[0, e], rows_v.at[0, e], ss_x.at[e], rs_1.at[e], sib).wait_recv()
            rows_across(e).start()
            rows_share(e).start()

        def forward_far(e):
            rows_across(e).wait_recv()
            rows_share_far(e).start()

        def near_send(e, j):
            return remote(back_v.at[2 * j + 1, e], back_near.at[j, e], ss_bn.at[e, j], rs_bn.at[e, j], sib)

        def near_out(e, j):
            return remote(out_v.at[2 * j + 1, e], out_near.at[j, e], ss_on.at[e, j], rs_on.at[e, j], sib)

        def far_send(e):
            return remote(back_far.at[e], back_got.at[e], ss_bf.at[e], rs_bf.at[e], xn)

        def store_own(e):
            return pltpu.make_async_copy(own_v.at[e], later.at[:, pl.ds(pl.multiple_of(slab + e * cap, cap), cap)], st_o.at[e])

        def far_out(e):
            return remote(far_v.at[e], out_got.at[e], ss_of.at[e], rs_of.at[e], xn)

        def store_rows(e):
            return pltpu.make_async_copy(rows_v.at[:, e], rows_out.at[:, e], st_r.at[e])

        def store_active(e, slot):
            return pltpu.make_async_copy(active_v.at[slot], active_out.at[e], st_a.at[slot])

        def store_hidden(e, slot):
            return pltpu.make_async_copy(hidden_v.at[slot], hidden_out.at[e], st_h.at[slot])

        def sum_far(e):
            near_send(e, 1).wait_recv()
            back_far[e] = (back_v[2, e].astype(F32) + back_near[1, e].astype(F32)).astype(BF)
            far_send(e).start()

        def sum_outputs(e):
            for j in range(2):
                near_out(e, j).wait_recv()
            own_v[e] = (out_v[0, e].astype(F32) + out_near[0, e].astype(F32)).astype(BF)
            far_v[e] = (out_v[2, e].astype(F32) + out_near[1, e].astype(F32)).astype(BF)

        def home(e, i):
            ct = (c + i) % count
            return remote(summed.at[e, ct], home_got.at[c, e], ss_h.at[e], rs_h, (ct, f))

        def go_home(e):
            near_send(e, 0).wait_recv()
            far_send(e).wait_recv()
            summed[e] = (
                back_v[0, e].astype(F32) + back_near[0, e].astype(F32) + back_got[e].astype(F32)
            ).astype(BF)
            for i in range(1, count):
                home(e, i).start()
            pltpu.make_async_copy(summed.at[e, c], home_got.at[c, e], rs_h).start()

        def expert(e, carry):
            slot = e % 2

            @pl.when(e + 2 < number)
            def _():
                forward(e + 2)
                forward_grads(e + 2)

            @pl.when(e + 1 < number)
            def _():
                forward_far(e + 1)
                start_load_grads(e + 1, 1 - slot)

            rows_share(e).wait_recv()
            rows_share_far(e).wait_recv()
            store_rows(e).start()
            for load in load_grads(e, slot):
                load.wait()

            @pl.when(e >= 2)
            def _():
                store_active(e, slot).wait()
                store_hidden(e, slot).wait()

            row = rows_v[:, e].reshape(total_rows, width)
            grad = g_buf[slot].reshape(total_rows, width)
            term = jnp.zeros((total_rows, width), F32)
            firsts, seconds = [], []
            for u in range(splits):
                load_first(e, u).wait()
                load_second(e, u).wait()
                first = first_buf[u].astype(BF)
                second = second_buf[u].astype(BF)
                seconds.append(second)
                hidden = jnp.dot(row, first, preferred_element_type=F32)
                upstream = lax.dot_general(grad, second, CONTRACT_LAST, preferred_element_type=F32)
                bent = jnp.tanh(ROOT * (hidden + CUBIC * hidden * hidden * hidden))
                cols = pl.ds(u * part_units, part_units)
                active_v[slot, :, cols] = (0.5 * hidden * (1.0 + bent)).astype(BF)
                slope = 0.5 * (1.0 + bent) + 0.5 * hidden * (1.0 - bent * bent) * (
                    ROOT * (1.0 + 3.0 * CUBIC * hidden * hidden)
                )
                grad_hidden = (upstream * slope).astype(BF)
                hidden_v[slot, :, cols] = grad_hidden
                term += lax.dot_general(grad_hidden, first, CONTRACT_LAST, preferred_element_type=F32)
            back_v[:, e] = term.astype(BF).reshape(4, count, cap, width)
            near_send(e, 1).start()
            near_send(e, 0).start()
            result = jnp.zeros((total_rows, width), F32)
            for u in range(splits):
                cols = pl.ds(u * part_units, part_units)
                result += jnp.dot(active_v[slot, :, cols], seconds[u], preferred_element_type=F32)
            out_v[:, e] = result.astype(BF).reshape(4, count, cap, width)
            near_out(e, 1).start()
            near_out(e, 0).start()

            @pl.when(e + 1 < number)
            def _():
                for u in range(splits):
                    load_first(e + 1, u).start()
                    load_second(e + 1, u).start()

            store_active(e, slot).start()
            store_hidden(e, slot).start()

            @pl.when(e >= 1)
            def _():
                sum_far(e - 1)
                sum_outputs(e - 1)

            @pl.when(e >= 3)
            def _():
                go_home(e - 3)

            return carry

        forward_grads(0)
        forward_grads(1)
        forward(0)
        forward(1)
        start_load_grads(0, 0)
        forward_far(0)
        lax.fori_loop(0, number, expert, 0)
        sum_far(number - 1)
        sum_outputs(number - 1)
        for e in range(number - 3, number):
            go_home(e)
        for e in range(number):
            far_out(e).start()
        hat, inverse = statistics(middle[...])
        remote(home_got, home_got, ss_h.at[0], rs_h, sib).wait_recv()

        returned = lax.dot_general(d_ref[...], home_got[...].reshape(-1, width), CONTRACT_FIRST, preferred_element_type=F32)
        scaled = returned * g_ref[...]
        mean_grad = jnp.mean(scaled, axis=1, keepdims=True)
        mean_proj = jnp.mean(scaled * hat, axis=1, keepdims=True)
        gain_out[...] = jnp.sum(returned * hat, axis=0, keepdims=True)
        gradient = c_ref[...].astype(F32) + inverse * (scaled - mean_grad - hat * mean_proj)
        grad_middle[...] = gradient
        low = gradient.astype(BF)
        for j, w_ref in enumerate((w0_ref, w1_ref, w2_ref, w3_ref)):
            back[:, :, j * quarter : (j + 1) * quarter] = (
                lax.dot_general(low, w_ref[...], CONTRACT_LAST, preferred_element_type=F32)
                .astype(BF)
                .reshape(2, half_rows, quarter)
            )

        def part(half, number_of_pair):
            column = (2 * relative(number_of_pair // 2, f) + number_of_pair % 2) * lanes
            return back.at[half, :, pl.ds(pl.multiple_of(column, lanes), lanes)]

        def send_heads(i, half):
            other = (2 * z + k + i) % count
            b = block_at(c, half, count)
            dev = (2 * (other // 2) + k, 2 * x + other % 2)
            return remote(part(half, other), heads.at[b], ss_t.at[i, half], rs_t.at[b], dev)

        for i in range(1, count):
            for half in range(2):
                send_heads(i, half).start()

        @pl.when(k == y)
        def _():
            for half in range(2):
                b = block_at(c, half, count)
                pltpu.make_async_copy(part(half, 2 * z + k), heads.at[b], rs_t.at[b]).start()

        @pl.when(k != y)
        def _():
            for half in range(2):
                send_heads(0, half).start()

        for e in range(number):
            for j in range(2):
                near_send(e, j).wait_send()

        def term_place(j):
            return back_v.at[j, 0 : quarter // (count * cap)]

        def shard_term(j):
            half_quarter = quarter // 2
            mixed_part = [mixed[half, :, j * quarter : (j + 1) * quarter] for half in range(2)]
            value = sum(
                lax.dot_general(
                    mixed_part[half], low[half * half_rows : (half + 1) * half_rows], CONTRACT_FIRST, preferred_element_type=F32
                )
                for half in range(2)
            )
            return value.astype(BF).reshape(shard_far.shape)

        def core_send(j):
            return remote(term_place(2 * j + 1), shard_near.at[j], ss_n.at[j], rs_n.at[j], sib)

        across = remote(shard_far, shard_got, ss_w, rs_w, xn)
        for j in (1, 0):
            back_v[2 * j + 1, 0 : quarter // (count * cap)] = shard_term(2 * j + 1)
            core_send(j).start()
        own_far = shard_term(2)
        core_send(1).wait_recv()
        shard_far[...] = (own_far.astype(F32) + shard_near[1].astype(F32)).astype(BF)
        across.start()
        own_near = shard_term(0)
        core_send(0).wait_recv()

        def finish_output(e, carry):
            far_out(e).wait_recv()
            own_v[e] = (own_v[e].astype(F32) + out_got[e].astype(F32)).astype(BF)
            store_own(e).start()
            return carry

        lax.fori_loop(0, number, finish_output, 0)
        across.wait_recv()
        shard_v[...] = (
            (own_near.astype(F32) + shard_near[0].astype(F32) + shard_got[...].astype(F32)).astype(BF).reshape(shard_v.shape)
        )
        store_shard = pltpu.make_async_copy(shard_v, later.at[:, pl.ds(0, slab)], st_w)
        store_shard.start()

        for b in range(2 * count):
            remote(part(0, 0), heads.at[b], ss_t.at[0, 0], rs_t.at[b], sib).wait_recv()

        def leave(e, carry):
            sent = pl.ds(0, count - 1)
            remote(slots.at[sent, e], rows_v.at[0, e, sent], ss_1.at[e], rs_1.at[e], sib).wait_send()
            remote(summed.at[e, sent], home_got.at[sent, e], ss_h.at[e], rs_h, sib).wait_send()
            rows_across(e).wait_send()
            rows_share(e).wait_send()
            rows_share_far(e).wait_send()
            grads_across(e).wait_send()
            grads_share(e).wait_send()
            grads_share_far(e).wait_send()
            far_send(e).wait_send()
            for j in range(2):
                near_out(e, j).wait_send()
            store_own(e).wait()
            far_out(e).wait_send()
            store_rows(e).wait()
            return carry

        lax.fori_loop(0, number, leave, 0)
        store_shard.wait()
        for e in (number - 2, number - 1):
            store_active(e, e % 2).wait()
            store_hidden(e, e % 2).wait()
        for i in range(1, count):
            for half in range(2):
                send(i, half).wait_send()
                send_heads(i, half).wait_send()

        @pl.when(k != y)
        def _():
            for half in range(2):
                send(0, half).wait_send()
                send_heads(0, half).wait_send()

        core_send(0).wait_send()
        core_send(1).wait_send()
        across.wait_send()

    vmem = pl.BlockSpec(memory_space=pltpu.VMEM)
    block = (count, cap, width)
    low = lambda *shape: pltpu.VMEM(shape, BF)
    fold = (quarter // (count * cap),) + block
    return pl.pallas_call(
        kernel,
        name="experts_exchange",
        cost_estimate=lasting(100),
        out_shape=(
            jax.ShapeDtypeStruct((2, half_rows, width), BF),
            jax.ShapeDtypeStruct((rows, width), F32),
            jax.ShapeDtypeStruct((4, number) + block, BF),
            *[jax.ShapeDtypeStruct(near.shape, BF)] * 3,
            jax.ShapeDtypeStruct((number, total_rows, units), BF),
            jax.ShapeDtypeStruct((number, total_rows, units), BF),
            jax.ShapeDtypeStruct((2 * count, half_rows, lanes), BF),
            jax.ShapeDtypeStruct((rows, width), F32),
            jax.ShapeDtypeStruct((1, width), F32),
            jax.ShapeDtypeStruct((count, slab + number * cap, width), BF),
        ),
        in_specs=[ANY] + [vmem] * 8 + [ANY] * 3,
        out_specs=(vmem, vmem) + (ANY,) * 7 + (vmem, vmem, ANY),
        scratch_shapes=[
            low(rows, width), low(count, number, cap, width), low(4, number, *block), low(2, 4, *block),
            pltpu.VMEM((splits, width, part_units), F32), pltpu.VMEM((splits, part_units, width), F32),
            low(2, total_rows, units), low(2, total_rows, units),
            low(4, number, *block), low(2, number, *block), low(number, *block), low(number, *block),
            low(4, number, *block), low(2, number, *block), low(number, *block), low(number, *block), low(number, *block),
            low(number, *block), low(count, number, cap, width), low(2, half_rows, width),
            low(2, *fold), low(*fold), low(*fold), low(count, slab, width),
            DMA((count, 2)), DMA((count, 2)), DMA((number,)), DMA((number,)), DMA((number,)), DMA((number,)),
            DMA((number,)), DMA((number,)), DMA((number,)), DMA((number,)), DMA((number, 2)), DMA((number, 2)),
            DMA((number,)), DMA((number,)), DMA((number, 2)), DMA((number, 2)), DMA((number,)), DMA,
            DMA((count, 2)), DMA((2 * count,)), DMA((2,)), DMA((2,)), DMA, DMA, DMA((3, number)), DMA((3, number)),
            DMA((splits,)), DMA((splits,)), DMA((2, 4)), DMA((number,)), DMA((2,)), DMA((2,)), DMA((number,)), DMA((number,)), DMA((number,)), DMA,
        ],
        compiler_params=pltpu.CompilerParams(has_side_effects=True, vmem_limit_bytes=60 << 20),
    )(by_head, *out_proj, tokens, dispatch, gain, cotangent, near, first_proj, second_proj)


def after(value, *others):
    return lax.optimization_barrier((value,) + others)[0]


def finish_exchange(grads, parts, slabs, gain_part, weight):
    count = lax.axis_size("ctx")
    depth = count // 2
    part = grads.shape[2]
    half_rows = grads.shape[1]
    _, rows, _ = parts.shape
    pieces = 4
    piece = rows // pieces
    slab = rows // count

    def kernel(
        a_ref, p_ref, h_ref, g_ref, w_ref, tok_out, w_out, o_out, g_out, w_all, o_ref, got, held, got_g, sum_g, got_gc,
        ss, rs, ss_r, rs_r, ss_up, ss_dn, rs_z, ss_a, ss_b, rs_o,
        ss_of, rs_of, ss_g, rs_g, ss_gc, rs_gc, ss_wx, rs_wx, ss_ws, rs_ws, ss_wf, rs_wf, loc,
    ):
        c, f, z, y, x, k = place()
        pair = 2 * z + k
        target = 2 * x + y
        sib = (c, f + 1 - 2 * k)
        xn = (c, (f + 2) % 4)
        up = (c + 2, f)
        down = (c - 2, f)

        def columns(ref, number):
            return ref.at[:, pl.ds(pl.multiple_of(number * part, part), part)]

        peers = [
            (2 * z + 1 - y, f, 2 * x + 1 - y),
            (c, (f + 2) % 4, 2 * (1 - x) + y),
            (2 * z + 1 - y, (f + 2) % 4, 2 * (1 - x) + 1 - y),
        ]

        def scatter(d):
            cp, fp, shard = peers[d]
            return remote(p_ref.at[shard], got.at[d], ss_r.at[d], rs_r.at[d], (cp, fp))

        for d in (2, 1, 0):
            scatter(d).start()

        def weight_part(shard, i):
            return w_all.at[shard, pl.ds(i * piece, piece)]

        def weight_across(i):
            return remote(w_ref.at[pl.ds(i * piece, piece)], weight_part(f, i), ss_wx.at[i], rs_wx.at[i], xn)

        def weight_on(i, shard):
            return remote(weight_part(shard, i), weight_part(shard, i), ss_wf.at[i], rs_wf.at[i], sib)

        def weight_pass(i):
            shard = (f + 2) % 4
            remote(weight_part(shard, i), weight_part(shard, i), ss_wf.at[i], rs_wx.at[i], sib).wait_recv()
            weight_on(i, shard).start()

        weight_share = remote(w_ref, w_all.at[f], ss_ws, rs_ws, sib)
        weight_own = pltpu.make_async_copy(w_ref, w_all.at[f], loc)
        for i in range(pieces):
            weight_across(i).start()

        def there(half):
            return columns(tok_out.at[half], pair)

        def send(i, half):
            ct = (c + i) % count
            return remote(a_ref.at[block_at(ct, half, count)], there(half), ss.at[i, half], rs.at[pair, half], (ct, target))

        def send_all(numbers):
            for i in numbers:
                for half in range(2):
                    send(i, half).start()

        send_all(range(2, count, 2))

        def gain_send(j):
            return remote(sum_g.at[j], got_g.at[j], ss_g.at[j], rs_g.at[j], sib if j == 0 else xn)

        sum_g[0] = g_ref[...]
        gain_send(0).start()

        def chain(zb, sem, dev):
            return remote(held.at[zb], held.at[zb], sem, rs_z.at[zb], dev)

        def own_column(zb):
            return remote(held.at[zb], columns(w_out, 2 * zb + k), ss_a.at[zb], rs_o.at[2 * zb + k], (c, target))

        def own_local(zb):
            return pltpu.make_async_copy(held.at[zb], columns(w_out, 2 * zb + k), rs_o.at[2 * zb + k])

        def next_column(zb):
            return remote(
                held.at[zb], columns(w_out, 2 * zb + k), ss_b.at[zb], rs_o.at[2 * zb + k], (2 * z + 1 - y, target)
            )

        def spread(zb):
            next_column(zb).start()

            @pl.when(k == y)
            def _():
                own_local(zb).start()

            @pl.when(k != y)
            def _():
                own_column(zb).start()

        total = p_ref[2 * x + y].astype(F32)
        for d in range(3):
            scatter(d).wait_recv()
            total += got[d].astype(F32)
        held[z] = total.astype(BF)

        @pl.when(z < depth - 1)
        def _():
            chain(z, ss_up.at[0], up).start()

        @pl.when(z > 0)
        def _():
            chain(z, ss_dn.at[0], down).start()

        spread(z)
        send_all(range(1, count, 2))

        @pl.when(k == y)
        def _():
            for half in range(2):
                pltpu.make_async_copy(a_ref.at[block_at(c, half, count)], there(half), rs.at[pair, half]).start()

        @pl.when(k != y)
        def _():
            for half in range(2):
                send(0, half).start()

        weight_share.start()
        weight_own.start()
        gain_send(0).wait_recv()
        sum_g[1] = sum_g[0] + got_g[0]
        gain_send(1).start()

        across_y = (c + 1 - 2 * y, f)

        def slab_send(i):
            zt = (z + i) % depth
            return remote(o_ref, o_out.at[c], ss_of.at[i], rs_of.at[c], (2 * zt + y, f))

        def slab_on(i):
            cs = 2 * ((z + i) % depth) + y
            src = o_out.at[cs] if i else o_ref
            return remote(src, o_out.at[cs], ss_of.at[depth + i], rs_of.at[cs], across_y)

        def gain_spread(i):
            return remote(sum_g.at[2], got_gc.at[c], ss_gc.at[i], rs_gc.at[c], ((c + i) % count, f))

        slab_sum = h_ref[0, 0:slab].astype(F32)
        for i in range(1, count):
            slab_sum += h_ref[i, 0:slab].astype(F32)
        o_ref[...] = slab_sum.astype(BF)
        slab_own = pltpu.make_async_copy(o_ref, o_out.at[c], rs_of.at[c])
        slab_own.start()
        slab_on(0).start()
        for i in range(1, depth):
            slab_send(i).start()
        for hop in range(1, depth):

            @pl.when(z - hop >= 0)
            def _(hop=hop):
                chain(z - hop, ss_up.at[hop], sib).wait_recv()

                @pl.when(z < depth - 1)
                def _():
                    chain(z - hop, ss_up.at[hop], up).start()

                spread(z - hop)

            @pl.when(z + hop <= depth - 1)
            def _(hop=hop):
                chain(z + hop, ss_dn.at[hop], sib).wait_recv()

                @pl.when(z > 0)
                def _():
                    chain(z + hop, ss_dn.at[hop], down).start()

                spread(z + hop)

            weight_pass(hop - 1)
            if hop == 2:
                for i in range(1, depth):
                    cs = 2 * ((z + i) % depth) + y
                    remote(o_ref, o_out.at[cs], ss_of.at[i], rs_of.at[cs], sib).wait_recv()
                    slab_on(i).start()
            if hop == 1:
                gain_send(1).wait_recv()
                sum_g[2] = sum_g[1] + got_g[1]
                for i in range(1, count):
                    gain_spread(i).start()
        for i in range(depth - 1, pieces):
            weight_pass(i)
        total_g = sum_g[2]
        for i in range(1, count):
            cs = (c + i) % count
            remote(sum_g.at[2], got_gc.at[cs], ss_gc.at[i], rs_gc.at[cs], sib).wait_recv()
            total_g += got_gc[cs]
        g_out[...] = total_g

        gain_send(0).wait_send()
        gain_send(1).wait_send()
        for i in range(pieces):
            weight_across(i).wait_send()
            weight_on(i, (f + 2) % 4).wait_send()
            remote(weight_part(0, i), weight_part(0, i), ss_wf.at[i], rs_wf.at[i], sib).wait_recv()
        weight_share.wait()
        weight_own.wait()
        for d in range(3):
            scatter(d).wait_send()
        for other in range(count):
            for half in range(2):
                remote(a_ref.at[0], columns(tok_out.at[half], other), ss.at[0, half], rs.at[other, half], sib).wait_recv()
            remote(held.at[0], columns(w_out, other), ss_a.at[0], rs_o.at[other], sib).wait_recv()
        for i in range(1, count):
            for half in range(2):
                send(i, half).wait_send()
            gain_spread(i).wait_send()
        for i in range(depth):
            if i:
                slab_send(i).wait_send()
            slab_on(i).wait_send()
            cs = 2 * ((z + i) % depth) + 1 - y
            remote(o_ref, o_out.at[cs], ss_of.at[i], rs_of.at[cs], sib).wait_recv()
        slab_own.wait()

        @pl.when(k != y)
        def _():
            for half in range(2):
                send(0, half).wait_send()
            for zb in range(depth):
                own_column(zb).wait_send()

        for zb in range(depth):
            next_column(zb).wait_send()
        for hop in range(depth):

            @pl.when((z < depth - 1) & (z - hop >= 0))
            def _(hop=hop):
                chain(z - hop, ss_up.at[hop], up).wait_send()

            @pl.when((z > 0) & (z + hop <= depth - 1))
            def _(hop=hop):
                chain(z + hop, ss_dn.at[hop], down).wait_send()

    vmem = pl.BlockSpec(memory_space=pltpu.VMEM)
    eighth = gain_part.shape
    return pl.pallas_call(
        kernel,
        name="finish_exchange",
        cost_estimate=lasting(60),
        out_shape=(
            jax.ShapeDtypeStruct((2, half_rows, count * part), BF),
            jax.ShapeDtypeStruct((rows, count * part), BF),
            jax.ShapeDtypeStruct((count, slab, slabs.shape[2]), BF),
            jax.ShapeDtypeStruct(eighth, F32),
            jax.ShapeDtypeStruct((4,) + weight.shape, BF),
        ),
        in_specs=[vmem] * 5,
        out_specs=(ANY, ANY, ANY, vmem, ANY),
        scratch_shapes=[
            pltpu.VMEM((slab, slabs.shape[2]), BF),
            pltpu.VMEM((3, rows, part), BF),
            pltpu.VMEM((depth, rows, part), BF),
            pltpu.VMEM((2,) + eighth, F32),
            pltpu.VMEM((3,) + eighth, F32),
            pltpu.VMEM((count,) + eighth, F32),
            DMA((count, 2)), DMA((count, 2)), DMA((3,)), DMA((3,)), DMA((depth,)), DMA((depth,)), DMA((depth,)),
            DMA((depth,)), DMA((depth,)), DMA((count,)),
            DMA((count,)), DMA((count,)), DMA((2,)), DMA((2,)), DMA((count,)), DMA((count,)),
            DMA((pieces,)), DMA((pieces,)), DMA, DMA, DMA((pieces,)), DMA((pieces,)), DMA,
        ],
        compiler_params=params(),
    )(grads, parts, slabs, gain_part, weight)


def finish_local(
    grad_projected, projection, tokens, gain, grad_middle, middle, dispatch, home, weight_grad, weight, out_slabs, gain_sum
):
    rows, width = tokens.shape
    quarter, wide = weight.shape
    lanes = 128
    part = 3 * lanes
    count = wide // part
    slot_rows = EXPERTS // count * CAP

    def kernel(p_ref, w_ref, x_ref, g_ref, m_ref, mid_ref, d_ref, e_ref, wg_ref, wl_ref, o_ref, gs_ref, block, token, wout, oout, gout, gout_two, acc):
        j = pl.program_id(0)
        own = pl.ds(pl.multiple_of(lax.axis_index("fsdp") * quarter, quarter), quarter)
        acc[j] = lax.dot_general(p_ref[...], w_ref[0], CONTRACT_LAST, preferred_element_type=F32)

        @pl.when(j == 0)
        def _():
            slots = e_ref[:, home.shape[1] - slot_rows :].reshape(-1, width)
            summed = lax.dot_general(d_ref[...], slots, CONTRACT_FIRST, preferred_element_type=F32)
            block[...] = (mid_ref[...] + summed).astype(BF)
            oout[...] = o_ref[...].astype(F32)

        @pl.when(j == 1)
        def _():
            total = jnp.zeros((quarter, 1), F32)
            for number in range(count):
                for kind in range(3):
                    at = number * part + kind * lanes
                    value = wg_ref[:, at : at + lanes].astype(F32)
                    to = (kind * count + number) * lanes
                    wout[:, to : to + lanes] = value
                    total += jnp.sum(value * wl_ref[:, at : at + lanes].astype(F32), axis=1, keepdims=True)
            gout[...] = jnp.broadcast_to(total, (quarter, lanes)).T[0:1] / g_ref[:, own]
            gout_two[...] = gs_ref[:, own]

        @pl.when(j == 3)
        def _():
            hat, inverse = statistics(x_ref[...].astype(F32))
            scaled = jnp.concatenate([acc[i] for i in range(4)], axis=1) * g_ref[...]
            mean_grad = jnp.mean(scaled, axis=1, keepdims=True)
            mean_proj = jnp.mean(scaled * hat, axis=1, keepdims=True)
            token[...] = m_ref[...] + inverse * (scaled - mean_grad - hat * mean_proj)

    def whole(value):
        return pl.BlockSpec(value.shape, lambda j: (0,) * value.ndim)

    shapes = (
        jax.ShapeDtypeStruct((rows, width), BF),
        jax.ShapeDtypeStruct((rows, width), F32),
        jax.ShapeDtypeStruct((quarter, wide), F32),
        jax.ShapeDtypeStruct((quarter, width), F32),
        jax.ShapeDtypeStruct((1, quarter), F32),
        jax.ShapeDtypeStruct((1, quarter), F32),
    )
    rest = (tokens, gain, grad_middle, middle, dispatch, home, weight_grad, weight, out_slabs, gain_sum)
    return pl.pallas_call(
        kernel,
        name="finish_local",
        cost_estimate=lasting(9),
        grid=(4,),
        in_specs=[whole(grad_projected), pl.BlockSpec((1, quarter, wide), lambda j: (j, 0, 0))] + [whole(v) for v in rest],
        out_specs=[whole(v) for v in shapes],
        out_shape=shapes,
        scratch_shapes=[pltpu.VMEM((4, rows, quarter), F32)],
        compiler_params=params(False),
    )(grad_projected, projection, *rest)


def by_head_pairs(
    tokens, doc_starts, expert_ids, query_key_value_weight, output_weight_matrix, expert_in, expert_out, gain_one, gain_two, grad_output
):
    half_rows = tokens.shape[3]
    width = tokens.shape[4]
    count = lax.axis_size("ctx")
    rows = 2 * half_rows
    length = count * rows
    scale = (width // HEADS) ** (-0.5)
    lanes = 2 * (width // HEADS)
    shard_rows = width // 4
    own_tokens = tokens.reshape(rows, width)
    cotangent = grad_output.reshape(rows, width)
    gain_row = gain_one.reshape(1, width)
    stream, starts, columns, out_beside, out_far, out_diagonal, send_grads, qkv_low, out_own, dispatch = gather_stream(
        own_tokens.reshape(2, half_rows, width),
        gain_row,
        expert_ids.reshape(1, rows),
        cotangent,
        doc_starts.reshape(2, half_rows),
        query_key_value_weight,
        output_weight_matrix,
    )
    grads_near = lax.all_to_all(send_grads, "ctx", split_axis=0, concat_axis=0, tiled=True)
    stream = stream.reshape(length, width)
    start_row = jnp.concatenate([starts[:, 0].reshape(-1), starts[::-1, 1].reshape(-1)])[None]
    numbers = jnp.min(start_row.reshape(-1, TILE), axis=1) // TILE
    qkv, mixed16, mixed32, logs = attend_forward(stream, columns, start_row, numbers, scale)
    grads_near = after(grads_near, mixed16)
    mixed, middle, all_rows, *other_grads, active, grad_hidden, grad_heads, grad_middle, grad_gain_two, later = experts_exchange(
        mixed16.reshape(2 * count, half_rows, lanes),
        [out_own, out_beside, out_far, out_diagonal],
        own_tokens,
        dispatch,
        gain_two.reshape(1, width),
        cotangent,
        grads_near,
        expert_in,
        expert_out,
    )
    home = lax.all_to_all(later, "ctx", split_axis=0, concat_axis=0, tiled=True)
    own_grads, parts, grad_in, grad_outw = backward_local(
        qkv,
        after(grad_heads, later).reshape(length, lanes),
        mixed32,
        logs,
        start_row,
        numbers,
        scale,
        stream,
        all_rows,
        [grads_near, *other_grads],
        active,
        grad_hidden,
    )
    home = after(home, own_grads)
    grad_projected, weight_grad, shard_out, gain_sum, projection = finish_exchange(
        own_grads.reshape(2 * count, half_rows, 3 * lanes),
        parts.reshape(4, shard_rows, 3 * lanes),
        home,
        grad_gain_two,
        qkv_low,
    )
    block_out, grad_start, weight_grad, shard_out, shard_gain_one, shard_gain_two = finish_local(
        grad_projected.reshape(rows, 3 * width),
        projection,
        own_tokens,
        gain_row,
        grad_middle,
        middle,
        dispatch,
        home,
        weight_grad,
        qkv_low,
        shard_out.reshape(shard_rows, width),
        gain_sum,
    )
    shard_gain_one = shard_gain_one.reshape(shard_rows)
    shard_gain_two = shard_gain_two.reshape(shard_rows)
    return (
        block_out.reshape(tokens.shape),
        grad_start.reshape(tokens.shape),
        weight_grad,
        shard_out,
        grad_in,
        grad_outw,
        shard_gain_one,
        shard_gain_two,
    )


def solution(mesh):
    pairs = mesh.shape["ctx"] * 2 == HEADS and mesh.shape["fsdp"] == 4
    return jax.shard_map(
        by_head_pairs if pairs else shards,
        mesh=mesh,
        in_specs=(
            P("fsdp", "ctx", None, None, None),
            P("fsdp", "ctx", None, None),
            P("fsdp", "ctx", None, None, None),
            P("fsdp", None),
            P("fsdp", None),
            P("ctx", None, "fsdp"),
            P("ctx", "fsdp", None),
            P(),
            P(),
            P("fsdp", "ctx", None, None, None),
        ),
        out_specs=(
            P("fsdp", "ctx", None, None, None),
            P("fsdp", "ctx", None, None, None),
            P("fsdp", None),
            P("fsdp", None),
            P("ctx", None, "fsdp"),
            P("ctx", "fsdp", None),
            P("fsdp"),
            P("fsdp"),
        ),
        check_vma=False,
    )
```

```python
import math

import jax
import jax.numpy as jnp
from jax import lax
from jax.experimental import pallas as pl
from jax.experimental.pallas import tpu as pltpu
from jax.sharding import PartitionSpec as P

HEADS = 16
EXPERTS = 64
CAP = 8


EPS = 1e-05
NEGATIVE = -1e30


def position_of(row_ids, ctx_count, half_rows):
    device = row_ids // (2 * half_rows)
    upper_half = row_ids // half_rows % 2
    offset = row_ids % half_rows
    return jnp.where(
        upper_half == 0,
        device * half_rows + offset,
        (2 * ctx_count - 1 - device) * half_rows + offset,
    )


def norm_forward(value, gain):
    row_mean = jnp.mean(value, axis=-1, keepdims=True)
    centred = value - row_mean
    inverse = lax.rsqrt(jnp.mean(centred * centred, axis=-1, keepdims=True) + EPS)
    normed = centred * inverse
    return (normed * gain, normed, inverse)


def norm_backward(gradient, normed, inverse, gain):
    scaled = gradient * gain
    mean_grad = jnp.mean(scaled, axis=-1, keepdims=True)
    mean_proj = jnp.mean(scaled * normed, axis=-1, keepdims=True)
    return (
        inverse * (scaled - mean_grad - normed * mean_proj),
        jnp.sum(gradient * normed, axis=(0, 1)),
    )


def scores(query, keys, query_pos, key_pos, query_start, score_scale):
    raw_scores = (
        jnp.einsum("qshe,kshe->shqk", query, keys, preferred_element_type=jnp.float32) * score_scale
    )
    visible = (key_pos[None, None, None, :] <= query_pos[None, None, :, None]) & (
        key_pos[None, None, None, :] >= query_start.T[:, None, :, None]
    )
    return jnp.where(visible, raw_scores, NEGATIVE)


def log_totals(query, keys, query_pos, query_start, score_scale, ctx_count, half_rows, key_block):
    block_count = keys.shape[0] // key_block
    carry_shape = (query.shape[1], query.shape[2], query.shape[0])

    def log_one_block(block_index, carried):
        running_max, running = carried
        first_row = block_index * key_block
        key_piece = lax.dynamic_slice_in_dim(keys, first_row, key_block, 0)
        key_pos = position_of(
            first_row + jnp.arange(key_block, dtype=jnp.int32), ctx_count, half_rows
        )
        score_rows = scores(query, key_piece, query_pos, key_pos, query_start, score_scale)
        new_max = jnp.maximum(running_max, jnp.max(score_rows, axis=-1))
        running = running * jnp.exp(running_max - new_max) + jnp.sum(
            jnp.exp(score_rows - new_max[..., None]), axis=-1
        )
        return (new_max, running)

    running_max, running = lax.fori_loop(
        0,
        block_count,
        log_one_block,
        (jnp.full(carry_shape, NEGATIVE, jnp.float32), jnp.zeros(carry_shape, jnp.float32)),
    )
    return running_max + jnp.log(running)


def attend(
    query,
    keys,
    values,
    query_pos,
    query_start,
    log_total,
    score_scale,
    ctx_count,
    half_rows,
    key_block,
):
    block_count = keys.shape[0] // key_block
    zeros_init = jnp.zeros(query.shape, jnp.float32)

    def attend_one_block(block_index, carried):
        output, remainder = carried
        first_row = block_index * key_block
        key_piece = lax.dynamic_slice_in_dim(keys, first_row, key_block, 0)
        value_piece = lax.dynamic_slice_in_dim(values, first_row, key_block, 0)
        key_pos = position_of(
            first_row + jnp.arange(key_block, dtype=jnp.int32), ctx_count, half_rows
        )
        weights = jnp.exp(
            scores(query, key_piece, query_pos, key_pos, query_start, score_scale)
            - log_total[..., None]
        )
        rounded = weights.astype(jnp.bfloat16)
        leftover = (weights - rounded.astype(jnp.float32)).astype(jnp.bfloat16)
        output = output + jnp.einsum(
            "shqk,kshe->qshe", rounded, value_piece, preferred_element_type=jnp.float32
        )
        remainder = remainder + jnp.einsum(
            "shqk,kshe->qshe", leftover, value_piece, preferred_element_type=jnp.float32
        )
        return (output, remainder)

    return lax.fori_loop(0, block_count, attend_one_block, (zeros_init, zeros_init))


def query_grads(
    query,
    keys,
    values,
    grad_heads,
    query_pos,
    query_start,
    log_total,
    row_delta,
    score_scale,
    ctx_count,
    half_rows,
    key_block,
):
    block_count = keys.shape[0] // key_block

    def query_one_block(block_index, running):
        first_row = block_index * key_block
        key_piece = lax.dynamic_slice_in_dim(keys, first_row, key_block, 0)
        value_piece = lax.dynamic_slice_in_dim(values, first_row, key_block, 0)
        key_pos = position_of(
            first_row + jnp.arange(key_block, dtype=jnp.int32), ctx_count, half_rows
        )
        weights = jnp.exp(
            scores(query, key_piece, query_pos, key_pos, query_start, score_scale)
            - log_total[..., None]
        )
        grad_weight = jnp.einsum(
            "qshe,kshe->shqk", grad_heads, value_piece, preferred_element_type=jnp.float32
        )
        grad_score = (weights * (grad_weight - row_delta[..., None])).astype(jnp.bfloat16)
        return running + jnp.einsum(
            "shqk,kshe->qshe", grad_score, key_piece, preferred_element_type=jnp.float32
        )

    return (
        lax.fori_loop(0, block_count, query_one_block, jnp.zeros(query.shape, jnp.float32))
        * score_scale
    )


def key_grads(
    query,
    grad_heads,
    query_pos,
    query_start,
    log_total,
    row_delta,
    key_piece,
    value_piece,
    key_pos,
    score_scale,
):
    weights = jnp.exp(
        scores(query, key_piece, query_pos, key_pos, query_start, score_scale)
        - log_total[..., None]
    )
    grad_weight = jnp.einsum(
        "qshe,kshe->shqk", grad_heads, value_piece, preferred_element_type=jnp.float32
    )
    grad_score = (weights * (grad_weight - row_delta[..., None])).astype(jnp.bfloat16)
    key_part = (
        jnp.einsum("shqk,qshe->kshe", grad_score, query, preferred_element_type=jnp.float32)
        * score_scale
    )
    value_part = jnp.einsum(
        "shqk,qshe->kshe",
        weights.astype(jnp.bfloat16),
        grad_heads,
        preferred_element_type=jnp.float32,
    )
    return (key_part, value_part)


def shards(
    tokens,
    doc_starts,
    expert_ids,
    query_key_value_weight,
    output_weight_matrix,
    expert_in,
    expert_out,
    gain_one,
    gain_two,
    grad_output,
):
    seq_dev = tokens.shape[0]
    half_rows = tokens.shape[3]
    model_width = tokens.shape[4]
    local_rows = 2 * half_rows
    ctx_count = lax.axis_size("ctx")
    head_count = HEADS
    head_size = model_width // head_count
    score_scale = head_size ** (-0.5)
    keys_total = ctx_count * local_rows
    key_block = min(512, keys_total)
    own_rows = lax.axis_index("ctx") * local_rows + jnp.arange(local_rows, dtype=jnp.int32)
    query_pos = position_of(own_rows, ctx_count, half_rows)
    query_start = doc_starts.reshape(seq_dev, local_rows).T
    routes_local = expert_ids.reshape(seq_dev, local_rows).T
    start_x = (
        tokens.reshape(seq_dev, local_rows, model_width).transpose(1, 0, 2).astype(jnp.float32)
    )
    cotangent = grad_output.reshape(seq_dev, local_rows, model_width).transpose(1, 0, 2)
    projection, out_proj = (
        lax.all_gather(query_key_value_weight.astype(jnp.bfloat16), "fsdp", axis=0, tiled=True),
        lax.all_gather(output_weight_matrix.astype(jnp.bfloat16), "fsdp", axis=0, tiled=True),
    )
    first_normed_rows, hat_one, inverse_one = norm_forward(start_x, gain_one)
    normed_low = first_normed_rows.astype(jnp.bfloat16)
    projected_rows = jnp.einsum(
        "tsd,de->tse", normed_low, projection, preferred_element_type=jnp.float32
    ).astype(jnp.bfloat16)
    query = projected_rows[..., :model_width]
    keys = projected_rows[..., model_width : 2 * model_width]
    values = projected_rows[..., 2 * model_width :]
    key_all, value_all = (
        lax.all_gather(keys, "ctx", axis=0, tiled=True),
        lax.all_gather(values, "ctx", axis=0, tiled=True),
    )
    query_heads = query.reshape(local_rows, seq_dev, head_count, head_size)
    key_heads = key_all.reshape(keys_total, seq_dev, head_count, head_size)
    value_heads = value_all.reshape(keys_total, seq_dev, head_count, head_size)
    log_total = log_totals(
        query_heads, key_heads, query_pos, query_start, score_scale, ctx_count, half_rows, key_block
    )
    mixed_heads_out, remainder = attend(
        query_heads,
        key_heads,
        value_heads,
        query_pos,
        query_start,
        log_total,
        score_scale,
        ctx_count,
        half_rows,
        key_block,
    )
    mixed_low = mixed_heads_out.astype(jnp.bfloat16).reshape(local_rows, seq_dev, model_width)
    attention_rows_out = jnp.einsum(
        "tsd,de->tse", mixed_low, out_proj, preferred_element_type=jnp.float32
    )
    middle = start_x + attention_rows_out
    normed_two, hat_two, inverse_two = norm_forward(middle, gain_two)
    routed = normed_two.astype(jnp.bfloat16)
    slot_count = EXPERTS * CAP
    per_owner = EXPERTS // ctx_count
    chosen = (routes_local[..., None] == jnp.arange(EXPERTS, dtype=jnp.int32)).astype(jnp.int32)
    earlier = (
        jnp.arange(local_rows)[:, None] >= jnp.arange(local_rows)[None, :]
    ).astype(jnp.bfloat16)
    running = jnp.einsum(
        "tu,use->tse", earlier, chosen.astype(jnp.bfloat16), preferred_element_type=jnp.float32
    )
    rank_within = jnp.sum(chosen * running.astype(jnp.int32), axis=-1) - 1
    slot_index = routes_local * CAP + rank_within
    dispatch = (
        slot_index.T[:, None, :] == jnp.arange(slot_count, dtype=jnp.int32)[None, :, None]
    ).astype(jnp.bfloat16)
    dispatch = dispatch.reshape(seq_dev, ctx_count, per_owner, CAP, local_rows)
    send_rows = jnp.einsum(
        "snect,tsd->nescd", dispatch, routed, preferred_element_type=jnp.float32
    ).astype(jnp.bfloat16)
    send_grads = jnp.einsum(
        "snect,tsd->nescd", dispatch, cotangent, preferred_element_type=jnp.float32
    ).astype(jnp.bfloat16)
    got_rows, got_grads = (
        lax.all_to_all(send_rows, "ctx", split_axis=0, concat_axis=0, tiled=True),
        lax.all_to_all(send_grads, "ctx", split_axis=0, concat_axis=0, tiled=True),
    )
    in_low = expert_in.astype(jnp.bfloat16)
    out_low = expert_out.astype(jnp.bfloat16)
    all_rows, all_grads = (
        lax.all_gather(got_rows, "fsdp", axis=2, tiled=True),
        lax.all_gather(got_grads, "fsdp", axis=2, tiled=True),
    )
    hidden = jnp.einsum("nercd,edf->nercf", all_rows, in_low, preferred_element_type=jnp.float32)
    active = jax.nn.gelu(hidden).astype(jnp.bfloat16)
    partial_rows = jnp.einsum(
        "nercf,efd->nercd", active, out_low, preferred_element_type=jnp.float32
    )
    result = lax.psum_scatter(
        partial_rows.astype(jnp.bfloat16), "fsdp", scatter_dimension=2, tiled=True
    )
    upstream = jnp.einsum(
        "nercd,efd->nercf", all_grads, out_low, preferred_element_type=jnp.float32
    )
    unused, gelu_back = jax.vjp(jax.nn.gelu, hidden)
    grad_hidden = gelu_back(upstream)[0].astype(jnp.bfloat16)
    grad_in = jnp.einsum(
        "nercd,nercf->edf", all_rows, grad_hidden, preferred_element_type=jnp.float32
    )
    grad_outw = jnp.einsum(
        "nercf,nercd->efd", active, all_grads, preferred_element_type=jnp.float32
    )
    row_part = jnp.einsum(
        "nercf,edf->nercd", grad_hidden, in_low, preferred_element_type=jnp.float32
    )
    row_grad = lax.psum_scatter(row_part, "fsdp", scatter_dimension=2, tiled=True).astype(
        jnp.bfloat16
    )
    back_rows = lax.all_to_all(result, "ctx", split_axis=0, concat_axis=0, tiled=True)
    expert_sum = jnp.einsum(
        "snect,nescd->tsd", dispatch, back_rows, preferred_element_type=jnp.float32
    )
    output_rows = middle + expert_sum
    returned = lax.all_to_all(row_grad, "ctx", split_axis=0, concat_axis=0, tiled=True)
    grad_routed = jnp.einsum(
        "snect,nescd->tsd", dispatch, returned, preferred_element_type=jnp.float32
    )
    grad_mid_norm, grad_gain_two = norm_backward(grad_routed, hat_two, inverse_two, gain_two)
    grad_middle = cotangent.astype(jnp.float32) + grad_mid_norm
    grad_attn = grad_middle.astype(jnp.bfloat16)
    grad_outproj = jnp.einsum(
        "tsd,tse->de", mixed_low, grad_attn, preferred_element_type=jnp.float32
    )
    grad_mixed = jnp.einsum(
        "tse,de->tsd", grad_attn, out_proj, preferred_element_type=jnp.float32
    ).astype(jnp.bfloat16)
    grad_heads = grad_mixed.reshape(local_rows, seq_dev, head_count, head_size)
    full_mixed = mixed_heads_out + remainder
    row_delta = jnp.sum(grad_heads.astype(jnp.float32) * full_mixed, axis=-1).transpose(1, 2, 0)
    grad_query = query_grads(
        query_heads,
        key_heads,
        value_heads,
        grad_heads,
        query_pos,
        query_start,
        log_total,
        row_delta,
        score_scale,
        ctx_count,
        half_rows,
        key_block,
    ).astype(jnp.bfloat16)
    sub_rows = math.gcd(local_rows * lax.axis_size("ctx"), key_block)

    def one_piece(piece_index):
        piece_start = piece_index * sub_rows
        key_piece = lax.dynamic_slice_in_dim(key_heads, piece_start, sub_rows, 0)
        value_piece = lax.dynamic_slice_in_dim(value_heads, piece_start, sub_rows, 0)
        key_pos = position_of(
            piece_start + jnp.arange(sub_rows, dtype=jnp.int32), ctx_count, half_rows
        )
        key_part, value_part = key_grads(
            query_heads,
            grad_heads,
            query_pos,
            query_start,
            log_total,
            row_delta,
            key_piece,
            value_piece,
            key_pos,
            score_scale,
        )
        return jnp.concatenate(
            [
                key_part.reshape(sub_rows, seq_dev, model_width),
                value_part.reshape(sub_rows, seq_dev, model_width),
            ],
            axis=-1,
        )

    summed = lax.psum_scatter(
        lax.map(
            one_piece, jnp.arange(local_rows * lax.axis_size("ctx") // sub_rows, dtype=jnp.int32)
        ).reshape(local_rows * lax.axis_size("ctx"), seq_dev, 2 * model_width),
        "ctx",
        scatter_dimension=0,
        tiled=True,
    )
    grad_key = summed[..., :model_width].astype(jnp.bfloat16)
    grad_value = summed[..., model_width:].astype(jnp.bfloat16)
    grad_projected = jnp.concatenate(
        [grad_query.reshape(local_rows, seq_dev, model_width), grad_key, grad_value], axis=-1
    )
    grad_projection = jnp.einsum(
        "tsd,tse->de", normed_low, grad_projected, preferred_element_type=jnp.float32
    )
    grad_normed = jnp.einsum(
        "tse,de->tsd", grad_projected, projection, preferred_element_type=jnp.float32
    )
    grad_in_norm, grad_gain_one = norm_backward(grad_normed, hat_one, inverse_one, gain_one)
    grad_start = grad_middle + grad_in_norm
    shard_proj, shard_outproj, shard_gain_one, shard_gain_two = (
        lax.psum_scatter(
            grad_projection.astype(jnp.bfloat16), "fsdp", scatter_dimension=0, tiled=True
        ).astype(jnp.float32),
        lax.psum_scatter(
            grad_outproj.astype(jnp.bfloat16), "fsdp", scatter_dimension=0, tiled=True
        ).astype(jnp.float32),
        lax.psum_scatter(
            grad_gain_one.astype(jnp.bfloat16), "fsdp", scatter_dimension=0, tiled=True
        ).astype(jnp.float32),
        lax.psum_scatter(
            grad_gain_two.astype(jnp.bfloat16), "fsdp", scatter_dimension=0, tiled=True
        ).astype(jnp.float32),
    )
    shard_proj, shard_outproj, shard_gain_one, shard_gain_two = (
        lax.psum(shard_proj.astype(jnp.bfloat16), "ctx").astype(jnp.float32),
        lax.psum(shard_outproj.astype(jnp.bfloat16), "ctx").astype(jnp.float32),
        lax.psum(shard_gain_one.astype(jnp.bfloat16), "ctx").astype(jnp.float32),
        lax.psum(shard_gain_two.astype(jnp.bfloat16), "ctx").astype(jnp.float32),
    )
    block_out = output_rows.transpose(1, 0, 2).reshape(tokens.shape).astype(jnp.bfloat16)
    grad_tokens = grad_start.transpose(1, 0, 2).reshape(tokens.shape)
    return (
        block_out,
        grad_tokens,
        shard_proj,
        shard_outproj,
        grad_in,
        grad_outw,
        shard_gain_one,
        shard_gain_two,
    )


BF = jnp.bfloat16
F32 = jnp.float32
CONTRACT_FIRST = (((0,), (0,)), ((), ()))
CONTRACT_LAST = (((1,), (1,)), ((), ()))
MESH_ID = pl.DeviceIdType.MESH
ANY = pl.BlockSpec(memory_space=pl.ANY)
DMA = pltpu.SemaphoreType.DMA
VMEM_CAP = 56 << 20


def place():
    c = lax.axis_index("ctx")
    f = lax.axis_index("fsdp")
    return c, f, c // 2, c % 2, f // 2, f % 2


def remote(src, dst, send, recv, device):
    return pltpu.make_async_remote_copy(
        src_ref=src, dst_ref=dst, send_sem=send, recv_sem=recv, device_id=device, device_id_type=MESH_ID
    )


def block_at(c, half, count):
    return c if half == 0 else 2 * count - 1 - c


def statistics(value):
    row_mean = jnp.mean(value, axis=1, keepdims=True)
    centred = value - row_mean
    inverse = lax.rsqrt(jnp.mean(centred * centred, axis=1, keepdims=True) + EPS)
    return centred * inverse, inverse


def stacked(value):
    return value.reshape(-1, value.shape[-1])


def relative(a, b):
    return (a // 2 + b // 2) % 2 * 2 + (a + b) % 2


def swap(value, axis, bit):
    size = lax.axis_size(axis)
    return lax.ppermute(value, axis, [(i, i ^ bit) for i in range(size)])


def lasting(microseconds):
    return pl.CostEstimate(flops=0, bytes_accessed=int(microseconds * 3.3e6), transcendentals=0)


def params(side=True):
    return pltpu.CompilerParams(has_side_effects=side, vmem_limit_bytes=VMEM_CAP)


def gather_stream(tokens, gain, routes, cotangent, starts, weight, matrix):
    count = lax.axis_size("ctx")
    depth = count // 2
    rows, wide = weight.shape
    part = wide // count
    lanes = part // 3
    half_rows, width = tokens.shape[1:]
    own_rows = 2 * half_rows
    own_experts = EXPERTS // count

    def kernel(
        x_ref, g_ref, e_ref, c_ref, s_ref, wf_ref, of_ref, tok, st, cols, beside, far, diagonal, d_ref, w_ref, o_ref, hot,
        n_ref, rs_t, ss_p, ss_up, ss_dn, ss_sib, rs_s, ss_s, rs_w, ss_w, ss_o, rs_o,
    ):
        c, f, z, y, x, k = place()
        sib = (c, f + 1 - 2 * k)
        partner = (c + 1 - 2 * y, f + 1 - 2 * k)
        up = (c + 2, f)
        down = (c - 2, f)
        holder = k == y
        for h in range(2):
            hat, _ = statistics(x_ref[h].astype(F32))
            n_ref[h] = (hat * g_ref[...]).astype(BF)

        def send_in(h):
            b = block_at(c, h, count)
            return remote(n_ref.at[h], tok.at[b], ss_p.at[h], rs_t.at[b], partner)

        def local_in(h):
            b = block_at(c, h, count)
            return pltpu.make_async_copy(n_ref.at[h], tok.at[b], rs_t.at[b])

        @pl.when(holder)
        def _():
            for h in range(2):
                local_in(h).start()

        @pl.when(jnp.logical_not(holder))
        def _():
            for h in range(2):
                send_in(h).start()

        for zt in range(depth):
            for kt in range(2):
                mine = holder & (z == zt) & (k == kt)

                @pl.when(mine)
                def _():
                    pltpu.make_async_copy(s_ref, st.at[c], rs_s.at[c]).start()

                @pl.when(jnp.logical_not(mine))
                def _(zt=zt, kt=kt):
                    remote(s_ref, st.at[c], ss_s.at[2 * zt + kt], rs_s.at[c], (2 * zt + k, 2 * x + kt)).start()

        goals = [(2 * z + k, (c, (f + 2) % 4)), (2 * z + 1 - k, (c, (sib[1] + 2) % 4)), (2 * z + 1 - k, sib)]

        def columns(pair):
            return w_ref.at[:, pl.ds(pl.multiple_of(pair * part, part), part)]

        def weight_place(shard):
            return cols.at[pl.ds(pl.multiple_of(shard * rows, rows), rows)]

        def weight_send(t):
            pair, dev = goals[t]
            return remote(columns(pair), weight_place(f), ss_w.at[t], rs_w.at[f], dev)

        for number in range(count):
            for j in range(3):
                at = number * part + j * lanes
                w_ref[:, at : at + lanes] = wf_ref[:, j * count * lanes + number * lanes :][:, :lanes].astype(BF)
        for t in range(3):
            weight_send(t).start()
        pltpu.make_async_copy(columns(2 * z + k), weight_place(f), rs_w.at[f]).start()
        o_ref[...] = of_ref[...].astype(BF)
        matrix_far = remote(o_ref, far, ss_o.at[0], rs_o.at[0], goals[0][1])
        matrix_beside = remote(o_ref, beside, ss_o.at[1], rs_o.at[1], sib)
        matrix_on = remote(far, diagonal, ss_o.at[2], rs_o.at[2], sib)
        matrix_far.start()
        matrix_beside.start()

        def copy_block(zb, h, ss, dev):
            b = block_at(2 * zb + k, h, count)
            return remote(tok.at[b], tok.at[b], ss, rs_t.at[b], dev)

        for j in range(depth):
            for h in range(2):
                if j == 0:
                    copy_block(z, h, ss_p.at[h], sib).wait_recv()

                    @pl.when(z < depth - 1)
                    def _(h=h):
                        copy_block(z, h, ss_up.at[0, h], up).start()

                    @pl.when(z > 0)
                    def _(h=h):
                        copy_block(z, h, ss_dn.at[0, h], down).start()

                    copy_block(z, h, ss_sib.at[z, h], sib).start()
                    if h == 1:
                        expert = lax.broadcasted_iota(jnp.int32, (EXPERTS, own_rows), 0)
                        chosen = expert == e_ref[...]
                        earlier = lax.broadcasted_iota(jnp.int32, (own_rows, own_rows), 0) <= lax.broadcasted_iota(
                            jnp.int32, (own_rows, own_rows), 1
                        )
                        running = jnp.dot(
                            jnp.where(chosen, 1.0, 0.0).astype(BF),
                            jnp.where(earlier, 1.0, 0.0).astype(BF),
                            preferred_element_type=F32,
                        )
                        rank = jnp.sum(jnp.where(chosen, running, 0.0), axis=0, keepdims=True).astype(jnp.int32) - 1
                        slot = e_ref[...] * CAP + rank
                        index = lax.broadcasted_iota(jnp.int32, (EXPERTS * CAP, own_rows), 0)
                        hot[...] = jnp.where(index == slot, 1.0, 0.0).astype(BF)
                        d_ref[...] = (
                            jnp.dot(hot[...], c_ref[...], preferred_element_type=F32).astype(BF).reshape(d_ref.shape)
                        )
                    continue

                @pl.when(z - j >= 0)
                def _(j=j, h=h):
                    copy_block(z - j, h, ss_p.at[h], sib).wait_recv()

                    @pl.when(z < depth - 1)
                    def _():
                        copy_block(z - j, h, ss_up.at[j, h], up).start()

                    copy_block(z - j, h, ss_sib.at[z - j, h], sib).start()

                @pl.when(z + j <= depth - 1)
                def _(j=j, h=h):
                    copy_block(z + j, h, ss_p.at[h], sib).wait_recv()

                    @pl.when(z > 0)
                    def _():
                        copy_block(z + j, h, ss_dn.at[j, h], down).start()

                    copy_block(z + j, h, ss_sib.at[z + j, h], sib).start()

        matrix_far.wait_recv()
        matrix_on.start()
        for zt in range(depth):
            for h in range(2):
                b = block_at(2 * zt + 1 - k, h, count)
                remote(tok.at[b], tok.at[b], ss_p.at[h], rs_t.at[b], sib).wait_recv()
                copy_block(zt, h, ss_sib.at[zt, h], sib).wait_send()
        for ct in range(count):
            remote(s_ref, st.at[ct], ss_s.at[0], rs_s.at[ct], sib).wait_recv()
        for shard in range(4):
            remote(columns(0), weight_place(shard), ss_w.at[0], rs_w.at[shard], sib).wait_recv()
        for t in range(3):
            weight_send(t).wait_send()
        matrix_far.wait_send()
        matrix_beside.wait()
        matrix_on.wait()

        @pl.when(jnp.logical_not(holder))
        def _():
            for h in range(2):
                send_in(h).wait_send()

        for j in range(depth):

            @pl.when((z < depth - 1) & (z - j >= 0))
            def _(j=j):
                for h in range(2):
                    copy_block(z - j, h, ss_up.at[j, h], up).wait_send()

            @pl.when((z > 0) & (z + j <= depth - 1))
            def _(j=j):
                for h in range(2):
                    copy_block(z + j, h, ss_dn.at[j, h], down).wait_send()

        for zt in range(depth):
            for kt in range(2):
                mine = holder & (z == zt) & (k == kt)

                @pl.when(jnp.logical_not(mine))
                def _(zt=zt, kt=kt):
                    remote(s_ref, st.at[c], ss_s.at[2 * zt + kt], rs_s.at[c], sib).wait_send()

    return pl.pallas_call(
        kernel,
        name="gather_stream",
        cost_estimate=lasting(50),
        out_shape=(
            jax.ShapeDtypeStruct((2 * count, half_rows, width), BF),
            jax.ShapeDtypeStruct((count,) + starts.shape, starts.dtype),
            jax.ShapeDtypeStruct((4 * rows, part), BF),
            *[jax.ShapeDtypeStruct(matrix.shape, BF)] * 3,
            jax.ShapeDtypeStruct((count, own_experts, CAP, width), BF),
            jax.ShapeDtypeStruct((rows, wide), BF),
            jax.ShapeDtypeStruct(matrix.shape, BF),
            jax.ShapeDtypeStruct((EXPERTS * CAP, own_rows), BF),
        ),
        in_specs=[pl.BlockSpec(memory_space=pltpu.VMEM)] * 7,
        out_specs=(ANY,) * 6 + (pl.BlockSpec(memory_space=pltpu.VMEM),) * 4,
        scratch_shapes=[
            pltpu.VMEM((2, half_rows, width), BF),
            DMA((2 * count,)), DMA((2,)), DMA((depth, 2)), DMA((depth, 2)), DMA((depth, 2)),
            DMA((count,)), DMA((count,)), DMA((4,)), DMA((3,)), DMA((3,)), DMA((3,)),
        ],
        compiler_params=params(),
    )(tokens, gain, routes, cotangent, starts, weight, matrix)


TILE = 256


def halves(value, axis):
    size = value.shape[axis] // 2
    at = lax.broadcasted_iota(jnp.int32, value.shape, axis)
    zero = jnp.zeros_like(value)
    return [jnp.where(at < size, value, zero), jnp.where(at >= size, value, zero)]


def attend_forward(stream, columns, start_row, numbers, scale):
    length, width = stream.shape
    tiles = length // TILE
    lanes = 128
    size = lanes // 2

    def kernel(first, x_ref, w_ref, s_ref, out, m16, m32, lse, k_rows, v_turned):
        i = pl.program_id(0)
        own = pl.ds(pl.multiple_of(i * TILE, TILE), TILE)
        rows = x_ref[...]
        projected = jnp.dot(rows, w_ref[...], preferred_element_type=F32).astype(BF)
        out[...] = projected
        query, key, value = [projected[:, j * lanes : (j + 1) * lanes] for j in range(3)]
        k_rows[own, :] = key
        v_turned[:, own] = value.T
        queries = halves((query * scale).T, 0)
        start = s_ref[...]
        key_row = lax.broadcasted_iota(jnp.int32, (TILE, TILE), 0)
        query_column = i * TILE + lax.broadcasted_iota(jnp.int32, (TILE, TILE), 1)

        def step(j, carried):
            at = pl.multiple_of(j * TILE, TILE)
            keys = k_rows[pl.ds(at, TILE), :]
            seen = (key_row + at <= query_column) & (key_row + at >= start)
            out = []
            for h in range(2):
                top, total, mixed = carried[h]
                score = jnp.where(seen, jnp.dot(keys, queries[h], preferred_element_type=F32), NEGATIVE)
                new_top = jnp.maximum(top, jnp.max(score, axis=0, keepdims=True))
                weight = jnp.exp(score - new_top)
                shrink = jnp.exp(top - new_top)
                total = total * shrink + jnp.sum(weight, axis=0, keepdims=True)
                values = v_turned[h * size : (h + 1) * size, pl.ds(at, TILE)]
                mixed = mixed * shrink + jnp.dot(values, weight.astype(BF), preferred_element_type=F32)
                out.append((new_top, total, mixed))
            return tuple(out)

        begin = (
            jnp.full((1, TILE), NEGATIVE, F32),
            jnp.zeros((1, TILE), F32),
            jnp.zeros((size, TILE), F32),
        )
        done = lax.fori_loop(first[i], i + 1, step, (begin, begin))
        mixed = jnp.concatenate([part / total for _, total, part in done], axis=0)
        m32[...] = mixed
        m16[...] = mixed.T.astype(BF)
        lse[...] = jnp.concatenate([top + jnp.log(total) for top, total, _ in done], axis=0)

    tile = pl.BlockSpec((TILE, lanes), lambda i, n: (i, 0))
    turned = pl.BlockSpec((lanes, TILE), lambda i, n: (0, i))
    return pl.pallas_call(
        kernel,
        name="attend_forward",
        cost_estimate=lasting(22),
        grid_spec=pltpu.PrefetchScalarGridSpec(
            num_scalar_prefetch=1,
            grid=(tiles,),
            in_specs=[
                pl.BlockSpec((TILE, width), lambda i, n: (i, 0)),
                pl.BlockSpec((width, 3 * lanes), lambda i, n: (0, 0)),
                pl.BlockSpec((1, TILE), lambda i, n: (0, i)),
            ],
            out_specs=[
                pl.BlockSpec((TILE, 3 * lanes), lambda i, n: (i, 0)),
                tile,
                turned,
                pl.BlockSpec((2, TILE), lambda i, n: (0, i)),
            ],
            scratch_shapes=[pltpu.VMEM((length, lanes), BF), pltpu.VMEM((lanes, length), BF)],
        ),
        out_shape=(
            jax.ShapeDtypeStruct((length, 3 * lanes), BF),
            jax.ShapeDtypeStruct((length, lanes), BF),
            jax.ShapeDtypeStruct((lanes, length), F32),
            jax.ShapeDtypeStruct((2, length), F32),
        ),
        compiler_params=params(False),
    )(numbers, stream, columns, start_row)


def backward_local(qkv, grad, mixed, logs, start_row, numbers, scale, stream, rows, cotangents, active, grad_hidden):
    length = qkv.shape[0]
    lanes = 128
    tiles = length // TILE
    size = lanes // 2
    _, number, count, cap, width = rows.shape
    total_rows, units = active.shape[1:]
    assert tiles == number

    def kernel(
        first, q_ref, k_ref, v_ref, g_ref, m_ref, l_ref, s_ref, x_ref, r_ref, g0_ref, g1_ref, a_ref, h_ref,
        out, weight, da, db, acc_k, acc_v, k_turned,
    ):
        i = pl.program_id(0)
        gradient = jnp.concatenate([stacked(g0_ref[...]), stacked(g1_ref[...])], axis=0)
        da[0] = lax.dot_general(stacked(r_ref[...]), h_ref[0], CONTRACT_FIRST, preferred_element_type=F32)
        db[0] = lax.dot_general(a_ref[0], gradient, CONTRACT_FIRST, preferred_element_type=F32)

        @pl.when(i == 0)
        def _():
            acc_k[...] = jnp.zeros_like(acc_k)
            acc_v[...] = jnp.zeros_like(acc_v)
            for t in range(tiles):
                k_turned[:, t * TILE : (t + 1) * TILE] = k_ref[t * TILE : (t + 1) * TILE, :].T

        scaled = q_ref[...] * scale
        grads = g_ref[...]
        turned = grads.T
        queries, queries_turned = halves(scaled, 1), halves(scaled.T, 0)
        grad_rows, grads_turned = halves(grads, 1), halves(turned, 0)
        product = turned.astype(F32) * m_ref[...]
        deltas = [jnp.sum(product[h * size : (h + 1) * size], axis=0, keepdims=True) for h in range(2)]
        logs_row = [l_ref[h : h + 1, :] for h in range(2)]
        start = s_ref[...]
        key_row = lax.broadcasted_iota(jnp.int32, (TILE, TILE), 0)
        query_column = i * TILE + lax.broadcasted_iota(jnp.int32, (TILE, TILE), 1)

        def step(j, running):
            at = pl.multiple_of(j * TILE, TILE)
            keys = k_ref[pl.ds(at, TILE), :]
            values = v_ref[pl.ds(at, TILE), :]
            seen = (key_row + at <= query_column) & (key_row + at >= start)
            key_sum = jnp.zeros((TILE, lanes), F32)
            value_sum = jnp.zeros((TILE, lanes), F32)
            out = []
            for h in range(2):
                score = jnp.dot(keys, queries_turned[h], preferred_element_type=F32)
                weight = jnp.exp(jnp.where(seen, score - logs_row[h], NEGATIVE))
                grad_weight = jnp.dot(values, grads_turned[h], preferred_element_type=F32)
                grad_score = (weight * (grad_weight - deltas[h])).astype(BF)
                value_sum += jnp.dot(weight.astype(BF), grad_rows[h], preferred_element_type=F32)
                key_sum += jnp.dot(grad_score, queries[h], preferred_element_type=F32)
                part = k_turned[h * size : (h + 1) * size, pl.ds(at, TILE)]
                out.append(running[h] + jnp.dot(part, grad_score, preferred_element_type=F32))
            acc_k[pl.ds(at, TILE), :] += key_sum
            acc_v[pl.ds(at, TILE), :] += value_sum
            return tuple(out)

        zero = jnp.zeros((size, TILE), F32)
        total = lax.fori_loop(first[i], i + 1, step, (zero, zero))
        own = pl.ds(pl.multiple_of(i * TILE, TILE), TILE)
        out[own, 0:lanes] = (jnp.concatenate(total, axis=0) * scale).T.astype(BF)

        @pl.when(i == tiles - 1)
        def _():
            out[:, lanes : 2 * lanes] = acc_k[...].astype(BF)
            out[:, 2 * lanes : 3 * lanes] = acc_v[...].astype(BF)
            weight[...] = lax.dot_general(x_ref[...], out[...], CONTRACT_FIRST, preferred_element_type=F32).astype(BF)

    tile = pl.BlockSpec((TILE, lanes), lambda i, n: (i, 0))
    quarter = pl.BlockSpec((count, 1, cap, width), lambda i, n: (0, i, 0, 0))
    wide = pl.BlockSpec((1, total_rows, units), lambda i, n: (i, 0, 0))
    return pl.pallas_call(
        kernel,
        name="backward_local",
        cost_estimate=lasting(30),
        grid_spec=pltpu.PrefetchScalarGridSpec(
            num_scalar_prefetch=1,
            grid=(tiles,),
            in_specs=[
                tile,
                pl.BlockSpec((length, lanes), lambda i, n: (0, 1)),
                pl.BlockSpec((length, lanes), lambda i, n: (0, 2)),
                tile,
                pl.BlockSpec((lanes, TILE), lambda i, n: (0, i)),
                pl.BlockSpec((2, TILE), lambda i, n: (0, i)),
                pl.BlockSpec((1, TILE), lambda i, n: (0, i)),
                pl.BlockSpec((length, width), lambda i, n: (0, 0), pipeline_mode=pl.Buffered(1)),
                pl.BlockSpec((4, 1, count, cap, width), lambda i, n: (0, i, 0, 0, 0)),
                quarter,
                pl.BlockSpec((3, count, 1, cap, width), lambda i, n: (0, 0, i, 0, 0)),
                wide,
                wide,
            ],
            out_specs=[
                pl.BlockSpec((length, 3 * lanes), lambda i, n: (0, 0)),
                pl.BlockSpec((width, 3 * lanes), lambda i, n: (0, 0)),
                pl.BlockSpec((1, width, units), lambda i, n: (i, 0, 0)),
                pl.BlockSpec((1, units, width), lambda i, n: (i, 0, 0)),
            ],
            scratch_shapes=[
                pltpu.VMEM((length, lanes), F32),
                pltpu.VMEM((length, lanes), F32),
                pltpu.VMEM((lanes, length), BF),
            ],
        ),
        out_shape=(
            jax.ShapeDtypeStruct((length, 3 * lanes), BF),
            jax.ShapeDtypeStruct((width, 3 * lanes), BF),
            jax.ShapeDtypeStruct((number, width, units), F32),
            jax.ShapeDtypeStruct((number, units, width), F32),
        ),
        compiler_params=params(False),
    )(numbers, qkv, qkv, qkv, grad, mixed, logs, start_row, stream, rows, *cotangents, active, grad_hidden)


ROOT = math.sqrt(2.0 / math.pi)
CUBIC = 0.044715


def experts_exchange(by_head, out_proj, tokens, dispatch, gain, cotangent, near, first_proj, second_proj):
    count = lax.axis_size("ctx")
    half_rows, lanes = by_head.shape[1:]
    rows, width = tokens.shape
    number, _, units = first_proj.shape
    cap = CAP
    total_rows = 4 * count * cap
    quarter = width // 4
    slab = quarter // count
    splits = 2
    part_units = units // splits

    def kernel(
        a_ref, w0_ref, w1_ref, w2_ref, w3_ref, x_ref, d_ref, g_ref, c_ref, g0_ref, first_ref, second_ref,
        mixed, middle, rows_out, g_ref_rest, active_out, hidden_out, heads, grad_middle, gain_out, later,
        routed, slots, rows_v, g_buf, first_buf, second_buf, first_low, second_low, active_v, hidden_v, back_v, back_near, back_far, back_got,
        out_v, out_near, own_v, far_v, out_got, summed, home_got, back, shard_near, shard_far, shard_got, shard_v,
        ss_m, rs_m, ss_1, rs_1, ss_x, rs_x, ss_s, rs_s, ss_f, rs_f, ss_bn, rs_bn, ss_bf, rs_bf, ss_on, rs_on, ss_h, rs_h,
        ss_t, rs_t, ss_n, rs_n, ss_w, rs_w, ss_g, rs_g, l_first, l_second, l_g, st_r, st_a, st_h, st_o, ss_of, rs_of, st_w,
    ):
        c, f, z, y, x, k = place()
        sib = (c, f + 1 - 2 * k)
        xn = (c, (f + 2) % 4)
        pair = 2 * z + k
        target = 2 * x + y

        def load_first(e, u):
            cols = pl.ds(u * part_units, part_units)
            return pltpu.make_async_copy(first_ref.at[e, :, cols], first_buf.at[u], l_first.at[u])

        def load_second(e, u):
            part = pl.ds(u * part_units, part_units)
            return pltpu.make_async_copy(second_ref.at[e, part], second_buf.at[u], l_second.at[u])

        def load_grads(e, slot):
            return [
                pltpu.make_async_copy(g0_ref.at[:, e], g_buf.at[slot, 0], l_g.at[slot, 0]),
                pltpu.make_async_copy(g_ref_rest.at[:, :, e], g_buf.at[slot, pl.ds(1, 3)], l_g.at[slot, 1]),
            ]

        def two(e):
            return pl.ds(pl.multiple_of(e // 2 * 2, 2), 2)

        def grads_across(e):
            return remote(g0_ref.at[:, two(e)], g_ref_rest.at[1, :, two(e)], ss_g.at[0, e // 2], rs_g.at[0, e // 2], xn)

        def grads_share(e):
            return remote(g0_ref.at[:, two(e)], g_ref_rest.at[0, :, two(e)], ss_g.at[1, e // 2], rs_g.at[1, e // 2], sib)

        def grads_share_far(e):
            here, there_too = g_ref_rest.at[1, :, two(e)], g_ref_rest.at[2, :, two(e)]
            return remote(here, there_too, ss_g.at[2, e // 2], rs_g.at[2, e // 2], sib)

        def forward_grads(e):
            grads_across(e).wait_recv()
            grads_share_far(e).start()

        def start_load_grads(e, slot):
            @pl.when(e % 2 == 0)
            def _():
                grads_share(e).wait_recv()
                grads_share_far(e).wait_recv()

            for load in load_grads(e, slot):
                load.start()

        def there(half):
            column = (2 * relative(z, target) + k) * lanes
            return mixed.at[half, :, pl.ds(pl.multiple_of(column, lanes), lanes)]

        def send(i, half):
            ct = (c + i) % count
            return remote(
                a_ref.at[block_at(ct, half, count)], there(half), ss_m.at[i, half], rs_m.at[pair, half], (ct, target)
            )

        def keep(half):
            return pltpu.make_async_copy(a_ref.at[block_at(c, half, count)], there(half), rs_m.at[pair, half])

        for half in range(2):
            for i in range(1, count):
                send(i, half).start()

            @pl.when(k == y)
            def _(half=half):
                keep(half).start()

            @pl.when(k != y)
            def _(half=half):
                send(0, half).start()

        for u in range(splits):
            load_first(0, u).start()
            load_second(0, u).start()

        def start_grads(p, carry):
            grads_across(2 * p).start()
            grads_share(2 * p).start()
            return carry

        lax.fori_loop(0, number // 2, start_grads, 0)
        for half in range(2):
            for other in range(count):
                column = (2 * relative(other // 2, f) + other % 2) * lanes
                cols = pl.ds(pl.multiple_of(column, lanes), lanes)
                remote(a_ref.at[0], mixed.at[half, :, cols], ss_m.at[0, half], rs_m.at[other, half], sib).wait_recv()
            here = pl.ds(half * half_rows, half_rows)
            value = x_ref[here, :].astype(F32)
            for j, w_ref in enumerate((w0_ref, w1_ref, w2_ref, w3_ref)):
                cols = pl.ds(j * quarter, quarter)
                value += jnp.dot(mixed[half, :, cols], w_ref[...], preferred_element_type=F32)
            middle[here, :] = value
            hat, _ = statistics(value)
            routed[here, :] = (hat * g_ref[...]).astype(BF)
        slots[...] = jnp.dot(d_ref[...], routed[...], preferred_element_type=F32).astype(BF).reshape(slots.shape)

        def rows_first(e, i):
            owner = (c + i) % count
            return remote(slots.at[owner, two(e)], rows_v.at[0, two(e), c], ss_1.at[e // 2], rs_1.at[e // 2], (owner, f))

        def hop(e, rel, dst, send_sem, recv_sem, dev):
            return remote(rows_v.at[rel, e], rows_v.at[dst, e], send_sem.at[e], recv_sem.at[e], dev)

        def rows_across(e):
            return hop(e, 0, 2, ss_x, rs_x, xn)

        def rows_share(e):
            return hop(e, 0, 1, ss_s, rs_s, sib)

        def rows_share_far(e):
            return hop(e, 2, 3, ss_f, rs_f, sib)

        def start_rows(p, carry):
            for i in range(1, count):
                rows_first(2 * p, i).start()
            pltpu.make_async_copy(slots.at[c, two(2 * p)], rows_v.at[0, two(2 * p), c], rs_1.at[p]).start()
            return carry

        lax.fori_loop(0, number // 2, start_rows, 0)

        def forward(e):
            @pl.when(e % 2 == 0)
            def _():
                remote(rows_v.at[0, two(e)], rows_v.at[0, two(e)], ss_x.at[e], rs_1.at[e // 2], sib).wait_recv()

            rows_across(e).start()
            rows_share(e).start()

        def forward_far(e):
            rows_across(e).wait_recv()
            rows_share_far(e).start()

        def near_send(e):
            return remote(back_v.at[pl.ds(2, 2), e], back_near.at[:, e], ss_bn.at[e], rs_bn.at[e], sib)

        def near_out(e):
            return remote(out_v.at[pl.ds(2, 2), e], out_near.at[:, e], ss_on.at[e], rs_on.at[e], sib)

        def hold(ref, e, value):
            parts = value.astype(BF).reshape(4, count, cap, width)
            for at, rel in enumerate((0, 2, 1, 3)):
                ref[at, e] = parts[rel]

        def far_send(e):
            return remote(back_far.at[e], back_got.at[e], ss_bf.at[e], rs_bf.at[e], xn)

        def store_own(e):
            return pltpu.make_async_copy(own_v.at[e], later.at[:, pl.ds(pl.multiple_of(slab + e * cap, cap), cap)], st_o.at[e])

        def far_out(e):
            return remote(far_v.at[e], out_got.at[e], ss_of.at[e], rs_of.at[e], xn)

        def store_rows(e):
            return pltpu.make_async_copy(rows_v.at[:, e], rows_out.at[:, e], st_r.at[e])

        def store_active(e, slot):
            return pltpu.make_async_copy(active_v.at[slot], active_out.at[e], st_a.at[slot])

        def store_hidden(e, slot):
            return pltpu.make_async_copy(hidden_v.at[slot], hidden_out.at[e], st_h.at[slot])

        def sum_far(e):
            near_send(e).wait_recv()
            back_far[e] = (back_v[1, e].astype(F32) + back_near[1, e].astype(F32)).astype(BF)
            far_send(e).start()

        def sum_outputs(e):
            near_out(e).wait_recv()
            own_v[e] = (out_v[0, e].astype(F32) + out_near[0, e].astype(F32)).astype(BF)
            far_v[e] = (out_v[1, e].astype(F32) + out_near[1, e].astype(F32)).astype(BF)

        def home(e, i):
            ct = (c + i) % count
            return remote(summed.at[two(e), ct], home_got.at[c, two(e)], ss_h.at[e // 2], rs_h, (ct, f))

        def go_home(e):
            far_send(e).wait_recv()
            summed[e] = (
                back_v[0, e].astype(F32) + back_near[0, e].astype(F32) + back_got[e].astype(F32)
            ).astype(BF)

            @pl.when(e % 2 == 1)
            def _():
                for i in range(1, count):
                    home(e, i).start()
                pltpu.make_async_copy(summed.at[two(e), c], home_got.at[c, two(e)], rs_h).start()

        def expert(e, carry):
            slot = e % 2

            @pl.when(e >= 1)
            def _():
                sum_far(e - 1)

            @pl.when(e + 1 < number)
            def _():
                start_load_grads(e + 1, 1 - slot)

            rows_share(e).wait_recv()
            rows_share_far(e).wait_recv()
            store_rows(e).start()
            for load in load_grads(e, slot):
                load.wait()

            @pl.when(e >= 2)
            def _():
                store_active(e, slot).wait()
                store_hidden(e, slot).wait()

            row = rows_v[:, e].reshape(total_rows, width)
            grad = g_buf[slot].reshape(total_rows, width)
            term = jnp.zeros((total_rows, width), F32)
            for u in range(splits):
                load_first(e, u).wait()
                load_second(e, u).wait()
                first_low[u] = first_buf[u].astype(BF)
                second_low[u] = second_buf[u].astype(BF)

                @pl.when(e + 1 < number)
                def _(u=u):
                    load_first(e + 1, u).start()
                    load_second(e + 1, u).start()

                first, second = first_low[u], second_low[u]
                hidden = jnp.dot(row, first, preferred_element_type=F32)
                upstream = lax.dot_general(grad, second, CONTRACT_LAST, preferred_element_type=F32)
                bent = jnp.tanh(ROOT * (hidden + CUBIC * hidden * hidden * hidden))
                cols = pl.ds(u * part_units, part_units)
                active_v[slot, :, cols] = (0.5 * hidden * (1.0 + bent)).astype(BF)
                slope = 0.5 * (1.0 + bent) + 0.5 * hidden * (1.0 - bent * bent) * (
                    ROOT * (1.0 + 3.0 * CUBIC * hidden * hidden)
                )
                grad_hidden = (upstream * slope).astype(BF)
                hidden_v[slot, :, cols] = grad_hidden
                term += lax.dot_general(grad_hidden, first, CONTRACT_LAST, preferred_element_type=F32)
            hold(back_v, e, term)
            near_send(e).start()
            result = jnp.zeros((total_rows, width), F32)
            for u in range(splits):
                cols = pl.ds(u * part_units, part_units)
                result += jnp.dot(active_v[slot, :, cols], second_low[u], preferred_element_type=F32)
            hold(out_v, e, result)
            near_out(e).start()

            store_active(e, slot).start()
            store_hidden(e, slot).start()

            @pl.when(e + 3 < number)
            def _():
                forward(e + 3)

            @pl.when((e + 4 < number) & (e % 2 == 0))
            def _():
                forward_grads(e + 4)

            @pl.when(e + 2 < number)
            def _():
                forward_far(e + 2)

            @pl.when(e >= 1)
            def _():
                sum_outputs(e - 1)

            @pl.when(e >= 2)
            def _():
                go_home(e - 2)

            @pl.when(e >= number - 3)
            def _():
                far_out(e - (number - 3)).start()

            return carry

        forward_grads(0)
        forward(0)
        forward(1)
        start_load_grads(0, 0)
        forward_far(0)
        forward_grads(2)
        forward(2)
        forward_far(1)
        lax.fori_loop(0, number, expert, 0)
        sum_far(number - 1)
        sum_outputs(number - 1)
        far_out(3).start()
        for e in range(number - 2, number):
            go_home(e)
        for e in range(4, number):
            far_out(e).start()
        hat, inverse = statistics(middle[...])
        remote(home_got, home_got, ss_h.at[0], rs_h, sib).wait_recv()

        returned = lax.dot_general(d_ref[...], home_got[...].reshape(-1, width), CONTRACT_FIRST, preferred_element_type=F32)
        scaled = returned * g_ref[...]
        mean_grad = jnp.mean(scaled, axis=1, keepdims=True)
        mean_proj = jnp.mean(scaled * hat, axis=1, keepdims=True)
        gain_out[...] = jnp.sum(returned * hat, axis=0, keepdims=True)
        gradient = c_ref[...].astype(F32) + inverse * (scaled - mean_grad - hat * mean_proj)
        grad_middle[...] = gradient
        low = gradient.astype(BF)
        for j, w_ref in enumerate((w0_ref, w1_ref, w2_ref, w3_ref)):
            back[:, :, j * quarter : (j + 1) * quarter] = (
                lax.dot_general(low, w_ref[...], CONTRACT_LAST, preferred_element_type=F32)
                .astype(BF)
                .reshape(2, half_rows, quarter)
            )

        def part(half, number_of_pair):
            column = (2 * relative(number_of_pair // 2, f) + number_of_pair % 2) * lanes
            return back.at[half, :, pl.ds(pl.multiple_of(column, lanes), lanes)]

        def send_heads(i, half):
            other = (2 * z + k + i) % count
            b = block_at(c, half, count)
            dev = (2 * (other // 2) + k, 2 * x + other % 2)
            return remote(part(half, other), heads.at[b], ss_t.at[i, half], rs_t.at[b], dev)

        for i in range(1, count):
            for half in range(2):
                send_heads(i, half).start()

        @pl.when(k == y)
        def _():
            for half in range(2):
                b = block_at(c, half, count)
                pltpu.make_async_copy(part(half, 2 * z + k), heads.at[b], rs_t.at[b]).start()

        @pl.when(k != y)
        def _():
            for half in range(2):
                send_heads(0, half).start()

        for e in range(number):
            near_send(e).wait_send()

        def shard_term(j):
            half_quarter = quarter // 2
            mixed_part = [mixed[half, :, j * quarter : (j + 1) * quarter] for half in range(2)]
            value = sum(
                lax.dot_general(
                    mixed_part[half], low[half * half_rows : (half + 1) * half_rows], CONTRACT_FIRST, preferred_element_type=F32
                )
                for half in range(2)
            )
            return value.astype(BF).reshape(shard_far.shape)

        sheet = pl.ds(0, quarter // (count * cap))
        core_send = remote(back_v.at[pl.ds(2, 2), sheet], shard_near, ss_n, rs_n, sib)
        across = remote(shard_far, shard_got, ss_w, rs_w, xn)
        for j in range(2):
            back_v[2 + j, sheet] = shard_term(2 * j + 1)
        core_send.start()
        own_far = shard_term(2)
        core_send.wait_recv()
        shard_far[...] = (own_far.astype(F32) + shard_near[1].astype(F32)).astype(BF)
        across.start()
        own_near = shard_term(0)

        def finish_output(e, carry):
            far_out(e).wait_recv()
            own_v[e] = (own_v[e].astype(F32) + out_got[e].astype(F32)).astype(BF)
            store_own(e).start()
            return carry

        lax.fori_loop(0, number, finish_output, 0)
        across.wait_recv()
        shard_v[...] = (
            (own_near.astype(F32) + shard_near[0].astype(F32) + shard_got[...].astype(F32)).astype(BF).reshape(shard_v.shape)
        )
        store_shard = pltpu.make_async_copy(shard_v, later.at[:, pl.ds(0, slab)], st_w)
        store_shard.start()

        for b in range(2 * count):
            remote(part(0, 0), heads.at[b], ss_t.at[0, 0], rs_t.at[b], sib).wait_recv()

        def leave(e, carry):
            rows_across(e).wait_send()
            rows_share(e).wait_send()
            rows_share_far(e).wait_send()
            far_send(e).wait_send()
            near_out(e).wait_send()
            store_own(e).wait()
            far_out(e).wait_send()
            store_rows(e).wait()
            return carry

        def leave_two(p, carry):
            sent = pl.ds(0, count - 1)
            first, last = slots.at[sent, two(2 * p)], summed.at[two(2 * p), sent]
            remote(first, first, ss_1.at[p], rs_1.at[p], sib).wait_send()
            remote(last, last, ss_h.at[p], rs_h, sib).wait_send()
            grads_across(2 * p).wait_send()
            grads_share(2 * p).wait_send()
            grads_share_far(2 * p).wait_send()
            return carry

        lax.fori_loop(0, number, leave, 0)
        lax.fori_loop(0, number // 2, leave_two, 0)
        store_shard.wait()
        for e in (number - 2, number - 1):
            store_active(e, e % 2).wait()
            store_hidden(e, e % 2).wait()
        for i in range(1, count):
            for half in range(2):
                send(i, half).wait_send()
                send_heads(i, half).wait_send()

        @pl.when(k != y)
        def _():
            for half in range(2):
                send(0, half).wait_send()
                send_heads(0, half).wait_send()

        core_send.wait_send()
        across.wait_send()

    vmem = pl.BlockSpec(memory_space=pltpu.VMEM)
    block = (count, cap, width)
    low = lambda *shape: pltpu.VMEM(shape, BF)
    fold = (quarter // (count * cap),) + block
    return pl.pallas_call(
        kernel,
        name="experts_exchange",
        cost_estimate=lasting(100),
        out_shape=(
            jax.ShapeDtypeStruct((2, half_rows, width), BF),
            jax.ShapeDtypeStruct((rows, width), F32),
            jax.ShapeDtypeStruct((4, number) + block, BF),
            jax.ShapeDtypeStruct((3,) + near.shape, BF),
            jax.ShapeDtypeStruct((number, total_rows, units), BF),
            jax.ShapeDtypeStruct((number, total_rows, units), BF),
            jax.ShapeDtypeStruct((2 * count, half_rows, lanes), BF),
            jax.ShapeDtypeStruct((rows, width), F32),
            jax.ShapeDtypeStruct((1, width), F32),
            jax.ShapeDtypeStruct((count, slab + number * cap, width), BF),
        ),
        in_specs=[ANY] + [vmem] * 8 + [ANY] * 3,
        out_specs=(vmem, vmem) + (ANY,) * 5 + (vmem, vmem, ANY),
        scratch_shapes=[
            low(rows, width), low(count, number, cap, width), low(4, number, *block), low(2, 4, *block),
            pltpu.VMEM((splits, width, part_units), F32), pltpu.VMEM((splits, part_units, width), F32),
            low(splits, width, part_units), low(splits, part_units, width),
            low(2, total_rows, units), low(2, total_rows, units),
            low(4, number, *block), low(2, number, *block), low(number, *block), low(number, *block),
            low(4, number, *block), low(2, number, *block), low(number, *block), low(number, *block), low(number, *block),
            low(number, *block), low(count, number, cap, width), low(2, half_rows, width),
            low(2, *fold), low(*fold), low(*fold), low(count, slab, width),
            DMA((count, 2)), DMA((count, 2)), DMA((number // 2,)), DMA((number // 2,)), DMA((number,)), DMA((number,)),
            DMA((number,)), DMA((number,)), DMA((number,)), DMA((number,)), DMA((number,)), DMA((number,)),
            DMA((number,)), DMA((number,)), DMA((number,)), DMA((number,)), DMA((number // 2,)), DMA,
            DMA((count, 2)), DMA((2 * count,)), DMA, DMA, DMA, DMA, DMA((3, number // 2)), DMA((3, number // 2)),
            DMA((splits,)), DMA((splits,)), DMA((2, 2)), DMA((number,)), DMA((2,)), DMA((2,)), DMA((number,)), DMA((number,)), DMA((number,)), DMA,
        ],
        compiler_params=pltpu.CompilerParams(has_side_effects=True, vmem_limit_bytes=60 << 20),
    )(by_head, *out_proj, tokens, dispatch, gain, cotangent, near, first_proj, second_proj)


def after(value, *others):
    return lax.optimization_barrier((value,) + others)[0]


def finish_exchange(grads, parts, slabs, gain_part, weight):
    count = lax.axis_size("ctx")
    depth = count // 2
    part = grads.shape[2]
    half_rows = grads.shape[1]
    _, rows, _ = parts.shape
    pieces = 4
    piece = rows // pieces
    slab = rows // count

    def kernel(
        a_ref, p_ref, h_ref, g_ref, w_ref, tok_out, w_out, o_out, g_out, w_all, o_ref, got, held, got_g, sum_g, got_gc,
        ss, rs, ss_r, rs_r, ss_up, ss_dn, rs_z, ss_a, ss_b, rs_o,
        ss_of, rs_of, ss_g, rs_g, ss_gc, rs_gc, ss_wx, rs_wx, ss_ws, rs_ws, ss_wf, rs_wf, loc,
    ):
        c, f, z, y, x, k = place()
        pair = 2 * z + k
        target = 2 * x + y
        sib = (c, f + 1 - 2 * k)
        xn = (c, (f + 2) % 4)
        up = (c + 2, f)
        down = (c - 2, f)

        def columns(ref, number):
            return ref.at[:, pl.ds(pl.multiple_of(number * part, part), part)]

        peers = [
            (2 * z + 1 - y, f, 2 * x + 1 - y),
            (c, (f + 2) % 4, 2 * (1 - x) + y),
            (2 * z + 1 - y, (f + 2) % 4, 2 * (1 - x) + 1 - y),
        ]

        def scatter(d):
            cp, fp, shard = peers[d]
            return remote(p_ref.at[shard], got.at[d], ss_r.at[d], rs_r.at[d], (cp, fp))

        for d in (2, 1, 0):
            scatter(d).start()

        def weight_part(shard, i):
            return w_all.at[shard, pl.ds(i * piece, piece)]

        def weight_across(i):
            return remote(w_ref.at[pl.ds(i * piece, piece)], weight_part(f, i), ss_wx.at[i], rs_wx.at[i], xn)

        def weight_on(i, shard):
            return remote(weight_part(shard, i), weight_part(shard, i), ss_wf.at[i], rs_wf.at[i], sib)

        def weight_pass(i):
            shard = (f + 2) % 4
            remote(weight_part(shard, i), weight_part(shard, i), ss_wf.at[i], rs_wx.at[i], sib).wait_recv()
            weight_on(i, shard).start()

        weight_share = remote(w_ref, w_all.at[f], ss_ws, rs_ws, sib)
        weight_own = pltpu.make_async_copy(w_ref, w_all.at[f], loc)
        for i in range(pieces):
            weight_across(i).start()

        def there(half):
            return columns(tok_out.at[half], pair)

        def send(i, half):
            ct = (c + i) % count
            return remote(a_ref.at[block_at(ct, half, count)], there(half), ss.at[i, half], rs.at[pair, half], (ct, target))

        def send_all(numbers):
            for i in numbers:
                for half in range(2):
                    send(i, half).start()

        send_all(range(2, count, 2))

        def gain_send(j):
            return remote(sum_g.at[j], got_g.at[j], ss_g.at[j], rs_g.at[j], sib if j == 0 else xn)

        sum_g[0] = g_ref[...]
        gain_send(0).start()

        def chain(zb, sem, dev):
            return remote(held.at[zb], held.at[zb], sem, rs_z.at[zb], dev)

        def own_column(zb):
            return remote(held.at[zb], columns(w_out, 2 * zb + k), ss_a.at[zb], rs_o.at[2 * zb + k], (c, target))

        def own_local(zb):
            return pltpu.make_async_copy(held.at[zb], columns(w_out, 2 * zb + k), rs_o.at[2 * zb + k])

        def next_column(zb):
            return remote(
                held.at[zb], columns(w_out, 2 * zb + k), ss_b.at[zb], rs_o.at[2 * zb + k], (2 * z + 1 - y, target)
            )

        def spread(zb):
            next_column(zb).start()

            @pl.when(k == y)
            def _():
                own_local(zb).start()

            @pl.when(k != y)
            def _():
                own_column(zb).start()

        total = p_ref[2 * x + y].astype(F32)
        for d in range(3):
            scatter(d).wait_recv()
            total += got[d].astype(F32)
        held[z] = total.astype(BF)

        @pl.when(z < depth - 1)
        def _():
            chain(z, ss_up.at[0], up).start()

        @pl.when(z > 0)
        def _():
            chain(z, ss_dn.at[0], down).start()

        spread(z)
        send_all(range(1, count, 2))

        @pl.when(k == y)
        def _():
            for half in range(2):
                pltpu.make_async_copy(a_ref.at[block_at(c, half, count)], there(half), rs.at[pair, half]).start()

        @pl.when(k != y)
        def _():
            for half in range(2):
                send(0, half).start()

        weight_share.start()
        weight_own.start()
        gain_send(0).wait_recv()
        sum_g[1] = sum_g[0] + got_g[0]
        gain_send(1).start()

        across_y = (c + 1 - 2 * y, f)

        def slab_send(i):
            zt = (z + i) % depth
            return remote(o_ref, o_out.at[c], ss_of.at[i], rs_of.at[c], (2 * zt + y, f))

        def slab_on(i):
            cs = 2 * ((z + i) % depth) + y
            src = o_out.at[cs] if i else o_ref
            return remote(src, o_out.at[cs], ss_of.at[depth + i], rs_of.at[cs], across_y)

        def gain_spread(i):
            return remote(sum_g.at[2], got_gc.at[c], ss_gc.at[i], rs_gc.at[c], ((c + i) % count, f))

        slab_sum = h_ref[0, 0:slab].astype(F32)
        for i in range(1, count):
            slab_sum += h_ref[i, 0:slab].astype(F32)
        o_ref[...] = slab_sum.astype(BF)
        slab_own = pltpu.make_async_copy(o_ref, o_out.at[c], rs_of.at[c])
        slab_own.start()
        slab_on(0).start()
        for i in range(1, depth):
            slab_send(i).start()
        for hop in range(1, depth):

            @pl.when(z - hop >= 0)
            def _(hop=hop):
                chain(z - hop, ss_up.at[hop], sib).wait_recv()

                @pl.when(z < depth - 1)
                def _():
                    chain(z - hop, ss_up.at[hop], up).start()

                spread(z - hop)

            @pl.when(z + hop <= depth - 1)
            def _(hop=hop):
                chain(z + hop, ss_dn.at[hop], sib).wait_recv()

                @pl.when(z > 0)
                def _():
                    chain(z + hop, ss_dn.at[hop], down).start()

                spread(z + hop)

            weight_pass(hop - 1)
            if hop == 2:
                for i in range(1, depth):
                    cs = 2 * ((z + i) % depth) + y
                    remote(o_ref, o_out.at[cs], ss_of.at[i], rs_of.at[cs], sib).wait_recv()
                    slab_on(i).start()
            if hop == 1:
                gain_send(1).wait_recv()
                sum_g[2] = sum_g[1] + got_g[1]
                for i in range(1, count):
                    gain_spread(i).start()
        for i in range(depth - 1, pieces):
            weight_pass(i)
        total_g = sum_g[2]
        for i in range(1, count):
            cs = (c + i) % count
            remote(sum_g.at[2], got_gc.at[cs], ss_gc.at[i], rs_gc.at[cs], sib).wait_recv()
            total_g += got_gc[cs]
        g_out[...] = total_g

        gain_send(0).wait_send()
        gain_send(1).wait_send()
        for i in range(pieces):
            weight_across(i).wait_send()
            weight_on(i, (f + 2) % 4).wait_send()
            remote(weight_part(0, i), weight_part(0, i), ss_wf.at[i], rs_wf.at[i], sib).wait_recv()
        weight_share.wait()
        weight_own.wait()
        for d in range(3):
            scatter(d).wait_send()
        for other in range(count):
            for half in range(2):
                remote(a_ref.at[0], columns(tok_out.at[half], other), ss.at[0, half], rs.at[other, half], sib).wait_recv()
            remote(held.at[0], columns(w_out, other), ss_a.at[0], rs_o.at[other], sib).wait_recv()
        for i in range(1, count):
            for half in range(2):
                send(i, half).wait_send()
            gain_spread(i).wait_send()
        for i in range(depth):
            if i:
                slab_send(i).wait_send()
            slab_on(i).wait_send()
            cs = 2 * ((z + i) % depth) + 1 - y
            remote(o_ref, o_out.at[cs], ss_of.at[i], rs_of.at[cs], sib).wait_recv()
        slab_own.wait()

        @pl.when(k != y)
        def _():
            for half in range(2):
                send(0, half).wait_send()
            for zb in range(depth):
                own_column(zb).wait_send()

        for zb in range(depth):
            next_column(zb).wait_send()
        for hop in range(depth):

            @pl.when((z < depth - 1) & (z - hop >= 0))
            def _(hop=hop):
                chain(z - hop, ss_up.at[hop], up).wait_send()

            @pl.when((z > 0) & (z + hop <= depth - 1))
            def _(hop=hop):
                chain(z + hop, ss_dn.at[hop], down).wait_send()

    vmem = pl.BlockSpec(memory_space=pltpu.VMEM)
    eighth = gain_part.shape
    return pl.pallas_call(
        kernel,
        name="finish_exchange",
        cost_estimate=lasting(60),
        out_shape=(
            jax.ShapeDtypeStruct((2, half_rows, count * part), BF),
            jax.ShapeDtypeStruct((rows, count * part), BF),
            jax.ShapeDtypeStruct((count, slab, slabs.shape[2]), BF),
            jax.ShapeDtypeStruct(eighth, F32),
            jax.ShapeDtypeStruct((4,) + weight.shape, BF),
        ),
        in_specs=[vmem] * 5,
        out_specs=(ANY, ANY, ANY, vmem, ANY),
        scratch_shapes=[
            pltpu.VMEM((slab, slabs.shape[2]), BF),
            pltpu.VMEM((3, rows, part), BF),
            pltpu.VMEM((depth, rows, part), BF),
            pltpu.VMEM((2,) + eighth, F32),
            pltpu.VMEM((3,) + eighth, F32),
            pltpu.VMEM((count,) + eighth, F32),
            DMA((count, 2)), DMA((count, 2)), DMA((3,)), DMA((3,)), DMA((depth,)), DMA((depth,)), DMA((depth,)),
            DMA((depth,)), DMA((depth,)), DMA((count,)),
            DMA((count,)), DMA((count,)), DMA((2,)), DMA((2,)), DMA((count,)), DMA((count,)),
            DMA((pieces,)), DMA((pieces,)), DMA, DMA, DMA((pieces,)), DMA((pieces,)), DMA,
        ],
        compiler_params=params(),
    )(grads, parts, slabs, gain_part, weight)


def finish_local(
    grad_projected, projection, tokens, gain, grad_middle, middle, dispatch, home, weight_grad, weight, out_slabs, gain_sum
):
    rows, width = tokens.shape
    quarter, wide = weight.shape
    lanes = 128
    part = 3 * lanes
    count = wide // part
    slot_rows = EXPERTS // count * CAP

    def kernel(p_ref, w_ref, x_ref, g_ref, m_ref, mid_ref, d_ref, e_ref, wg_ref, wl_ref, o_ref, gs_ref, block, token, wout, oout, gout, gout_two, acc):
        j = pl.program_id(0)
        own = pl.ds(pl.multiple_of(lax.axis_index("fsdp") * quarter, quarter), quarter)
        acc[j] = lax.dot_general(p_ref[...], w_ref[0], CONTRACT_LAST, preferred_element_type=F32)

        @pl.when(j == 0)
        def _():
            slots = e_ref[:, home.shape[1] - slot_rows :].reshape(-1, width)
            summed = lax.dot_general(d_ref[...], slots, CONTRACT_FIRST, preferred_element_type=F32)
            block[...] = (mid_ref[...] + summed).astype(BF)
            oout[...] = o_ref[...].astype(F32)

        @pl.when(j == 1)
        def _():
            total = jnp.zeros((quarter, 1), F32)
            for number in range(count):
                for kind in range(3):
                    at = number * part + kind * lanes
                    value = wg_ref[:, at : at + lanes].astype(F32)
                    to = (kind * count + number) * lanes
                    wout[:, to : to + lanes] = value
                    total += jnp.sum(value * wl_ref[:, at : at + lanes].astype(F32), axis=1, keepdims=True)
            gout[...] = jnp.broadcast_to(total, (quarter, lanes)).T[0:1] / g_ref[:, own]
            gout_two[...] = gs_ref[:, own]

        @pl.when(j == 3)
        def _():
            hat, inverse = statistics(x_ref[...].astype(F32))
            scaled = jnp.concatenate([acc[i] for i in range(4)], axis=1) * g_ref[...]
            mean_grad = jnp.mean(scaled, axis=1, keepdims=True)
            mean_proj = jnp.mean(scaled * hat, axis=1, keepdims=True)
            token[...] = m_ref[...] + inverse * (scaled - mean_grad - hat * mean_proj)

    def whole(value):
        return pl.BlockSpec(value.shape, lambda j: (0,) * value.ndim)

    shapes = (
        jax.ShapeDtypeStruct((rows, width), BF),
        jax.ShapeDtypeStruct((rows, width), F32),
        jax.ShapeDtypeStruct((quarter, wide), F32),
        jax.ShapeDtypeStruct((quarter, width), F32),
        jax.ShapeDtypeStruct((1, quarter), F32),
        jax.ShapeDtypeStruct((1, quarter), F32),
    )
    rest = (tokens, gain, grad_middle, middle, dispatch, home, weight_grad, weight, out_slabs, gain_sum)
    return pl.pallas_call(
        kernel,
        name="finish_local",
        cost_estimate=lasting(9),
        grid=(4,),
        in_specs=[whole(grad_projected), pl.BlockSpec((1, quarter, wide), lambda j: (j, 0, 0))] + [whole(v) for v in rest],
        out_specs=[whole(v) for v in shapes],
        out_shape=shapes,
        scratch_shapes=[pltpu.VMEM((4, rows, quarter), F32)],
        compiler_params=params(False),
    )(grad_projected, projection, *rest)


def by_head_pairs(
    tokens, doc_starts, expert_ids, query_key_value_weight, output_weight_matrix, expert_in, expert_out, gain_one, gain_two, grad_output
):
    half_rows = tokens.shape[3]
    width = tokens.shape[4]
    count = lax.axis_size("ctx")
    rows = 2 * half_rows
    length = count * rows
    scale = (width // HEADS) ** (-0.5)
    lanes = 2 * (width // HEADS)
    shard_rows = width // 4
    own_tokens = tokens.reshape(rows, width)
    cotangent = grad_output.reshape(rows, width)
    gain_row = gain_one.reshape(1, width)
    stream, starts, columns, out_beside, out_far, out_diagonal, send_grads, qkv_low, out_own, dispatch = gather_stream(
        own_tokens.reshape(2, half_rows, width),
        gain_row,
        expert_ids.reshape(1, rows),
        cotangent,
        doc_starts.reshape(2, half_rows),
        query_key_value_weight,
        output_weight_matrix,
    )
    grads_near = lax.all_to_all(send_grads, "ctx", split_axis=0, concat_axis=0, tiled=True)
    stream = stream.reshape(length, width)
    start_row = jnp.concatenate([starts[:, 0].reshape(-1), starts[::-1, 1].reshape(-1)])[None]
    numbers = jnp.min(start_row.reshape(-1, TILE), axis=1) // TILE
    qkv, mixed16, mixed32, logs = attend_forward(stream, columns, start_row, numbers, scale)
    grads_near = after(grads_near, mixed16)
    mixed, middle, all_rows, other_grads, active, grad_hidden, grad_heads, grad_middle, grad_gain_two, later = experts_exchange(
        mixed16.reshape(2 * count, half_rows, lanes),
        [out_own, out_beside, out_far, out_diagonal],
        own_tokens,
        dispatch,
        gain_two.reshape(1, width),
        cotangent,
        grads_near,
        expert_in,
        expert_out,
    )
    home = lax.all_to_all(later, "ctx", split_axis=0, concat_axis=0, tiled=True)
    own_grads, parts, grad_in, grad_outw = backward_local(
        qkv,
        after(grad_heads, later).reshape(length, lanes),
        mixed32,
        logs,
        start_row,
        numbers,
        scale,
        stream,
        all_rows,
        [grads_near, other_grads],
        active,
        grad_hidden,
    )
    home = after(home, own_grads)
    grad_projected, weight_grad, shard_out, gain_sum, projection = finish_exchange(
        own_grads.reshape(2 * count, half_rows, 3 * lanes),
        parts.reshape(4, shard_rows, 3 * lanes),
        home,
        grad_gain_two,
        qkv_low,
    )
    block_out, grad_start, weight_grad, shard_out, shard_gain_one, shard_gain_two = finish_local(
        grad_projected.reshape(rows, 3 * width),
        projection,
        own_tokens,
        gain_row,
        grad_middle,
        middle,
        dispatch,
        home,
        weight_grad,
        qkv_low,
        shard_out.reshape(shard_rows, width),
        gain_sum,
    )
    shard_gain_one = shard_gain_one.reshape(shard_rows)
    shard_gain_two = shard_gain_two.reshape(shard_rows)
    return (
        block_out.reshape(tokens.shape),
        grad_start.reshape(tokens.shape),
        weight_grad,
        shard_out,
        grad_in,
        grad_outw,
        shard_gain_one,
        shard_gain_two,
    )


def solution(mesh):
    pairs = mesh.shape["ctx"] * 2 == HEADS and mesh.shape["fsdp"] == 4
    return jax.shard_map(
        by_head_pairs if pairs else shards,
        mesh=mesh,
        in_specs=(
            P("fsdp", "ctx", None, None, None),
            P("fsdp", "ctx", None, None),
            P("fsdp", "ctx", None, None, None),
            P("fsdp", None),
            P("fsdp", None),
            P("ctx", None, "fsdp"),
            P("ctx", "fsdp", None),
            P(),
            P(),
            P("fsdp", "ctx", None, None, None),
        ),
        out_specs=(
            P("fsdp", "ctx", None, None, None),
            P("fsdp", "ctx", None, None, None),
            P("fsdp", None),
            P("fsdp", None),
            P("ctx", None, "fsdp"),
            P("ctx", "fsdp", None),
            P("fsdp"),
            P("fsdp"),
        ),
        check_vma=False,
    )
```

```python
import math

import jax
import jax.numpy as jnp
from jax import lax
from jax.experimental import pallas as pl
from jax.experimental.pallas import tpu as pltpu
from jax.sharding import PartitionSpec as P

HEADS = 16
EXPERTS = 64
CAP = 8


EPS = 1e-05
NEGATIVE = -1e30


def position_of(row_ids, ctx_count, half_rows):
    device = row_ids // (2 * half_rows)
    upper_half = row_ids // half_rows % 2
    offset = row_ids % half_rows
    return jnp.where(
        upper_half == 0,
        device * half_rows + offset,
        (2 * ctx_count - 1 - device) * half_rows + offset,
    )


def norm_forward(value, gain):
    row_mean = jnp.mean(value, axis=-1, keepdims=True)
    centred = value - row_mean
    inverse = lax.rsqrt(jnp.mean(centred * centred, axis=-1, keepdims=True) + EPS)
    normed = centred * inverse
    return (normed * gain, normed, inverse)


def norm_backward(gradient, normed, inverse, gain):
    scaled = gradient * gain
    mean_grad = jnp.mean(scaled, axis=-1, keepdims=True)
    mean_proj = jnp.mean(scaled * normed, axis=-1, keepdims=True)
    return (
        inverse * (scaled - mean_grad - normed * mean_proj),
        jnp.sum(gradient * normed, axis=(0, 1)),
    )


def scores(query, keys, query_pos, key_pos, query_start, score_scale):
    raw_scores = (
        jnp.einsum("qshe,kshe->shqk", query, keys, preferred_element_type=jnp.float32) * score_scale
    )
    visible = (key_pos[None, None, None, :] <= query_pos[None, None, :, None]) & (
        key_pos[None, None, None, :] >= query_start.T[:, None, :, None]
    )
    return jnp.where(visible, raw_scores, NEGATIVE)


def log_totals(query, keys, query_pos, query_start, score_scale, ctx_count, half_rows, key_block):
    block_count = keys.shape[0] // key_block
    carry_shape = (query.shape[1], query.shape[2], query.shape[0])

    def log_one_block(block_index, carried):
        running_max, running = carried
        first_row = block_index * key_block
        key_piece = lax.dynamic_slice_in_dim(keys, first_row, key_block, 0)
        key_pos = position_of(
            first_row + jnp.arange(key_block, dtype=jnp.int32), ctx_count, half_rows
        )
        score_rows = scores(query, key_piece, query_pos, key_pos, query_start, score_scale)
        new_max = jnp.maximum(running_max, jnp.max(score_rows, axis=-1))
        running = running * jnp.exp(running_max - new_max) + jnp.sum(
            jnp.exp(score_rows - new_max[..., None]), axis=-1
        )
        return (new_max, running)

    running_max, running = lax.fori_loop(
        0,
        block_count,
        log_one_block,
        (jnp.full(carry_shape, NEGATIVE, jnp.float32), jnp.zeros(carry_shape, jnp.float32)),
    )
    return running_max + jnp.log(running)


def attend(
    query,
    keys,
    values,
    query_pos,
    query_start,
    log_total,
    score_scale,
    ctx_count,
    half_rows,
    key_block,
):
    block_count = keys.shape[0] // key_block
    zeros_init = jnp.zeros(query.shape, jnp.float32)

    def attend_one_block(block_index, carried):
        output, remainder = carried
        first_row = block_index * key_block
        key_piece = lax.dynamic_slice_in_dim(keys, first_row, key_block, 0)
        value_piece = lax.dynamic_slice_in_dim(values, first_row, key_block, 0)
        key_pos = position_of(
            first_row + jnp.arange(key_block, dtype=jnp.int32), ctx_count, half_rows
        )
        weights = jnp.exp(
            scores(query, key_piece, query_pos, key_pos, query_start, score_scale)
            - log_total[..., None]
        )
        rounded = weights.astype(jnp.bfloat16)
        leftover = (weights - rounded.astype(jnp.float32)).astype(jnp.bfloat16)
        output = output + jnp.einsum(
            "shqk,kshe->qshe", rounded, value_piece, preferred_element_type=jnp.float32
        )
        remainder = remainder + jnp.einsum(
            "shqk,kshe->qshe", leftover, value_piece, preferred_element_type=jnp.float32
        )
        return (output, remainder)

    return lax.fori_loop(0, block_count, attend_one_block, (zeros_init, zeros_init))


def query_grads(
    query,
    keys,
    values,
    grad_heads,
    query_pos,
    query_start,
    log_total,
    row_delta,
    score_scale,
    ctx_count,
    half_rows,
    key_block,
):
    block_count = keys.shape[0] // key_block

    def query_one_block(block_index, running):
        first_row = block_index * key_block
        key_piece = lax.dynamic_slice_in_dim(keys, first_row, key_block, 0)
        value_piece = lax.dynamic_slice_in_dim(values, first_row, key_block, 0)
        key_pos = position_of(
            first_row + jnp.arange(key_block, dtype=jnp.int32), ctx_count, half_rows
        )
        weights = jnp.exp(
            scores(query, key_piece, query_pos, key_pos, query_start, score_scale)
            - log_total[..., None]
        )
        grad_weight = jnp.einsum(
            "qshe,kshe->shqk", grad_heads, value_piece, preferred_element_type=jnp.float32
        )
        grad_score = (weights * (grad_weight - row_delta[..., None])).astype(jnp.bfloat16)
        return running + jnp.einsum(
            "shqk,kshe->qshe", grad_score, key_piece, preferred_element_type=jnp.float32
        )

    return (
        lax.fori_loop(0, block_count, query_one_block, jnp.zeros(query.shape, jnp.float32))
        * score_scale
    )


def key_grads(
    query,
    grad_heads,
    query_pos,
    query_start,
    log_total,
    row_delta,
    key_piece,
    value_piece,
    key_pos,
    score_scale,
):
    weights = jnp.exp(
        scores(query, key_piece, query_pos, key_pos, query_start, score_scale)
        - log_total[..., None]
    )
    grad_weight = jnp.einsum(
        "qshe,kshe->shqk", grad_heads, value_piece, preferred_element_type=jnp.float32
    )
    grad_score = (weights * (grad_weight - row_delta[..., None])).astype(jnp.bfloat16)
    key_part = (
        jnp.einsum("shqk,qshe->kshe", grad_score, query, preferred_element_type=jnp.float32)
        * score_scale
    )
    value_part = jnp.einsum(
        "shqk,qshe->kshe",
        weights.astype(jnp.bfloat16),
        grad_heads,
        preferred_element_type=jnp.float32,
    )
    return (key_part, value_part)


def shards(
    tokens,
    doc_starts,
    expert_ids,
    query_key_value_weight,
    output_weight_matrix,
    expert_in,
    expert_out,
    gain_one,
    gain_two,
    grad_output,
):
    seq_dev = tokens.shape[0]
    half_rows = tokens.shape[3]
    model_width = tokens.shape[4]
    local_rows = 2 * half_rows
    ctx_count = lax.axis_size("ctx")
    head_count = HEADS
    head_size = model_width // head_count
    score_scale = head_size ** (-0.5)
    keys_total = ctx_count * local_rows
    key_block = min(512, keys_total)
    own_rows = lax.axis_index("ctx") * local_rows + jnp.arange(local_rows, dtype=jnp.int32)
    query_pos = position_of(own_rows, ctx_count, half_rows)
    query_start = doc_starts.reshape(seq_dev, local_rows).T
    routes_local = expert_ids.reshape(seq_dev, local_rows).T
    start_x = (
        tokens.reshape(seq_dev, local_rows, model_width).transpose(1, 0, 2).astype(jnp.float32)
    )
    cotangent = grad_output.reshape(seq_dev, local_rows, model_width).transpose(1, 0, 2)
    projection, out_proj = (
        lax.all_gather(query_key_value_weight.astype(jnp.bfloat16), "fsdp", axis=0, tiled=True),
        lax.all_gather(output_weight_matrix.astype(jnp.bfloat16), "fsdp", axis=0, tiled=True),
    )
    first_normed_rows, hat_one, inverse_one = norm_forward(start_x, gain_one)
    normed_low = first_normed_rows.astype(jnp.bfloat16)
    projected_rows = jnp.einsum(
        "tsd,de->tse", normed_low, projection, preferred_element_type=jnp.float32
    ).astype(jnp.bfloat16)
    query = projected_rows[..., :model_width]
    keys = projected_rows[..., model_width : 2 * model_width]
    values = projected_rows[..., 2 * model_width :]
    key_all, value_all = (
        lax.all_gather(keys, "ctx", axis=0, tiled=True),
        lax.all_gather(values, "ctx", axis=0, tiled=True),
    )
    query_heads = query.reshape(local_rows, seq_dev, head_count, head_size)
    key_heads = key_all.reshape(keys_total, seq_dev, head_count, head_size)
    value_heads = value_all.reshape(keys_total, seq_dev, head_count, head_size)
    log_total = log_totals(
        query_heads, key_heads, query_pos, query_start, score_scale, ctx_count, half_rows, key_block
    )
    mixed_heads_out, remainder = attend(
        query_heads,
        key_heads,
        value_heads,
        query_pos,
        query_start,
        log_total,
        score_scale,
        ctx_count,
        half_rows,
        key_block,
    )
    mixed_low = mixed_heads_out.astype(jnp.bfloat16).reshape(local_rows, seq_dev, model_width)
    attention_rows_out = jnp.einsum(
        "tsd,de->tse", mixed_low, out_proj, preferred_element_type=jnp.float32
    )
    middle = start_x + attention_rows_out
    normed_two, hat_two, inverse_two = norm_forward(middle, gain_two)
    routed = normed_two.astype(jnp.bfloat16)
    slot_count = EXPERTS * CAP
    per_owner = EXPERTS // ctx_count
    chosen = (routes_local[..., None] == jnp.arange(EXPERTS, dtype=jnp.int32)).astype(jnp.int32)
    earlier = (
        jnp.arange(local_rows)[:, None] >= jnp.arange(local_rows)[None, :]
    ).astype(jnp.bfloat16)
    running = jnp.einsum(
        "tu,use->tse", earlier, chosen.astype(jnp.bfloat16), preferred_element_type=jnp.float32
    )
    rank_within = jnp.sum(chosen * running.astype(jnp.int32), axis=-1) - 1
    slot_index = routes_local * CAP + rank_within
    dispatch = (
        slot_index.T[:, None, :] == jnp.arange(slot_count, dtype=jnp.int32)[None, :, None]
    ).astype(jnp.bfloat16)
    dispatch = dispatch.reshape(seq_dev, ctx_count, per_owner, CAP, local_rows)
    send_rows = jnp.einsum(
        "snect,tsd->nescd", dispatch, routed, preferred_element_type=jnp.float32
    ).astype(jnp.bfloat16)
    send_grads = jnp.einsum(
        "snect,tsd->nescd", dispatch, cotangent, preferred_element_type=jnp.float32
    ).astype(jnp.bfloat16)
    got_rows, got_grads = (
        lax.all_to_all(send_rows, "ctx", split_axis=0, concat_axis=0, tiled=True),
        lax.all_to_all(send_grads, "ctx", split_axis=0, concat_axis=0, tiled=True),
    )
    in_low = expert_in.astype(jnp.bfloat16)
    out_low = expert_out.astype(jnp.bfloat16)
    all_rows, all_grads = (
        lax.all_gather(got_rows, "fsdp", axis=2, tiled=True),
        lax.all_gather(got_grads, "fsdp", axis=2, tiled=True),
    )
    hidden = jnp.einsum("nercd,edf->nercf", all_rows, in_low, preferred_element_type=jnp.float32)
    active = jax.nn.gelu(hidden).astype(jnp.bfloat16)
    partial_rows = jnp.einsum(
        "nercf,efd->nercd", active, out_low, preferred_element_type=jnp.float32
    )
    result = lax.psum_scatter(
        partial_rows.astype(jnp.bfloat16), "fsdp", scatter_dimension=2, tiled=True
    )
    upstream = jnp.einsum(
        "nercd,efd->nercf", all_grads, out_low, preferred_element_type=jnp.float32
    )
    unused, gelu_back = jax.vjp(jax.nn.gelu, hidden)
    grad_hidden = gelu_back(upstream)[0].astype(jnp.bfloat16)
    grad_in = jnp.einsum(
        "nercd,nercf->edf", all_rows, grad_hidden, preferred_element_type=jnp.float32
    )
    grad_outw = jnp.einsum(
        "nercf,nercd->efd", active, all_grads, preferred_element_type=jnp.float32
    )
    row_part = jnp.einsum(
        "nercf,edf->nercd", grad_hidden, in_low, preferred_element_type=jnp.float32
    )
    row_grad = lax.psum_scatter(row_part, "fsdp", scatter_dimension=2, tiled=True).astype(
        jnp.bfloat16
    )
    back_rows = lax.all_to_all(result, "ctx", split_axis=0, concat_axis=0, tiled=True)
    expert_sum = jnp.einsum(
        "snect,nescd->tsd", dispatch, back_rows, preferred_element_type=jnp.float32
    )
    output_rows = middle + expert_sum
    returned = lax.all_to_all(row_grad, "ctx", split_axis=0, concat_axis=0, tiled=True)
    grad_routed = jnp.einsum(
        "snect,nescd->tsd", dispatch, returned, preferred_element_type=jnp.float32
    )
    grad_mid_norm, grad_gain_two = norm_backward(grad_routed, hat_two, inverse_two, gain_two)
    grad_middle = cotangent.astype(jnp.float32) + grad_mid_norm
    grad_attn = grad_middle.astype(jnp.bfloat16)
    grad_outproj = jnp.einsum(
        "tsd,tse->de", mixed_low, grad_attn, preferred_element_type=jnp.float32
    )
    grad_mixed = jnp.einsum(
        "tse,de->tsd", grad_attn, out_proj, preferred_element_type=jnp.float32
    ).astype(jnp.bfloat16)
    grad_heads = grad_mixed.reshape(local_rows, seq_dev, head_count, head_size)
    full_mixed = mixed_heads_out + remainder
    row_delta = jnp.sum(grad_heads.astype(jnp.float32) * full_mixed, axis=-1).transpose(1, 2, 0)
    grad_query = query_grads(
        query_heads,
        key_heads,
        value_heads,
        grad_heads,
        query_pos,
        query_start,
        log_total,
        row_delta,
        score_scale,
        ctx_count,
        half_rows,
        key_block,
    ).astype(jnp.bfloat16)
    sub_rows = math.gcd(local_rows * lax.axis_size("ctx"), key_block)

    def one_piece(piece_index):
        piece_start = piece_index * sub_rows
        key_piece = lax.dynamic_slice_in_dim(key_heads, piece_start, sub_rows, 0)
        value_piece = lax.dynamic_slice_in_dim(value_heads, piece_start, sub_rows, 0)
        key_pos = position_of(
            piece_start + jnp.arange(sub_rows, dtype=jnp.int32), ctx_count, half_rows
        )
        key_part, value_part = key_grads(
            query_heads,
            grad_heads,
            query_pos,
            query_start,
            log_total,
            row_delta,
            key_piece,
            value_piece,
            key_pos,
            score_scale,
        )
        return jnp.concatenate(
            [
                key_part.reshape(sub_rows, seq_dev, model_width),
                value_part.reshape(sub_rows, seq_dev, model_width),
            ],
            axis=-1,
        )

    summed = lax.psum_scatter(
        lax.map(
            one_piece, jnp.arange(local_rows * lax.axis_size("ctx") // sub_rows, dtype=jnp.int32)
        ).reshape(local_rows * lax.axis_size("ctx"), seq_dev, 2 * model_width),
        "ctx",
        scatter_dimension=0,
        tiled=True,
    )
    grad_key = summed[..., :model_width].astype(jnp.bfloat16)
    grad_value = summed[..., model_width:].astype(jnp.bfloat16)
    grad_projected = jnp.concatenate(
        [grad_query.reshape(local_rows, seq_dev, model_width), grad_key, grad_value], axis=-1
    )
    grad_projection = jnp.einsum(
        "tsd,tse->de", normed_low, grad_projected, preferred_element_type=jnp.float32
    )
    grad_normed = jnp.einsum(
        "tse,de->tsd", grad_projected, projection, preferred_element_type=jnp.float32
    )
    grad_in_norm, grad_gain_one = norm_backward(grad_normed, hat_one, inverse_one, gain_one)
    grad_start = grad_middle + grad_in_norm
    shard_proj, shard_outproj, shard_gain_one, shard_gain_two = (
        lax.psum_scatter(
            grad_projection.astype(jnp.bfloat16), "fsdp", scatter_dimension=0, tiled=True
        ).astype(jnp.float32),
        lax.psum_scatter(
            grad_outproj.astype(jnp.bfloat16), "fsdp", scatter_dimension=0, tiled=True
        ).astype(jnp.float32),
        lax.psum_scatter(
            grad_gain_one.astype(jnp.bfloat16), "fsdp", scatter_dimension=0, tiled=True
        ).astype(jnp.float32),
        lax.psum_scatter(
            grad_gain_two.astype(jnp.bfloat16), "fsdp", scatter_dimension=0, tiled=True
        ).astype(jnp.float32),
    )
    shard_proj, shard_outproj, shard_gain_one, shard_gain_two = (
        lax.psum(shard_proj.astype(jnp.bfloat16), "ctx").astype(jnp.float32),
        lax.psum(shard_outproj.astype(jnp.bfloat16), "ctx").astype(jnp.float32),
        lax.psum(shard_gain_one.astype(jnp.bfloat16), "ctx").astype(jnp.float32),
        lax.psum(shard_gain_two.astype(jnp.bfloat16), "ctx").astype(jnp.float32),
    )
    block_out = output_rows.transpose(1, 0, 2).reshape(tokens.shape).astype(jnp.bfloat16)
    grad_tokens = grad_start.transpose(1, 0, 2).reshape(tokens.shape)
    return (
        block_out,
        grad_tokens,
        shard_proj,
        shard_outproj,
        grad_in,
        grad_outw,
        shard_gain_one,
        shard_gain_two,
    )


BF = jnp.bfloat16
F32 = jnp.float32
CONTRACT_FIRST = (((0,), (0,)), ((), ()))
CONTRACT_LAST = (((1,), (1,)), ((), ()))
MESH_ID = pl.DeviceIdType.MESH
ANY = pl.BlockSpec(memory_space=pl.ANY)
DMA = pltpu.SemaphoreType.DMA
VMEM_CAP = 56 << 20


def place():
    c = lax.axis_index("ctx")
    f = lax.axis_index("fsdp")
    return c, f, c // 2, c % 2, f // 2, f % 2


def remote(src, dst, send, recv, device):
    return pltpu.make_async_remote_copy(
        src_ref=src, dst_ref=dst, send_sem=send, recv_sem=recv, device_id=device, device_id_type=MESH_ID
    )


def block_at(c, half, count):
    return c if half == 0 else 2 * count - 1 - c


def statistics(value):
    row_mean = jnp.mean(value, axis=1, keepdims=True)
    centred = value - row_mean
    inverse = lax.rsqrt(jnp.mean(centred * centred, axis=1, keepdims=True) + EPS)
    return centred * inverse, inverse


def stacked(value):
    return value.reshape(-1, value.shape[-1])


def relative(a, b):
    return (a // 2 + b // 2) % 2 * 2 + (a + b) % 2


def swap(value, axis, bit):
    size = lax.axis_size(axis)
    return lax.ppermute(value, axis, [(i, i ^ bit) for i in range(size)])


def lasting(microseconds):
    return pl.CostEstimate(flops=0, bytes_accessed=int(microseconds * 3.3e6), transcendentals=0)


def params(side=True):
    return pltpu.CompilerParams(has_side_effects=side, vmem_limit_bytes=VMEM_CAP)


def gather_stream(tokens, gain, routes, cotangent, starts, weight, matrix):
    count = lax.axis_size("ctx")
    depth = count // 2
    rows, wide = weight.shape
    part = wide // count
    lanes = part // 3
    half_rows, width = tokens.shape[1:]
    own_rows = 2 * half_rows
    own_experts = EXPERTS // count

    def kernel(
        x_ref, g_ref, e_ref, c_ref, s_ref, wide_ref, matrix_ref, tok, st, cols, beside, far, diagonal, d_ref, w_ref, o_ref, hot,
        n_ref, wf_ref, of_ref, loads, rs_t, ss_p, ss_up, ss_dn, ss_sib, rs_s, ss_s, rs_w, ss_w, ss_o, rs_o,
    ):
        c, f, z, y, x, k = place()
        sib = (c, f + 1 - 2 * k)
        partner = (c + 1 - 2 * y, f + 1 - 2 * k)
        up = (c + 2, f)
        down = (c - 2, f)
        holder = k == y
        load_weight = pltpu.make_async_copy(wide_ref, wf_ref, loads.at[0])
        load_matrix = pltpu.make_async_copy(matrix_ref, of_ref, loads.at[1])
        load_weight.start()
        load_matrix.start()
        for h in range(2):
            hat, _ = statistics(x_ref[h].astype(F32))
            n_ref[h] = (hat * g_ref[...]).astype(BF)

        def send_in(h):
            b = block_at(c, h, count)
            return remote(n_ref.at[h], tok.at[b], ss_p.at[h], rs_t.at[b], partner)

        def local_in(h):
            b = block_at(c, h, count)
            return pltpu.make_async_copy(n_ref.at[h], tok.at[b], rs_t.at[b])

        @pl.when(holder)
        def _():
            for h in range(2):
                local_in(h).start()

        @pl.when(jnp.logical_not(holder))
        def _():
            for h in range(2):
                send_in(h).start()

        for zt in range(depth):
            for kt in range(2):
                mine = holder & (z == zt) & (k == kt)

                @pl.when(mine)
                def _():
                    pltpu.make_async_copy(s_ref, st.at[c], rs_s.at[c]).start()

                @pl.when(jnp.logical_not(mine))
                def _(zt=zt, kt=kt):
                    remote(s_ref, st.at[c], ss_s.at[2 * zt + kt], rs_s.at[c], (2 * zt + k, 2 * x + kt)).start()

        goals = [(2 * z + k, (c, (f + 2) % 4)), (2 * z + 1 - k, (c, (sib[1] + 2) % 4)), (2 * z + 1 - k, sib)]

        def columns(pair):
            return w_ref.at[:, pl.ds(pl.multiple_of(pair * part, part), part)]

        def weight_place(shard):
            return cols.at[pl.ds(pl.multiple_of(shard * rows, rows), rows)]

        def weight_send(t):
            pair, dev = goals[t]
            return remote(columns(pair), weight_place(f), ss_w.at[t], rs_w.at[f], dev)

        load_weight.wait()
        for number in range(count):
            for j in range(3):
                at = number * part + j * lanes
                w_ref[:, at : at + lanes] = wf_ref[:, j * count * lanes + number * lanes :][:, :lanes].astype(BF)
        for t in range(3):
            weight_send(t).start()
        pltpu.make_async_copy(columns(2 * z + k), weight_place(f), rs_w.at[f]).start()
        load_matrix.wait()
        o_ref[...] = of_ref[...].astype(BF)
        matrix_far = remote(o_ref, far, ss_o.at[0], rs_o.at[0], goals[0][1])
        matrix_beside = remote(o_ref, beside, ss_o.at[1], rs_o.at[1], sib)
        matrix_on = remote(far, diagonal, ss_o.at[2], rs_o.at[2], sib)
        matrix_far.start()
        matrix_beside.start()

        def copy_block(zb, h, ss, dev):
            b = block_at(2 * zb + k, h, count)
            return remote(tok.at[b], tok.at[b], ss, rs_t.at[b], dev)

        for j in range(depth):
            for h in range(2):
                if j == 0:
                    copy_block(z, h, ss_p.at[h], sib).wait_recv()

                    @pl.when(z < depth - 1)
                    def _(h=h):
                        copy_block(z, h, ss_up.at[0, h], up).start()

                    @pl.when(z > 0)
                    def _(h=h):
                        copy_block(z, h, ss_dn.at[0, h], down).start()

                    copy_block(z, h, ss_sib.at[z, h], sib).start()
                    if h == 1:
                        expert = lax.broadcasted_iota(jnp.int32, (EXPERTS, own_rows), 0)
                        chosen = expert == e_ref[...]
                        earlier = lax.broadcasted_iota(jnp.int32, (own_rows, own_rows), 0) <= lax.broadcasted_iota(
                            jnp.int32, (own_rows, own_rows), 1
                        )
                        running = jnp.dot(
                            jnp.where(chosen, 1.0, 0.0).astype(BF),
                            jnp.where(earlier, 1.0, 0.0).astype(BF),
                            preferred_element_type=F32,
                        )
                        rank = jnp.sum(jnp.where(chosen, running, 0.0), axis=0, keepdims=True).astype(jnp.int32) - 1
                        slot = e_ref[...] * CAP + rank
                        index = lax.broadcasted_iota(jnp.int32, (EXPERTS * CAP, own_rows), 0)
                        hot[...] = jnp.where(index == slot, 1.0, 0.0).astype(BF)
                        d_ref[...] = (
                            jnp.dot(hot[...], c_ref[...], preferred_element_type=F32).astype(BF).reshape(d_ref.shape)
                        )
                    continue

                @pl.when(z - j >= 0)
                def _(j=j, h=h):
                    copy_block(z - j, h, ss_p.at[h], sib).wait_recv()

                    @pl.when(z < depth - 1)
                    def _():
                        copy_block(z - j, h, ss_up.at[j, h], up).start()

                    copy_block(z - j, h, ss_sib.at[z - j, h], sib).start()

                @pl.when(z + j <= depth - 1)
                def _(j=j, h=h):
                    copy_block(z + j, h, ss_p.at[h], sib).wait_recv()

                    @pl.when(z > 0)
                    def _():
                        copy_block(z + j, h, ss_dn.at[j, h], down).start()

                    copy_block(z + j, h, ss_sib.at[z + j, h], sib).start()

        matrix_far.wait_recv()
        matrix_on.start()
        for zt in range(depth):
            for h in range(2):
                b = block_at(2 * zt + 1 - k, h, count)
                remote(tok.at[b], tok.at[b], ss_p.at[h], rs_t.at[b], sib).wait_recv()
                copy_block(zt, h, ss_sib.at[zt, h], sib).wait_send()
        for ct in range(count):
            remote(s_ref, st.at[ct], ss_s.at[0], rs_s.at[ct], sib).wait_recv()
        for shard in range(4):
            remote(columns(0), weight_place(shard), ss_w.at[0], rs_w.at[shard], sib).wait_recv()
        for t in range(3):
            weight_send(t).wait_send()
        matrix_far.wait_send()
        matrix_beside.wait()
        matrix_on.wait()

        @pl.when(jnp.logical_not(holder))
        def _():
            for h in range(2):
                send_in(h).wait_send()

        for j in range(depth):

            @pl.when((z < depth - 1) & (z - j >= 0))
            def _(j=j):
                for h in range(2):
                    copy_block(z - j, h, ss_up.at[j, h], up).wait_send()

            @pl.when((z > 0) & (z + j <= depth - 1))
            def _(j=j):
                for h in range(2):
                    copy_block(z + j, h, ss_dn.at[j, h], down).wait_send()

        for zt in range(depth):
            for kt in range(2):
                mine = holder & (z == zt) & (k == kt)

                @pl.when(jnp.logical_not(mine))
                def _(zt=zt, kt=kt):
                    remote(s_ref, st.at[c], ss_s.at[2 * zt + kt], rs_s.at[c], sib).wait_send()

    return pl.pallas_call(
        kernel,
        name="gather_stream",
        cost_estimate=lasting(50),
        out_shape=(
            jax.ShapeDtypeStruct((2 * count, half_rows, width), BF),
            jax.ShapeDtypeStruct((count,) + starts.shape, starts.dtype),
            jax.ShapeDtypeStruct((4 * rows, part), BF),
            *[jax.ShapeDtypeStruct(matrix.shape, BF)] * 3,
            jax.ShapeDtypeStruct((count, own_experts, CAP, width), BF),
            jax.ShapeDtypeStruct((rows, wide), BF),
            jax.ShapeDtypeStruct(matrix.shape, BF),
            jax.ShapeDtypeStruct((EXPERTS * CAP, own_rows), BF),
        ),
        in_specs=[pl.BlockSpec(memory_space=pltpu.VMEM)] * 5 + [ANY] * 2,
        out_specs=(ANY,) * 6 + (pl.BlockSpec(memory_space=pltpu.VMEM),) * 4,
        scratch_shapes=[
            pltpu.VMEM((2, half_rows, width), BF), pltpu.VMEM((rows, wide), F32), pltpu.VMEM(matrix.shape, F32), DMA((2,)),
            DMA((2 * count,)), DMA((2,)), DMA((depth, 2)), DMA((depth, 2)), DMA((depth, 2)),
            DMA((count,)), DMA((count,)), DMA((4,)), DMA((3,)), DMA((3,)), DMA((3,)),
        ],
        compiler_params=params(),
    )(tokens, gain, routes, cotangent, starts, weight, matrix)


TILE = 256


def halves(value, axis):
    size = value.shape[axis] // 2
    at = lax.broadcasted_iota(jnp.int32, value.shape, axis)
    zero = jnp.zeros_like(value)
    return [jnp.where(at < size, value, zero), jnp.where(at >= size, value, zero)]


def attend_forward(stream, columns, start_row, numbers, scale):
    length, width = stream.shape
    tiles = length // TILE
    lanes = 128
    size = lanes // 2

    def kernel(first, x_ref, w_ref, s_ref, out, m16, m32, lse, k_rows, v_turned):
        i = pl.program_id(0)
        own = pl.ds(pl.multiple_of(i * TILE, TILE), TILE)
        rows = x_ref[...]
        projected = jnp.dot(rows, w_ref[...], preferred_element_type=F32).astype(BF)
        out[...] = projected
        query, key, value = [projected[:, j * lanes : (j + 1) * lanes] for j in range(3)]
        k_rows[own, :] = key
        v_turned[:, own] = value.T
        queries = halves((query * scale).T, 0)
        start = s_ref[...]
        key_row = lax.broadcasted_iota(jnp.int32, (TILE, TILE), 0)
        query_column = i * TILE + lax.broadcasted_iota(jnp.int32, (TILE, TILE), 1)

        def step(j, carried):
            at = pl.multiple_of(j * TILE, TILE)
            keys = k_rows[pl.ds(at, TILE), :]
            seen = (key_row + at <= query_column) & (key_row + at >= start)
            out = []
            for h in range(2):
                top, total, mixed = carried[h]
                score = jnp.where(seen, jnp.dot(keys, queries[h], preferred_element_type=F32), NEGATIVE)
                new_top = jnp.maximum(top, jnp.max(score, axis=0, keepdims=True))
                weight = jnp.exp(score - new_top)
                shrink = jnp.exp(top - new_top)
                total = total * shrink + jnp.sum(weight, axis=0, keepdims=True)
                values = v_turned[h * size : (h + 1) * size, pl.ds(at, TILE)]
                mixed = mixed * shrink + jnp.dot(values, weight.astype(BF), preferred_element_type=F32)
                out.append((new_top, total, mixed))
            return tuple(out)

        begin = (
            jnp.full((1, TILE), NEGATIVE, F32),
            jnp.zeros((1, TILE), F32),
            jnp.zeros((size, TILE), F32),
        )
        done = lax.fori_loop(first[i], i + 1, step, (begin, begin))
        mixed = jnp.concatenate([part / total for _, total, part in done], axis=0)
        m32[...] = mixed
        m16[...] = mixed.T.astype(BF)
        lse[...] = jnp.concatenate([top + jnp.log(total) for top, total, _ in done], axis=0)

    tile = pl.BlockSpec((TILE, lanes), lambda i, n: (i, 0))
    turned = pl.BlockSpec((lanes, TILE), lambda i, n: (0, i))
    return pl.pallas_call(
        kernel,
        name="attend_forward",
        cost_estimate=lasting(22),
        grid_spec=pltpu.PrefetchScalarGridSpec(
            num_scalar_prefetch=1,
            grid=(tiles,),
            in_specs=[
                pl.BlockSpec((TILE, width), lambda i, n: (i, 0)),
                pl.BlockSpec((width, 3 * lanes), lambda i, n: (0, 0)),
                pl.BlockSpec((1, TILE), lambda i, n: (0, i)),
            ],
            out_specs=[
                pl.BlockSpec((TILE, 3 * lanes), lambda i, n: (i, 0)),
                tile,
                turned,
                pl.BlockSpec((2, TILE), lambda i, n: (0, i)),
            ],
            scratch_shapes=[pltpu.VMEM((length, lanes), BF), pltpu.VMEM((lanes, length), BF)],
        ),
        out_shape=(
            jax.ShapeDtypeStruct((length, 3 * lanes), BF),
            jax.ShapeDtypeStruct((length, lanes), BF),
            jax.ShapeDtypeStruct((lanes, length), F32),
            jax.ShapeDtypeStruct((2, length), F32),
        ),
        compiler_params=params(False),
    )(numbers, stream, columns, start_row)


def backward_local(qkv, grad, mixed, logs, start_row, numbers, scale, stream, rows, cotangents, active, grad_hidden):
    length = qkv.shape[0]
    lanes = 128
    tiles = length // TILE
    size = lanes // 2
    _, number, count, cap, width = rows.shape
    total_rows, units = active.shape[1:]
    assert tiles == number

    def kernel(
        first, q_ref, k_ref, v_ref, g_ref, m_ref, l_ref, s_ref, x_ref, r_ref, g0_ref, g1_ref, a_ref, h_ref,
        out, weight, da, db, acc_k, acc_v, k_turned,
    ):
        i = pl.program_id(0)
        gradient = jnp.concatenate([stacked(g0_ref[...]), stacked(g1_ref[...])], axis=0)
        da[0] = lax.dot_general(stacked(r_ref[...]), h_ref[0], CONTRACT_FIRST, preferred_element_type=F32)
        db[0] = lax.dot_general(a_ref[0], gradient, CONTRACT_FIRST, preferred_element_type=F32)

        @pl.when(i == 0)
        def _():
            acc_k[...] = jnp.zeros_like(acc_k)
            acc_v[...] = jnp.zeros_like(acc_v)
            for t in range(tiles):
                k_turned[:, t * TILE : (t + 1) * TILE] = k_ref[t * TILE : (t + 1) * TILE, :].T

        scaled = q_ref[...] * scale
        grads = g_ref[...]
        turned = grads.T
        queries, queries_turned = halves(scaled, 1), halves(scaled.T, 0)
        grad_rows, grads_turned = halves(grads, 1), halves(turned, 0)
        product = turned.astype(F32) * m_ref[...]
        deltas = [jnp.sum(product[h * size : (h + 1) * size], axis=0, keepdims=True) for h in range(2)]
        logs_row = [l_ref[h : h + 1, :] for h in range(2)]
        start = s_ref[...]
        key_row = lax.broadcasted_iota(jnp.int32, (TILE, TILE), 0)
        query_column = i * TILE + lax.broadcasted_iota(jnp.int32, (TILE, TILE), 1)

        def step(j, running):
            at = pl.multiple_of(j * TILE, TILE)
            keys = k_ref[pl.ds(at, TILE), :]
            values = v_ref[pl.ds(at, TILE), :]
            seen = (key_row + at <= query_column) & (key_row + at >= start)
            key_sum = jnp.zeros((TILE, lanes), F32)
            value_sum = jnp.zeros((TILE, lanes), F32)
            out = []
            for h in range(2):
                score = jnp.dot(keys, queries_turned[h], preferred_element_type=F32)
                weight = jnp.exp(jnp.where(seen, score - logs_row[h], NEGATIVE))
                grad_weight = jnp.dot(values, grads_turned[h], preferred_element_type=F32)
                grad_score = (weight * (grad_weight - deltas[h])).astype(BF)
                value_sum += jnp.dot(weight.astype(BF), grad_rows[h], preferred_element_type=F32)
                key_sum += jnp.dot(grad_score, queries[h], preferred_element_type=F32)
                part = k_turned[h * size : (h + 1) * size, pl.ds(at, TILE)]
                out.append(running[h] + jnp.dot(part, grad_score, preferred_element_type=F32))
            acc_k[pl.ds(at, TILE), :] += key_sum
            acc_v[pl.ds(at, TILE), :] += value_sum
            return tuple(out)

        zero = jnp.zeros((size, TILE), F32)
        total = lax.fori_loop(first[i], i + 1, step, (zero, zero))
        own = pl.ds(pl.multiple_of(i * TILE, TILE), TILE)
        out[own, 0:lanes] = (jnp.concatenate(total, axis=0) * scale).T.astype(BF)

        @pl.when(i == tiles - 1)
        def _():
            out[:, lanes : 2 * lanes] = acc_k[...].astype(BF)
            out[:, 2 * lanes : 3 * lanes] = acc_v[...].astype(BF)
            weight[...] = lax.dot_general(x_ref[...], out[...], CONTRACT_FIRST, preferred_element_type=F32).astype(BF)

    tile = pl.BlockSpec((TILE, lanes), lambda i, n: (i, 0))
    quarter = pl.BlockSpec((count, 1, cap, width), lambda i, n: (0, i, 0, 0))
    wide = pl.BlockSpec((1, total_rows, units), lambda i, n: (i, 0, 0))
    return pl.pallas_call(
        kernel,
        name="backward_local",
        cost_estimate=lasting(30),
        grid_spec=pltpu.PrefetchScalarGridSpec(
            num_scalar_prefetch=1,
            grid=(tiles,),
            in_specs=[
                tile,
                pl.BlockSpec((length, lanes), lambda i, n: (0, 1)),
                pl.BlockSpec((length, lanes), lambda i, n: (0, 2)),
                tile,
                pl.BlockSpec((lanes, TILE), lambda i, n: (0, i)),
                pl.BlockSpec((2, TILE), lambda i, n: (0, i)),
                pl.BlockSpec((1, TILE), lambda i, n: (0, i)),
                pl.BlockSpec((length, width), lambda i, n: (0, 0), pipeline_mode=pl.Buffered(1)),
                pl.BlockSpec((4, 1, count, cap, width), lambda i, n: (0, i, 0, 0, 0)),
                quarter,
                pl.BlockSpec((3, count, 1, cap, width), lambda i, n: (0, 0, i, 0, 0)),
                wide,
                wide,
            ],
            out_specs=[
                pl.BlockSpec((length, 3 * lanes), lambda i, n: (0, 0)),
                pl.BlockSpec((width, 3 * lanes), lambda i, n: (0, 0)),
                pl.BlockSpec((1, width, units), lambda i, n: (i, 0, 0)),
                pl.BlockSpec((1, units, width), lambda i, n: (i, 0, 0)),
            ],
            scratch_shapes=[
                pltpu.VMEM((length, lanes), F32),
                pltpu.VMEM((length, lanes), F32),
                pltpu.VMEM((lanes, length), BF),
            ],
        ),
        out_shape=(
            jax.ShapeDtypeStruct((length, 3 * lanes), BF),
            jax.ShapeDtypeStruct((width, 3 * lanes), BF),
            jax.ShapeDtypeStruct((number, width, units), F32),
            jax.ShapeDtypeStruct((number, units, width), F32),
        ),
        compiler_params=params(False),
    )(numbers, qkv, qkv, qkv, grad, mixed, logs, start_row, stream, rows, *cotangents, active, grad_hidden)


ROOT = math.sqrt(2.0 / math.pi)
CUBIC = 0.044715


def experts_exchange(by_head, out_proj, tokens, dispatch, gain, cotangent, near, first_proj, second_proj):
    count = lax.axis_size("ctx")
    half_rows, lanes = by_head.shape[1:]
    rows, width = tokens.shape
    number, _, units = first_proj.shape
    cap = CAP
    total_rows = 4 * count * cap
    quarter = width // 4
    slab = quarter // count
    splits = 2
    part_units = units // splits

    def kernel(
        a_ref, m0_ref, m1_ref, m2_ref, m3_ref, x_ref, d_ref, g_ref, c_ref, g0_ref, first_ref, second_ref,
        mixed, middle, rows_out, g_ref_rest, active_out, hidden_out, heads, grad_middle, gain_out, later,
        w_refs, l_w, routed, slots, rows_v, g_buf, first_buf, second_buf, first_low, second_low, active_v, hidden_v, back_v, back_near, back_far, back_got,
        out_v, out_near, own_v, far_v, out_got, summed, home_got, back, shard_near, shard_far, shard_got, shard_v,
        ss_m, rs_m, ss_1, rs_1, ss_x, rs_x, ss_s, rs_s, ss_f, rs_f, ss_bn, rs_bn, ss_bf, rs_bf, ss_on, rs_on, ss_h, rs_h,
        ss_t, rs_t, ss_n, rs_n, ss_w, rs_w, ss_g, rs_g, l_first, l_second, l_g, st_r, st_a, st_h, st_o, ss_of, rs_of, st_w,
    ):
        c, f, z, y, x, k = place()
        sib = (c, f + 1 - 2 * k)
        xn = (c, (f + 2) % 4)
        pair = 2 * z + k
        target = 2 * x + y

        def load_first(e, u):
            cols = pl.ds(u * part_units, part_units)
            return pltpu.make_async_copy(first_ref.at[e, :, cols], first_buf.at[u], l_first.at[u])

        def load_second(e, u):
            part = pl.ds(u * part_units, part_units)
            return pltpu.make_async_copy(second_ref.at[e, part], second_buf.at[u], l_second.at[u])

        def load_grads(e, slot):
            return [
                pltpu.make_async_copy(g0_ref.at[:, e], g_buf.at[slot, 0], l_g.at[slot, 0]),
                pltpu.make_async_copy(g_ref_rest.at[:, :, e], g_buf.at[slot, pl.ds(1, 3)], l_g.at[slot, 1]),
            ]

        def two(e):
            return pl.ds(pl.multiple_of(e // 2 * 2, 2), 2)

        def grads_across(e):
            return remote(g0_ref.at[:, two(e)], g_ref_rest.at[1, :, two(e)], ss_g.at[0, e // 2], rs_g.at[0, e // 2], xn)

        def grads_share(e):
            return remote(g0_ref.at[:, two(e)], g_ref_rest.at[0, :, two(e)], ss_g.at[1, e // 2], rs_g.at[1, e // 2], sib)

        def grads_share_far(e):
            here, there_too = g_ref_rest.at[1, :, two(e)], g_ref_rest.at[2, :, two(e)]
            return remote(here, there_too, ss_g.at[2, e // 2], rs_g.at[2, e // 2], sib)

        def forward_grads(e):
            grads_across(e).wait_recv()
            grads_share_far(e).start()

        def start_load_grads(e, slot):
            @pl.when(e % 2 == 0)
            def _():
                grads_share(e).wait_recv()
                grads_share_far(e).wait_recv()

            for load in load_grads(e, slot):
                load.start()

        matrix_loads = [
            pltpu.make_async_copy(ref, w_refs.at[j], l_w.at[j]) for j, ref in enumerate((m0_ref, m1_ref, m2_ref, m3_ref))
        ]

        def there(half):
            column = (2 * relative(z, target) + k) * lanes
            return mixed.at[half, :, pl.ds(pl.multiple_of(column, lanes), lanes)]

        def send(i, half):
            ct = (c + i) % count
            return remote(
                a_ref.at[block_at(ct, half, count)], there(half), ss_m.at[i, half], rs_m.at[pair, half], (ct, target)
            )

        def keep(half):
            return pltpu.make_async_copy(a_ref.at[block_at(c, half, count)], there(half), rs_m.at[pair, half])

        for half in range(2):
            for i in range(1, count):
                send(i, half).start()

            @pl.when(k == y)
            def _(half=half):
                keep(half).start()

            @pl.when(k != y)
            def _(half=half):
                send(0, half).start()

        for load in matrix_loads:
            load.start()
        for u in range(splits):
            load_first(0, u).start()
            load_second(0, u).start()

        def start_grads(p, carry):
            grads_across(2 * p).start()
            grads_share(2 * p).start()
            return carry

        lax.fori_loop(0, number // 2, start_grads, 0)
        for load in matrix_loads:
            load.wait()
        for half in range(2):
            for other in range(count):
                column = (2 * relative(other // 2, f) + other % 2) * lanes
                cols = pl.ds(pl.multiple_of(column, lanes), lanes)
                remote(a_ref.at[0], mixed.at[half, :, cols], ss_m.at[0, half], rs_m.at[other, half], sib).wait_recv()
            here = pl.ds(half * half_rows, half_rows)
            value = x_ref[here, :].astype(F32)
            for j in range(4):
                cols = pl.ds(j * quarter, quarter)
                value += jnp.dot(mixed[half, :, cols], w_refs[j], preferred_element_type=F32)
            middle[here, :] = value
            hat, _ = statistics(value)
            routed[here, :] = (hat * g_ref[...]).astype(BF)
        slots[...] = jnp.dot(d_ref[...], routed[...], preferred_element_type=F32).astype(BF).reshape(slots.shape)

        def rows_first(e, i):
            owner = (c + i) % count
            return remote(slots.at[owner, two(e)], rows_v.at[0, two(e), c], ss_1.at[e // 2], rs_1.at[e // 2], (owner, f))

        def hop(e, rel, dst, send_sem, recv_sem, dev):
            return remote(rows_v.at[rel, e], rows_v.at[dst, e], send_sem.at[e], recv_sem.at[e], dev)

        def rows_across(e):
            return hop(e, 0, 2, ss_x, rs_x, xn)

        def rows_share(e):
            return hop(e, 0, 1, ss_s, rs_s, sib)

        def rows_share_far(e):
            return hop(e, 2, 3, ss_f, rs_f, sib)

        def start_rows(p, carry):
            for i in range(1, count):
                rows_first(2 * p, i).start()
            pltpu.make_async_copy(slots.at[c, two(2 * p)], rows_v.at[0, two(2 * p), c], rs_1.at[p]).start()
            return carry

        lax.fori_loop(0, number // 2, start_rows, 0)

        def forward(e):
            @pl.when(e % 2 == 0)
            def _():
                remote(rows_v.at[0, two(e)], rows_v.at[0, two(e)], ss_x.at[e], rs_1.at[e // 2], sib).wait_recv()

            rows_across(e).start()
            rows_share(e).start()

        def forward_far(e):
            rows_across(e).wait_recv()
            rows_share_far(e).start()

        def near_send(e):
            return remote(back_v.at[pl.ds(2, 2), e], back_near.at[:, e], ss_bn.at[e], rs_bn.at[e], sib)

        def near_out(e):
            return remote(out_v.at[pl.ds(2, 2), e], out_near.at[:, e], ss_on.at[e], rs_on.at[e], sib)

        def hold(ref, e, value):
            parts = value.astype(BF).reshape(4, count, cap, width)
            for at, rel in enumerate((0, 2, 1, 3)):
                ref[at, e] = parts[rel]

        def far_send(e):
            return remote(back_far.at[e], back_got.at[e], ss_bf.at[e], rs_bf.at[e], xn)

        def store_own(e):
            return pltpu.make_async_copy(own_v.at[e], later.at[:, pl.ds(pl.multiple_of(slab + e * cap, cap), cap)], st_o.at[e])

        def far_out(e):
            return remote(far_v.at[e], out_got.at[e], ss_of.at[e], rs_of.at[e], xn)

        def store_rows(e):
            return pltpu.make_async_copy(rows_v.at[:, e], rows_out.at[:, e], st_r.at[e])

        def store_active(e, slot):
            return pltpu.make_async_copy(active_v.at[slot], active_out.at[e], st_a.at[slot])

        def store_hidden(e, slot):
            return pltpu.make_async_copy(hidden_v.at[slot], hidden_out.at[e], st_h.at[slot])

        def sum_far(e):
            near_send(e).wait_recv()
            back_far[e] = (back_v[1, e].astype(F32) + back_near[1, e].astype(F32)).astype(BF)
            far_send(e).start()

        def sum_outputs(e):
            near_out(e).wait_recv()
            own_v[e] = (out_v[0, e].astype(F32) + out_near[0, e].astype(F32)).astype(BF)
            far_v[e] = (out_v[1, e].astype(F32) + out_near[1, e].astype(F32)).astype(BF)

        def home(e, i):
            ct = (c + i) % count
            return remote(summed.at[two(e), ct], home_got.at[c, two(e)], ss_h.at[e // 2], rs_h, (ct, f))

        def go_home(e):
            far_send(e).wait_recv()
            summed[e] = (
                back_v[0, e].astype(F32) + back_near[0, e].astype(F32) + back_got[e].astype(F32)
            ).astype(BF)

            @pl.when(e % 2 == 1)
            def _():
                for i in range(1, count):
                    home(e, i).start()
                pltpu.make_async_copy(summed.at[two(e), c], home_got.at[c, two(e)], rs_h).start()

        def expert(e, carry):
            slot = e % 2

            @pl.when(e >= 1)
            def _():
                sum_far(e - 1)

            @pl.when(e + 1 < number)
            def _():
                start_load_grads(e + 1, 1 - slot)

            rows_share(e).wait_recv()
            rows_share_far(e).wait_recv()
            store_rows(e).start()
            for load in load_grads(e, slot):
                load.wait()

            @pl.when(e >= 2)
            def _():
                store_active(e, slot).wait()
                store_hidden(e, slot).wait()

            row = rows_v[:, e].reshape(total_rows, width)
            grad = g_buf[slot].reshape(total_rows, width)
            term = jnp.zeros((total_rows, width), F32)
            for u in range(splits):
                load_first(e, u).wait()
                load_second(e, u).wait()
                first_low[u] = first_buf[u].astype(BF)
                second_low[u] = second_buf[u].astype(BF)

                @pl.when(e + 1 < number)
                def _(u=u):
                    load_first(e + 1, u).start()
                    load_second(e + 1, u).start()

                first, second = first_low[u], second_low[u]
                hidden = jnp.dot(row, first, preferred_element_type=F32)
                upstream = lax.dot_general(grad, second, CONTRACT_LAST, preferred_element_type=F32)
                bent = jnp.tanh(ROOT * (hidden + CUBIC * hidden * hidden * hidden))
                cols = pl.ds(u * part_units, part_units)
                active_v[slot, :, cols] = (0.5 * hidden * (1.0 + bent)).astype(BF)
                slope = 0.5 * (1.0 + bent) + 0.5 * hidden * (1.0 - bent * bent) * (
                    ROOT * (1.0 + 3.0 * CUBIC * hidden * hidden)
                )
                grad_hidden = (upstream * slope).astype(BF)
                hidden_v[slot, :, cols] = grad_hidden
                term += lax.dot_general(grad_hidden, first, CONTRACT_LAST, preferred_element_type=F32)
            hold(back_v, e, term)
            near_send(e).start()
            result = jnp.zeros((total_rows, width), F32)
            for u in range(splits):
                cols = pl.ds(u * part_units, part_units)
                result += jnp.dot(active_v[slot, :, cols], second_low[u], preferred_element_type=F32)
            hold(out_v, e, result)
            near_out(e).start()

            store_active(e, slot).start()
            store_hidden(e, slot).start()

            @pl.when(e + 3 < number)
            def _():
                forward(e + 3)

            @pl.when((e + 4 < number) & (e % 2 == 0))
            def _():
                forward_grads(e + 4)

            @pl.when(e + 2 < number)
            def _():
                forward_far(e + 2)

            @pl.when(e >= 1)
            def _():
                sum_outputs(e - 1)

            @pl.when(e >= 2)
            def _():
                go_home(e - 2)

            @pl.when(e >= number - 3)
            def _():
                far_out(e - (number - 3)).start()

            return carry

        forward_grads(0)
        forward(0)
        forward(1)
        start_load_grads(0, 0)
        forward_far(0)
        forward_grads(2)
        forward(2)
        forward_far(1)
        lax.fori_loop(0, number, expert, 0)
        sum_far(number - 1)
        sum_outputs(number - 1)
        far_out(3).start()
        for e in range(number - 2, number):
            go_home(e)
        for e in range(4, number):
            far_out(e).start()
        hat, inverse = statistics(middle[...])
        remote(home_got, home_got, ss_h.at[0], rs_h, sib).wait_recv()

        returned = lax.dot_general(d_ref[...], home_got[...].reshape(-1, width), CONTRACT_FIRST, preferred_element_type=F32)
        scaled = returned * g_ref[...]
        mean_grad = jnp.mean(scaled, axis=1, keepdims=True)
        mean_proj = jnp.mean(scaled * hat, axis=1, keepdims=True)
        gain_out[...] = jnp.sum(returned * hat, axis=0, keepdims=True)
        gradient = c_ref[...].astype(F32) + inverse * (scaled - mean_grad - hat * mean_proj)
        grad_middle[...] = gradient
        low = gradient.astype(BF)
        for j in range(4):
            back[:, :, j * quarter : (j + 1) * quarter] = (
                lax.dot_general(low, w_refs[j], CONTRACT_LAST, preferred_element_type=F32)
                .astype(BF)
                .reshape(2, half_rows, quarter)
            )

        def part(half, number_of_pair):
            column = (2 * relative(number_of_pair // 2, f) + number_of_pair % 2) * lanes
            return back.at[half, :, pl.ds(pl.multiple_of(column, lanes), lanes)]

        def send_heads(i, half):
            other = (2 * z + k + i) % count
            b = block_at(c, half, count)
            dev = (2 * (other // 2) + k, 2 * x + other % 2)
            return remote(part(half, other), heads.at[b], ss_t.at[i, half], rs_t.at[b], dev)

        for i in range(1, count):
            for half in range(2):
                send_heads(i, half).start()

        @pl.when(k == y)
        def _():
            for half in range(2):
                b = block_at(c, half, count)
                pltpu.make_async_copy(part(half, 2 * z + k), heads.at[b], rs_t.at[b]).start()

        @pl.when(k != y)
        def _():
            for half in range(2):
                send_heads(0, half).start()

        for e in range(number):
            near_send(e).wait_send()

        def shard_term(j):
            half_quarter = quarter // 2
            mixed_part = [mixed[half, :, j * quarter : (j + 1) * quarter] for half in range(2)]
            value = sum(
                lax.dot_general(
                    mixed_part[half], low[half * half_rows : (half + 1) * half_rows], CONTRACT_FIRST, preferred_element_type=F32
                )
                for half in range(2)
            )
            return value.astype(BF).reshape(shard_far.shape)

        sheet = pl.ds(0, quarter // (count * cap))
        core_send = remote(back_v.at[pl.ds(2, 2), sheet], shard_near, ss_n, rs_n, sib)
        across = remote(shard_far, shard_got, ss_w, rs_w, xn)
        for j in range(2):
            back_v[2 + j, sheet] = shard_term(2 * j + 1)
        core_send.start()
        own_far = shard_term(2)
        core_send.wait_recv()
        shard_far[...] = (own_far.astype(F32) + shard_near[1].astype(F32)).astype(BF)
        across.start()
        own_near = shard_term(0)

        def finish_output(e, carry):
            far_out(e).wait_recv()
            own_v[e] = (own_v[e].astype(F32) + out_got[e].astype(F32)).astype(BF)
            store_own(e).start()
            return carry

        lax.fori_loop(0, number, finish_output, 0)
        across.wait_recv()
        shard_v[...] = (
            (own_near.astype(F32) + shard_near[0].astype(F32) + shard_got[...].astype(F32)).astype(BF).reshape(shard_v.shape)
        )
        store_shard = pltpu.make_async_copy(shard_v, later.at[:, pl.ds(0, slab)], st_w)
        store_shard.start()

        for b in range(2 * count):
            remote(part(0, 0), heads.at[b], ss_t.at[0, 0], rs_t.at[b], sib).wait_recv()

        def leave(e, carry):
            rows_across(e).wait_send()
            rows_share(e).wait_send()
            rows_share_far(e).wait_send()
            far_send(e).wait_send()
            near_out(e).wait_send()
            store_own(e).wait()
            far_out(e).wait_send()
            store_rows(e).wait()
            return carry

        def leave_two(p, carry):
            sent = pl.ds(0, count - 1)
            first, last = slots.at[sent, two(2 * p)], summed.at[two(2 * p), sent]
            remote(first, first, ss_1.at[p], rs_1.at[p], sib).wait_send()
            remote(last, last, ss_h.at[p], rs_h, sib).wait_send()
            grads_across(2 * p).wait_send()
            grads_share(2 * p).wait_send()
            grads_share_far(2 * p).wait_send()
            return carry

        lax.fori_loop(0, number, leave, 0)
        lax.fori_loop(0, number // 2, leave_two, 0)
        store_shard.wait()
        for e in (number - 2, number - 1):
            store_active(e, e % 2).wait()
            store_hidden(e, e % 2).wait()
        for i in range(1, count):
            for half in range(2):
                send(i, half).wait_send()
                send_heads(i, half).wait_send()

        @pl.when(k != y)
        def _():
            for half in range(2):
                send(0, half).wait_send()
                send_heads(0, half).wait_send()

        core_send.wait_send()
        across.wait_send()

    vmem = pl.BlockSpec(memory_space=pltpu.VMEM)
    block = (count, cap, width)
    low = lambda *shape: pltpu.VMEM(shape, BF)
    fold = (quarter // (count * cap),) + block
    return pl.pallas_call(
        kernel,
        name="experts_exchange",
        cost_estimate=lasting(100),
        out_shape=(
            jax.ShapeDtypeStruct((2, half_rows, width), BF),
            jax.ShapeDtypeStruct((rows, width), F32),
            jax.ShapeDtypeStruct((4, number) + block, BF),
            jax.ShapeDtypeStruct((3,) + near.shape, BF),
            jax.ShapeDtypeStruct((number, total_rows, units), BF),
            jax.ShapeDtypeStruct((number, total_rows, units), BF),
            jax.ShapeDtypeStruct((2 * count, half_rows, lanes), BF),
            jax.ShapeDtypeStruct((rows, width), F32),
            jax.ShapeDtypeStruct((1, width), F32),
            jax.ShapeDtypeStruct((count, slab + number * cap, width), BF),
        ),
        in_specs=[ANY] * 5 + [vmem] * 4 + [ANY] * 3,
        out_specs=(vmem, vmem) + (ANY,) * 5 + (vmem, vmem, ANY),
        scratch_shapes=[
            low(4, quarter, width), DMA((4,)),
            low(rows, width), low(count, number, cap, width), low(4, number, *block), low(2, 4, *block),
            pltpu.VMEM((splits, width, part_units), F32), pltpu.VMEM((splits, part_units, width), F32),
            low(splits, width, part_units), low(splits, part_units, width),
            low(2, total_rows, units), low(2, total_rows, units),
            low(4, number, *block), low(2, number, *block), low(number, *block), low(number, *block),
            low(4, number, *block), low(2, number, *block), low(number, *block), low(number, *block), low(number, *block),
            low(number, *block), low(count, number, cap, width), low(2, half_rows, width),
            low(2, *fold), low(*fold), low(*fold), low(count, slab, width),
            DMA((count, 2)), DMA((count, 2)), DMA((number // 2,)), DMA((number // 2,)), DMA((number,)), DMA((number,)),
            DMA((number,)), DMA((number,)), DMA((number,)), DMA((number,)), DMA((number,)), DMA((number,)),
            DMA((number,)), DMA((number,)), DMA((number,)), DMA((number,)), DMA((number // 2,)), DMA,
            DMA((count, 2)), DMA((2 * count,)), DMA, DMA, DMA, DMA, DMA((3, number // 2)), DMA((3, number // 2)),
            DMA((splits,)), DMA((splits,)), DMA((2, 2)), DMA((number,)), DMA((2,)), DMA((2,)), DMA((number,)), DMA((number,)), DMA((number,)), DMA,
        ],
        compiler_params=pltpu.CompilerParams(has_side_effects=True, vmem_limit_bytes=60 << 20),
    )(by_head, *out_proj, tokens, dispatch, gain, cotangent, near, first_proj, second_proj)


def after(value, *others):
    return lax.optimization_barrier((value,) + others)[0]


def finish_exchange(grads, parts, slabs, gain_part, weight):
    count = lax.axis_size("ctx")
    depth = count // 2
    part = grads.shape[2]
    half_rows = grads.shape[1]
    _, rows, _ = parts.shape
    pieces = 4
    piece = rows // pieces
    slab = rows // count

    def kernel(
        a_ref, p_ref, home_ref, g_ref, w_ref, tok_out, w_out, o_out, g_out, w_all, h_ref, w_held, loads, o_ref, got, held, got_g, sum_g, got_gc,
        ss, rs, ss_r, rs_r, ss_up, ss_dn, rs_z, ss_a, ss_b, rs_o,
        ss_of, rs_of, ss_g, rs_g, ss_gc, rs_gc, ss_wx, rs_wx, ss_ws, rs_ws, ss_wf, rs_wf, loc,
    ):
        c, f, z, y, x, k = place()
        pair = 2 * z + k
        target = 2 * x + y
        sib = (c, f + 1 - 2 * k)
        xn = (c, (f + 2) % 4)
        up = (c + 2, f)
        down = (c - 2, f)

        def columns(ref, number):
            return ref.at[:, pl.ds(pl.multiple_of(number * part, part), part)]

        peers = [
            (2 * z + 1 - y, f, 2 * x + 1 - y),
            (c, (f + 2) % 4, 2 * (1 - x) + y),
            (2 * z + 1 - y, (f + 2) % 4, 2 * (1 - x) + 1 - y),
        ]

        def scatter(d):
            cp, fp, shard = peers[d]
            return remote(p_ref.at[shard], got.at[d], ss_r.at[d], rs_r.at[d], (cp, fp))

        for d in (2, 1, 0):
            scatter(d).start()
        load_slabs = pltpu.make_async_copy(home_ref.at[:, pl.ds(0, slab)], h_ref, loads.at[0])
        load_weight = pltpu.make_async_copy(w_ref, w_held, loads.at[1])
        load_slabs.start()
        load_weight.start()

        def weight_part(shard, i):
            return w_all.at[shard, pl.ds(i * piece, piece)]

        def weight_across(i):
            return remote(w_ref.at[pl.ds(i * piece, piece)], weight_part(f, i), ss_wx.at[i], rs_wx.at[i], xn)

        def weight_on(i, shard):
            return remote(weight_part(shard, i), weight_part(shard, i), ss_wf.at[i], rs_wf.at[i], sib)

        def weight_pass(i):
            shard = (f + 2) % 4
            remote(weight_part(shard, i), weight_part(shard, i), ss_wf.at[i], rs_wx.at[i], sib).wait_recv()
            weight_on(i, shard).start()

        weight_share = remote(w_ref, w_all.at[f], ss_ws, rs_ws, sib)
        weight_own = pltpu.make_async_copy(w_held, w_all.at[f], loc)
        for i in range(pieces):
            weight_across(i).start()

        def there(half):
            return columns(tok_out.at[half], pair)

        def send(i, half):
            ct = (c + i) % count
            return remote(a_ref.at[block_at(ct, half, count)], there(half), ss.at[i, half], rs.at[pair, half], (ct, target))

        def send_all(numbers):
            for i in numbers:
                for half in range(2):
                    send(i, half).start()

        send_all(range(2, count, 2))

        def gain_send(j):
            return remote(sum_g.at[j], got_g.at[j], ss_g.at[j], rs_g.at[j], sib if j == 0 else xn)

        sum_g[0] = g_ref[...]
        gain_send(0).start()

        def chain(zb, sem, dev):
            return remote(held.at[zb], held.at[zb], sem, rs_z.at[zb], dev)

        def own_column(zb):
            return remote(held.at[zb], columns(w_out, 2 * zb + k), ss_a.at[zb], rs_o.at[2 * zb + k], (c, target))

        def own_local(zb):
            return pltpu.make_async_copy(held.at[zb], columns(w_out, 2 * zb + k), rs_o.at[2 * zb + k])

        def next_column(zb):
            return remote(
                held.at[zb], columns(w_out, 2 * zb + k), ss_b.at[zb], rs_o.at[2 * zb + k], (2 * z + 1 - y, target)
            )

        def spread(zb):
            next_column(zb).start()

            @pl.when(k == y)
            def _():
                own_local(zb).start()

            @pl.when(k != y)
            def _():
                own_column(zb).start()

        total = p_ref[2 * x + y].astype(F32)
        for d in range(3):
            scatter(d).wait_recv()
            total += got[d].astype(F32)
        held[z] = total.astype(BF)

        @pl.when(z < depth - 1)
        def _():
            chain(z, ss_up.at[0], up).start()

        @pl.when(z > 0)
        def _():
            chain(z, ss_dn.at[0], down).start()

        spread(z)
        send_all(range(1, count, 2))

        @pl.when(k == y)
        def _():
            for half in range(2):
                pltpu.make_async_copy(a_ref.at[block_at(c, half, count)], there(half), rs.at[pair, half]).start()

        @pl.when(k != y)
        def _():
            for half in range(2):
                send(0, half).start()

        weight_share.start()
        load_weight.wait()
        weight_own.start()
        gain_send(0).wait_recv()
        sum_g[1] = sum_g[0] + got_g[0]
        gain_send(1).start()

        across_y = (c + 1 - 2 * y, f)

        def slab_send(i):
            zt = (z + i) % depth
            return remote(o_ref, o_out.at[c], ss_of.at[i], rs_of.at[c], (2 * zt + y, f))

        def slab_on(i):
            cs = 2 * ((z + i) % depth) + y
            src = o_out.at[cs] if i else o_ref
            return remote(src, o_out.at[cs], ss_of.at[depth + i], rs_of.at[cs], across_y)

        def gain_spread(i):
            return remote(sum_g.at[2], got_gc.at[c], ss_gc.at[i], rs_gc.at[c], ((c + i) % count, f))

        load_slabs.wait()
        slab_sum = h_ref[0].astype(F32)
        for i in range(1, count):
            slab_sum += h_ref[i].astype(F32)
        o_ref[...] = slab_sum.astype(BF)
        slab_own = pltpu.make_async_copy(o_ref, o_out.at[c], rs_of.at[c])
        slab_own.start()
        slab_on(0).start()
        for i in range(1, depth):
            slab_send(i).start()
        for hop in range(1, depth):

            @pl.when(z - hop >= 0)
            def _(hop=hop):
                chain(z - hop, ss_up.at[hop], sib).wait_recv()

                @pl.when(z < depth - 1)
                def _():
                    chain(z - hop, ss_up.at[hop], up).start()

                spread(z - hop)

            @pl.when(z + hop <= depth - 1)
            def _(hop=hop):
                chain(z + hop, ss_dn.at[hop], sib).wait_recv()

                @pl.when(z > 0)
                def _():
                    chain(z + hop, ss_dn.at[hop], down).start()

                spread(z + hop)

            weight_pass(hop - 1)
            if hop == 2:
                for i in range(1, depth):
                    cs = 2 * ((z + i) % depth) + y
                    remote(o_ref, o_out.at[cs], ss_of.at[i], rs_of.at[cs], sib).wait_recv()
                    slab_on(i).start()
            if hop == 1:
                gain_send(1).wait_recv()
                sum_g[2] = sum_g[1] + got_g[1]
                for i in range(1, count):
                    gain_spread(i).start()
        for i in range(depth - 1, pieces):
            weight_pass(i)
        total_g = sum_g[2]
        for i in range(1, count):
            cs = (c + i) % count
            remote(sum_g.at[2], got_gc.at[cs], ss_gc.at[i], rs_gc.at[cs], sib).wait_recv()
            total_g += got_gc[cs]
        g_out[...] = total_g

        gain_send(0).wait_send()
        gain_send(1).wait_send()
        for i in range(pieces):
            weight_across(i).wait_send()
            weight_on(i, (f + 2) % 4).wait_send()
            remote(weight_part(0, i), weight_part(0, i), ss_wf.at[i], rs_wf.at[i], sib).wait_recv()
        weight_share.wait()
        weight_own.wait()
        for d in range(3):
            scatter(d).wait_send()
        for other in range(count):
            for half in range(2):
                remote(a_ref.at[0], columns(tok_out.at[half], other), ss.at[0, half], rs.at[other, half], sib).wait_recv()
            remote(held.at[0], columns(w_out, other), ss_a.at[0], rs_o.at[other], sib).wait_recv()
        for i in range(1, count):
            for half in range(2):
                send(i, half).wait_send()
            gain_spread(i).wait_send()
        for i in range(depth):
            if i:
                slab_send(i).wait_send()
            slab_on(i).wait_send()
            cs = 2 * ((z + i) % depth) + 1 - y
            remote(o_ref, o_out.at[cs], ss_of.at[i], rs_of.at[cs], sib).wait_recv()
        slab_own.wait()

        @pl.when(k != y)
        def _():
            for half in range(2):
                send(0, half).wait_send()
            for zb in range(depth):
                own_column(zb).wait_send()

        for zb in range(depth):
            next_column(zb).wait_send()
        for hop in range(depth):

            @pl.when((z < depth - 1) & (z - hop >= 0))
            def _(hop=hop):
                chain(z - hop, ss_up.at[hop], up).wait_send()

            @pl.when((z > 0) & (z + hop <= depth - 1))
            def _(hop=hop):
                chain(z + hop, ss_dn.at[hop], down).wait_send()

    vmem = pl.BlockSpec(memory_space=pltpu.VMEM)
    eighth = gain_part.shape
    return pl.pallas_call(
        kernel,
        name="finish_exchange",
        cost_estimate=lasting(60),
        out_shape=(
            jax.ShapeDtypeStruct((2, half_rows, count * part), BF),
            jax.ShapeDtypeStruct((rows, count * part), BF),
            jax.ShapeDtypeStruct((count, slab, slabs.shape[2]), BF),
            jax.ShapeDtypeStruct(eighth, F32),
            jax.ShapeDtypeStruct((4,) + weight.shape, BF),
        ),
        in_specs=[vmem, vmem, ANY, vmem, ANY],
        out_specs=(ANY, ANY, ANY, vmem, ANY),
        scratch_shapes=[
            pltpu.VMEM((count, slab, slabs.shape[2]), BF), pltpu.VMEM(weight.shape, BF), DMA((2,)),
            pltpu.VMEM((slab, slabs.shape[2]), BF),
            pltpu.VMEM((3, rows, part), BF),
            pltpu.VMEM((depth, rows, part), BF),
            pltpu.VMEM((2,) + eighth, F32),
            pltpu.VMEM((3,) + eighth, F32),
            pltpu.VMEM((count,) + eighth, F32),
            DMA((count, 2)), DMA((count, 2)), DMA((3,)), DMA((3,)), DMA((depth,)), DMA((depth,)), DMA((depth,)),
            DMA((depth,)), DMA((depth,)), DMA((count,)),
            DMA((count,)), DMA((count,)), DMA((2,)), DMA((2,)), DMA((count,)), DMA((count,)),
            DMA((pieces,)), DMA((pieces,)), DMA, DMA, DMA((pieces,)), DMA((pieces,)), DMA,
        ],
        compiler_params=params(),
    )(grads, parts, slabs, gain_part, weight)


def finish_local(
    grad_projected, projection, tokens, gain, grad_middle, middle, dispatch, home, weight_grad, weight, out_slabs, gain_sum
):
    rows, width = tokens.shape
    quarter, wide = weight.shape
    lanes = 128
    part = 3 * lanes
    count = wide // part
    slot_rows = EXPERTS // count * CAP

    def kernel(p_ref, w_ref, x_ref, g_ref, m_ref, mid_ref, d_ref, e_ref, wg_ref, wl_ref, o_ref, gs_ref, block, token, wout, oout, gout, gout_two, acc):
        j = pl.program_id(0)
        own = pl.ds(pl.multiple_of(lax.axis_index("fsdp") * quarter, quarter), quarter)
        acc[j] = lax.dot_general(p_ref[...], w_ref[0], CONTRACT_LAST, preferred_element_type=F32)

        @pl.when(j == 0)
        def _():
            slots = e_ref[:, home.shape[1] - slot_rows :].reshape(-1, width)
            summed = lax.dot_general(d_ref[...], slots, CONTRACT_FIRST, preferred_element_type=F32)
            block[...] = (mid_ref[...] + summed).astype(BF)
            oout[...] = o_ref[...].astype(F32)

        @pl.when(j == 1)
        def _():
            total = jnp.zeros((quarter, 1), F32)
            for number in range(count):
                for kind in range(3):
                    at = number * part + kind * lanes
                    value = wg_ref[:, at : at + lanes].astype(F32)
                    to = (kind * count + number) * lanes
                    wout[:, to : to + lanes] = value
                    total += jnp.sum(value * wl_ref[:, at : at + lanes].astype(F32), axis=1, keepdims=True)
            gout[...] = jnp.broadcast_to(total, (quarter, lanes)).T[0:1] / g_ref[:, own]
            gout_two[...] = gs_ref[:, own]

        @pl.when(j == 3)
        def _():
            hat, inverse = statistics(x_ref[...].astype(F32))
            scaled = jnp.concatenate([acc[i] for i in range(4)], axis=1) * g_ref[...]
            mean_grad = jnp.mean(scaled, axis=1, keepdims=True)
            mean_proj = jnp.mean(scaled * hat, axis=1, keepdims=True)
            token[...] = m_ref[...] + inverse * (scaled - mean_grad - hat * mean_proj)

    def whole(value):
        return pl.BlockSpec(value.shape, lambda j: (0,) * value.ndim)

    shapes = (
        jax.ShapeDtypeStruct((rows, width), BF),
        jax.ShapeDtypeStruct((rows, width), F32),
        jax.ShapeDtypeStruct((quarter, wide), F32),
        jax.ShapeDtypeStruct((quarter, width), F32),
        jax.ShapeDtypeStruct((1, quarter), F32),
        jax.ShapeDtypeStruct((1, quarter), F32),
    )
    rest = (tokens, gain, grad_middle, middle, dispatch, home, weight_grad, weight, out_slabs, gain_sum)
    return pl.pallas_call(
        kernel,
        name="finish_local",
        cost_estimate=lasting(9),
        grid=(4,),
        in_specs=[whole(grad_projected), pl.BlockSpec((1, quarter, wide), lambda j: (j, 0, 0))] + [whole(v) for v in rest],
        out_specs=[whole(v) for v in shapes],
        out_shape=shapes,
        scratch_shapes=[pltpu.VMEM((4, rows, quarter), F32)],
        compiler_params=params(False),
    )(grad_projected, projection, *rest)


def by_head_pairs(
    tokens, doc_starts, expert_ids, query_key_value_weight, output_weight_matrix, expert_in, expert_out, gain_one, gain_two, grad_output
):
    half_rows = tokens.shape[3]
    width = tokens.shape[4]
    count = lax.axis_size("ctx")
    rows = 2 * half_rows
    length = count * rows
    scale = (width // HEADS) ** (-0.5)
    lanes = 2 * (width // HEADS)
    shard_rows = width // 4
    own_tokens = tokens.reshape(rows, width)
    cotangent = grad_output.reshape(rows, width)
    gain_row = gain_one.reshape(1, width)
    stream, starts, columns, out_beside, out_far, out_diagonal, send_grads, qkv_low, out_own, dispatch = gather_stream(
        own_tokens.reshape(2, half_rows, width),
        gain_row,
        expert_ids.reshape(1, rows),
        cotangent,
        doc_starts.reshape(2, half_rows),
        query_key_value_weight,
        output_weight_matrix,
    )
    grads_near = lax.all_to_all(send_grads, "ctx", split_axis=0, concat_axis=0, tiled=True)
    stream = stream.reshape(length, width)
    start_row = jnp.concatenate([starts[:, 0].reshape(-1), starts[::-1, 1].reshape(-1)])[None]
    numbers = jnp.min(start_row.reshape(-1, TILE), axis=1) // TILE
    qkv, mixed16, mixed32, logs = attend_forward(stream, columns, start_row, numbers, scale)
    grads_near = after(grads_near, mixed16)
    mixed, middle, all_rows, other_grads, active, grad_hidden, grad_heads, grad_middle, grad_gain_two, later = experts_exchange(
        mixed16.reshape(2 * count, half_rows, lanes),
        [out_own, out_beside, out_far, out_diagonal],
        own_tokens,
        dispatch,
        gain_two.reshape(1, width),
        cotangent,
        grads_near,
        expert_in,
        expert_out,
    )
    home = lax.all_to_all(later, "ctx", split_axis=0, concat_axis=0, tiled=True)
    own_grads, parts, grad_in, grad_outw = backward_local(
        qkv,
        after(grad_heads, later).reshape(length, lanes),
        mixed32,
        logs,
        start_row,
        numbers,
        scale,
        stream,
        all_rows,
        [grads_near, other_grads],
        active,
        grad_hidden,
    )
    home = after(home, own_grads)
    grad_projected, weight_grad, shard_out, gain_sum, projection = finish_exchange(
        own_grads.reshape(2 * count, half_rows, 3 * lanes),
        parts.reshape(4, shard_rows, 3 * lanes),
        home,
        grad_gain_two,
        qkv_low,
    )
    block_out, grad_start, weight_grad, shard_out, shard_gain_one, shard_gain_two = finish_local(
        grad_projected.reshape(rows, 3 * width),
        projection,
        own_tokens,
        gain_row,
        grad_middle,
        middle,
        dispatch,
        home,
        weight_grad,
        qkv_low,
        shard_out.reshape(shard_rows, width),
        gain_sum,
    )
    shard_gain_one = shard_gain_one.reshape(shard_rows)
    shard_gain_two = shard_gain_two.reshape(shard_rows)
    return (
        block_out.reshape(tokens.shape),
        grad_start.reshape(tokens.shape),
        weight_grad,
        shard_out,
        grad_in,
        grad_outw,
        shard_gain_one,
        shard_gain_two,
    )


def solution(mesh):
    pairs = mesh.shape["ctx"] * 2 == HEADS and mesh.shape["fsdp"] == 4
    return jax.shard_map(
        by_head_pairs if pairs else shards,
        mesh=mesh,
        in_specs=(
            P("fsdp", "ctx", None, None, None),
            P("fsdp", "ctx", None, None),
            P("fsdp", "ctx", None, None, None),
            P("fsdp", None),
            P("fsdp", None),
            P("ctx", None, "fsdp"),
            P("ctx", "fsdp", None),
            P(),
            P(),
            P("fsdp", "ctx", None, None, None),
        ),
        out_specs=(
            P("fsdp", "ctx", None, None, None),
            P("fsdp", "ctx", None, None, None),
            P("fsdp", None),
            P("fsdp", None),
            P("ctx", None, "fsdp"),
            P("ctx", "fsdp", None),
            P("fsdp"),
            P("fsdp"),
        ),
        check_vma=False,
    )
```
